32 devices in a mesh: shard: 8 (over z, x), seq: 4 (over y, core).
Axes of the slice: x: 2, y: 2, z: 4, core: 2. Of those that a mesh axis runs over, the one named last changes fastest.
Arguments:
- tokens: bfloat16 [8, 8, 512, 768], P(None, 'shard', 'seq'), may hold values from -6 to 6
- lengths: int32 [8], replicated, may hold values from 512 to 4096, as said below
- deal_order: int32 [8], replicated, may hold values from 0 to 7, as said below
- w_query: bfloat16 [768, 768], P('shard'), may hold values from -0.3125 to 0.3125
- w_key: bfloat16 [768, 768], P('shard'), may hold values from -0.3125 to 0.3125
- w_value: bfloat16 [768, 768], P('shard'), may hold values from -0.21875 to 0.21875
- w_output: bfloat16 [768, 768], P('shard'), may hold values from -0.625 to 0.625
- b_query: bfloat16 [768], P('shard'), may hold values from -4 to 4
- b_value: bfloat16 [768], P('shard'), may hold values from -4 to 4
- b_output: bfloat16 [768], P('shard'), may hold values from -4 to 4
- ln1_gain: bfloat16 [768], P('shard'), may hold values from 0.5 to 1.5
- ln1_shift: bfloat16 [768], P('shard'), may hold values from -4 to 4
- w_inner: bfloat16 [768, 3072], P('shard'), may hold values from -0.21875 to 0.21875
- b_inner: bfloat16 [3072], P('shard'), may hold values from -4 to 4
- w_outer: bfloat16 [3072, 768], P('shard'), may hold values from -0.15625 to 0.15625
- b_outer: bfloat16 [768], P('shard'), may hold values from -4 to 4
- ln2_gain: bfloat16 [768], P('shard'), may hold values from 0.5 to 1.5
- ln2_shift: bfloat16 [768], P('shard'), may hold values from -4 to 4
- cotangent: bfloat16 [8, 8, 512, 768], P('shard', None, 'seq'), may hold values from -6 to 6
Outputs:
- activations: bfloat16 [8, 8, 512, 768], P('shard', None, 'seq')
- d_tokens: bfloat16 [8, 8, 512, 768], P(None, 'shard', 'seq')
- d_w_query: float32 [768, 768], P('shard')
- d_w_key: float32 [768, 768], P('shard')
- d_w_value: float32 [768, 768], P('shard')
- d_w_output: float32 [768, 768], P('shard')
- d_b_query: float32 [768], P('shard')
- d_b_value: float32 [768], P('shard')
- d_b_output: float32 [768], P('shard')
- d_ln1_gain: float32 [768], P('shard')
- d_ln1_shift: float32 [768], P('shard')
- d_w_inner: float32 [768, 3072], P('shard')
- d_b_inner: float32 [3072], P('shard')
- d_w_outer: float32 [3072, 768], P('shard')
- d_b_outer: float32 [768], P('shard')
- d_ln2_gain: float32 [768], P('shard')
- d_ln2_shift: float32 [768], P('shard')
The draws below stay inside these ranges and needn't reach their ends.
Inputs may be any that keep to these rules, and one draw needn't show every extreme that they name: Sequence q has lengths[q] real tokens, the rest of its 4096 slots are padding; some sequence has exactly 4096. `deal_order`: each number 0 to 7 once.
All inputs are finite; a program needn't handle non-finite values.
Results may differ from the reference program's by a relative error of at most 0.018.
Values may be sent and summed in bfloat16 or wider, within the bound.
No kernel may reach another device: no remote copies, remote signals or barrier semaphores. Data moves between devices by JAX's collectives and lax.ppermute only.
A program may use at most 256 MiB of HBM per device.

```python
import math
import jax
import jax.numpy as jnp
from jax import lax

D = 768
HEADS = 12
HD = 64
FF = 3072
SLOT = 4096
MINLEN = 512
SEQS = 8
SPAN = 512
N_SHARD = 8
N_SEQ = 4


def length_table(key):
    inner_key = jax.random.fold_in(key, 11)
    first_key, second_key = jax.random.split(inner_key)
    drawn = jax.random.randint(first_key, (SEQS,), MINLEN, SLOT + 1, dtype=jnp.int32)
    longest = jax.random.randint(second_key, (), 0, SEQS, dtype=jnp.int32)
    return jnp.where(jnp.arange(SEQS, dtype=jnp.int32) == longest, SLOT, drawn).astype(jnp.int32)


def draw_lengths(key, part):
    return length_table(key)


def draw_deal_order(key, part):
    table = length_table(key)
    scores = table * SEQS + jnp.arange(SEQS, dtype=jnp.int32)
    ranked = jnp.argsort(-scores, stable=True).astype(jnp.int32)
    half_count = SEQS // 2
    longer = ranked[:half_count]
    shorter = ranked[half_count:][::-1]
    return jnp.stack([longer, shorter], axis=1).reshape(SEQS).astype(jnp.int32)


def steps_of(stream_key, dims, cuts, low, high):
    loudness, own = 1.0, jax.random.fold_in(stream_key, 6)
    for position, blocks in cuts:
        heights = jnp.exp(jax.random.uniform(jax.random.fold_in(own, position), (blocks,), jnp.float32, low / len(cuts), high / len(cuts)))
        loudness = loudness * jnp.repeat(heights, dims[position] // blocks).reshape([-1 if axis == position else 1 for axis in range(len(dims))])
    return loudness


def normal_values(rng, extent, scale, bound, pieces=(), held_as=jnp.bfloat16):
    factor_of = steps_of(rng, extent, pieces, -0.22, 0.18) if pieces else 1.0
    entries = jax.random.normal(rng, extent, jnp.float32) * scale * factor_of
    return jnp.minimum(jnp.maximum(entries, -bound), bound).astype(held_as)


def setup_inputs(seed: int = 0) -> dict:
    seeds = jax.random.split(jax.random.key(seed), 20)
    return {
        "tokens": normal_values(seeds[0], (SEQS, N_SHARD, SPAN, D), 1.0, 6.0, ((1, 8), (2, 4))),
        "lengths": draw_lengths(jax.random.fold_in(seeds[19], 71), 0),
        "deal_order": draw_deal_order(jax.random.fold_in(seeds[19], 71), 0),
        "w_query": normal_values(seeds[3], (D, D), (D // 2) ** -0.5, 0.3125, ((0, 8),)),
        "w_key": normal_values(seeds[4], (D, D), (D // 2) ** -0.5, 0.3125, ((0, 8),)),
        "w_value": normal_values(seeds[5], (D, D), D ** -0.5, 0.21875, ((0, 8),)),
        "w_output": normal_values(seeds[6], (D, D), (D // 8) ** -0.5, 0.625, ((0, 8),)),
        "b_query": normal_values(seeds[7], (D,), 0.3, 4.0, ((0, 8),)),
        "b_value": normal_values(seeds[8], (D,), 0.3, 4.0, ((0, 8),)),
        "b_output": normal_values(seeds[9], (D,), 0.3, 4.0, ((0, 8),)),
        "ln1_gain": jnp.clip(1.0 + 0.1 * jax.random.normal(seeds[10], (D,), jnp.float32), 0.5, 1.5).astype(jnp.bfloat16),
        "ln1_shift": normal_values(seeds[11], (D,), 0.3, 4.0, ((0, 8),)),
        "w_inner": normal_values(seeds[12], (D, FF), D ** -0.5, 0.21875, ((0, 8),)),
        "b_inner": normal_values(seeds[13], (FF,), 0.3, 4.0, ((0, 8),)),
        "w_outer": normal_values(seeds[14], (FF, D), (FF // 2) ** -0.5, 0.15625, ((0, 8),)),
        "b_outer": normal_values(seeds[15], (D,), 0.3, 4.0, ((0, 8),)),
        "ln2_gain": jnp.clip(1.0 + 0.1 * jax.random.normal(seeds[16], (D,), jnp.float32), 0.5, 1.5).astype(jnp.bfloat16),
        "ln2_shift": normal_values(seeds[17], (D,), 0.3, 4.0, ((0, 8),)),
        "cotangent": normal_values(seeds[18], (SEQS, N_SHARD, SPAN, D), 1.0, 6.0, ((0, 8), (2, 4))),
    }


@jax.custom_vjp
def low(v):
    return lax.optimization_barrier(v.astype(jnp.bfloat16)).astype(jnp.float32)

@jax.custom_vjp
def low_back(v):
    return v

def low_keep(v):
    return (low(v), None)

def low_pass(kept, grad):
    return (grad,)

def back_keep(v):
    return (v, None)

def back_low(kept, grad):
    return (low(grad),)
low.defvjp(low_keep, low_pass)
low_back.defvjp(back_keep, back_low)

def layer_norm(residual, ln_gain, ln_shift):
    centred = residual - lax.optimization_barrier(jnp.mean(residual, axis=-1, keepdims=True))
    variance = lax.optimization_barrier(jnp.mean(centred * centred, axis=-1, keepdims=True))
    return centred * lax.rsqrt(variance + 1e-12) * ln_gain + ln_shift

def project(left_side, right_side):
    return jnp.dot(left_side, right_side, precision=lax.Precision.HIGHEST)

def attend(packed):
    query_rows, key_rows, value_rows, length = packed
    scores = jnp.einsum('qhd,khd->hqk', query_rows, key_rows, precision=lax.Precision.HIGHEST) * (1.0 / math.sqrt(HD))
    counted = jnp.arange(SLOT, dtype=jnp.int32) < length
    scores = low_back(jnp.where(counted[None, None, :], scores, -1000000000.0))
    soft_probs = jax.nn.softmax(scores, axis=-1)
    return jnp.einsum('hqk,khd->qhd', low(soft_probs), value_rows, precision=lax.Precision.HIGHEST)

def whole_layer(flat_rows, params, slot_lengths):
    w_query, w_key, w_value, w_output, b_query, b_value, b_output, ln1_gain, ln1_shift, w_inner, b_inner, w_outer, b_outer, ln2_gain, ln2_shift = params
    query_rows = low_back(low(project(flat_rows, w_query) + b_query))
    key_rows = low_back(low(project(flat_rows, w_key)))
    value_rows = low_back(low(project(flat_rows, w_value) + b_value))
    mixed_rows = lax.map(jax.checkpoint(attend), (query_rows.reshape(SEQS, SLOT, HEADS, HD), key_rows.reshape(SEQS, SLOT, HEADS, HD), value_rows.reshape(SEQS, SLOT, HEADS, HD), slot_lengths))
    mixed_rows = low_back(low(mixed_rows.reshape(SEQS * SLOT, D)))
    branch = low_back(project(mixed_rows, w_output) + b_output)
    normed = layer_norm(flat_rows + branch, ln1_gain, ln1_shift)
    inner_pre = low_back(project(low(normed), w_inner) + b_inner)
    active = low(jax.nn.gelu(inner_pre, approximate=False))
    outer_out = low_back(project(active, w_outer) + b_outer)
    return layer_norm(normed + outer_out, ln2_gain, ln2_shift)

def reference(tokens, lengths, deal_order, w_query, w_key, w_value, w_output, b_query, b_value, b_output, ln1_gain, ln1_shift, w_inner, b_inner, w_outer, b_outer, ln2_gain, ln2_shift, cotangent):
    dealt = jnp.take(tokens, deal_order, axis=0).astype(jnp.float32).reshape(SEQS * SLOT, D)
    slot_lengths = jnp.take(lengths, deal_order, axis=0).astype(jnp.int32)
    params = tuple((tensor.astype(jnp.float32) for tensor in (w_query, w_key, w_value, w_output, b_query, b_value, b_output, ln1_gain, ln1_shift, w_inner, b_inner, w_outer, b_outer, ln2_gain, ln2_shift)))

    def layer_of(flat_rows, params_in):
        return whole_layer(flat_rows, params_in, slot_lengths)
    outputs, pullback = jax.vjp(layer_of, dealt, params)
    d_flat, d_params = pullback(cotangent.astype(jnp.float32).reshape(SEQS * SLOT, D))
    d_dealt = d_flat.astype(jnp.bfloat16).reshape(SEQS, N_SHARD, SPAN, D)
    d_tokens = jnp.zeros_like(d_dealt).at[deal_order].set(d_dealt)
    factor = 1.0 / (N_SHARD * N_SEQ)
    grads = tuple((gradient * factor for gradient in d_params))
    activations = outputs.astype(jnp.bfloat16).reshape(SEQS, N_SHARD, SPAN, D)
    return (activations, d_tokens, grads[0], grads[1], grads[2], grads[3], grads[4], grads[5], grads[6], grads[7], grads[8], grads[9], grads[10], grads[11], grads[12], grads[13], grads[14])
```

```python
import functools, math
import jax
import jax.numpy as jnp
from jax import lax
from jax.experimental import pallas as pl
from jax.experimental.pallas import tpu as pltpu
from jax.sharding import Mesh, PartitionSpec as P

f32, bf16 = jnp.float32, jnp.bfloat16
LOG2E = 1.4426950408889634
LN2 = 0.6931471805599453
CH = 512
BQ = 1024
RB = 256
HD = 64
FAR = -1.0e30

def dg(a, b, ca, cb):
    return lax.dot_general(a, b, (((ca,), (cb,)), ((), ())), preferred_element_type=f32)


def three_parts(row):
    hi = row.astype(bf16).astype(f32)
    rest = row - hi
    mid = rest.astype(bf16).astype(f32)
    return hi, mid, rest - mid


def with_shift(top, shift):
    hi, mid, low = three_parts(shift)
    row = lax.broadcasted_iota(jnp.int32, (HD, top.shape[1]), 0)
    tail = jnp.where(row == 0, -hi, jnp.where(row == 1, -mid, jnp.where(row == 2, -low, jnp.where(row == 3, 1.0, 0.0))))
    return jnp.concatenate([top.astype(f32), tail], axis=0)


def qkv_kernel(stretch, spans_in, len_ref, x_ref, w_ref, b_ref, q_out, k_out, v_out, size_out):
    seq, owner, half = pl.program_id(0), pl.program_id(1), pl.program_id(2)
    rows = jnp.concatenate([x_ref[a, 0, z, 0] for z in range(spans_in) for a in range(2)], axis=0)
    made = dg(rows, w_ref[...], 1, 0) + b_ref[...]
    count = rows.shape[0]
    q_t = (made[:, :128] * (LOG2E / 8.0)).T
    q_out[0, 0, 0] = q_t[:HD].astype(bf16)
    q_out[0, 1, 0] = q_t[HD:].astype(bf16)
    lane = lax.broadcasted_iota(jnp.int32, (count, 128), 1)
    row = lax.broadcasted_iota(jnp.int32, (count, 128), 0) + half * count
    shift = int(math.log2(stretch))
    position = lax.shift_left(lax.shift_right_logical(row, shift), shift + 2) + owner * stretch + (row & (stretch - 1))
    hidden = jnp.where(position < len_ref[seq], 0.0, FAR)
    tail = jnp.where(lane == HD + 3, hidden, jnp.where(lane < HD + 3, 1.0, 0.0))
    keys = made[:, 128:256]
    picks = lax.broadcasted_iota(jnp.int32, (128, 128), 0) // HD == lax.broadcasted_iota(jnp.int32, (128, 128), 1)
    sizes = dg((keys * keys).astype(bf16), jnp.where(picks, 1.0, 0.0).astype(bf16), 1, 0)
    size_out[0, 0, 0] = jnp.max(sizes, axis=0, keepdims=True)
    for head in range(2):
        turned = keys if head == 0 else pltpu.roll(keys, HD, 1)
        full = jnp.where(lane < HD, turned, tail).astype(bf16)
        for j in range(count // 128):
            k_out[0, head, j] = full[j * 128:(j + 1) * 128]
    v_t = made[:, 256:384].T
    ones = jnp.where(lax.broadcasted_iota(jnp.int32, (HD, count), 0) < 3, 1.0, 0.0)
    for head in range(2):
        full = jnp.concatenate([v_t[head * HD:(head + 1) * HD], ones], axis=0).astype(bf16)
        for j in range(count // 128):
            v_out[0, head, j] = full[:, j * 128:(j + 1) * 128]


def project(gathered, weight, bias, lens):
    _, owners, zs, seqs, stretch, width = gathered.shape
    local = 2 * zs * stretch
    spans = 512 // (2 * stretch)
    halves = local // 512
    chunks = owners * local // CH
    per = chunks // halves
    return pl.pallas_call(
        functools.partial(qkv_kernel, stretch, spans),
        grid_spec=pltpu.PrefetchScalarGridSpec(
            num_scalar_prefetch=1, grid=(seqs, owners, halves),
            in_specs=[
                pl.BlockSpec((2, 1, spans, 1, stretch, width), lambda s, o, h, n: (0, o, h, s, 0, 0)),
                pl.BlockSpec((width, 384), lambda s, o, h, n: (0, 0)),
                pl.BlockSpec((1, 384), lambda s, o, h, n: (0, 0)),
            ],
            out_specs=[
                pl.BlockSpec((1, 2, 1, HD, 512), lambda s, o, h, n: (s, 0, o, 0, h)),
                pl.BlockSpec((1, 2, per, 128, 128), lambda s, o, h, n: (s, 0, h, o, 0)),
                pl.BlockSpec((1, 2, per, 128, 128), lambda s, o, h, n: (s, 0, h, 0, o)),
                pl.BlockSpec((1, 1, 1, 1, 128), lambda s, o, h, n: (s, o, h, 0, 0)),
            ]),
        out_shape=[
            jax.ShapeDtypeStruct((seqs, 2, owners, HD, local), bf16),
            jax.ShapeDtypeStruct((seqs, 2, chunks, CH, 128), bf16),
            jax.ShapeDtypeStruct((seqs, 2, chunks, 128, CH), bf16),
            jax.ShapeDtypeStruct((seqs, owners, halves, 1, 128), f32),
        ],
        compiler_params=pltpu.CompilerParams(vmem_limit_bytes=40 << 20),
        name="qkv",
    )(lens, gathered, weight, bias)


def step_on(q, j, count):
    last = j + 1 == count
    return jnp.where(last, q + 1, q), jnp.where(last, 0, j + 1)


def assemble(ref, q, head, core):
    if head == 0:
        return ref[0, 0, q]
    at = pl.multiple_of(core * 512, 512)
    return jnp.concatenate([ref[0, 0, 2 * q, :, pl.ds(at, 512)], ref[0, 0, 2 * q + 1, :, pl.ds(at, 512)]], axis=1)


def fwd_kernel(len_ref, core_ref, q_ref, k_ref, v_ref, size_ref, own_ref, sh_ref, lse_ref, acc, probs, qa, shifts):
    seq, head = pl.program_id(0), pl.program_id(1)
    count = lax.div(len_ref[seq] + (CH - 1), CH)
    parts = jnp.where(head == 0, 4, 2)
    lane = lax.broadcasted_iota(jnp.int32, (1, 128), 1)
    sizes = functools.reduce(jnp.maximum, [size_ref[0, o, h] for o in range(size_ref.shape[1]) for h in range(size_ref.shape[2])])
    widest = jnp.sqrt(jnp.max(jnp.where(lane == head, sizes, 0.0), axis=1, keepdims=True))

    def prepare(part, q_t):
        wide = q_t.astype(f32)
        shift = jnp.sqrt(jnp.sum(wide * wide, axis=0, keepdims=True)) * widest
        shifts[part] = shift
        qa[part] = with_shift(q_t, shift).astype(bf16)

    @pl.when(head == 0)
    def _():
        for part in range(4):
            prepare(part, assemble(q_ref, part, 0, 0))

    @pl.when(head == 1)
    def _():
        for part in range(2):
            prepare(part, assemble(q_ref, part, 1, core_ref[0]))

    def raised(part, j):
        return jnp.exp2(dg(k_ref[0, 0, j], qa[part], 1, 0)).astype(bf16)

    probs[0] = raised(0, 0)

    def body(t, carry):
        part, j = carry
        now = t & 1
        part_next, j_next = step_on(part, j, count)
        before = jnp.where(j == 0, 0.0, acc[...])
        acc[...] = before + dg(v_ref[0, 0, j], probs[now], 1, 0)
        probs[1 - now] = raised(jnp.minimum(part_next, parts - 1), j_next)

        @pl.when(j + 1 == count)
        def _():
            total = acc[HD:HD + 1]
            fine = (jnp.min(total) > 2.0 ** -90) & (jnp.max(total) < 2.0 ** 60)

            @pl.when(jnp.logical_not(fine))
            def _():
                plain = qa[part].astype(f32)
                row = lax.broadcasted_iota(jnp.int32, plain.shape, 0)
                qa[part] = jnp.where((row >= HD) & (row < HD + 3), 0.0, plain).astype(bf16)

                def peak(i, top):
                    return jnp.maximum(top, jnp.max(dg(k_ref[0, 0, i], qa[part], 1, 0), axis=0, keepdims=True))
                shift = lax.fori_loop(0, count, peak, jnp.full((1, BQ), FAR, f32))
                shifts[part] = shift
                qa[part] = with_shift(plain[:HD], shift).astype(bf16)
                acc[...] = jnp.zeros_like(acc)

                def again(i, carry):
                    acc[...] += dg(v_ref[0, 0, i], raised(part, i), 1, 0)
                    return carry
                lax.fori_loop(0, count, again, 0)

            total = acc[HD:HD + 1]
            mixed = (acc[:HD] * (1.0 / total)).astype(bf16)
            lse_ref[0, 0, part] = shifts[part] + jnp.log2(total)

            @pl.when(head == 0)
            def _():
                own_ref[0, part] = mixed

            @pl.when(head == 1)
            def _():
                sh_ref[0, 2 * part] = mixed[:, :512]
                sh_ref[0, 2 * part + 1] = mixed[:, 512:]
        return part_next, j_next

    lax.fori_loop(0, parts * count, body, (0, 0))


def head_spec(*dims):
    zeros = (0,) * len(dims)
    return pl.BlockSpec((1, 1) + dims, lambda s, h, n, c: (s, h) + zeros)


def seq_spec(*dims):
    zeros = (0,) * len(dims)
    return pl.BlockSpec((1,) + dims, lambda s, h, n, c: (s,) + zeros)


def attend_forward(q, k, v, sizes, lens, core):
    seqs, _, owners, _, local = q.shape
    chunks = k.shape[2]
    return pl.pallas_call(
        fwd_kernel,
        grid_spec=pltpu.PrefetchScalarGridSpec(
            num_scalar_prefetch=2, grid=(seqs, 2),
            in_specs=[
                head_spec(owners, HD, local), head_spec(chunks, CH, 128), head_spec(chunks, 128, CH),
                seq_spec(*sizes.shape[1:]),
            ],
            out_specs=[seq_spec(owners, HD, local), seq_spec(owners, HD, local // 2), head_spec(owners, 1, local)],
            scratch_shapes=[
                pltpu.VMEM((128, BQ), f32), pltpu.VMEM((2, CH, BQ), bf16), pltpu.VMEM((4, 128, BQ), bf16),
                pltpu.VMEM((4, 1, BQ), f32),
            ]),
        out_shape=[
            jax.ShapeDtypeStruct((seqs, owners, HD, local), bf16),
            jax.ShapeDtypeStruct((seqs, owners, HD, local // 2), bf16),
            jax.ShapeDtypeStruct((seqs, 2, owners, 1, local), f32),
        ],
        compiler_params=pltpu.CompilerParams(vmem_limit_bytes=48 << 20),
        name="attend_forward",
    )(lens, core, q, k, v, sizes)


def bwd_kernel(len_ref, core_ref, q_ref, k_ref, v_ref, lse_ref, own_ref, sh_ref, gown_ref, gsh_ref,
               dq_own, dq_sh, dkv_own, dkv_sh, dk_acc, dv_acc, dq_acc, qa, qat, ga, gat, pb, db):
    seq, head = pl.program_id(0), pl.program_id(1)
    count = lax.div(len_ref[seq] + (CH - 1), CH)
    chunks = k_ref.shape[2]
    parts = jnp.where(head == 0, 4, 2)
    dk_acc[...] = jnp.zeros_like(dk_acc)
    dv_acc[...] = jnp.zeros_like(dv_acc)

    def prepare(part, q_t, o_t, g_t):
        q_full = with_shift(q_t, lse_ref[0, 0, part])
        qat[part] = q_full.astype(bf16)
        qa[part] = q_full.T.astype(bf16)
        g_wide = g_t.astype(f32)
        meet = jnp.sum(g_wide * o_t.astype(f32), axis=0, keepdims=True)
        g_full = with_shift(g_t, meet)
        gat[part] = g_full.astype(bf16)
        ga[part] = g_full.T.astype(bf16)

    @pl.when(head == 0)
    def _():
        for part in range(4):
            prepare(part, assemble(q_ref, part, 0, 0), own_ref[0, part], gown_ref[0, part])

    @pl.when(head == 1)
    def _():
        for part in range(2):
            pair = [jnp.concatenate([ref[0, 2 * part], ref[0, 2 * part + 1]], axis=1) for ref in (sh_ref, gsh_ref)]
            prepare(part, assemble(q_ref, part, 1, core_ref[0]), *pair)

    def ahead(part, j, slot):
        raised = jnp.exp2(dg(qa[part], k_ref[0, 0, j], 1, 1))
        pb[slot] = raised.astype(bf16)
        db[slot] = (raised * dg(ga[part], v_ref[0, 0, j], 1, 0)).astype(bf16)

    ahead(0, 0, 0)

    def body(t, carry):
        part, j = carry
        now = t & 1
        part_next, j_next = step_on(part, j, count)
        dv_acc[j] += dg(gat[part], pb[now], 1, 0)[:HD]
        dk_acc[j] += dg(qat[part], db[now], 1, 0)[:HD]
        before = jnp.where(j == 0, 0.0, dq_acc[...])
        dq_acc[...] = before + dg(db[now], k_ref[0, 0, j], 1, 0)
        ahead(jnp.minimum(part_next, parts - 1), j_next, 1 - now)

        @pl.when(j + 1 == count)
        def _():
            dq_t = (dq_acc[...] * 0.125).T[:HD].astype(bf16)

            @pl.when(head == 0)
            def _():
                dq_own[0, part] = dq_t

            @pl.when(head == 1)
            def _():
                dq_sh[0, 2 * part] = dq_t[:, :512]
                dq_sh[0, 2 * part + 1] = dq_t[:, 512:]
        return part_next, j_next

    lax.fori_loop(0, parts * count, body, (0, 0))

    def flush(out):
        for j in range(chunks):
            for owner in range(4):
                cols = slice(owner * 128, (owner + 1) * 128)
                out[0, owner, 0, :, j * 128:(j + 1) * 128] = (dk_acc[j, :, cols] * LN2).astype(bf16)
                out[0, owner, 1, :, j * 128:(j + 1) * 128] = dv_acc[j, :, cols].astype(bf16)

    @pl.when(head == 0)
    def _():
        flush(dkv_own)

    @pl.when(head == 1)
    def _():
        flush(dkv_sh)


def attend_backward(q, k, v, lse, own, sh, g_own, g_sh, lens, core):
    seqs, _, owners, _, local = q.shape
    chunks = k.shape[2]
    own_spec, sh_spec = seq_spec(owners, HD, local), seq_spec(owners, HD, local // 2)
    return pl.pallas_call(
        bwd_kernel,
        grid_spec=pltpu.PrefetchScalarGridSpec(
            num_scalar_prefetch=2, grid=(seqs, 2),
            in_specs=[
                head_spec(owners, HD, local), head_spec(chunks, CH, 128), head_spec(chunks, 128, CH),
                head_spec(owners, 1, local), own_spec, sh_spec, own_spec, sh_spec,
            ],
            out_specs=[own_spec, sh_spec, seq_spec(owners, 2, HD, local), seq_spec(owners, 2, HD, local)],
            scratch_shapes=[
                pltpu.VMEM((chunks, HD, CH), f32), pltpu.VMEM((chunks, HD, CH), f32), pltpu.VMEM((BQ, 128), f32),
                pltpu.VMEM((4, BQ, 128), bf16), pltpu.VMEM((4, 128, BQ), bf16),
                pltpu.VMEM((4, BQ, 128), bf16), pltpu.VMEM((4, 128, BQ), bf16),
                pltpu.VMEM((2, BQ, CH), bf16), pltpu.VMEM((2, BQ, CH), bf16),
            ]),
        out_shape=[
            jax.ShapeDtypeStruct((seqs, owners, HD, local), bf16),
            jax.ShapeDtypeStruct((seqs, owners, HD, local // 2), bf16),
            jax.ShapeDtypeStruct((seqs, owners, 2, HD, local), bf16),
            jax.ShapeDtypeStruct((seqs, owners, 2, HD, local), bf16),
        ],
        compiler_params=pltpu.CompilerParams(vmem_limit_bytes=56 << 20),
        name="attend_backward",
    )(lens, core, q, k, v, lse, own, sh, g_own, g_sh)


def gelu_pair(u):
    half = 0.5 * (1.0 + lax.erf(u * 0.7071067811865476))
    return u * half, half + u * (0.3989422804014327 * jnp.exp2(u * u * (-0.5 * LOG2E)))


def norm_stats(v):
    mean = jnp.mean(v, axis=-1, keepdims=True)
    centred = v - mean
    inverse = lax.rsqrt(jnp.mean(centred * centred, axis=-1, keepdims=True) + 1e-12)
    return centred * inverse, inverse


def norm_back(grad, xhat, inverse, gain):
    g = grad * gain
    return (g - jnp.mean(g, axis=-1, keepdims=True) - xhat * jnp.mean(g * xhat, axis=-1, keepdims=True)) * inverse


def weight_part(ref, first, rows):
    part = ref[:, first:first + rows, :]
    return part.reshape(part.shape[0] * rows, part.shape[2])


def ffn_kernel(spans, at_ref, x_ref, own_ref, sh_ref, cot_ref, w_ref, bin_ref, vec_ref,
               act_out, resid_out, gown_out, gsh_out, active_out, dinner_out, normed_out, douter_out, dbranch_out,
               vec_sum, bin_sum, slope):
    step = pl.program_id(0)
    width = x_ref.shape[-1]
    rows = jnp.concatenate([x_ref[a, 0, z, 0] for z in range(spans) for a in range(2)], axis=0).astype(f32)
    mixed_t = jnp.concatenate(
        [part for p in range(4) for part in (own_ref[p, 0], sh_ref[p, 0], own_ref[p, 1])], axis=0)
    vec = vec_ref[...]
    branch = dg(mixed_t, weight_part(w_ref, 768, 96), 0, 0) + vec[0:1]
    xhat1, inv1 = norm_stats(rows + branch)
    normed = xhat1 * vec[1:2] + vec[2:3]
    low = normed.astype(bf16)
    normed_out[...] = low
    outer = normed + vec[3:4]
    for n in range(4):
        cols = slice(n * 768, (n + 1) * 768)
        inner = dg(low, weight_part(w_ref, 384 + 96 * n, 96), 1, 0) + bin_ref[:, cols]
        value, bend = gelu_pair(inner)
        active_out[:, cols] = value.astype(bf16)
        slope[:, cols] = bend.astype(bf16)
    outer = outer + dg(active_out[...], weight_part(w_ref, 0, 384), 1, 0)
    xhat2, inv2 = norm_stats(outer)
    act_out[...] = (xhat2 * vec[4:5] + vec[5:6]).astype(bf16)
    cot = cot_ref[...].astype(f32)
    d2 = norm_back(cot, xhat2, inv2, vec[4:5])
    d_outer = d2.astype(bf16)
    douter_out[...] = d_outer
    d_normed = d2
    sums_in = []
    for n in range(4):
        cols = slice(n * 768, (n + 1) * 768)
        d_active = dg(d_outer, weight_part(w_ref.at[2 * n:2 * n + 2], 0, 384), 1, 1)
        d_inner = (d_active * slope[:, cols].astype(f32)).astype(bf16)
        dinner_out[:, cols] = d_inner
        sums_in.append(jnp.sum(d_inner.astype(f32), axis=0, keepdims=True))
        d_normed = d_normed + dg(d_inner, weight_part(w_ref, 384 + 96 * n, 96), 1, 1)
    d1 = norm_back(d_normed, xhat1, inv1, vec[1:2])
    resid_out[...] = d1
    d_branch = d1.astype(bf16)
    dbranch_out[...] = d_branch
    g_t = dg(weight_part(w_ref, 768, 96), d_branch, 1, 1).astype(bf16)
    for p in range(4):
        gown_out[p, 0] = g_t[192 * p:192 * p + 64]
        gsh_out[p, 0] = g_t[192 * p + 64:192 * p + 128]
        gown_out[p, 1] = g_t[192 * p + 128:192 * p + 192]
    total = lambda a: jnp.sum(a, axis=0, keepdims=True)
    sums = jnp.concatenate([
        total(d_branch.astype(f32)), total(d_normed * xhat1), total(d_normed),
        total(d_outer.astype(f32)), total(cot * xhat2), total(cot), jnp.zeros((2, width), f32)], axis=0)

    @pl.when(step == 0)
    def _():
        vec_sum[...] = sums
        for n in range(4):
            bin_sum[:, n * 768:(n + 1) * 768] = sums_in[n]

    @pl.when(step > 0)
    def _():
        vec_sum[...] += sums
        for n in range(4):
            bin_sum[:, n * 768:(n + 1) * 768] += sums_in[n]


def feed_forward(gathered, own, sh, cotangent, weights, inner_bias, vectors, at):
    _, _, _, _, stretch, width = gathered.shape
    local = cotangent.shape[0]
    spans = RB // (2 * stretch)
    steps = local // RB
    half_steps = steps // 2
    wide = inner_bias.shape[1]
    rows = lambda n: pl.BlockSpec((RB, n), lambda r, a: (r, 0))
    fixed = lambda *dims: pl.BlockSpec(dims, lambda r, a: (0,) * len(dims))
    own_spec = pl.BlockSpec((4, 2, HD, RB), lambda r, a: (0, 0, 0, r))
    sh_spec = pl.BlockSpec((4, 1, HD, RB), lambda r, a: (0, r // half_steps, 0, r % half_steps))
    shape = jax.ShapeDtypeStruct
    return pl.pallas_call(
        functools.partial(ffn_kernel, spans),
        grid_spec=pltpu.PrefetchScalarGridSpec(
            num_scalar_prefetch=1, grid=(steps,),
            in_specs=[
                pl.BlockSpec((2, 1, spans, 1, stretch, width), lambda r, a: (0, a[1], r, a[0], 0, 0)),
                own_spec, sh_spec, rows(width),
                pl.BlockSpec(weights.shape, lambda r, a: (0, 0, 0), pipeline_mode=pl.Buffered(1)),
                fixed(1, wide), fixed(8, width),
            ],
            out_specs=[
                rows(width), rows(width), own_spec, sh_spec, rows(wide), rows(wide), rows(width), rows(width), rows(width),
                fixed(8, width), fixed(1, wide),
            ],
            scratch_shapes=[pltpu.VMEM((RB, wide), bf16)]),
        out_shape=[
            shape((local, width), bf16), shape((local, width), f32), shape(own.shape, bf16), shape(sh.shape, bf16),
            shape((local, wide), bf16), shape((local, wide), bf16), shape((local, width), bf16),
            shape((local, width), bf16), shape((local, width), bf16), shape((8, width), f32), shape((1, wide), f32),
        ],
        compiler_params=pltpu.CompilerParams(vmem_limit_bytes=60 << 20),
        name="feed_forward",
    )(at, gathered, own, sh, cotangent, weights, inner_bias, vectors)


def outer_grad_kernel(scale, active_ref, douter_ref, out_ref):
    made = (dg(active_ref[...], douter_ref[...], 0, 0) * scale).astype(bf16)
    out_ref[...] = made.reshape(out_ref.shape)


def inner_grad_kernel(scale, packed_ref, normed_ref, dinner_ref, own_ref, sh_ref, dbranch_ref, out_ref):
    step = pl.program_id(0)

    @pl.when(step < 4)
    def _():
        out_ref[...] = (dg(normed_ref[...], dinner_ref[...], 0, 0) * scale).astype(bf16).reshape(out_ref.shape)

    @pl.when(step == 4)
    def _():
        mixed_t = jnp.concatenate([
            part for p in range(4)
            for part in (own_ref[p, 0], jnp.concatenate([sh_ref[p, 0], sh_ref[p, 1]], axis=1), own_ref[p, 1])], axis=0)
        out_ref[...] = (dg(mixed_t, dbranch_ref[...], 1, 0) * scale).astype(bf16).reshape(out_ref.shape)


def weight_grads(scale, active, d_outer, normed, d_inner, own, sh, d_branch):
    local, wide = active.shape
    width = normed.shape[1]
    packed = pl.pallas_call(
        functools.partial(outer_grad_kernel, scale), grid=(4,),
        in_specs=[pl.BlockSpec((local, width), lambda m: (0, m)), pl.BlockSpec((local, width), lambda m: (0, 0))],
        out_specs=pl.BlockSpec((2, 384, width), lambda m: (m, 0, 0)),
        out_shape=jax.ShapeDtypeStruct((8, 896, width), bf16),
        compiler_params=pltpu.CompilerParams(vmem_limit_bytes=40 << 20), name="outer_grad",
    )(active, d_outer)
    fixed = lambda a: pl.BlockSpec(a.shape, lambda n: (0,) * a.ndim)
    return pl.pallas_call(
        functools.partial(inner_grad_kernel, scale), grid=(5,),
        in_specs=[
            pl.BlockSpec(memory_space=pl.ANY), fixed(normed),
            pl.BlockSpec((local, width), lambda n: (0, jnp.minimum(n, 3))), fixed(own), fixed(sh), fixed(d_branch)],
        out_specs=pl.BlockSpec((8, 96, width), lambda n: (0, 4 + n, 0)),
        out_shape=jax.ShapeDtypeStruct((8, 896, width), bf16), input_output_aliases={0: 0},
        compiler_params=pltpu.CompilerParams(vmem_limit_bytes=40 << 20), name="inner_grad",
    )(packed, normed, d_inner, own, sh, d_branch)


def head_grad_kernel(scale, spans, core_ref, x_ref, dqo_ref, dqs_ref, dko_ref, dks_ref, out_ref, bias_out, acc, bias_acc, stack):
    seq, owner, half = pl.program_id(0), pl.program_id(1), pl.program_id(2)
    first = (seq == 0) & (owner == 0) & (half == 0)
    last = (seq == pl.num_programs(0) - 1) & (owner == pl.num_programs(1) - 1) & (half == pl.num_programs(2) - 1)
    rows = jnp.concatenate([x_ref[a, 0, z, 0] for z in range(spans) for a in range(2)], axis=0)
    d_t = jnp.concatenate([
        dqo_ref[0, 0], jnp.where(half == core_ref[0], dqs_ref[0, 0].astype(f32), 0.0).astype(bf16),
        dko_ref[0, 0, 0], dks_ref[0, 0, 0], dko_ref[0, 0, 1], dks_ref[0, 0, 1]], axis=0)

    @pl.when(first)
    def _():
        acc[...] = jnp.zeros_like(acc)
        bias_acc[...] = jnp.zeros_like(bias_acc)
    acc[...] += dg(d_t, rows, 1, 0)
    bias_acc[...] += dg(jnp.ones((8, d_t.shape[1]), bf16), d_t, 1, 1)

    @pl.when(last)
    def _():
        out_ref[...] = (acc[...] * scale).T.astype(bf16)
        bias_out[...] = bias_acc[...] * scale


def head_grads(scale, gathered, dq_own, dq_sh, dkv_own, dkv_sh, core):
    _, owners, zs, seqs, stretch, width = gathered.shape
    local = 2 * zs * stretch
    spans = 512 // (2 * stretch)
    pair = pl.BlockSpec((1, 1, 2, HD, 512), lambda s, o, h, c: (s, o, 0, 0, h))
    return pl.pallas_call(
        functools.partial(head_grad_kernel, scale, spans),
        grid_spec=pltpu.PrefetchScalarGridSpec(
            num_scalar_prefetch=1, grid=(seqs, owners, local // 512),
            in_specs=[
                pl.BlockSpec((2, 1, spans, 1, stretch, width), lambda s, o, h, c: (0, o, h, s, 0, 0)),
                pl.BlockSpec((1, 1, HD, 512), lambda s, o, h, c: (s, o, 0, h)),
                pl.BlockSpec((1, 1, HD, 512), lambda s, o, h, c: (s, o, 0, 0)),
                pair, pair],
            out_specs=[pl.BlockSpec((width, 384), lambda s, o, h, c: (0, 0)), pl.BlockSpec((8, 384), lambda s, o, h, c: (0, 0))],
            scratch_shapes=[pltpu.VMEM((384, width), f32), pltpu.VMEM((8, 384), f32), pltpu.VMEM((8, 128), f32)]),
        out_shape=[jax.ShapeDtypeStruct((width, 384), bf16), jax.ShapeDtypeStruct((8, 384), f32)],
        compiler_params=pltpu.CompilerParams(vmem_limit_bytes=40 << 20), name="head_grads",
    )(core, gathered, dq_own, dq_sh, dkv_own, dkv_sh)


def token_grad_kernel(dqo_ref, dqs_ref, dko_ref, dks_ref, w_ref, resid_ref, out_ref):
    total = resid_ref[...]
    made = [[part for p in range(4) for part in (dqo_ref[p, 0], dqs_ref[p, 0], dqo_ref[p, 1])]]
    for kind in range(2):
        made.append([part for p in range(4) for part in (
            dko_ref[p, 0, kind],
            (dks_ref[p, 0, kind].astype(f32) + dks_ref[p, 1, kind].astype(f32)).astype(bf16),
            dko_ref[p, 1, kind])])
    for kind in range(3):
        total = total + dg(jnp.concatenate(made[kind], axis=0), weight_part(w_ref, 96 * kind, 96), 0, 1)
    out_ref[...] = total.astype(bf16)


def token_grad(dq_own, dq_sh, dkv_own, dkv_sh, weights, resid):
    local, width = resid.shape
    steps = local // RB
    half_steps = steps // 2
    rows = pl.BlockSpec((RB, width), lambda r: (r, 0))
    pair = pl.BlockSpec((4, 2, 2, HD, RB), lambda r: (0, 0, 0, 0, r))
    return pl.pallas_call(
        token_grad_kernel, grid=(steps,),
        in_specs=[
            pl.BlockSpec((4, 2, HD, RB), lambda r: (0, 0, 0, r)),
            pl.BlockSpec((4, 1, HD, RB), lambda r: (0, r // half_steps, 0, r % half_steps)),
            pair, pair, pl.BlockSpec(weights.shape, lambda r: (0, 0, 0)), rows],
        out_specs=rows, out_shape=jax.ShapeDtypeStruct((local, width), bf16),
        compiler_params=pltpu.CompilerParams(vmem_limit_bytes=40 << 20), name="token_grad",
    )(dq_own, dq_sh, dkv_own, dkv_sh, weights, resid)


PAIR = ("x", "y", "c")
ALL = ("z", "x", "y", "c")
SHARD = ("z", "x")


def canonical(packed, shards):
    if shards == 8:
        return packed
    width = packed.shape[2]
    per, keep = 96 * 8 // shards, shards // 8
    outer = packed[:, :4 * per].reshape(8, 384, width)
    inner = packed[:, 4 * per:8 * per].reshape(8, keep, 4, per, width).transpose(0, 2, 1, 3, 4).reshape(8, 384, width)
    output = packed[:, 8 * per:9 * per].reshape(8, 96, width)
    return jnp.concatenate([outer, inner, output, jnp.zeros((8, 32, width), packed.dtype)], axis=1)


def from_canonical(packed, shards):
    if shards == 8:
        return packed
    width = packed.shape[2]
    per, keep = 96 * 8 // shards, shards // 8
    outer = packed[:, :384].reshape(shards, 4 * per, width)
    inner = packed[:, 384:768].reshape(8, 4, keep, per, width).transpose(0, 2, 1, 3, 4).reshape(shards, 4 * per, width)
    output = packed[:, 768:864].reshape(shards, per, width)
    return jnp.concatenate([outer, inner, output, jnp.zeros((shards, 32, width), packed.dtype)], axis=1)


def canonical_heads(packed, shards):
    if shards == 8:
        return packed
    width = packed.shape[2]
    per = 96 * 8 // shards
    parts = [packed[:, k * per:(k + 1) * per].reshape(8, 96, width) for k in range(3)]
    return jnp.concatenate(parts + [jnp.zeros((8, 32, width), packed.dtype)], axis=1)


def quarter(rows):
    place = lax.axis_index("y") * 2 + lax.axis_index("c")
    part = rows.shape[0] // 4
    return lax.dynamic_slice_in_dim(rows, place * part, part)


def body(tokens, lengths, deal_order, w_query, w_key, w_value, w_output, b_query, b_value, b_output,
         ln1_gain, ln1_shift, w_inner, b_inner, w_outer, b_outer, ln2_gain, ln2_shift, cotangent):
    zs = lax.axis_size("z")
    shards = 2 * zs
    devices = shards * 4
    scale = 1.0 / devices
    seq_count, _, stretch, width = tokens.shape
    per = w_query.shape[0]
    x, y, c = lax.axis_index("x"), lax.axis_index("y"), lax.axis_index("c")
    core = c.astype(jnp.int32)[None]

    ordered = jnp.take(tokens[:, 0], deal_order, axis=0).reshape(zs, 2, stretch, width)
    spread = lax.all_to_all(ordered, "z", split_axis=0, concat_axis=0, tiled=True)

    def head_columns(matrix):
        heads = matrix.reshape(per, 2, 2, 3, HD)
        mine = lax.dynamic_index_in_dim(heads, y, axis=2, keepdims=False)
        own = lax.dynamic_index_in_dim(mine, 2 * c, axis=2, keepdims=False)
        return [own, mine[:, :, 1]]
    columns = jnp.concatenate(
        [col for matrix in (w_query, w_key, w_value) for col in head_columns(matrix)], axis=2).reshape(per, 768)
    pad = lambda v, n: jnp.pad(v, (0, n - v.shape[0]))[None]
    head_pack = jnp.concatenate(
        [columns, pad(b_query, width), pad(b_value, width), jnp.zeros((14, width), bf16)], axis=0)
    head_all = lax.all_gather(head_pack, SHARD, axis=0, tiled=False)
    head_weight = lax.dynamic_index_in_dim(
        head_all[:, :per].reshape(width, 2, 384), x, axis=1, keepdims=False)

    def head_bias(row):
        heads = head_all[:, per + row, :per].reshape(2, 2, 3, HD)
        mine = lax.dynamic_slice(heads, (x, y, 0, 0), (1, 1, 3, HD))[0, 0]
        return [lax.dynamic_index_in_dim(mine, 2 * c, axis=0, keepdims=False), mine[1]]
    bias_row = jnp.concatenate(head_bias(0) + [jnp.zeros((2 * HD,), bf16)] + head_bias(1)).astype(f32)[None]

    gathered = lax.all_gather(spread, PAIR, axis=0, tiled=False).reshape(2, 4, zs, 2, stretch, width)

    panels = w_inner.reshape(per, 4, 768)
    vectors = (b_output, ln1_gain, ln1_shift, b_outer, ln2_gain, ln2_shift)
    layer_pack = jnp.concatenate(
        [w_outer] + [panels[:, n] for n in range(4)] + [w_output]
        + [pad(b_inner, width)] + [pad(v, width) for v in vectors] + [jnp.zeros((25, width), bf16)], axis=0)
    layer_all = lax.all_gather(quarter(layer_pack), ALL, axis=0, tiled=True).reshape(shards, 9 * per + 32, width)
    layer_weights = canonical(layer_all, shards)
    inner_bias = layer_all[:, 9 * per, :4 * per].reshape(1, 3072).astype(f32)
    vector_rows = jnp.concatenate(
        [layer_all[:, 9 * per + 1 + n, :per].reshape(1, width) for n in range(6)] + [jnp.zeros((2, width), bf16)],
        axis=0).astype(f32)
    back_pack = jnp.concatenate([w_query, w_key, w_value, jnp.zeros((32, width), bf16)], axis=0)
    back_all = lax.all_gather(quarter(back_pack), ALL, axis=0, tiled=True).reshape(shards, 3 * per + 32, width)
    back_weights = canonical_heads(back_all, shards)

    group = lax.axis_index("z")
    slots = lax.dynamic_slice_in_dim(deal_order, group * 2, 2)
    matches = slots[:, None] == jnp.arange(seq_count, dtype=jnp.int32)[None, :]
    lens = jnp.sum(jnp.where(matches, lengths[None, :], 0), axis=1).astype(jnp.int32)

    q, k, v, sizes = project(gathered, head_weight, bias_row, lens)
    own, sh, lse = attend_forward(q, k, v, sizes, lens, core)

    def swap(array):
        flat = array.reshape((8,) + array.shape[2:])
        return lax.all_to_all(flat, PAIR, split_axis=0, concat_axis=0, tiled=True)

    def to_tokens(array):
        return swap(array).reshape((4, 2) + array.shape[2:])

    def to_heads(array):
        return swap(array).reshape((2, 4) + array.shape[2:])

    own_t, sh_t = to_tokens(own), to_tokens(sh)
    at = jnp.stack([x, y * 2 + c]).astype(jnp.int32)
    (act, resid, g_own, g_sh, active, d_inner, normed, d_outer, d_branch, vec_sums, bin_sums) = feed_forward(
        gathered, own_t, sh_t, cotangent.reshape(-1, width), layer_weights, inner_bias, vector_rows, at)
    g_own_h, g_sh_h = to_heads(g_own), to_heads(g_sh)
    packed = weight_grads(scale, active, d_outer, normed, d_inner, own_t, sh_t, d_branch)
    sums = jnp.concatenate([bin_sums.reshape(4, width), vec_sums, jnp.zeros((20, width), f32)], axis=0) * scale
    packed = packed.at[:, 864:].set(jnp.broadcast_to(sums.astype(bf16)[None], (8, 32, width)))
    ready = from_canonical(packed, shards)
    if shards != 8:
        ready = ready.at[:, 9 * per:].set(jnp.broadcast_to(sums.astype(bf16)[None], (shards, 32, width)))
    layer_part = lax.psum_scatter(ready.reshape(-1, width), ALL, scatter_dimension=0, tiled=True)
    layer_grads = lax.all_gather(layer_part, ("y", "c"), axis=0, tiled=True)

    dq_own, dq_sh, dkv_own, dkv_sh = attend_backward(q, k, v, lse, own, sh, g_own_h, g_sh_h, lens, core)
    back = (to_tokens(dq_own), to_tokens(dq_sh), to_tokens(dkv_own), to_tokens(dkv_sh))
    d_heads, d_bias = head_grads(scale, gathered, dq_own, dq_sh, dkv_own, dkv_sh, core)
    chunk = width // zs
    head_ready = jnp.concatenate([
        d_heads.reshape(zs, chunk, 384),
        jnp.broadcast_to(d_bias[:1].astype(bf16)[None], (zs, 16, 384))], axis=1)
    head_part = lax.psum_scatter(head_ready.reshape(-1, 384), "z", scatter_dimension=0, tiled=True)
    head_grads_all = lax.all_gather(head_part, PAIR, axis=0, tiled=False).reshape(4, 2, chunk + 16, 6, HD).astype(f32)

    d_rows = token_grad(*back, back_weights, resid)
    returned = lax.all_to_all(
        d_rows.reshape(shards, stretch, width), SHARD, split_axis=0, concat_axis=0, tiled=True)
    d_tokens = jnp.zeros_like(returned).at[deal_order].set(returned)[:, None]

    mine = lax.dynamic_slice_in_dim(head_grads_all, x * per, per, axis=2)

    def full(part, kind):
        own_part, shared = part[:, :, :, 2 * kind], part[:, :, :, 2 * kind + 1]
        both = shared[:, 0] + shared[:, 1]
        joined = jnp.stack([own_part[:, 0], both, own_part[:, 1]], axis=1)
        return joined.transpose(2, 0, 1, 3).reshape(part.shape[2], width)
    d_wq, d_wk, d_wv = (full(mine, kind) for kind in range(3))
    bias_part = head_grads_all[:, :, chunk:chunk + 1]
    place = lax.axis_index("z") * 2 + x
    own_slice = lambda row, n: lax.dynamic_slice_in_dim(row, place * n, n)
    d_bq = own_slice(full(bias_part, 0)[0], per)
    d_bv = own_slice(full(bias_part, 2)[0], per)

    layer_grads = layer_grads.astype(f32)
    d_wouter = layer_grads[:4 * per]
    d_winner = layer_grads[4 * per:8 * per].reshape(4, per, width).transpose(1, 0, 2).reshape(per, 4 * width)
    d_woutput = layer_grads[8 * per:9 * per]
    d_binner = own_slice(layer_grads[9 * per:9 * per + 4].reshape(-1), 4 * per)
    d_bo, d_g1, d_s1, d_bout, d_g2, d_s2 = (own_slice(layer_grads[9 * per + 4 + n], per) for n in range(6))
    return (act.reshape(1, shards, stretch, width), d_tokens, d_wq, d_wk, d_wv, d_woutput, d_bq, d_bv, d_bo,
            d_g1, d_s1, d_winner, d_binner, d_wouter, d_bout, d_g2, d_s2)


def solution(mesh):
    shards, splits = mesh.devices.shape
    fine = Mesh(mesh.devices.reshape(shards // 2, 2, splits // 2, 2), ALL)
    S, Q = SHARD, ("y", "c")
    row, mat = P(S), P(S, None)
    return jax.shard_map(
        body, mesh=fine,
        in_specs=(P(None, S, Q, None), P(), P(), mat, mat, mat, mat, row, row, row, row, row, mat, row, mat, row, row, row,
                  P(S, None, Q, None)),
        out_specs=(P(S, None, Q, None), P(None, S, Q, None), mat, mat, mat, mat, row, row, row, row, row, mat, row, mat,
                   row, row, row),
        check_vma=False)
```

```python
import functools, math
import jax
import jax.numpy as jnp
from jax import lax
from jax.experimental import pallas as pl
from jax.experimental.pallas import tpu as pltpu
from jax.sharding import Mesh, PartitionSpec as P

f32, bf16 = jnp.float32, jnp.bfloat16
LOG2E = 1.4426950408889634
LN2 = 0.6931471805599453
CH = 512
BQ = 1024
RB = 256
HD = 64
FAR = -1.0e30

def dg(a, b, ca, cb):
    return lax.dot_general(a, b, (((ca,), (cb,)), ((), ())), preferred_element_type=f32)


def three_parts(row):
    hi = row.astype(bf16).astype(f32)
    rest = row - hi
    mid = rest.astype(bf16).astype(f32)
    return hi, mid, rest - mid


def with_shift(top, shift):
    hi, mid, low = three_parts(shift)
    row = lax.broadcasted_iota(jnp.int32, (HD, top.shape[1]), 0)
    tail = jnp.where(row == 0, -hi, jnp.where(row == 1, -mid, jnp.where(row == 2, -low, jnp.where(row == 3, 1.0, 0.0))))
    return jnp.concatenate([top.astype(f32), tail], axis=0)


def qkv_kernel(stretch, spans_in, len_ref, x_ref, w_ref, b_ref, q_out, k_out, v_out, size_out):
    seq, owner, half = pl.program_id(0), pl.program_id(1), pl.program_id(2)
    rows = jnp.concatenate([x_ref[a, 0, z, 0] for z in range(spans_in) for a in range(2)], axis=0)
    made = dg(rows, w_ref[...], 1, 0) + b_ref[...]
    count = rows.shape[0]
    q_t = (made[:, :128] * (LOG2E / 8.0)).T
    q_out[0, 0, 0] = q_t[:HD].astype(bf16)
    q_out[0, 1, 0] = q_t[HD:].astype(bf16)
    lane = lax.broadcasted_iota(jnp.int32, (count, 128), 1)
    row = lax.broadcasted_iota(jnp.int32, (count, 128), 0) + half * count
    shift = int(math.log2(stretch))
    position = lax.shift_left(lax.shift_right_logical(row, shift), shift + 2) + owner * stretch + (row & (stretch - 1))
    hidden = jnp.where(position < len_ref[seq], 0.0, FAR)
    tail = jnp.where(lane == HD + 3, hidden, jnp.where(lane < HD + 3, 1.0, 0.0))
    keys = made[:, 128:256]
    picks = lax.broadcasted_iota(jnp.int32, (128, 128), 0) // HD == lax.broadcasted_iota(jnp.int32, (128, 128), 1)
    sizes = dg((keys * keys).astype(bf16), jnp.where(picks, 1.0, 0.0).astype(bf16), 1, 0)
    size_out[0, 0, 0] = jnp.max(sizes, axis=0, keepdims=True)
    for head in range(2):
        turned = keys if head == 0 else pltpu.roll(keys, HD, 1)
        full = jnp.where(lane < HD, turned, tail).astype(bf16)
        for j in range(count // 128):
            k_out[0, head, j] = full[j * 128:(j + 1) * 128]
    v_t = made[:, 256:384].T
    ones = jnp.where(lax.broadcasted_iota(jnp.int32, (HD, count), 0) < 3, 1.0, 0.0)
    for head in range(2):
        full = jnp.concatenate([v_t[head * HD:(head + 1) * HD], ones], axis=0).astype(bf16)
        for j in range(count // 128):
            v_out[0, head, j] = full[:, j * 128:(j + 1) * 128]


def project(gathered, weight, bias, lens):
    _, owners, zs, seqs, stretch, width = gathered.shape
    local = 2 * zs * stretch
    spans = 512 // (2 * stretch)
    halves = local // 512
    chunks = owners * local // CH
    per = chunks // halves
    return pl.pallas_call(
        functools.partial(qkv_kernel, stretch, spans),
        grid_spec=pltpu.PrefetchScalarGridSpec(
            num_scalar_prefetch=1, grid=(seqs, owners, halves),
            in_specs=[
                pl.BlockSpec((2, 1, spans, 1, stretch, width), lambda s, o, h, n: (0, o, h, s, 0, 0)),
                pl.BlockSpec((width, 384), lambda s, o, h, n: (0, 0)),
                pl.BlockSpec((1, 384), lambda s, o, h, n: (0, 0)),
            ],
            out_specs=[
                pl.BlockSpec((1, 2, 1, HD, 512), lambda s, o, h, n: (s, 0, o, 0, h)),
                pl.BlockSpec((1, 2, per, 128, 128), lambda s, o, h, n: (s, 0, h, o, 0)),
                pl.BlockSpec((1, 2, per, 128, 128), lambda s, o, h, n: (s, 0, h, 0, o)),
                pl.BlockSpec((1, 1, 1, 1, 128), lambda s, o, h, n: (s, o, h, 0, 0)),
            ]),
        out_shape=[
            jax.ShapeDtypeStruct((seqs, 2, owners, HD, local), bf16),
            jax.ShapeDtypeStruct((seqs, 2, chunks, CH, 128), bf16),
            jax.ShapeDtypeStruct((seqs, 2, chunks, 128, CH), bf16),
            jax.ShapeDtypeStruct((seqs, owners, halves, 1, 128), f32),
        ],
        compiler_params=pltpu.CompilerParams(vmem_limit_bytes=40 << 20),
        name="qkv",
        cost_estimate=cost(2 * gathered.size * 384, gathered.size * 4),
    )(lens, gathered, weight, bias)


def step_on(q, j, count):
    last = j + 1 == count
    return jnp.where(last, q + 1, q), jnp.where(last, 0, j + 1)


def assemble(ref, q, head, core):
    if not head:
        return ref[0, 0, q]
    at = pl.multiple_of(core * 512, 512)
    return jnp.concatenate([ref[0, 0, 2 * q, :, pl.ds(at, 512)], ref[0, 0, 2 * q + 1, :, pl.ds(at, 512)]], axis=1)


def fwd_kernel(shared, len_ref, core_ref, q_ref, k_ref, v_ref, size_ref, out_ref, lse_ref, acc, probs, qa, shifts):
    seq = pl.program_id(0)
    count = lax.div(len_ref[seq] + (CH - 1), CH)
    parts = 2 if shared else 4
    lane = lax.broadcasted_iota(jnp.int32, (1, 128), 1)
    sizes = functools.reduce(jnp.maximum, [size_ref[0, o, h] for o in range(size_ref.shape[1]) for h in range(size_ref.shape[2])])
    widest = jnp.sqrt(jnp.max(jnp.where(lane == int(shared), sizes, 0.0), axis=1, keepdims=True))

    for part in range(parts):
        q_t = assemble(q_ref, part, shared, core_ref[0])
        wide = q_t.astype(f32)
        shift = jnp.sqrt(jnp.sum(wide * wide, axis=0, keepdims=True)) * widest
        shifts[part] = shift
        qa[part] = with_shift(q_t, shift).astype(bf16)

    def raised(part, j):
        return jnp.exp2(dg(k_ref[0, 0, j], qa[part], 1, 0)).astype(bf16)

    probs[0] = raised(0, 0)

    def body(t, carry):
        part, j = carry
        now = t & 1
        part_next, j_next = step_on(part, j, count)
        before = jnp.where(j == 0, 0.0, acc[...])
        acc[...] = before + dg(v_ref[0, 0, j], probs[now], 1, 0)
        probs[1 - now] = raised(jnp.minimum(part_next, parts - 1), j_next)

        @pl.when(j + 1 == count)
        def _():
            total = acc[HD:HD + 1]
            fine = (jnp.min(total) > 2.0 ** -90) & (jnp.max(total) < 2.0 ** 60)

            @pl.when(jnp.logical_not(fine))
            def _():
                plain = qa[part].astype(f32)
                row = lax.broadcasted_iota(jnp.int32, plain.shape, 0)
                qa[part] = jnp.where((row >= HD) & (row < HD + 3), 0.0, plain).astype(bf16)

                def peak(i, top):
                    return jnp.maximum(top, jnp.max(dg(k_ref[0, 0, i], qa[part], 1, 0), axis=0, keepdims=True))
                shift = lax.fori_loop(0, count, peak, jnp.full((1, BQ), FAR, f32))
                shifts[part] = shift
                qa[part] = with_shift(plain[:HD], shift).astype(bf16)
                acc[...] = jnp.zeros_like(acc)

                def again(i, carry):
                    acc[...] += dg(v_ref[0, 0, i], raised(part, i), 1, 0)
                    return carry
                lax.fori_loop(0, count, again, 0)

            total = acc[HD:HD + 1]
            mixed = (acc[:HD] * (1.0 / total)).astype(bf16)
            lse_ref[0, part] = shifts[part] + jnp.log2(total)
            if shared:
                out_ref[0, 2 * part] = mixed[:, :512]
                out_ref[0, 2 * part + 1] = mixed[:, 512:]
            else:
                out_ref[0, part] = mixed
        return part_next, j_next

    lax.fori_loop(0, parts * count, body, (0, 0))


def head_spec(shared, *dims):
    zeros = (0,) * len(dims)
    return pl.BlockSpec((1, 1) + dims, lambda s, n, c: (s, int(shared)) + zeros)


def seq_spec(*dims):
    zeros = (0,) * len(dims)
    return pl.BlockSpec((1,) + dims, lambda s, n, c: (s,) + zeros)


def cost(flops, moved, exps=0):
    return pl.CostEstimate(flops=int(flops), bytes_accessed=int(moved), transcendentals=int(exps))


def attend_forward(shared, q, k, v, sizes, lens, core):
    seqs, _, owners, _, local = q.shape
    chunks = k.shape[2]
    held = local // 2 if shared else local
    parts = owners * held // BQ
    pairs = seqs * parts * BQ * chunks * CH * 0.6
    return pl.pallas_call(
        functools.partial(fwd_kernel, shared),
        grid_spec=pltpu.PrefetchScalarGridSpec(
            num_scalar_prefetch=2, grid=(seqs,),
            in_specs=[
                head_spec(shared, owners, HD, local), head_spec(shared, chunks, CH, 128), head_spec(shared, chunks, 128, CH),
                seq_spec(*sizes.shape[1:]),
            ],
            out_specs=[seq_spec(owners, HD, held), seq_spec(parts, 1, BQ)],
            scratch_shapes=[
                pltpu.VMEM((128, BQ), f32), pltpu.VMEM((2, CH, BQ), bf16), pltpu.VMEM((parts, 128, BQ), bf16),
                pltpu.VMEM((parts, 1, BQ), f32),
            ]),
        out_shape=[
            jax.ShapeDtypeStruct((seqs, owners, HD, held), bf16),
            jax.ShapeDtypeStruct((seqs, parts, 1, BQ), f32),
        ],
        compiler_params=pltpu.CompilerParams(vmem_limit_bytes=48 << 20),
        cost_estimate=cost(pairs * 1024, seqs * chunks * CH * 512, pairs),
        name="attend_forward_shared" if shared else "attend_forward_own",
    )(lens, core, q, k, v, sizes)


def bwd_kernel(shared, len_ref, core_ref, q_ref, k_ref, v_ref, lse_ref, out_ref, gout_ref, *rest):
    if shared:
        dq_ref, dkv_ref, dk_acc, dv_acc, dq_acc, qa, qat, ga, gat, pb, db = rest
    else:
        dqkv_ref, dk_acc, dv_acc, dq_acc, qa, qat, ga, gat, pb, db = rest
    seq = pl.program_id(0)
    count = lax.div(len_ref[seq] + (CH - 1), CH)
    chunks = k_ref.shape[2]
    parts = 2 if shared else 4
    dk_acc[...] = jnp.zeros_like(dk_acc)
    dv_acc[...] = jnp.zeros_like(dv_acc)

    def piece(ref, part):
        if shared:
            return jnp.concatenate([ref[0, 2 * part], ref[0, 2 * part + 1]], axis=1)
        return ref[0, part]

    for part in range(parts):
        q_full = with_shift(assemble(q_ref, part, shared, core_ref[0]), lse_ref[0, part])
        qat[part] = q_full.astype(bf16)
        qa[part] = q_full.T.astype(bf16)
        g_t = piece(gout_ref, part)
        meet = jnp.sum(g_t.astype(f32) * piece(out_ref, part).astype(f32), axis=0, keepdims=True)
        g_full = with_shift(g_t, meet)
        gat[part] = g_full.astype(bf16)
        ga[part] = g_full.T.astype(bf16)

    def ahead(part, j, slot):
        raised = jnp.exp2(dg(qa[part], k_ref[0, 0, j], 1, 1))
        pb[slot] = raised.astype(bf16)
        db[slot] = (raised * dg(ga[part], v_ref[0, 0, j], 1, 0)).astype(bf16)

    ahead(0, 0, 0)

    def body(t, carry):
        part, j = carry
        now = t & 1
        part_next, j_next = step_on(part, j, count)
        dv_acc[j] += dg(gat[part], pb[now], 1, 0)[:HD]
        dk_acc[j] += dg(qat[part], db[now], 1, 0)[:HD]
        before = jnp.where(j == 0, 0.0, dq_acc[...])
        dq_acc[...] = before + dg(db[now], k_ref[0, 0, j], 1, 0)
        ahead(jnp.minimum(part_next, parts - 1), j_next, 1 - now)

        @pl.when(j + 1 == count)
        def _():
            dq_t = (dq_acc[...] * 0.125).T[:HD].astype(bf16)
            if shared:
                dq_ref[0, 2 * part] = dq_t[:, :512]
                dq_ref[0, 2 * part + 1] = dq_t[:, 512:]
            else:
                dqkv_ref[0, part, 0] = dq_t
        return part_next, j_next

    lax.fori_loop(0, parts * count, body, (0, 0))
    for j in range(chunks):
        for owner in range(4):
            cols = slice(owner * 128, (owner + 1) * 128)
            dk = (dk_acc[j, :, cols] * LN2).astype(bf16)
            dv = dv_acc[j, :, cols].astype(bf16)
            if shared:
                dkv_ref[0, 0, owner, :, j * 128:(j + 1) * 128] = dk
                dkv_ref[1, 0, owner, :, j * 128:(j + 1) * 128] = dv
            else:
                dqkv_ref[0, owner, 1, :, j * 128:(j + 1) * 128] = dk
                dqkv_ref[0, owner, 2, :, j * 128:(j + 1) * 128] = dv


def attend_backward(shared, q, k, v, lse, out, g_out, lens, core):
    seqs, _, owners, _, local = q.shape
    chunks = k.shape[2]
    held = out.shape[3]
    parts = owners * held // BQ
    pairs = seqs * parts * BQ * chunks * CH * 0.6
    shape = jax.ShapeDtypeStruct
    if shared:
        out_specs = [seq_spec(owners, HD, held), pl.BlockSpec((2, 1, owners, HD, local), lambda s, n, c: (0, s, 0, 0, 0))]
        out_shape = [shape((seqs, owners, HD, held), bf16), shape((2, seqs, owners, HD, local), bf16)]
    else:
        out_specs = [seq_spec(owners, 3, HD, local)]
        out_shape = [shape((seqs, owners, 3, HD, local), bf16)]
    return pl.pallas_call(
        functools.partial(bwd_kernel, shared),
        grid_spec=pltpu.PrefetchScalarGridSpec(
            num_scalar_prefetch=2, grid=(seqs,),
            in_specs=[
                head_spec(shared, owners, HD, local), head_spec(shared, chunks, CH, 128), head_spec(shared, chunks, 128, CH),
                seq_spec(parts, 1, BQ), seq_spec(owners, HD, held), seq_spec(owners, HD, held),
            ],
            out_specs=out_specs,
            scratch_shapes=[
                pltpu.VMEM((chunks, HD, CH), f32), pltpu.VMEM((chunks, HD, CH), f32), pltpu.VMEM((BQ, 128), f32),
                pltpu.VMEM((parts, BQ, 128), bf16), pltpu.VMEM((parts, 128, BQ), bf16),
                pltpu.VMEM((parts, BQ, 128), bf16), pltpu.VMEM((parts, 128, BQ), bf16),
                pltpu.VMEM((2, BQ, CH), bf16), pltpu.VMEM((2, BQ, CH), bf16),
            ]),
        out_shape=out_shape,
        compiler_params=pltpu.CompilerParams(vmem_limit_bytes=56 << 20),
        cost_estimate=cost(pairs * 100, seqs * chunks * CH * 2048),
        name="attend_backward_shared" if shared else "attend_backward_own",
    )(lens, core, q, k, v, lse, out, g_out)


def gelu_pair(u):
    half = 0.5 * (1.0 + lax.erf(u * 0.7071067811865476))
    return u * half, half + u * (0.3989422804014327 * jnp.exp2(u * u * (-0.5 * LOG2E)))


def norm_stats(v):
    mean = jnp.mean(v, axis=-1, keepdims=True)
    centred = v - mean
    inverse = lax.rsqrt(jnp.mean(centred * centred, axis=-1, keepdims=True) + 1e-12)
    return centred * inverse, inverse


def norm_back(grad, xhat, inverse, gain):
    g = grad * gain
    return (g - jnp.mean(g, axis=-1, keepdims=True) - xhat * jnp.mean(g * xhat, axis=-1, keepdims=True)) * inverse


def weight_part(ref, first, rows):
    part = ref[:, first:first + rows, :]
    return part.reshape(part.shape[0] * rows, part.shape[2])


def ffn_kernel(spans, at_ref, x_ref, own_ref, sh_ref, cot_ref, w_ref, bin_ref, vec_ref,
               act_out, resid_out, gown_out, gsh_out, active_out, dinner_out, normed_out, douter_out, dbranch_out,
               vec_sum, bin_sum, slope):
    step = pl.program_id(0)
    width = x_ref.shape[-1]
    rows = jnp.concatenate([x_ref[a, 0, z, 0] for z in range(spans) for a in range(2)], axis=0).astype(f32)
    mixed_t = jnp.concatenate(
        [part for p in range(4) for part in (own_ref[p, 0], sh_ref[p, 0], own_ref[p, 1])], axis=0)
    vec = vec_ref[...]
    branch = dg(mixed_t, weight_part(w_ref, 768, 96), 0, 0) + vec[0:1]
    xhat1, inv1 = norm_stats(rows + branch)
    normed = xhat1 * vec[1:2] + vec[2:3]
    low = normed.astype(bf16)
    normed_out[...] = low
    outer = normed + vec[3:4]
    for n in range(4):
        cols = slice(n * 768, (n + 1) * 768)
        inner = dg(low, weight_part(w_ref, 384 + 96 * n, 96), 1, 0) + bin_ref[:, cols]
        value, bend = gelu_pair(inner)
        active_out[:, cols] = value.astype(bf16)
        slope[:, cols] = bend.astype(bf16)
    outer = outer + dg(active_out[...], weight_part(w_ref, 0, 384), 1, 0)
    xhat2, inv2 = norm_stats(outer)
    act_out[...] = (xhat2 * vec[4:5] + vec[5:6]).astype(bf16)
    cot = cot_ref[...].astype(f32)
    d2 = norm_back(cot, xhat2, inv2, vec[4:5])
    d_outer = d2.astype(bf16)
    douter_out[...] = d_outer
    d_normed = d2
    sums_in = []
    for n in range(4):
        cols = slice(n * 768, (n + 1) * 768)
        d_active = dg(d_outer, weight_part(w_ref.at[2 * n:2 * n + 2], 0, 384), 1, 1)
        d_inner = (d_active * slope[:, cols].astype(f32)).astype(bf16)
        dinner_out[:, cols] = d_inner
        sums_in.append(jnp.sum(d_inner.astype(f32), axis=0, keepdims=True))
        d_normed = d_normed + dg(d_inner, weight_part(w_ref, 384 + 96 * n, 96), 1, 1)
    d1 = norm_back(d_normed, xhat1, inv1, vec[1:2])
    resid_out[...] = d1
    d_branch = d1.astype(bf16)
    dbranch_out[...] = d_branch
    g_t = dg(weight_part(w_ref, 768, 96), d_branch, 1, 1).astype(bf16)
    for p in range(4):
        gown_out[p, 0] = g_t[192 * p:192 * p + 64]
        gsh_out[p, 0] = g_t[192 * p + 64:192 * p + 128]
        gown_out[p, 1] = g_t[192 * p + 128:192 * p + 192]
    total = lambda a: jnp.sum(a, axis=0, keepdims=True)
    sums = jnp.concatenate([
        total(d_branch.astype(f32)), total(d_normed * xhat1), total(d_normed),
        total(d_outer.astype(f32)), total(cot * xhat2), total(cot), jnp.zeros((2, width), f32)], axis=0)

    @pl.when(step == 0)
    def _():
        vec_sum[...] = sums
        for n in range(4):
            bin_sum[:, n * 768:(n + 1) * 768] = sums_in[n]

    @pl.when(step > 0)
    def _():
        vec_sum[...] += sums
        for n in range(4):
            bin_sum[:, n * 768:(n + 1) * 768] += sums_in[n]


def feed_forward(gathered, own, sh, cotangent, weights, inner_bias, vectors, at):
    _, _, _, _, stretch, width = gathered.shape
    local = cotangent.shape[0]
    spans = RB // (2 * stretch)
    steps = local // RB
    half_steps = steps // 2
    wide = inner_bias.shape[1]
    rows = lambda n: pl.BlockSpec((RB, n), lambda r, a: (r, 0))
    fixed = lambda *dims: pl.BlockSpec(dims, lambda r, a: (0,) * len(dims))
    own_spec = pl.BlockSpec((4, 2, HD, RB), lambda r, a: (0, 0, 0, r))
    sh_spec = pl.BlockSpec((4, 1, HD, RB), lambda r, a: (0, r // half_steps, 0, r % half_steps))
    shape = jax.ShapeDtypeStruct
    return pl.pallas_call(
        functools.partial(ffn_kernel, spans),
        grid_spec=pltpu.PrefetchScalarGridSpec(
            num_scalar_prefetch=1, grid=(steps,),
            in_specs=[
                pl.BlockSpec((2, 1, spans, 1, stretch, width), lambda r, a: (0, a[1], r, a[0], 0, 0)),
                own_spec, sh_spec, rows(width),
                pl.BlockSpec(weights.shape, lambda r, a: (0, 0, 0), pipeline_mode=pl.Buffered(1)),
                fixed(1, wide), fixed(8, width),
            ],
            out_specs=[
                rows(width), rows(width), own_spec, sh_spec, rows(wide), rows(wide), rows(width), rows(width), rows(width),
                fixed(8, width), fixed(1, wide),
            ],
            scratch_shapes=[pltpu.VMEM((RB, wide), bf16)]),
        out_shape=[
            shape((local, width), bf16), shape((local, width), f32), shape(own.shape, bf16), shape(sh.shape, bf16),
            shape((local, wide), bf16), shape((local, wide), bf16), shape((local, width), bf16),
            shape((local, width), bf16), shape((local, width), bf16), shape((8, width), f32), shape((1, wide), f32),
        ],
        compiler_params=pltpu.CompilerParams(vmem_limit_bytes=60 << 20),
        name="feed_forward",
        cost_estimate=cost(local * width * (width + 2 * wide) * 4, local * wide * 20),
    )(at, gathered, own, sh, cotangent, weights, inner_bias, vectors)


def outer_grad_kernel(scale, active_ref, douter_ref, out_ref):
    made = (dg(active_ref[...], douter_ref[...], 0, 0) * scale).astype(bf16)
    out_ref[...] = made.reshape(out_ref.shape)


def inner_grad_kernel(scale, packed_ref, normed_ref, dinner_ref, own_ref, sh_ref, dbranch_ref, out_ref):
    step = pl.program_id(0)

    @pl.when(step < 4)
    def _():
        out_ref[...] = (dg(normed_ref[...], dinner_ref[...], 0, 0) * scale).astype(bf16).reshape(out_ref.shape)

    @pl.when(step == 4)
    def _():
        mixed_t = jnp.concatenate([
            part for p in range(4)
            for part in (own_ref[p, 0], jnp.concatenate([sh_ref[p, 0], sh_ref[p, 1]], axis=1), own_ref[p, 1])], axis=0)
        out_ref[...] = (dg(mixed_t, dbranch_ref[...], 1, 0) * scale).astype(bf16).reshape(out_ref.shape)


def weight_grads(scale, active, d_outer, normed, d_inner, own, sh, d_branch):
    local, wide = active.shape
    width = normed.shape[1]
    packed = pl.pallas_call(
        functools.partial(outer_grad_kernel, scale), grid=(4,),
        in_specs=[pl.BlockSpec((local, width), lambda m: (0, m)), pl.BlockSpec((local, width), lambda m: (0, 0))],
        out_specs=pl.BlockSpec((2, 384, width), lambda m: (m, 0, 0)),
        out_shape=jax.ShapeDtypeStruct((8, 896, width), bf16),
        compiler_params=pltpu.CompilerParams(vmem_limit_bytes=40 << 20), name="outer_grad",
        cost_estimate=cost(2 * local * wide * width, 2 * wide * (local + width)),
    )(active, d_outer)
    fixed = lambda a: pl.BlockSpec(a.shape, lambda n: (0,) * a.ndim)
    return pl.pallas_call(
        functools.partial(inner_grad_kernel, scale), grid=(5,),
        in_specs=[
            pl.BlockSpec(memory_space=pl.ANY), fixed(normed),
            pl.BlockSpec((local, width), lambda n: (0, jnp.minimum(n, 3))), fixed(own), fixed(sh), fixed(d_branch)],
        out_specs=pl.BlockSpec((8, 96, width), lambda n: (0, 4 + n, 0)),
        out_shape=jax.ShapeDtypeStruct((8, 896, width), bf16), input_output_aliases={0: 0},
        compiler_params=pltpu.CompilerParams(vmem_limit_bytes=40 << 20), name="inner_grad",
        cost_estimate=cost(2 * local * (wide + width) * width, 2 * (wide + width) * (local + width)),
    )(packed, normed, d_inner, own, sh, d_branch)


def head_grad_kernel(scale, spans, core_ref, x_ref, own_ref, dqs_ref, dks_ref, out_ref, bias_out, acc, bias_acc):
    seq, owner, half = pl.program_id(0), pl.program_id(1), pl.program_id(2)
    first = (seq == 0) & (owner == 0) & (half == 0)
    last = (seq == pl.num_programs(0) - 1) & (owner == pl.num_programs(1) - 1) & (half == pl.num_programs(2) - 1)
    rows = jnp.concatenate([x_ref[a, 0, z, 0] for z in range(spans) for a in range(2)], axis=0)
    d_t = jnp.concatenate([
        own_ref[0, 0, 0], jnp.where(half == core_ref[0], dqs_ref[0, 0].astype(f32), 0.0).astype(bf16),
        own_ref[0, 0, 1], dks_ref[0, 0, 0], own_ref[0, 0, 2], dks_ref[1, 0, 0]], axis=0)

    @pl.when(first)
    def _():
        acc[...] = jnp.zeros_like(acc)
        bias_acc[...] = jnp.zeros_like(bias_acc)
    acc[...] += dg(d_t, rows, 1, 0)
    bias_acc[...] += dg(jnp.ones((8, d_t.shape[1]), bf16), d_t, 1, 1)

    @pl.when(last)
    def _():
        out_ref[...] = (acc[...] * scale).T.astype(bf16)
        bias_out[...] = bias_acc[...] * scale


def head_grads(scale, gathered, dqkv_own, dq_sh, dkv_sh, core):
    _, owners, zs, seqs, stretch, width = gathered.shape
    local = 2 * zs * stretch
    spans = 512 // (2 * stretch)
    return pl.pallas_call(
        functools.partial(head_grad_kernel, scale, spans),
        grid_spec=pltpu.PrefetchScalarGridSpec(
            num_scalar_prefetch=1, grid=(seqs, owners, local // 512),
            in_specs=[
                pl.BlockSpec((2, 1, spans, 1, stretch, width), lambda s, o, h, c: (0, o, h, s, 0, 0)),
                pl.BlockSpec((1, 1, 3, HD, 512), lambda s, o, h, c: (s, o, 0, 0, h)),
                pl.BlockSpec((1, 1, HD, 512), lambda s, o, h, c: (s, o, 0, 0)),
                pl.BlockSpec((2, 1, 1, HD, 512), lambda s, o, h, c: (0, s, o, 0, h))],
            out_specs=[pl.BlockSpec((width, 384), lambda s, o, h, c: (0, 0)), pl.BlockSpec((8, 384), lambda s, o, h, c: (0, 0))],
            scratch_shapes=[pltpu.VMEM((384, width), f32), pltpu.VMEM((8, 384), f32)]),
        out_shape=[jax.ShapeDtypeStruct((width, 384), bf16), jax.ShapeDtypeStruct((8, 384), f32)],
        compiler_params=pltpu.CompilerParams(vmem_limit_bytes=40 << 20), name="head_grads",
        cost_estimate=cost(seqs * owners * local * 768 * width, gathered.size * 2),
    )(core, gathered, dqkv_own, dq_sh, dkv_sh)


def token_grad_kernel(own_ref, dqs_ref, dks_ref, w_ref, resid_ref, out_ref):
    total = resid_ref[...]
    for kind in range(3):
        made = jnp.concatenate([part for p in range(4) for part in (
            own_ref[p, 0, kind], dqs_ref[p, 0] if kind == 0 else dks_ref[p, kind - 1], own_ref[p, 1, kind])], axis=0)
        total = total + dg(made, weight_part(w_ref, 96 * kind, 96), 0, 1)
    out_ref[...] = total.astype(bf16)


def token_grad(own, dq_sh, dkv_sh, weights, resid):
    local, width = resid.shape
    steps = local // RB
    half_steps = steps // 2
    rows = pl.BlockSpec((RB, width), lambda r: (r, 0))
    return pl.pallas_call(
        token_grad_kernel, grid=(steps,),
        in_specs=[
            pl.BlockSpec((4, 2, 3, HD, RB), lambda r: (0, 0, 0, 0, r)),
            pl.BlockSpec((4, 1, HD, RB), lambda r: (0, r // half_steps, 0, r % half_steps)),
            pl.BlockSpec((4, 2, HD, RB), lambda r: (0, 0, 0, r)),
            pl.BlockSpec(weights.shape, lambda r: (0, 0, 0)), rows],
        out_specs=rows, out_shape=jax.ShapeDtypeStruct((local, width), bf16),
        compiler_params=pltpu.CompilerParams(vmem_limit_bytes=40 << 20), name="token_grad",
        cost_estimate=cost(local * width * width * 6, local * width * 12),
    )(own, dq_sh, dkv_sh, weights, resid)


PAIR = ("x", "y", "c")
ALL = ("z", "x", "y", "c")
SHARD = ("z", "x")


def canonical(packed, shards):
    if shards == 8:
        return packed
    width = packed.shape[2]
    per, keep = 96 * 8 // shards, shards // 8
    outer = packed[:, :4 * per].reshape(8, 384, width)
    inner = packed[:, 4 * per:8 * per].reshape(8, keep, 4, per, width).transpose(0, 2, 1, 3, 4).reshape(8, 384, width)
    output = packed[:, 8 * per:9 * per].reshape(8, 96, width)
    return jnp.concatenate([outer, inner, output, jnp.zeros((8, 32, width), packed.dtype)], axis=1)


def from_canonical(packed, shards):
    if shards == 8:
        return packed
    width = packed.shape[2]
    per, keep = 96 * 8 // shards, shards // 8
    outer = packed[:, :384].reshape(shards, 4 * per, width)
    inner = packed[:, 384:768].reshape(8, 4, keep, per, width).transpose(0, 2, 1, 3, 4).reshape(shards, 4 * per, width)
    output = packed[:, 768:864].reshape(shards, per, width)
    return jnp.concatenate([outer, inner, output, jnp.zeros((shards, 32, width), packed.dtype)], axis=1)


def canonical_heads(packed, shards):
    if shards == 8:
        return packed
    width = packed.shape[2]
    per = 96 * 8 // shards
    parts = [packed[:, k * per:(k + 1) * per].reshape(8, 96, width) for k in range(3)]
    return jnp.concatenate(parts + [jnp.zeros((8, 32, width), packed.dtype)], axis=1)


def quarter(rows):
    place = lax.axis_index("y") * 2 + lax.axis_index("c")
    part = rows.shape[0] // 4
    return lax.dynamic_slice_in_dim(rows, place * part, part)


def body(tokens, lengths, deal_order, w_query, w_key, w_value, w_output, b_query, b_value, b_output,
         ln1_gain, ln1_shift, w_inner, b_inner, w_outer, b_outer, ln2_gain, ln2_shift, cotangent):
    zs = lax.axis_size("z")
    shards = 2 * zs
    devices = shards * 4
    scale = 1.0 / devices
    seq_count, _, stretch, width = tokens.shape
    per = w_query.shape[0]
    x, y, c = lax.axis_index("x"), lax.axis_index("y"), lax.axis_index("c")
    core = c.astype(jnp.int32)[None]

    ordered = jnp.take(tokens[:, 0], deal_order, axis=0).reshape(zs, 2, stretch, width)
    spread = lax.all_to_all(ordered, "z", split_axis=0, concat_axis=0, tiled=True)

    def head_columns(matrix):
        heads = matrix.reshape(per, 2, 2, 3, HD)
        mine = lax.dynamic_index_in_dim(heads, y, axis=2, keepdims=False)
        own = lax.dynamic_index_in_dim(mine, 2 * c, axis=2, keepdims=False)
        return [own, mine[:, :, 1]]
    columns = jnp.concatenate(
        [col for matrix in (w_query, w_key, w_value) for col in head_columns(matrix)], axis=2).reshape(per, 768)
    pad = lambda v, n: jnp.pad(v, (0, n - v.shape[0]))[None]
    head_pack = jnp.concatenate(
        [columns, pad(b_query, width), pad(b_value, width), jnp.zeros((14, width), bf16)], axis=0)
    head_all = lax.all_gather(head_pack, SHARD, axis=0, tiled=False)
    head_weight = lax.dynamic_index_in_dim(
        head_all[:, :per].reshape(width, 2, 384), x, axis=1, keepdims=False)

    def head_bias(row):
        heads = head_all[:, per + row, :per].reshape(2, 2, 3, HD)
        mine = lax.dynamic_slice(heads, (x, y, 0, 0), (1, 1, 3, HD))[0, 0]
        return [lax.dynamic_index_in_dim(mine, 2 * c, axis=0, keepdims=False), mine[1]]
    bias_row = jnp.concatenate(head_bias(0) + [jnp.zeros((2 * HD,), bf16)] + head_bias(1)).astype(f32)[None]

    gathered = lax.all_gather(spread, PAIR, axis=0, tiled=False).reshape(2, 4, zs, 2, stretch, width)

    panels = w_inner.reshape(per, 4, 768)
    vectors = (b_output, ln1_gain, ln1_shift, b_outer, ln2_gain, ln2_shift)
    layer_pack = jnp.concatenate(
        [w_outer] + [panels[:, n] for n in range(4)] + [w_output]
        + [pad(b_inner, width)] + [pad(v, width) for v in vectors] + [jnp.zeros((25, width), bf16)], axis=0)
    layer_all = lax.all_gather(quarter(layer_pack), ALL, axis=0, tiled=True).reshape(shards, 9 * per + 32, width)
    layer_weights = canonical(layer_all, shards)
    inner_bias = layer_all[:, 9 * per, :4 * per].reshape(1, 3072).astype(f32)
    vector_rows = jnp.concatenate(
        [layer_all[:, 9 * per + 1 + n, :per].reshape(1, width) for n in range(6)] + [jnp.zeros((2, width), bf16)],
        axis=0).astype(f32)
    back_pack = jnp.concatenate([w_query, w_key, w_value, jnp.zeros((32, width), bf16)], axis=0)
    back_all = lax.all_gather(quarter(back_pack), ALL, axis=0, tiled=True).reshape(shards, 3 * per + 32, width)

    group = lax.axis_index("z")
    slots = lax.dynamic_slice_in_dim(deal_order, group * 2, 2)
    matches = slots[:, None] == jnp.arange(seq_count, dtype=jnp.int32)[None, :]
    lens = jnp.sum(jnp.where(matches, lengths[None, :], 0), axis=1).astype(jnp.int32)

    q, k, v, sizes = project(gathered, head_weight, bias_row, lens)

    def swap(array):
        flat = array.reshape((8,) + array.shape[2:])
        return lax.all_to_all(flat, PAIR, split_axis=0, concat_axis=0, tiled=True)

    def to_tokens(array):
        return swap(array).reshape((4, 2) + array.shape[2:])

    def to_heads(array):
        return swap(array).reshape((2, 4) + array.shape[2:])

    own, lse_own = attend_forward(False, q, k, v, sizes, lens, core)
    own_t = to_tokens(own)
    own, later_core = lax.optimization_barrier((own, core))
    sh, lse_sh = attend_forward(True, q, k, v, sizes, lens, later_core)
    sh_sent, own_t = lax.optimization_barrier((sh, own_t))
    sh_t = to_tokens(sh_sent)
    at = jnp.stack([x, y * 2 + c]).astype(jnp.int32)
    (act, resid, g_own, g_sh, active, d_inner, normed, d_outer, d_branch, vec_sums, bin_sums) = feed_forward(
        gathered, own_t, sh_t, cotangent.reshape(-1, width), layer_weights, inner_bias, vector_rows, at)
    g_own_h, g_sh_h = to_heads(g_own), to_heads(g_sh)
    active, back_all = lax.optimization_barrier((active, back_all))
    packed = weight_grads(scale, active, d_outer, normed, d_inner, own_t, sh_t, d_branch)
    sums = jnp.concatenate([bin_sums.reshape(4, width), vec_sums, jnp.zeros((20, width), f32)], axis=0) * scale
    packed = packed.at[:, 864:].set(jnp.broadcast_to(sums.astype(bf16)[None], (8, 32, width)))
    ready = from_canonical(packed, shards)
    if shards != 8:
        ready = ready.at[:, 9 * per:].set(jnp.broadcast_to(sums.astype(bf16)[None], (shards, 32, width)))
    ready, g_own_h = lax.optimization_barrier((ready, g_own_h))
    back_weights = canonical_heads(back_all, shards)
    layer_part = lax.psum_scatter(ready.reshape(-1, width), ALL, scatter_dimension=0, tiled=True)

    dqkv_own, = attend_backward(False, q, k, v, lse_own, own, g_own_h, lens, core)
    back_own = to_tokens(dqkv_own)
    dqkv_own, later_core = lax.optimization_barrier((dqkv_own, core))
    dq_sh, dkv_sh = attend_backward(True, q, k, v, lse_sh, sh, g_sh_h, lens, later_core)
    dq_sent, back_own = lax.optimization_barrier((dq_sh, back_own))
    back_q = to_tokens(dq_sent)
    kept = lax.dynamic_index_in_dim(dkv_sh, c, axis=0, keepdims=False)
    given = lax.dynamic_index_in_dim(dkv_sh, 1 - c, axis=0, keepdims=False)
    taken = lax.ppermute(given, "c", [(0, 1), (1, 0)])
    back_kv = to_tokens((kept.astype(f32) + taken.astype(f32)).astype(bf16))
    d_heads, d_bias = head_grads(scale, gathered, dqkv_own, dq_sh, dkv_sh, core)
    chunk = width // zs
    head_ready = jnp.concatenate([
        d_heads.reshape(zs, chunk, 384),
        jnp.broadcast_to(d_bias[:1].astype(bf16)[None], (zs, 16, 384))], axis=1)
    head_ready, layer_part = lax.optimization_barrier((head_ready, layer_part))
    head_part = lax.psum_scatter(head_ready.reshape(-1, 384), "z", scatter_dimension=0, tiled=True)
    head_grads_all = lax.all_gather(head_part, PAIR, axis=0, tiled=False).reshape(4, 2, chunk + 16, 6, HD).astype(f32)

    layer_grads = lax.all_gather(layer_part, ("y", "c"), axis=0, tiled=True)
    d_rows = token_grad(back_own, back_q, back_kv, back_weights, resid)
    returned = lax.all_to_all(
        d_rows.reshape(shards, stretch, width), SHARD, split_axis=0, concat_axis=0, tiled=True)
    d_tokens = jnp.zeros_like(returned).at[deal_order].set(returned)[:, None]

    mine = lax.dynamic_slice_in_dim(head_grads_all, x * per, per, axis=2)

    def full(part, kind):
        own_part, shared = part[:, :, :, 2 * kind], part[:, :, :, 2 * kind + 1]
        both = shared[:, 0] + shared[:, 1]
        joined = jnp.stack([own_part[:, 0], both, own_part[:, 1]], axis=1)
        return joined.transpose(2, 0, 1, 3).reshape(part.shape[2], width)
    d_wq, d_wk, d_wv = (full(mine, kind) for kind in range(3))
    bias_part = head_grads_all[:, :, chunk:chunk + 1]
    place = lax.axis_index("z") * 2 + x
    own_slice = lambda row, n: lax.dynamic_slice_in_dim(row, place * n, n)
    d_bq = own_slice(full(bias_part, 0)[0], per)
    d_bv = own_slice(full(bias_part, 2)[0], per)

    layer_grads = layer_grads.astype(f32)
    d_wouter = layer_grads[:4 * per]
    d_winner = layer_grads[4 * per:8 * per].reshape(4, per, width).transpose(1, 0, 2).reshape(per, 4 * width)
    d_woutput = layer_grads[8 * per:9 * per]
    d_binner = own_slice(layer_grads[9 * per:9 * per + 4].reshape(-1), 4 * per)
    d_bo, d_g1, d_s1, d_bout, d_g2, d_s2 = (own_slice(layer_grads[9 * per + 4 + n], per) for n in range(6))
    return (act.reshape(1, shards, stretch, width), d_tokens, d_wq, d_wk, d_wv, d_woutput, d_bq, d_bv, d_bo,
            d_g1, d_s1, d_winner, d_binner, d_wouter, d_bout, d_g2, d_s2)


def solution(mesh):
    shards, splits = mesh.devices.shape
    fine = Mesh(mesh.devices.reshape(shards // 2, 2, splits // 2, 2), ALL)
    S, Q = SHARD, ("y", "c")
    row, mat = P(S), P(S, None)
    return jax.shard_map(
        body, mesh=fine,
        in_specs=(P(None, S, Q, None), P(), P(), mat, mat, mat, mat, row, row, row, row, row, mat, row, mat, row, row, row,
                  P(S, None, Q, None)),
        out_specs=(P(S, None, Q, None), P(None, S, Q, None), mat, mat, mat, mat, row, row, row, row, row, mat, row, mat,
                   row, row, row),
        check_vma=False)
```

```python
import functools, math
import jax
import jax.numpy as jnp
from jax import lax
from jax.experimental import pallas as pl
from jax.experimental.pallas import tpu as pltpu
from jax.sharding import Mesh, PartitionSpec as P

f32, bf16 = jnp.float32, jnp.bfloat16
LOG2E = 1.4426950408889634
LN2 = 0.6931471805599453
CH = 512
BQ = 1024
RB = 256
HD = 64
FAR = -1.0e30

def dg(a, b, ca, cb):
    return lax.dot_general(a, b, (((ca,), (cb,)), ((), ())), preferred_element_type=f32)


def three_parts(row):
    hi = row.astype(bf16).astype(f32)
    rest = row - hi
    mid = rest.astype(bf16).astype(f32)
    return hi, mid, rest - mid


def with_shift(top, shift):
    hi, mid, low = three_parts(shift)
    row = lax.broadcasted_iota(jnp.int32, (HD, top.shape[1]), 0)
    tail = jnp.where(row == 0, -hi, jnp.where(row == 1, -mid, jnp.where(row == 2, -low, jnp.where(row == 3, 1.0, 0.0))))
    return jnp.concatenate([top.astype(f32), tail], axis=0)


def load_rows(rows, ref, spans, x):
    stretch = ref.shape[3]
    for z in range(spans):
        for a in range(2):
            at = (2 * z + a) * stretch
            rows[at:at + stretch] = ref[0, a ^ x, z]


def qkv_kernel(stretch, spans, info, near_ref, far_ref, w_ref, b_ref, q_out, k_out, v_out, size_out, rows):
    away, half = pl.program_id(0), pl.program_id(2)
    owner = ((pl.program_id(1) ^ info[2]) << 1) | (away ^ info[3])

    @pl.when(away == 0)
    def _():
        load_rows(rows, near_ref, spans, info[1])

    @pl.when(away == 1)
    def _():
        load_rows(rows, far_ref, spans, info[1])
    made = dg(rows[...], w_ref[...], 1, 0) + b_ref[...]
    count = rows.shape[0]
    q_t = (made[:, :128] * (LOG2E / 8.0)).T
    q_out[0, 0] = q_t[:HD].astype(bf16)
    q_out[1, 0] = q_t[HD:].astype(bf16)
    lane = lax.broadcasted_iota(jnp.int32, (count, 128), 1)
    row = lax.broadcasted_iota(jnp.int32, (count, 128), 0) + half * count
    shift = int(math.log2(stretch))
    position = lax.shift_left(lax.shift_right_logical(row, shift), shift + 2) + owner * stretch + (row & (stretch - 1))
    hidden = jnp.where(position < info[0], 0.0, FAR)
    tail = jnp.where(lane == HD + 3, hidden, jnp.where(lane < HD + 3, 1.0, 0.0))
    keys = made[:, 128:256]
    picks = lax.broadcasted_iota(jnp.int32, (128, 128), 0) // HD == lax.broadcasted_iota(jnp.int32, (128, 128), 1)
    sizes = dg((keys * keys).astype(bf16), jnp.where(picks, 1.0, 0.0).astype(bf16), 1, 0)
    size_out[0, 0] = jnp.max(sizes, axis=0, keepdims=True)
    for head in range(2):
        turned = keys if head == 0 else pltpu.roll(keys, HD, 1)
        full = jnp.where(lane < HD, turned, tail).astype(bf16)
        for j in range(count // 128):
            k_out[head, j] = full[j * 128:(j + 1) * 128]
    v_t = made[:, 256:384].T
    ones = jnp.where(lax.broadcasted_iota(jnp.int32, (HD, count), 0) < 3, 1.0, 0.0)
    for head in range(2):
        full = jnp.concatenate([v_t[head * HD:(head + 1) * HD], ones], axis=0).astype(bf16)
        for j in range(count // 128):
            v_out[head, j] = full[:, j * 128:(j + 1) * 128]


def owner_of(away, across, info):
    return ((across ^ info[2]) << 1) | (away ^ info[3])


def project(near, far, weight, bias, info):
    _, _, zs, stretch, width = near.shape
    local = 2 * zs * stretch
    spans = 512 // (2 * stretch)
    halves = local // 512
    chunks = 4 * local // CH
    per = chunks // halves
    block = (1, 2, spans, stretch, width)
    return pl.pallas_call(
        functools.partial(qkv_kernel, stretch, spans),
        grid_spec=pltpu.PrefetchScalarGridSpec(
            num_scalar_prefetch=1, grid=(2, 2, halves),
            in_specs=[
                pl.BlockSpec(block, lambda a, o, h, n: (jnp.where(a == 0, o, 1), 0, jnp.where(a == 0, h, halves - 1), 0, 0)),
                pl.BlockSpec(block, lambda a, o, h, n: (jnp.where(a == 0, 0, o), 0, jnp.where(a == 0, 0, h), 0, 0)),
                pl.BlockSpec((width, 384), lambda a, o, h, n: (0, 0)),
                pl.BlockSpec((1, 384), lambda a, o, h, n: (0, 0)),
            ],
            out_specs=[
                pl.BlockSpec((2, 1, HD, 512), lambda a, o, h, n: (0, owner_of(a, o, n), 0, h)),
                pl.BlockSpec((2, per, 128, 128), lambda a, o, h, n: (0, h, owner_of(a, o, n), 0)),
                pl.BlockSpec((2, per, 128, 128), lambda a, o, h, n: (0, h, 0, owner_of(a, o, n))),
                pl.BlockSpec((1, 1, 1, 128), lambda a, o, h, n: (owner_of(a, o, n), h, 0, 0)),
            ],
            scratch_shapes=[pltpu.VMEM((512, width), bf16)]),
        out_shape=[
            jax.ShapeDtypeStruct((2, 4, HD, local), bf16),
            jax.ShapeDtypeStruct((2, chunks, CH, 128), bf16),
            jax.ShapeDtypeStruct((2, chunks, 128, CH), bf16),
            jax.ShapeDtypeStruct((4, halves, 1, 128), f32),
        ],
        compiler_params=pltpu.CompilerParams(vmem_limit_bytes=40 << 20),
        name="qkv",
        cost_estimate=cost(4 * near.size * 384, near.size * 8),
    )(info, near, far, weight, bias)


def step_on(q, j, count):
    last = j + 1 == count
    return jnp.where(last, q + 1, q), jnp.where(last, 0, j + 1)


def assemble(ref, q, shared, core):
    if not shared:
        return ref[0, q]
    at = pl.multiple_of(core * 512, 512)
    return jnp.concatenate([ref[0, 2 * q, :, pl.ds(at, 512)], ref[0, 2 * q + 1, :, pl.ds(at, 512)]], axis=1)


def fwd_kernel(shared, info, q_ref, k_ref, v_ref, size_ref, held_ref, out_ref, lse_ref, acc, probs, qa, shifts):
    count = lax.div(info[0] + (CH - 1), CH)
    parts = 2 if shared else 4
    lane = lax.broadcasted_iota(jnp.int32, (1, 128), 1)
    sizes = functools.reduce(jnp.maximum, [size_ref[o, h] for o in range(size_ref.shape[0]) for h in range(size_ref.shape[1])])
    widest = jnp.sqrt(jnp.max(jnp.where(lane == int(shared), sizes, 0.0), axis=1, keepdims=True))

    for part in range(parts):
        q_t = assemble(q_ref, part, shared, info[3])
        wide = q_t.astype(f32)
        shift = jnp.sqrt(jnp.sum(wide * wide, axis=0, keepdims=True)) * widest
        shifts[part] = shift
        qa[part] = with_shift(q_t, shift).astype(bf16)

    def raised(part, j):
        return jnp.exp2(dg(k_ref[0, j], qa[part], 1, 0)).astype(bf16)

    probs[0] = raised(0, 0)

    def body(t, carry):
        part, j = carry
        now = t & 1
        part_next, j_next = step_on(part, j, count)
        before = jnp.where(j == 0, 0.0, acc[...])
        acc[...] = before + dg(v_ref[0, j], probs[now], 1, 0)
        probs[1 - now] = raised(jnp.minimum(part_next, parts - 1), j_next)

        @pl.when(j + 1 == count)
        def _():
            total = acc[HD:HD + 1]
            fine = (jnp.min(total) > 2.0 ** -90) & (jnp.max(total) < 2.0 ** 60)

            @pl.when(jnp.logical_not(fine))
            def _():
                plain = qa[part].astype(f32)
                row = lax.broadcasted_iota(jnp.int32, plain.shape, 0)
                qa[part] = jnp.where((row >= HD) & (row < HD + 3), 0.0, plain).astype(bf16)

                def peak(i, top):
                    return jnp.maximum(top, jnp.max(dg(k_ref[0, i], qa[part], 1, 0), axis=0, keepdims=True))
                shift = lax.fori_loop(0, count, peak, jnp.full((1, BQ), FAR, f32))
                shifts[part] = shift
                qa[part] = with_shift(plain[:HD], shift).astype(bf16)
                acc[...] = jnp.zeros_like(acc)

                def again(i, carry):
                    acc[...] += dg(v_ref[0, i], raised(part, i), 1, 0)
                    return carry
                lax.fori_loop(0, count, again, 0)

            total = acc[HD:HD + 1]
            mixed = (acc[:HD] * (1.0 / total)).astype(bf16)
            lse_ref[part] = shifts[part] + jnp.log2(total)
            if shared:
                out_ref[0, 2 * part] = mixed[:, :512]
                out_ref[0, 2 * part + 1] = mixed[:, 512:]
            else:
                out_ref[0, part] = mixed
        return part_next, j_next

    lax.fori_loop(0, parts * count, body, (0, 0))


def head_spec(shared, *dims):
    zeros = (0,) * len(dims)
    return pl.BlockSpec((1,) + dims, lambda i, n: (int(shared),) + zeros)


def whole_spec(*dims):
    return pl.BlockSpec(dims, lambda i, n: (0,) * len(dims))


def cost(flops, moved, exps=0):
    return pl.CostEstimate(flops=int(flops), bytes_accessed=int(moved), transcendentals=int(exps))


def attend_forward(shared, seq, q, k, v, sizes, info, held):
    _, owners, _, local = q.shape
    chunks = k.shape[1]
    wide = local // 2 if shared else local
    parts = owners * wide // BQ
    pairs = parts * BQ * chunks * CH * 0.6
    shape = jax.ShapeDtypeStruct((2, owners, HD, wide), bf16)
    first = held is None
    if first:
        kernel = lambda info, q, k, v, size, *rest: fwd_kernel(shared, info, q, k, v, size, None, *rest)
    else:
        kernel = functools.partial(fwd_kernel, shared)
    return pl.pallas_call(
        kernel,
        grid_spec=pltpu.PrefetchScalarGridSpec(
            num_scalar_prefetch=1, grid=(1,),
            in_specs=[
                head_spec(shared, owners, HD, local), head_spec(shared, chunks, CH, 128), head_spec(shared, chunks, 128, CH),
                whole_spec(*sizes.shape),
            ] + ([] if first else [pl.BlockSpec(memory_space=pl.ANY)]),
            out_specs=[pl.BlockSpec((1, owners, HD, wide), lambda i, n: (seq, 0, 0, 0)), whole_spec(parts, 1, BQ)],
            scratch_shapes=[
                pltpu.VMEM((128, BQ), f32), pltpu.VMEM((2, CH, BQ), bf16), pltpu.VMEM((parts, 128, BQ), bf16),
                pltpu.VMEM((parts, 1, BQ), f32),
            ]),
        out_shape=[shape, jax.ShapeDtypeStruct((parts, 1, BQ), f32)],
        input_output_aliases={} if first else {5: 0},
        compiler_params=pltpu.CompilerParams(vmem_limit_bytes=48 << 20),
        cost_estimate=cost(pairs * 1024, chunks * CH * 512, pairs),
        name="attend_forward_shared" if shared else "attend_forward_own",
    )(*((info, q, k, v, sizes) + (() if first else (held,))))


def bwd_kernel(shared, first, info, q_ref, k_ref, v_ref, lse_ref, out_ref, gout_ref, *rest):
    rest = rest if first else rest[2 if shared else 1:]
    if shared:
        dq_ref, dkv_ref, dk_acc, dv_acc, dq_acc, qa, qat, ga, gat, pb, db = rest
    else:
        dqkv_ref, dk_acc, dv_acc, dq_acc, qa, qat, ga, gat, pb, db = rest
    count = lax.div(info[0] + (CH - 1), CH)
    chunks = k_ref.shape[1]
    parts = 2 if shared else 4
    dk_acc[...] = jnp.zeros_like(dk_acc)
    dv_acc[...] = jnp.zeros_like(dv_acc)

    def piece(ref, part):
        if shared:
            return jnp.concatenate([ref[0, 2 * part], ref[0, 2 * part + 1]], axis=1)
        return ref[0, part]

    for part in range(parts):
        q_full = with_shift(assemble(q_ref, part, shared, info[3]), lse_ref[part])
        qat[part] = q_full.astype(bf16)
        qa[part] = q_full.T.astype(bf16)
        g_t = piece(gout_ref, part)
        meet = jnp.sum(g_t.astype(f32) * piece(out_ref, part).astype(f32), axis=0, keepdims=True)
        g_full = with_shift(g_t, meet)
        gat[part] = g_full.astype(bf16)
        ga[part] = g_full.T.astype(bf16)

    def ahead(part, j, slot):
        raised = jnp.exp2(dg(qa[part], k_ref[0, j], 1, 1))
        pb[slot] = raised.astype(bf16)
        db[slot] = (raised * dg(ga[part], v_ref[0, j], 1, 0)).astype(bf16)

    ahead(0, 0, 0)

    def body(t, carry):
        part, j = carry
        now = t & 1
        part_next, j_next = step_on(part, j, count)
        dv_acc[j] += dg(gat[part], pb[now], 1, 0)[:HD]
        dk_acc[j] += dg(qat[part], db[now], 1, 0)[:HD]
        before = jnp.where(j == 0, 0.0, dq_acc[...])
        dq_acc[...] = before + dg(db[now], k_ref[0, j], 1, 0)
        ahead(jnp.minimum(part_next, parts - 1), j_next, 1 - now)

        @pl.when(j + 1 == count)
        def _():
            dq_t = (dq_acc[...] * 0.125).T[:HD].astype(bf16)
            if shared:
                for a in range(2):
                    dq_ref[0, 2 * part + a, :, :512] = dq_t[:32, a * 512:(a + 1) * 512]
                    dq_ref[0, 2 * part + a, :, 512:] = dq_t[32:, a * 512:(a + 1) * 512]
            else:
                dqkv_ref[0, part, 0] = dq_t
        return part_next, j_next

    lax.fori_loop(0, parts * count, body, (0, 0))
    for j in range(chunks):
        for owner in range(4):
            cols = slice(owner * 128, (owner + 1) * 128)
            dk = (dk_acc[j, :, cols] * LN2).astype(bf16)
            dv = dv_acc[j, :, cols].astype(bf16)
            if shared:
                dkv_ref[0, 0, owner, :, j * 128:(j + 1) * 128] = dk
                dkv_ref[1, 0, owner, :, j * 128:(j + 1) * 128] = dv
            else:
                dqkv_ref[0, owner, 1, :, j * 128:(j + 1) * 128] = dk
                dqkv_ref[0, owner, 2, :, j * 128:(j + 1) * 128] = dv


def attend_backward(shared, seq, q, k, v, lse, out, g_out, info, held):
    _, owners, _, local = q.shape
    chunks = k.shape[1]
    wide = out.shape[3]
    parts = owners * wide // BQ
    pairs = parts * BQ * chunks * CH * 0.6
    shape = jax.ShapeDtypeStruct
    first = held is None
    if shared:
        out_specs = [pl.BlockSpec((1, owners, 32, local), lambda i, n: (seq, 0, 0, 0)),
                     pl.BlockSpec((2, 1, owners, HD, local), lambda i, n: (0, seq, 0, 0, 0))]
        out_shape = [shape((2, owners, 32, local), bf16), shape((2, 2, owners, HD, local), bf16)]
    else:
        out_specs = [pl.BlockSpec((1, owners, 3, HD, local), lambda i, n: (seq, 0, 0, 0, 0))]
        out_shape = [shape((2, owners, 3, HD, local), bf16)]
    kept = () if first else tuple(held)
    of_seq = pl.BlockSpec((1, owners, HD, wide), lambda i, n: (seq, 0, 0, 0))
    return pl.pallas_call(
        functools.partial(bwd_kernel, shared, first),
        grid_spec=pltpu.PrefetchScalarGridSpec(
            num_scalar_prefetch=1, grid=(1,),
            in_specs=[
                head_spec(shared, owners, HD, local), head_spec(shared, chunks, CH, 128), head_spec(shared, chunks, 128, CH),
                whole_spec(parts, 1, BQ), of_seq, of_seq,
            ] + [pl.BlockSpec(memory_space=pl.ANY)] * len(kept),
            out_specs=out_specs,
            scratch_shapes=[
                pltpu.VMEM((chunks, HD, CH), f32), pltpu.VMEM((chunks, HD, CH), f32), pltpu.VMEM((BQ, 128), f32),
                pltpu.VMEM((parts, BQ, 128), bf16), pltpu.VMEM((parts, 128, BQ), bf16),
                pltpu.VMEM((parts, BQ, 128), bf16), pltpu.VMEM((parts, 128, BQ), bf16),
                pltpu.VMEM((2, BQ, CH), bf16), pltpu.VMEM((2, BQ, CH), bf16),
            ]),
        out_shape=out_shape,
        input_output_aliases={7 + n: n for n in range(len(kept))},
        compiler_params=pltpu.CompilerParams(vmem_limit_bytes=56 << 20),
        cost_estimate=cost(pairs * 100, chunks * CH * 2048),
        name="attend_backward_shared" if shared else "attend_backward_own",
    )(info, q, k, v, lse, out, g_out, *kept)


def gelu_pair(u):
    half = 0.5 * (1.0 + lax.erf(u * 0.7071067811865476))
    return u * half, half + u * (0.3989422804014327 * jnp.exp2(u * u * (-0.5 * LOG2E)))


def norm_stats(v):
    mean = jnp.mean(v, axis=-1, keepdims=True)
    centred = v - mean
    inverse = lax.rsqrt(jnp.mean(centred * centred, axis=-1, keepdims=True) + 1e-12)
    return centred * inverse, inverse


def norm_back(grad, xhat, inverse, gain):
    g = grad * gain
    return (g - jnp.mean(g, axis=-1, keepdims=True) - xhat * jnp.mean(g * xhat, axis=-1, keepdims=True)) * inverse


def weight_part(ref, first, rows):
    part = ref[:, first:first + rows, :]
    return part.reshape(part.shape[0] * rows, part.shape[2])


def ffn_kernel(spans, info, x_ref, own_ref, sh_ref, cot_ref, w_ref, bin_ref, vec_ref,
               act_out, resid_out, gown_out, gsh_out, active_out, dinner_out, normed_out, douter_out, dbranch_out,
               vec_sum, bin_sum, slope, row_block):
    step = pl.program_id(0)
    width = x_ref.shape[-1]
    load_rows(row_block, x_ref, spans, info[1])
    rows = row_block[...].astype(f32)
    mixed_t = jnp.concatenate(
        [part for p in range(4) for part in (own_ref[p, 0], sh_ref[p, 0], own_ref[p, 1])], axis=0)
    vec = vec_ref[...]
    branch = dg(mixed_t, weight_part(w_ref, 768, 96), 0, 0) + vec[0:1]
    xhat1, inv1 = norm_stats(rows + branch)
    normed = xhat1 * vec[1:2] + vec[2:3]
    low = normed.astype(bf16)
    normed_out[...] = low
    outer = normed + vec[3:4]
    for n in range(4):
        cols = slice(n * 768, (n + 1) * 768)
        inner = dg(low, weight_part(w_ref, 384 + 96 * n, 96), 1, 0) + bin_ref[:, cols]
        value, bend = gelu_pair(inner)
        active_out[:, cols] = value.astype(bf16)
        slope[:, cols] = bend.astype(bf16)
    outer = outer + dg(active_out[...], weight_part(w_ref, 0, 384), 1, 0)
    xhat2, inv2 = norm_stats(outer)
    act_out[...] = (xhat2 * vec[4:5] + vec[5:6]).astype(bf16)
    cot = cot_ref[...].astype(f32)
    d2 = norm_back(cot, xhat2, inv2, vec[4:5])
    d_outer = d2.astype(bf16)
    douter_out[...] = d_outer
    d_normed = d2
    sums_in = []
    for n in range(4):
        cols = slice(n * 768, (n + 1) * 768)
        d_active = dg(d_outer, weight_part(w_ref.at[2 * n:2 * n + 2], 0, 384), 1, 1)
        d_inner = (d_active * slope[:, cols].astype(f32)).astype(bf16)
        dinner_out[:, cols] = d_inner
        sums_in.append(jnp.sum(d_inner.astype(f32), axis=0, keepdims=True))
        d_normed = d_normed + dg(d_inner, weight_part(w_ref, 384 + 96 * n, 96), 1, 1)
    d1 = norm_back(d_normed, xhat1, inv1, vec[1:2])
    resid_out[...] = d1
    d_branch = d1.astype(bf16)
    dbranch_out[...] = d_branch
    g_t = dg(weight_part(w_ref, 768, 96), d_branch, 1, 1).astype(bf16)
    for p in range(4):
        gown_out[p, 0] = g_t[192 * p:192 * p + 64]
        gsh_out[p, 0] = g_t[192 * p + 64:192 * p + 128]
        gown_out[p, 1] = g_t[192 * p + 128:192 * p + 192]
    total = lambda a: jnp.sum(a, axis=0, keepdims=True)
    sums = jnp.concatenate([
        total(d_branch.astype(f32)), total(d_normed * xhat1), total(d_normed),
        total(d_outer.astype(f32)), total(cot * xhat2), total(cot), jnp.zeros((2, width), f32)], axis=0)

    @pl.when(step == 0)
    def _():
        vec_sum[...] = sums
        for n in range(4):
            bin_sum[:, n * 768:(n + 1) * 768] = sums_in[n]

    @pl.when(step > 0)
    def _():
        vec_sum[...] += sums
        for n in range(4):
            bin_sum[:, n * 768:(n + 1) * 768] += sums_in[n]


def feed_forward(rows_in, own, sh, cotangent, weights, inner_bias, vectors, info):
    _, _, _, stretch, width = rows_in.shape
    local = cotangent.shape[0]
    spans = RB // (2 * stretch)
    steps = local // RB
    half_steps = steps // 2
    wide = inner_bias.shape[1]
    rows = lambda n: pl.BlockSpec((RB, n), lambda r, a: (r, 0))
    fixed = lambda *dims: pl.BlockSpec(dims, lambda r, a: (0,) * len(dims))
    own_spec = pl.BlockSpec((4, 2, HD, RB), lambda r, a: (0, 0, 0, r))
    sh_spec = pl.BlockSpec((4, 1, HD, RB), lambda r, a: (0, r // half_steps, 0, r % half_steps))
    shape = jax.ShapeDtypeStruct
    return pl.pallas_call(
        functools.partial(ffn_kernel, spans),
        grid_spec=pltpu.PrefetchScalarGridSpec(
            num_scalar_prefetch=1, grid=(steps,),
            in_specs=[
                pl.BlockSpec((1, 2, spans, stretch, width), lambda r, a: (0, 0, r, 0, 0)),
                own_spec, sh_spec, rows(width),
                pl.BlockSpec(weights.shape, lambda r, a: (0, 0, 0), pipeline_mode=pl.Buffered(1)),
                fixed(1, wide), fixed(8, width),
            ],
            out_specs=[
                rows(width), rows(width), own_spec, sh_spec, rows(wide), rows(wide), rows(width), rows(width), rows(width),
                fixed(8, width), fixed(1, wide),
            ],
            scratch_shapes=[pltpu.VMEM((RB, wide), bf16), pltpu.VMEM((RB, width), bf16)]),
        out_shape=[
            shape((local, width), bf16), shape((local, width), f32), shape(own.shape, bf16), shape(sh.shape, bf16),
            shape((local, wide), bf16), shape((local, wide), bf16), shape((local, width), bf16),
            shape((local, width), bf16), shape((local, width), bf16), shape((8, width), f32), shape((1, wide), f32),
        ],
        compiler_params=pltpu.CompilerParams(vmem_limit_bytes=60 << 20),
        name="feed_forward",
        cost_estimate=cost(local * width * (width + 2 * wide) * 4, local * wide * 20),
    )(info, rows_in, own, sh, cotangent, weights, inner_bias, vectors)


def outer_grad_kernel(scale, active_ref, douter_ref, out_ref):
    made = (dg(active_ref[...], douter_ref[...], 0, 0) * scale).astype(bf16)
    out_ref[...] = made.reshape(out_ref.shape)


def inner_grad_kernel(scale, packed_ref, normed_ref, dinner_ref, own_ref, sh_ref, dbranch_ref, out_ref):
    step = pl.program_id(0)

    @pl.when(step < 4)
    def _():
        out_ref[...] = (dg(normed_ref[...], dinner_ref[...], 0, 0) * scale).astype(bf16).reshape(out_ref.shape)

    @pl.when(step == 4)
    def _():
        mixed_t = jnp.concatenate([
            part for p in range(4)
            for part in (own_ref[p, 0], jnp.concatenate([sh_ref[p, 0], sh_ref[p, 1]], axis=1), own_ref[p, 1])], axis=0)
        out_ref[...] = (dg(mixed_t, dbranch_ref[...], 1, 0) * scale).astype(bf16).reshape(out_ref.shape)


def weight_grads(scale, active, d_outer, normed, d_inner, own, sh, d_branch):
    local, wide = active.shape
    width = normed.shape[1]
    packed = pl.pallas_call(
        functools.partial(outer_grad_kernel, scale), grid=(4,),
        in_specs=[pl.BlockSpec((local, width), lambda m: (0, m)), pl.BlockSpec((local, width), lambda m: (0, 0))],
        out_specs=pl.BlockSpec((2, 384, width), lambda m: (m, 0, 0)),
        out_shape=jax.ShapeDtypeStruct((8, 896, width), bf16),
        compiler_params=pltpu.CompilerParams(vmem_limit_bytes=40 << 20), name="outer_grad",
        cost_estimate=cost(2 * local * wide * width, 2 * wide * (local + width)),
    )(active, d_outer)
    fixed = lambda a: pl.BlockSpec(a.shape, lambda n: (0,) * a.ndim)
    return pl.pallas_call(
        functools.partial(inner_grad_kernel, scale), grid=(5,),
        in_specs=[
            pl.BlockSpec(memory_space=pl.ANY), fixed(normed),
            pl.BlockSpec((local, width), lambda n: (0, jnp.minimum(n, 3))), fixed(own), fixed(sh), fixed(d_branch)],
        out_specs=pl.BlockSpec((8, 96, width), lambda n: (0, 4 + n, 0)),
        out_shape=jax.ShapeDtypeStruct((8, 896, width), bf16), input_output_aliases={0: 0},
        compiler_params=pltpu.CompilerParams(vmem_limit_bytes=40 << 20), name="inner_grad",
        cost_estimate=cost(2 * local * (wide + width) * width, 2 * (wide + width) * (local + width)),
    )(packed, normed, d_inner, own, sh, d_branch)


def head_grad_kernel(scale, spans, info, *refs):
    x_refs, (own_ref, dq_ref, dkv_ref, out_ref, bias_out, acc, bias_acc, rows) = refs[:4], refs[4:]
    seq, away, half = pl.program_id(0), pl.program_id(1), pl.program_id(3)
    last = (seq == 1) & (away == 1) & (pl.program_id(2) == 1) & (half == pl.num_programs(3) - 1)
    for n in range(4):
        @pl.when(seq * 2 + away == n)
        def _(n=n):
            load_rows(rows, x_refs[n], spans, info[1])
    dq_t = jnp.where(half == info[3], jnp.concatenate([dq_ref[0, 0, :, :512], dq_ref[0, 0, :, 512:]], axis=0).astype(f32), 0.0)
    d_t = jnp.concatenate([
        own_ref[0, 0, 0], dq_t.astype(bf16), own_ref[0, 0, 1], dkv_ref[0, 0, 0], own_ref[0, 0, 2], dkv_ref[1, 0, 0]], axis=0)

    @pl.when((seq == 0) & (away == 0) & (pl.program_id(2) == 0) & (half == 0))
    def _():
        acc[...] = jnp.zeros_like(acc)
        bias_acc[...] = jnp.zeros_like(bias_acc)
    acc[...] += dg(d_t, rows[...], 1, 0)
    bias_acc[...] += dg(jnp.ones((8, d_t.shape[1]), bf16), d_t, 1, 1)

    @pl.when(last)
    def _():
        out_ref[...] = (acc[...] * scale).T.astype(bf16)
        bias_out[...] = bias_acc[...] * scale


def head_grads(scale, sources, dqkv_own, dq_sh, dkv_sh, info):
    _, _, zs, stretch, width = sources[0].shape
    local = 2 * zs * stretch
    spans = 512 // (2 * stretch)
    halves = local // 512

    def source_spec(n):
        def index(s, a, o, h, i):
            now = 2 * s + a
            across = jnp.where(now == n, o, jnp.where(now < n, 0, 1))
            return (across, 0, jnp.where(now == n, h, jnp.where(now < n, 0, halves - 1)), 0, 0)
        return pl.BlockSpec((1, 2, spans, stretch, width), index)
    return pl.pallas_call(
        functools.partial(head_grad_kernel, scale, spans),
        grid_spec=pltpu.PrefetchScalarGridSpec(
            num_scalar_prefetch=1, grid=(2, 2, 2, halves),
            in_specs=[source_spec(n) for n in range(4)] + [
                pl.BlockSpec((1, 1, 3, HD, 512), lambda s, a, o, h, i: (s, owner_of(a, o, i), 0, 0, h)),
                pl.BlockSpec((1, 1, 32, local), lambda s, a, o, h, i: (s, owner_of(a, o, i), 0, 0)),
                pl.BlockSpec((2, 1, 1, HD, 512), lambda s, a, o, h, i: (0, s, owner_of(a, o, i), 0, h))],
            out_specs=[pl.BlockSpec((width, 384), lambda s, a, o, h, i: (0, 0)), pl.BlockSpec((8, 384), lambda s, a, o, h, i: (0, 0))],
            scratch_shapes=[pltpu.VMEM((384, width), f32), pltpu.VMEM((8, 384), f32), pltpu.VMEM((512, width), bf16)]),
        out_shape=[jax.ShapeDtypeStruct((width, 384), bf16), jax.ShapeDtypeStruct((8, 384), f32)],
        compiler_params=pltpu.CompilerParams(vmem_limit_bytes=40 << 20), name="head_grads",
        cost_estimate=cost(8 * local * 768 * width, 8 * local * width * 2),
    )(info, *sources, dqkv_own, dq_sh, dkv_sh)


def token_grad_kernel(own_ref, low_ref, high_ref, dkv_ref, w_ref, resid_ref, out_ref):
    total = resid_ref[...]
    for kind in range(3):
        made = []
        for p in range(4):
            if kind == 0:
                middle = jnp.concatenate([low_ref[p, 0], high_ref[p, 0]], axis=0)
            else:
                middle = jnp.concatenate([dkv_ref[p, kind - 1, n] for n in range(2)], axis=0)
            made += [own_ref[p, 0, kind], middle, own_ref[p, 1, kind]]
        total = total + dg(jnp.concatenate(made, axis=0), weight_part(w_ref, 96 * kind, 96), 0, 1)
    out_ref[...] = total.astype(bf16)


def token_grad(own, shared, weights, resid):
    local, width = resid.shape
    steps = local // RB
    half_steps = steps // 2
    rows = pl.BlockSpec((RB, width), lambda r: (r, 0))
    return pl.pallas_call(
        token_grad_kernel, grid=(steps,),
        in_specs=[
            pl.BlockSpec((4, 2, 3, HD, RB), lambda r: (0, 0, 0, 0, r)),
            pl.BlockSpec((4, 1, None, 32, RB), lambda r: (0, r // half_steps, 0, 0, r % half_steps)),
            pl.BlockSpec((4, 1, None, 32, RB), lambda r: (0, r // half_steps, 0, 0, half_steps + r % half_steps)),
            pl.BlockSpec((4, 2, 2, 32, RB), lambda r: (0, 0, 0, 0, r)),
            pl.BlockSpec(weights.shape, lambda r: (0, 0, 0)), rows],
        out_specs=rows, out_shape=jax.ShapeDtypeStruct((local, width), bf16),
        compiler_params=pltpu.CompilerParams(vmem_limit_bytes=40 << 20), name="token_grad",
        cost_estimate=cost(local * width * width * 6, local * width * 12),
    )(own, shared[:, :, :1], shared[:, :, :1], shared[:, :, 1:], weights, resid)


SWAP = [(0, 1), (1, 0)]
PAIR = ("x", "y", "c")
ALL = ("z", "x", "y", "c")
SHARD = ("z", "x")


def canonical(packed, shards):
    if shards == 8:
        return packed
    width = packed.shape[2]
    per, keep = 96 * 8 // shards, shards // 8
    outer = packed[:, :4 * per].reshape(8, 384, width)
    inner = packed[:, 4 * per:8 * per].reshape(8, keep, 4, per, width).transpose(0, 2, 1, 3, 4).reshape(8, 384, width)
    output = packed[:, 8 * per:9 * per].reshape(8, 96, width)
    return jnp.concatenate([outer, inner, output, jnp.zeros((8, 32, width), packed.dtype)], axis=1)


def from_canonical(packed, shards):
    if shards == 8:
        return packed
    width = packed.shape[2]
    per, keep = 96 * 8 // shards, shards // 8
    outer = packed[:, :384].reshape(shards, 4 * per, width)
    inner = packed[:, 384:768].reshape(8, 4, keep, per, width).transpose(0, 2, 1, 3, 4).reshape(shards, 4 * per, width)
    output = packed[:, 768:864].reshape(shards, per, width)
    return jnp.concatenate([outer, inner, output, jnp.zeros((shards, 32, width), packed.dtype)], axis=1)


def canonical_heads(packed, shards):
    if shards == 8:
        return packed
    width = packed.shape[2]
    per = 96 * 8 // shards
    parts = [packed[:, k * per:(k + 1) * per].reshape(8, 96, width) for k in range(3)]
    return jnp.concatenate(parts + [jnp.zeros((8, 32, width), packed.dtype)], axis=1)


def quarter(rows):
    place = lax.axis_index("y") * 2 + lax.axis_index("c")
    part = rows.shape[0] // 4
    return lax.dynamic_slice_in_dim(rows, place * part, part)


def body(tokens, lengths, deal_order, w_query, w_key, w_value, w_output, b_query, b_value, b_output,
         ln1_gain, ln1_shift, w_inner, b_inner, w_outer, b_outer, ln2_gain, ln2_shift, cotangent):
    zs = lax.axis_size("z")
    shards = 2 * zs
    devices = shards * 4
    scale = 1.0 / devices
    seq_count, _, stretch, width = tokens.shape
    per = w_query.shape[0]
    x, y, c = lax.axis_index("x"), lax.axis_index("y"), lax.axis_index("c")
    def deal(seq):
        ordered = jnp.take(tokens[:, 0], deal_order[seq::2], axis=0)
        return lax.all_to_all(ordered, "z", split_axis=0, concat_axis=0, tiled=True)

    half = zs // 2

    def corner(across, along):
        return [lax.ppermute(across[:half], "y", SWAP), lax.ppermute(along[half:], "x", SWAP)]

    def this_core(own, across, along, corner):
        return jnp.concatenate([own, across, along] + corner, axis=0).reshape(2, 2, zs, stretch, width)

    first_own = deal(0)
    first_own, held_tokens = lax.optimization_barrier((first_own, tokens))
    tokens = held_tokens
    across_a, along_a = lax.ppermute(first_own, "x", SWAP), lax.ppermute(first_own, "y", SWAP)
    second_own = deal(1)
    across_a, along_a, second_own = lax.optimization_barrier((across_a, along_a, second_own))
    near_a = this_core(first_own, across_a, along_a, corner(across_a, along_a))
    far_a = lax.ppermute(near_a, "c", SWAP)
    near_a, second_own = lax.optimization_barrier((near_a, second_own))
    across_b, along_b = lax.ppermute(second_own, "x", SWAP), lax.ppermute(second_own, "y", SWAP)

    def head_columns(matrix):
        heads = matrix.reshape(per, 2, 2, 3, HD)
        mine = lax.dynamic_index_in_dim(heads, y, axis=2, keepdims=False)
        own = lax.dynamic_index_in_dim(mine, 2 * c, axis=2, keepdims=False)
        return [own, mine[:, :, 1]]
    columns = jnp.concatenate(
        [col for matrix in (w_query, w_key, w_value) for col in head_columns(matrix)], axis=2).reshape(per, 768)
    pad = lambda v, n: jnp.pad(v, (0, n - v.shape[0]))[None]
    head_pack = jnp.concatenate(
        [columns, pad(b_query, width), pad(b_value, width), jnp.zeros((14, width), bf16)], axis=0)
    head_all = lax.all_gather(head_pack, SHARD, axis=0, tiled=False)
    head_weight = lax.dynamic_index_in_dim(
        head_all[:, :per].reshape(width, 2, 384), x, axis=1, keepdims=False)

    def head_bias(row):
        heads = head_all[:, per + row, :per].reshape(2, 2, 3, HD)
        mine = lax.dynamic_slice(heads, (x, y, 0, 0), (1, 1, 3, HD))[0, 0]
        return [lax.dynamic_index_in_dim(mine, 2 * c, axis=0, keepdims=False), mine[1]]
    bias_row = jnp.concatenate(head_bias(0) + [jnp.zeros((2 * HD,), bf16)] + head_bias(1)).astype(f32)[None]

    mine_rows = jnp.where(x == 0, jnp.stack([first_own, across_a]), jnp.stack([second_own, across_b]))[None]

    panels = w_inner.reshape(per, 4, 768)
    vectors = (b_output, ln1_gain, ln1_shift, b_outer, ln2_gain, ln2_shift)
    layer_pack = jnp.concatenate(
        [w_outer] + [panels[:, n] for n in range(4)] + [w_output]
        + [pad(b_inner, width)] + [pad(v, width) for v in vectors] + [jnp.zeros((25, width), bf16)], axis=0)
    layer_all = lax.all_gather(quarter(layer_pack), ALL, axis=0, tiled=True).reshape(shards, 9 * per + 32, width)
    layer_weights = canonical(layer_all, shards)
    inner_bias = layer_all[:, 9 * per, :4 * per].reshape(1, 3072).astype(f32)
    vector_rows = jnp.concatenate(
        [layer_all[:, 9 * per + 1 + n, :per].reshape(1, width) for n in range(6)] + [jnp.zeros((2, width), bf16)],
        axis=0).astype(f32)
    back_pack = jnp.concatenate([w_query, w_key, w_value, jnp.zeros((32, width), bf16)], axis=0)
    back_all = lax.all_gather(quarter(back_pack), ALL, axis=0, tiled=True).reshape(shards, 3 * per + 32, width)

    group = lax.axis_index("z")
    slots = lax.dynamic_slice_in_dim(deal_order, group * 2, 2)
    matches = slots[:, None] == jnp.arange(seq_count, dtype=jnp.int32)[None, :]
    lens = jnp.sum(jnp.where(matches, lengths[None, :], 0), axis=1).astype(jnp.int32)

    infos = [jnp.stack([lens[n], x, y, c]).astype(jnp.int32) for n in range(2)]

    def swap(array):
        flat = array.reshape((8,) + array.shape[2:])
        return lax.all_to_all(flat, PAIR, split_axis=0, concat_axis=0, tiled=True)

    def to_tokens(array):
        return swap(array).reshape((4, 2) + array.shape[2:])

    def to_heads(array):
        return swap(array).reshape((2, 4) + array.shape[2:])

    heads_a = project(near_a, far_a, head_weight, bias_row, infos[0])
    heads_a, across_b, along_b = lax.optimization_barrier((heads_a, across_b, along_b))
    near_b = this_core(second_own, across_b, along_b, corner(across_b, along_b))
    own_first, lse_own_a = attend_forward(False, 0, *heads_a, infos[0], None)
    own_first, near_b = lax.optimization_barrier((own_first, near_b))
    far_b = lax.ppermute(near_b, "c", SWAP)
    sh_first, lse_sh_a = attend_forward(True, 0, *heads_a, infos[0], None)
    sh_first, far_b = lax.optimization_barrier((sh_first, far_b))
    heads_b = project(near_b, far_b, head_weight, bias_row, infos[1])
    own, lse_own_b = attend_forward(False, 1, *heads_b, infos[1], own_first)
    own_t = to_tokens(own)
    own, info_later = lax.optimization_barrier((own, infos[1]))
    sh, lse_sh_b = attend_forward(True, 1, *heads_b, info_later, sh_first)
    sh_sent, own_t = lax.optimization_barrier((sh, own_t))
    sh_t = to_tokens(sh_sent)
    (act, resid, g_own, g_sh, active, d_inner, normed, d_outer, d_branch, vec_sums, bin_sums) = feed_forward(
        mine_rows, own_t, sh_t, cotangent.reshape(-1, width), layer_weights, inner_bias, vector_rows, infos[0])
    g_own_h, g_sh_h = to_heads(g_own), to_heads(g_sh)
    active, back_all = lax.optimization_barrier((active, back_all))
    packed = weight_grads(scale, active, d_outer, normed, d_inner, own_t, sh_t, d_branch)
    sums = jnp.concatenate([bin_sums.reshape(4, width), vec_sums, jnp.zeros((20, width), f32)], axis=0) * scale
    packed = packed.at[:, 864:].set(jnp.broadcast_to(sums.astype(bf16)[None], (8, 32, width)))
    ready = from_canonical(packed, shards)
    if shards != 8:
        ready = ready.at[:, 9 * per:].set(jnp.broadcast_to(sums.astype(bf16)[None], (shards, 32, width)))
    ready, g_own_h = lax.optimization_barrier((ready, g_own_h))
    back_weights = canonical_heads(back_all, shards)
    layer_part = lax.psum_scatter(ready.reshape(-1, width), ALL, scatter_dimension=0, tiled=True)

    qkv_a, qkv_b = heads_a[:3], heads_b[:3]
    first = attend_backward(False, 0, *qkv_a, lse_own_a, own, g_own_h, infos[0], None)
    dqkv_own, = attend_backward(False, 1, *qkv_b, lse_own_b, own, g_own_h, infos[1], first)
    back_own = to_tokens(dqkv_own)
    dqkv_own, info_a, info_b = lax.optimization_barrier((dqkv_own, *infos))
    first = attend_backward(True, 0, *qkv_a, lse_sh_a, sh, g_sh_h, info_a, None)
    dq_sh, dkv_sh = attend_backward(True, 1, *qkv_b, lse_sh_b, sh, g_sh_h, info_b, first)
    kept = lax.dynamic_index_in_dim(dkv_sh, c, axis=0, keepdims=False)
    given = lax.dynamic_index_in_dim(dkv_sh, 1 - c, axis=0, keepdims=False)
    taken = lax.ppermute(given, "c", SWAP)
    shared_out = jnp.concatenate([dq_sh, (kept.astype(f32) + taken.astype(f32)).astype(bf16)], axis=2)
    shared_out, back_own, dqkv_own = lax.optimization_barrier((shared_out, back_own, dqkv_own))
    back_shared = to_tokens(shared_out.reshape(2, 4, 3, 32, -1))
    d_heads, d_bias = head_grads(scale, (near_a, far_a, near_b, far_b), dqkv_own, dq_sh, dkv_sh, infos[0])
    chunk = width // zs
    head_ready = jnp.concatenate([
        d_heads.reshape(zs, chunk, 384),
        jnp.broadcast_to(d_bias[:1].astype(bf16)[None], (zs, 16, 384))], axis=1)
    head_ready, layer_part, back_shared = lax.optimization_barrier((head_ready, layer_part, back_shared))
    head_part = lax.psum_scatter(head_ready.reshape(-1, 384), "z", scatter_dimension=0, tiled=True)
    head_grads_all = lax.all_gather(head_part, PAIR, axis=0, tiled=False).reshape(4, 2, chunk + 16, 6, HD).astype(f32)

    layer_grads = lax.all_gather(layer_part, ("y", "c"), axis=0, tiled=True)
    d_rows = token_grad(back_own, back_shared, back_weights, resid)
    returned = lax.all_to_all(
        d_rows.reshape(shards, stretch, width), SHARD, split_axis=0, concat_axis=0, tiled=True)
    place = lax.axis_index("z") * 2 + x
    own_slice = lambda row, n: lax.dynamic_slice_in_dim(row, place * n, n)
    layer_grads = layer_grads.astype(f32)
    d_wouter = layer_grads[:4 * per]
    d_winner = layer_grads[4 * per:8 * per].reshape(4, per, width).transpose(1, 0, 2).reshape(per, 4 * width)
    d_woutput = layer_grads[8 * per:9 * per]
    d_binner = own_slice(layer_grads[9 * per:9 * per + 4].reshape(-1), 4 * per)
    d_bo, d_g1, d_s1, d_bout, d_g2, d_s2 = (own_slice(layer_grads[9 * per + 4 + n], per) for n in range(6))
    returned, d_wouter, d_winner, d_woutput = lax.optimization_barrier((returned, d_wouter, d_winner, d_woutput))
    d_tokens = jnp.zeros_like(returned).at[deal_order].set(returned)[:, None]

    mine = lax.dynamic_slice_in_dim(head_grads_all, x * per, per, axis=2)

    def full(part, kind):
        own_part, shared = part[:, :, :, 2 * kind], part[:, :, :, 2 * kind + 1]
        both = shared[:, 0] + shared[:, 1]
        joined = jnp.stack([own_part[:, 0], both, own_part[:, 1]], axis=1)
        return joined.transpose(2, 0, 1, 3).reshape(part.shape[2], width)
    d_wq, d_wk, d_wv = (full(mine, kind) for kind in range(3))
    bias_part = head_grads_all[:, :, chunk:chunk + 1]
    d_bq = own_slice(full(bias_part, 0)[0], per)
    d_bv = own_slice(full(bias_part, 2)[0], per)

    return (act.reshape(1, shards, stretch, width), d_tokens, d_wq, d_wk, d_wv, d_woutput, d_bq, d_bv, d_bo,
            d_g1, d_s1, d_winner, d_binner, d_wouter, d_bout, d_g2, d_s2)


def solution(mesh):
    shards, splits = mesh.devices.shape
    fine = Mesh(mesh.devices.reshape(shards // 2, 2, splits // 2, 2), ALL)
    S, Q = SHARD, ("y", "c")
    row, mat = P(S), P(S, None)
    return jax.shard_map(
        body, mesh=fine,
        in_specs=(P(None, S, Q, None), P(), P(), mat, mat, mat, mat, row, row, row, row, row, mat, row, mat, row, row, row,
                  P(S, None, Q, None)),
        out_specs=(P(S, None, Q, None), P(None, S, Q, None), mat, mat, mat, mat, row, row, row, row, row, mat, row, mat,
                   row, row, row),
        check_vma=False)
```

```python
import functools, math
import jax
import jax.numpy as jnp
from jax import lax
from jax.experimental import pallas as pl
from jax.experimental.pallas import tpu as pltpu
from jax.sharding import Mesh, PartitionSpec as P

f32, bf16 = jnp.float32, jnp.bfloat16
LOG2E = 1.4426950408889634
LN2 = 0.6931471805599453
CH = 512
BQ = 1024
RB = 256
HD = 64
FAR = -1.0e30

def dg(a, b, ca, cb):
    return lax.dot_general(a, b, (((ca,), (cb,)), ((), ())), preferred_element_type=f32)


def three_parts(row):
    hi = row.astype(bf16).astype(f32)
    rest = row - hi
    mid = rest.astype(bf16).astype(f32)
    return hi, mid, rest - mid


def with_shift(top, shift):
    hi, mid, low = three_parts(shift)
    row = lax.broadcasted_iota(jnp.int32, (HD, top.shape[1]), 0)
    tail = jnp.where(row == 0, -hi, jnp.where(row == 1, -mid, jnp.where(row == 2, -low, jnp.where(row == 3, 1.0, 0.0))))
    return jnp.concatenate([top.astype(f32), tail], axis=0)


def load_rows(rows, ref, spans, x):
    stretch = ref.shape[3]
    for z in range(spans):
        for a in range(2):
            at = (2 * z + a) * stretch
            rows[at:at + stretch] = ref[0, a ^ x, z]


def qkv_kernel(stretch, spans, info, near_ref, far_ref, w_ref, b_ref, q_out, k_out, v_out, size_out, rows):
    away, half = pl.program_id(0), pl.program_id(2)
    owner = ((pl.program_id(1) ^ info[2]) << 1) | (away ^ info[3])

    @pl.when(away == 0)
    def _():
        load_rows(rows, near_ref, spans, info[1])

    @pl.when(away == 1)
    def _():
        load_rows(rows, far_ref, spans, info[1])
    weight = w_ref[...].reshape(rows.shape[1], 384)
    made = dg(rows[...], weight, 1, 0) + b_ref[...]
    count = rows.shape[0]
    q_t = (made[:, :128] * (LOG2E / 8.0)).T
    q_out[0, 0] = q_t[:HD].astype(bf16)
    q_out[1, 0] = q_t[HD:].astype(bf16)
    lane = lax.broadcasted_iota(jnp.int32, (count, 128), 1)
    row = lax.broadcasted_iota(jnp.int32, (count, 128), 0) + half * count
    shift = int(math.log2(stretch))
    position = lax.shift_left(lax.shift_right_logical(row, shift), shift + 2) + owner * stretch + (row & (stretch - 1))
    hidden = jnp.where(position < info[0], 0.0, FAR)
    tail = jnp.where(lane == HD + 3, hidden, jnp.where(lane < HD + 3, 1.0, 0.0))
    keys = made[:, 128:256]
    picks = lax.broadcasted_iota(jnp.int32, (128, 128), 0) // HD == lax.broadcasted_iota(jnp.int32, (128, 128), 1)
    sizes = dg((keys * keys).astype(bf16), jnp.where(picks, 1.0, 0.0).astype(bf16), 1, 0)
    size_out[0, 0] = jnp.max(sizes, axis=0, keepdims=True)
    for head in range(2):
        turned = keys if head == 0 else pltpu.roll(keys, HD, 1)
        full = jnp.where(lane < HD, turned, tail).astype(bf16)
        for j in range(count // 128):
            k_out[head, j] = full[j * 128:(j + 1) * 128]
    v_t = made[:, 256:384].T
    ones = jnp.where(lax.broadcasted_iota(jnp.int32, (HD, count), 0) < 3, 1.0, 0.0)
    for head in range(2):
        full = jnp.concatenate([v_t[head * HD:(head + 1) * HD], ones], axis=0).astype(bf16)
        for j in range(count // 128):
            v_out[head, j] = full[:, j * 128:(j + 1) * 128]


def owner_of(away, across, info):
    return ((across ^ info[2]) << 1) | (away ^ info[3])


def project(near, far, weight, bias, info):
    _, _, zs, stretch, width = near.shape
    local = 2 * zs * stretch
    spans = 512 // (2 * stretch)
    halves = local // 512
    chunks = 4 * local // CH
    per = chunks // halves
    block = (1, 2, spans, stretch, width)
    return pl.pallas_call(
        functools.partial(qkv_kernel, stretch, spans),
        grid_spec=pltpu.PrefetchScalarGridSpec(
            num_scalar_prefetch=1, grid=(2, 2, halves),
            in_specs=[
                pl.BlockSpec(block, lambda a, o, h, n: (jnp.where(a == 0, o, 1), 0, jnp.where(a == 0, h, halves - 1), 0, 0)),
                pl.BlockSpec(block, lambda a, o, h, n: (jnp.where(a == 0, 0, o), 0, jnp.where(a == 0, 0, h), 0, 0)),
                pl.BlockSpec((8, width // 8, 384), lambda a, o, h, n: (0, 0, n[1])),
                pl.BlockSpec((1, 384), lambda a, o, h, n: (0, 0)),
            ],
            out_specs=[
                pl.BlockSpec((2, 1, HD, 512), lambda a, o, h, n: (0, owner_of(a, o, n), 0, h)),
                pl.BlockSpec((2, per, 128, 128), lambda a, o, h, n: (0, h, owner_of(a, o, n), 0)),
                pl.BlockSpec((2, per, 128, 128), lambda a, o, h, n: (0, h, 0, owner_of(a, o, n))),
                pl.BlockSpec((1, 1, 1, 128), lambda a, o, h, n: (owner_of(a, o, n), h, 0, 0)),
            ],
            scratch_shapes=[pltpu.VMEM((512, width), bf16)]),
        out_shape=[
            jax.ShapeDtypeStruct((2, 4, HD, local), bf16),
            jax.ShapeDtypeStruct((2, chunks, CH, 128), bf16),
            jax.ShapeDtypeStruct((2, chunks, 128, CH), bf16),
            jax.ShapeDtypeStruct((4, halves, 1, 128), f32),
        ],
        compiler_params=pltpu.CompilerParams(vmem_limit_bytes=40 << 20),
        name="qkv",
        cost_estimate=cost(4 * near.size * 384, near.size * 8),
    )(info, near, far, weight, bias)


def step_on(q, j, count):
    last = j + 1 == count
    return jnp.where(last, q + 1, q), jnp.where(last, 0, j + 1)


def assemble(ref, q, shared, core):
    if not shared:
        return ref[0, q]
    at = pl.multiple_of(core * 512, 512)
    return jnp.concatenate([ref[0, 2 * q, :, pl.ds(at, 512)], ref[0, 2 * q + 1, :, pl.ds(at, 512)]], axis=1)


def fwd_kernel(shared, info, q_ref, k_ref, v_ref, size_ref, held_ref, out_ref, lse_ref, acc, probs, qa, shifts):
    count = lax.div(info[0] + (CH - 1), CH)
    parts = 2 if shared else 4
    lane = lax.broadcasted_iota(jnp.int32, (1, 128), 1)
    sizes = functools.reduce(jnp.maximum, [size_ref[o, h] for o in range(size_ref.shape[0]) for h in range(size_ref.shape[1])])
    widest = jnp.sqrt(jnp.max(jnp.where(lane == int(shared), sizes, 0.0), axis=1, keepdims=True))

    for part in range(parts):
        q_t = assemble(q_ref, part, shared, info[3])
        wide = q_t.astype(f32)
        shift = jnp.sqrt(jnp.sum(wide * wide, axis=0, keepdims=True)) * widest
        shifts[part] = shift
        qa[part] = with_shift(q_t, shift).astype(bf16)

    def raised(part, j):
        return jnp.exp2(dg(k_ref[0, j], qa[part], 1, 0)).astype(bf16)

    probs[0] = raised(0, 0)

    def body(t, carry):
        part, j = carry
        now = t & 1
        part_next, j_next = step_on(part, j, count)
        before = jnp.where(j == 0, 0.0, acc[...])
        acc[...] = before + dg(v_ref[0, j], probs[now], 1, 0)
        probs[1 - now] = raised(jnp.minimum(part_next, parts - 1), j_next)

        @pl.when(j + 1 == count)
        def _():
            total = acc[HD:HD + 1]
            fine = (jnp.min(total) > 2.0 ** -90) & (jnp.max(total) < 2.0 ** 60)

            @pl.when(jnp.logical_not(fine))
            def _():
                plain = qa[part].astype(f32)
                row = lax.broadcasted_iota(jnp.int32, plain.shape, 0)
                qa[part] = jnp.where((row >= HD) & (row < HD + 3), 0.0, plain).astype(bf16)

                def peak(i, top):
                    return jnp.maximum(top, jnp.max(dg(k_ref[0, i], qa[part], 1, 0), axis=0, keepdims=True))
                shift = lax.fori_loop(0, count, peak, jnp.full((1, BQ), FAR, f32))
                shifts[part] = shift
                qa[part] = with_shift(plain[:HD], shift).astype(bf16)
                acc[...] = jnp.zeros_like(acc)

                def again(i, carry):
                    acc[...] += dg(v_ref[0, i], raised(part, i), 1, 0)
                    return carry
                lax.fori_loop(0, count, again, 0)

            total = acc[HD:HD + 1]
            mixed = (acc[:HD] * (1.0 / total)).astype(bf16)
            lse_ref[part] = shifts[part] + jnp.log2(total)
            if shared:
                out_ref[0, 2 * part] = mixed[:, :512]
                out_ref[0, 2 * part + 1] = mixed[:, 512:]
            else:
                out_ref[0, part] = mixed
        return part_next, j_next

    lax.fori_loop(0, parts * count, body, (0, 0))


def head_spec(shared, *dims):
    zeros = (0,) * len(dims)
    return pl.BlockSpec((1,) + dims, lambda i, n: (int(shared),) + zeros)


def whole_spec(*dims):
    return pl.BlockSpec(dims, lambda i, n: (0,) * len(dims))


def cost(flops, moved, exps=0):
    return pl.CostEstimate(flops=int(flops), bytes_accessed=int(moved), transcendentals=int(exps))


def attend_forward(shared, seq, q, k, v, sizes, info, held):
    _, owners, _, local = q.shape
    chunks = k.shape[1]
    wide = local // 2 if shared else local
    parts = owners * wide // BQ
    pairs = parts * BQ * chunks * CH * 0.6
    shape = jax.ShapeDtypeStruct((2, owners, HD, wide), bf16)
    first = held is None
    if first:
        kernel = lambda info, q, k, v, size, *rest: fwd_kernel(shared, info, q, k, v, size, None, *rest)
    else:
        kernel = functools.partial(fwd_kernel, shared)
    return pl.pallas_call(
        kernel,
        grid_spec=pltpu.PrefetchScalarGridSpec(
            num_scalar_prefetch=1, grid=(1,),
            in_specs=[
                head_spec(shared, owners, HD, local), head_spec(shared, chunks, CH, 128), head_spec(shared, chunks, 128, CH),
                whole_spec(*sizes.shape),
            ] + ([] if first else [pl.BlockSpec(memory_space=pl.ANY)]),
            out_specs=[pl.BlockSpec((1, owners, HD, wide), lambda i, n: (seq, 0, 0, 0)), whole_spec(parts, 1, BQ)],
            scratch_shapes=[
                pltpu.VMEM((128, BQ), f32), pltpu.VMEM((2, CH, BQ), bf16), pltpu.VMEM((parts, 128, BQ), bf16),
                pltpu.VMEM((parts, 1, BQ), f32),
            ]),
        out_shape=[shape, jax.ShapeDtypeStruct((parts, 1, BQ), f32)],
        input_output_aliases={} if first else {5: 0},
        compiler_params=pltpu.CompilerParams(vmem_limit_bytes=48 << 20),
        cost_estimate=cost(pairs * 1024, chunks * CH * 512, pairs),
        name="attend_forward_shared" if shared else "attend_forward_own",
    )(*((info, q, k, v, sizes) + (() if first else (held,))))


def bwd_kernel(shared, first, info, q_ref, k_ref, v_ref, lse_ref, out_ref, gout_ref, *rest):
    rest = rest if first else rest[2 if shared else 1:]
    if shared:
        dq_ref, dkv_ref, dk_acc, dv_acc, dq_acc, qa, qat, ga, gat, pb, db = rest
    else:
        dqkv_ref, dk_acc, dv_acc, dq_acc, qa, qat, ga, gat, pb, db = rest
    count = lax.div(info[0] + (CH - 1), CH)
    chunks = k_ref.shape[1]
    parts = 2 if shared else 4
    dk_acc[...] = jnp.zeros_like(dk_acc)
    dv_acc[...] = jnp.zeros_like(dv_acc)

    def piece(ref, part):
        if shared:
            return jnp.concatenate([ref[0, 2 * part], ref[0, 2 * part + 1]], axis=1)
        return ref[0, part]

    for part in range(parts):
        q_full = with_shift(assemble(q_ref, part, shared, info[3]), lse_ref[part])
        qat[part] = q_full.astype(bf16)
        qa[part] = q_full.T.astype(bf16)
        g_t = piece(gout_ref, part)
        meet = jnp.sum(g_t.astype(f32) * piece(out_ref, part).astype(f32), axis=0, keepdims=True)
        g_full = with_shift(g_t, meet)
        gat[part] = g_full.astype(bf16)
        ga[part] = g_full.T.astype(bf16)

    def ahead(part, j, slot):
        raised = jnp.exp2(dg(qa[part], k_ref[0, j], 1, 1))
        pb[slot] = raised.astype(bf16)
        db[slot] = (raised * dg(ga[part], v_ref[0, j], 1, 0)).astype(bf16)

    ahead(0, 0, 0)

    def body(t, carry):
        part, j = carry
        now = t & 1
        part_next, j_next = step_on(part, j, count)
        dv_acc[j] += dg(gat[part], pb[now], 1, 0)[:HD]
        dk_acc[j] += dg(qat[part], db[now], 1, 0)[:HD]
        before = jnp.where(j == 0, 0.0, dq_acc[...])
        dq_acc[...] = before + dg(db[now], k_ref[0, j], 1, 0)
        ahead(jnp.minimum(part_next, parts - 1), j_next, 1 - now)

        @pl.when(j + 1 == count)
        def _():
            dq_t = (dq_acc[...] * 0.125).T[:HD].astype(bf16)
            if shared:
                for a in range(2):
                    dq_ref[0, 2 * part + a, :, :512] = dq_t[:32, a * 512:(a + 1) * 512]
                    dq_ref[0, 2 * part + a, :, 512:] = dq_t[32:, a * 512:(a + 1) * 512]
            else:
                dqkv_ref[0, part, 0] = dq_t
        return part_next, j_next

    lax.fori_loop(0, parts * count, body, (0, 0))
    for j in range(chunks):
        for owner in range(4):
            cols = slice(owner * 128, (owner + 1) * 128)
            dk = (dk_acc[j, :, cols] * LN2).astype(bf16)
            dv = dv_acc[j, :, cols].astype(bf16)
            if shared:
                dkv_ref[0, 0, owner, :, j * 128:(j + 1) * 128] = dk
                dkv_ref[1, 0, owner, :, j * 128:(j + 1) * 128] = dv
            else:
                dqkv_ref[0, owner, 1, :, j * 128:(j + 1) * 128] = dk
                dqkv_ref[0, owner, 2, :, j * 128:(j + 1) * 128] = dv


def attend_backward(shared, seq, q, k, v, lse, out, g_out, info, held):
    _, owners, _, local = q.shape
    chunks = k.shape[1]
    wide = out.shape[3]
    parts = owners * wide // BQ
    pairs = parts * BQ * chunks * CH * 0.6
    shape = jax.ShapeDtypeStruct
    first = held is None
    if shared:
        out_specs = [pl.BlockSpec((1, owners, 32, local), lambda i, n: (seq, 0, 0, 0)),
                     pl.BlockSpec((2, 1, owners, HD, local), lambda i, n: (0, seq, 0, 0, 0))]
        out_shape = [shape((2, owners, 32, local), bf16), shape((2, 2, owners, HD, local), bf16)]
    else:
        out_specs = [pl.BlockSpec((1, owners, 3, HD, local), lambda i, n: (seq, 0, 0, 0, 0))]
        out_shape = [shape((2, owners, 3, HD, local), bf16)]
    kept = () if first else tuple(held)
    of_seq = pl.BlockSpec((1, owners, HD, wide), lambda i, n: (seq, 0, 0, 0))
    return pl.pallas_call(
        functools.partial(bwd_kernel, shared, first),
        grid_spec=pltpu.PrefetchScalarGridSpec(
            num_scalar_prefetch=1, grid=(1,),
            in_specs=[
                head_spec(shared, owners, HD, local), head_spec(shared, chunks, CH, 128), head_spec(shared, chunks, 128, CH),
                whole_spec(parts, 1, BQ), of_seq, of_seq,
            ] + [pl.BlockSpec(memory_space=pl.ANY)] * len(kept),
            out_specs=out_specs,
            scratch_shapes=[
                pltpu.VMEM((chunks, HD, CH), f32), pltpu.VMEM((chunks, HD, CH), f32), pltpu.VMEM((BQ, 128), f32),
                pltpu.VMEM((parts, BQ, 128), bf16), pltpu.VMEM((parts, 128, BQ), bf16),
                pltpu.VMEM((parts, BQ, 128), bf16), pltpu.VMEM((parts, 128, BQ), bf16),
                pltpu.VMEM((2, BQ, CH), bf16), pltpu.VMEM((2, BQ, CH), bf16),
            ]),
        out_shape=out_shape,
        input_output_aliases={7 + n: n for n in range(len(kept))},
        compiler_params=pltpu.CompilerParams(vmem_limit_bytes=56 << 20),
        cost_estimate=cost(pairs * 100, chunks * CH * 2048),
        name="attend_backward_shared" if shared else "attend_backward_own",
    )(info, q, k, v, lse, out, g_out, *kept)


def gelu_pair(u):
    half = 0.5 * (1.0 + lax.erf(u * 0.7071067811865476))
    return u * half, half + u * (0.3989422804014327 * jnp.exp2(u * u * (-0.5 * LOG2E)))


def norm_stats(v):
    mean = jnp.mean(v, axis=-1, keepdims=True)
    centred = v - mean
    inverse = lax.rsqrt(jnp.mean(centred * centred, axis=-1, keepdims=True) + 1e-12)
    return centred * inverse, inverse


def norm_back(grad, xhat, inverse, gain):
    g = grad * gain
    return (g - jnp.mean(g, axis=-1, keepdims=True) - xhat * jnp.mean(g * xhat, axis=-1, keepdims=True)) * inverse


def weight_part(ref, first, rows):
    part = ref[:, first:first + rows, :]
    return part.reshape(part.shape[0] * rows, part.shape[2])


def ffn_kernel(spans, info, x_ref, own_ref, sh_ref, cot_ref, w_ref, bin_ref, vec_ref,
               act_out, resid_out, gown_out, gsh_out, active_out, dinner_out, normed_out, douter_out, dbranch_out,
               vec_sum, bin_sum, slope, row_block):
    step = pl.program_id(0)
    width = x_ref.shape[-1]
    load_rows(row_block, x_ref, spans, info[1])
    rows = row_block[...].astype(f32)
    mixed_t = jnp.concatenate(
        [part for p in range(4) for part in (own_ref[p, 0], sh_ref[p, 0], own_ref[p, 1])], axis=0)
    vec = vec_ref[...]
    branch = dg(mixed_t, weight_part(w_ref, 768, 96), 0, 0) + vec[0:1]
    xhat1, inv1 = norm_stats(rows + branch)
    normed = xhat1 * vec[1:2] + vec[2:3]
    low = normed.astype(bf16)
    normed_out[...] = low
    outer = normed + vec[3:4]
    for n in range(4):
        cols = slice(n * 768, (n + 1) * 768)
        inner = dg(low, weight_part(w_ref, 384 + 96 * n, 96), 1, 0) + bin_ref[:, cols]
        value, bend = gelu_pair(inner)
        active_out[:, cols] = value.astype(bf16)
        slope[:, cols] = bend.astype(bf16)
    outer = outer + dg(active_out[...], weight_part(w_ref, 0, 384), 1, 0)
    xhat2, inv2 = norm_stats(outer)
    act_out[...] = (xhat2 * vec[4:5] + vec[5:6]).astype(bf16)
    cot = cot_ref[...].astype(f32)
    d2 = norm_back(cot, xhat2, inv2, vec[4:5])
    d_outer = d2.astype(bf16)
    douter_out[...] = d_outer
    d_normed = d2
    sums_in = []
    for n in range(4):
        cols = slice(n * 768, (n + 1) * 768)
        d_active = dg(d_outer, weight_part(w_ref.at[2 * n:2 * n + 2], 0, 384), 1, 1)
        d_inner = (d_active * slope[:, cols].astype(f32)).astype(bf16)
        dinner_out[:, cols] = d_inner
        sums_in.append(jnp.sum(d_inner.astype(f32), axis=0, keepdims=True))
        d_normed = d_normed + dg(d_inner, weight_part(w_ref, 384 + 96 * n, 96), 1, 1)
    d1 = norm_back(d_normed, xhat1, inv1, vec[1:2])
    resid_out[...] = d1
    d_branch = d1.astype(bf16)
    dbranch_out[...] = d_branch
    g_t = dg(weight_part(w_ref, 768, 96), d_branch, 1, 1).astype(bf16)
    for p in range(4):
        gown_out[p, 0] = g_t[192 * p:192 * p + 64]
        gsh_out[p, 0] = g_t[192 * p + 64:192 * p + 128]
        gown_out[p, 1] = g_t[192 * p + 128:192 * p + 192]
    total = lambda a: jnp.sum(a, axis=0, keepdims=True)
    sums = jnp.concatenate([
        total(d_branch.astype(f32)), total(d_normed * xhat1), total(d_normed),
        total(d_outer.astype(f32)), total(cot * xhat2), total(cot), jnp.zeros((2, width), f32)], axis=0)

    @pl.when(step == 0)
    def _():
        vec_sum[...] = sums
        for n in range(4):
            bin_sum[:, n * 768:(n + 1) * 768] = sums_in[n]

    @pl.when(step > 0)
    def _():
        vec_sum[...] += sums
        for n in range(4):
            bin_sum[:, n * 768:(n + 1) * 768] += sums_in[n]


def feed_forward(rows_in, own, sh, cotangent, weights, inner_bias, vectors, info):
    _, _, _, stretch, width = rows_in.shape
    local = cotangent.shape[0]
    spans = RB // (2 * stretch)
    steps = local // RB
    half_steps = steps // 2
    wide = inner_bias.shape[1]
    rows = lambda n: pl.BlockSpec((RB, n), lambda r, a: (r, 0))
    fixed = lambda *dims: pl.BlockSpec(dims, lambda r, a: (0,) * len(dims))
    own_spec = pl.BlockSpec((4, 2, HD, RB), lambda r, a: (0, 0, 0, r))
    sh_spec = pl.BlockSpec((4, 1, HD, RB), lambda r, a: (0, r // half_steps, 0, r % half_steps))
    shape = jax.ShapeDtypeStruct
    return pl.pallas_call(
        functools.partial(ffn_kernel, spans),
        grid_spec=pltpu.PrefetchScalarGridSpec(
            num_scalar_prefetch=1, grid=(steps,),
            in_specs=[
                pl.BlockSpec((1, 2, spans, stretch, width), lambda r, a: (0, 0, r, 0, 0)),
                own_spec, sh_spec, rows(width),
                pl.BlockSpec(weights.shape, lambda r, a: (0, 0, 0), pipeline_mode=pl.Buffered(1)),
                fixed(1, wide), fixed(8, width),
            ],
            out_specs=[
                rows(width), rows(width), own_spec, sh_spec, rows(wide), rows(wide), rows(width), rows(width), rows(width),
                fixed(8, width), fixed(1, wide),
            ],
            scratch_shapes=[pltpu.VMEM((RB, wide), bf16), pltpu.VMEM((RB, width), bf16)]),
        out_shape=[
            shape((local, width), bf16), shape((local, width), f32), shape(own.shape, bf16), shape(sh.shape, bf16),
            shape((local, wide), bf16), shape((local, wide), bf16), shape((local, width), bf16),
            shape((local, width), bf16), shape((local, width), bf16), shape((8, width), f32), shape((1, wide), f32),
        ],
        compiler_params=pltpu.CompilerParams(vmem_limit_bytes=60 << 20),
        name="feed_forward",
        cost_estimate=cost(local * width * (width + 2 * wide) * 4, local * wide * 20),
    )(info, rows_in, own, sh, cotangent, weights, inner_bias, vectors)


def outer_grad_kernel(scale, active_ref, douter_ref, out_ref):
    made = (dg(active_ref[...], douter_ref[...], 0, 0) * scale).astype(bf16)
    out_ref[...] = made.reshape(out_ref.shape)


def inner_grad_kernel(scale, packed_ref, normed_ref, dinner_ref, own_ref, sh_ref, dbranch_ref, out_ref):
    step = pl.program_id(0)

    @pl.when(step < 4)
    def _():
        out_ref[...] = (dg(normed_ref[...], dinner_ref[...], 0, 0) * scale).astype(bf16).reshape(out_ref.shape)

    @pl.when(step == 4)
    def _():
        mixed_t = jnp.concatenate([
            part for p in range(4)
            for part in (own_ref[p, 0], jnp.concatenate([sh_ref[p, 0], sh_ref[p, 1]], axis=1), own_ref[p, 1])], axis=0)
        out_ref[...] = (dg(mixed_t, dbranch_ref[...], 1, 0) * scale).astype(bf16).reshape(out_ref.shape)


def weight_grads(scale, active, d_outer, normed, d_inner, own, sh, d_branch):
    local, wide = active.shape
    width = normed.shape[1]
    packed = pl.pallas_call(
        functools.partial(outer_grad_kernel, scale), grid=(4,),
        in_specs=[pl.BlockSpec((local, width), lambda m: (0, m)), pl.BlockSpec((local, width), lambda m: (0, 0))],
        out_specs=pl.BlockSpec((2, 384, width), lambda m: (m, 0, 0)),
        out_shape=jax.ShapeDtypeStruct((8, 896, width), bf16),
        compiler_params=pltpu.CompilerParams(vmem_limit_bytes=40 << 20), name="outer_grad",
        cost_estimate=cost(2 * local * wide * width, 2 * wide * (local + width)),
    )(active, d_outer)
    fixed = lambda a: pl.BlockSpec(a.shape, lambda n: (0,) * a.ndim)
    return pl.pallas_call(
        functools.partial(inner_grad_kernel, scale), grid=(5,),
        in_specs=[
            pl.BlockSpec(memory_space=pl.ANY), fixed(normed),
            pl.BlockSpec((local, width), lambda n: (0, jnp.minimum(n, 3))), fixed(own), fixed(sh), fixed(d_branch)],
        out_specs=pl.BlockSpec((8, 96, width), lambda n: (0, 4 + n, 0)),
        out_shape=jax.ShapeDtypeStruct((8, 896, width), bf16), input_output_aliases={0: 0},
        compiler_params=pltpu.CompilerParams(vmem_limit_bytes=40 << 20), name="inner_grad",
        cost_estimate=cost(2 * local * (wide + width) * width, 2 * (wide + width) * (local + width)),
    )(packed, normed, d_inner, own, sh, d_branch)


def head_grad_kernel(scale, spans, info, *refs):
    x_refs, (own_ref, dq_ref, dkv_ref, out_ref, bias_out, acc, bias_acc, rows) = refs[:4], refs[4:]
    seq, away, half = pl.program_id(0), pl.program_id(1), pl.program_id(3)
    last = (seq == 1) & (away == 1) & (pl.program_id(2) == 1) & (half == pl.num_programs(3) - 1)
    for n in range(4):
        @pl.when(seq * 2 + away == n)
        def _(n=n):
            load_rows(rows, x_refs[n], spans, info[1])
    dq_t = jnp.where(half == info[3], jnp.concatenate([dq_ref[0, 0, :, :512], dq_ref[0, 0, :, 512:]], axis=0).astype(f32), 0.0)
    d_t = jnp.concatenate([
        own_ref[0, 0, 0], dq_t.astype(bf16), own_ref[0, 0, 1], dkv_ref[0, 0, 0], own_ref[0, 0, 2], dkv_ref[1, 0, 0]], axis=0)

    @pl.when((seq == 0) & (away == 0) & (pl.program_id(2) == 0) & (half == 0))
    def _():
        acc[...] = jnp.zeros_like(acc)
        bias_acc[...] = jnp.zeros_like(bias_acc)
    acc[...] += dg(d_t, rows[...], 1, 0)
    bias_acc[...] += dg(jnp.ones((8, d_t.shape[1]), bf16), d_t, 1, 1)

    @pl.when(last)
    def _():
        out_ref[...] = (acc[...] * scale).T.astype(bf16)
        bias_out[...] = bias_acc[...] * scale


def head_grads(scale, sources, dqkv_own, dq_sh, dkv_sh, info):
    _, _, zs, stretch, width = sources[0].shape
    local = 2 * zs * stretch
    spans = 512 // (2 * stretch)
    halves = local // 512

    def source_spec(n):
        def index(s, a, o, h, i):
            now = 2 * s + a
            across = jnp.where(now == n, o, jnp.where(now < n, 0, 1))
            return (across, 0, jnp.where(now == n, h, jnp.where(now < n, 0, halves - 1)), 0, 0)
        return pl.BlockSpec((1, 2, spans, stretch, width), index)
    return pl.pallas_call(
        functools.partial(head_grad_kernel, scale, spans),
        grid_spec=pltpu.PrefetchScalarGridSpec(
            num_scalar_prefetch=1, grid=(2, 2, 2, halves),
            in_specs=[source_spec(n) for n in range(4)] + [
                pl.BlockSpec((1, 1, 3, HD, 512), lambda s, a, o, h, i: (s, owner_of(a, o, i), 0, 0, h)),
                pl.BlockSpec((1, 1, 32, local), lambda s, a, o, h, i: (s, owner_of(a, o, i), 0, 0)),
                pl.BlockSpec((2, 1, 1, HD, 512), lambda s, a, o, h, i: (0, s, owner_of(a, o, i), 0, h))],
            out_specs=[pl.BlockSpec((width, 384), lambda s, a, o, h, i: (0, 0)), pl.BlockSpec((8, 384), lambda s, a, o, h, i: (0, 0))],
            scratch_shapes=[pltpu.VMEM((384, width), f32), pltpu.VMEM((8, 384), f32), pltpu.VMEM((512, width), bf16)]),
        out_shape=[jax.ShapeDtypeStruct((width, 384), bf16), jax.ShapeDtypeStruct((8, 384), f32)],
        compiler_params=pltpu.CompilerParams(vmem_limit_bytes=40 << 20), name="head_grads",
        cost_estimate=cost(8 * local * 768 * width, 8 * local * width * 2),
    )(info, *sources, dqkv_own, dq_sh, dkv_sh)


def token_grad_kernel(own_ref, low_ref, high_ref, dkv_ref, w_ref, resid_ref, out_ref):
    total = resid_ref[...]
    for kind in range(3):
        made = []
        for p in range(4):
            if kind == 0:
                middle = jnp.concatenate([low_ref[p, 0], high_ref[p, 0]], axis=0)
            else:
                middle = jnp.concatenate([dkv_ref[p, kind - 1, n] for n in range(2)], axis=0)
            made += [own_ref[p, 0, kind], middle, own_ref[p, 1, kind]]
        total = total + dg(jnp.concatenate(made, axis=0), weight_part(w_ref, 96 * kind, 96), 0, 1)
    out_ref[...] = total.astype(bf16)


def token_grad(own, shared, weights, resid):
    local, width = resid.shape
    steps = local // RB
    half_steps = steps // 2
    rows = pl.BlockSpec((RB, width), lambda r: (r, 0))
    return pl.pallas_call(
        token_grad_kernel, grid=(steps,),
        in_specs=[
            pl.BlockSpec((4, 2, 3, HD, RB), lambda r: (0, 0, 0, 0, r)),
            pl.BlockSpec((4, 1, None, 32, RB), lambda r: (0, r // half_steps, 0, 0, r % half_steps)),
            pl.BlockSpec((4, 1, None, 32, RB), lambda r: (0, r // half_steps, 0, 0, half_steps + r % half_steps)),
            pl.BlockSpec((4, 2, 2, 32, RB), lambda r: (0, 0, 0, 0, r)),
            pl.BlockSpec(weights.shape, lambda r: (0, 0, 0)), rows],
        out_specs=rows, out_shape=jax.ShapeDtypeStruct((local, width), bf16),
        compiler_params=pltpu.CompilerParams(vmem_limit_bytes=40 << 20), name="token_grad",
        cost_estimate=cost(local * width * width * 6, local * width * 12),
    )(own, shared[:, :, :1], shared[:, :, :1], shared[:, :, 1:], weights, resid)


SWAP = [(0, 1), (1, 0)]
PAIR = ("x", "y", "c")
ALL = ("z", "x", "y", "c")
SHARD = ("z", "x")


def canonical(packed, shards):
    if shards == 8:
        return packed
    width = packed.shape[2]
    per, keep = 96 * 8 // shards, shards // 8
    outer = packed[:, :4 * per].reshape(8, 384, width)
    inner = packed[:, 4 * per:8 * per].reshape(8, keep, 4, per, width).transpose(0, 2, 1, 3, 4).reshape(8, 384, width)
    output = packed[:, 8 * per:9 * per].reshape(8, 96, width)
    return jnp.concatenate([outer, inner, output, jnp.zeros((8, 32, width), packed.dtype)], axis=1)


def from_canonical(packed, last, shards):
    width = packed.shape[2]
    if shards == 8:
        return packed.at[:, 864:].set(jnp.broadcast_to(last[None], (8, 32, width)))
    per, keep = 96 * 8 // shards, shards // 8
    outer = packed[:, :384].reshape(shards, 4 * per, width)
    inner = packed[:, 384:768].reshape(8, 4, keep, per, width).transpose(0, 2, 1, 3, 4).reshape(shards, 4 * per, width)
    output = packed[:, 768:864].reshape(shards, per, width)
    return jnp.concatenate([outer, inner, output, jnp.broadcast_to(last[None], (shards, 32, width))], axis=1)


def canonical_heads(packed, shards, parts):
    if shards == 8:
        return packed
    width = packed.shape[2]
    per = 96 * 8 // shards
    made = [packed[:, k * per:(k + 1) * per].reshape(8, 96, width) for k in range(parts)]
    return jnp.concatenate(made + [jnp.zeros((8, 32, width), packed.dtype)], axis=1)


def quarter(rows):
    place = lax.axis_index("y") * 2 + lax.axis_index("c")
    part = rows.shape[0] // 4
    return lax.dynamic_slice_in_dim(rows, place * part, part)


def flipped(array, axis, here):
    return jnp.where(here == 0, array, jnp.flip(array, axis))


def body(tokens, lengths, deal_order, w_query, w_key, w_value, w_output, b_query, b_value, b_output,
         ln1_gain, ln1_shift, w_inner, b_inner, w_outer, b_outer, ln2_gain, ln2_shift, cotangent):
    tie = lax.optimization_barrier
    zs = lax.axis_size("z")
    shards = 2 * zs
    scale = 1.0 / (shards * 4)
    seq_count, _, stretch, width = tokens.shape
    per = w_query.shape[0]
    half = zs // 2
    x, y, c = lax.axis_index("x"), lax.axis_index("y"), lax.axis_index("c")

    def deal(order):
        ordered = jnp.take(tokens[:, 0], order, axis=0)
        return lax.all_to_all(ordered, "z", split_axis=0, concat_axis=0, tiled=True)

    def corner(across, along):
        return [lax.ppermute(across[:half], "y", SWAP), lax.ppermute(along[half:], "x", SWAP)]

    def this_core(own, across, along, corner):
        return jnp.concatenate([own, across, along] + corner, axis=0).reshape(2, 2, zs, stretch, width)

    first_own = deal(deal_order[0::2])
    first_own, order_b, w_query, w_key, w_value, b_query, b_value = tie(
        (first_own, deal_order[1::2], w_query, w_key, w_value, b_query, b_value))

    def head_columns(matrix):
        heads = matrix.reshape(per, 2, 2, 3, HD)
        mine = lax.dynamic_index_in_dim(heads, y, axis=2, keepdims=False)
        own = lax.dynamic_index_in_dim(mine, 2 * c, axis=2, keepdims=False)
        return [own, mine[:, :, 1]]
    pad = lambda v: jnp.pad(v, (0, width - v.shape[0]))[None]
    columns = jnp.concatenate(
        [col for matrix in (w_query, w_key, w_value) for col in head_columns(matrix)], axis=2).reshape(per, width)
    head_pack = jnp.concatenate([columns, pad(b_query), pad(b_value), jnp.zeros((14, width), bf16)], axis=0)
    head_all = lax.all_gather(head_pack, SHARD, axis=0, tiled=False)
    head_weight = canonical_heads(head_all, shards, 1)

    def head_bias(row):
        heads = head_all[:, per + row, :per].reshape(2, 2, 3, HD)
        mine = lax.dynamic_slice(heads, (x, y, 0, 0), (1, 1, 3, HD))[0, 0]
        return [lax.dynamic_index_in_dim(mine, 2 * c, axis=0, keepdims=False), mine[1]]
    bias_row = jnp.concatenate(head_bias(0) + [jnp.zeros((2 * HD,), bf16)] + head_bias(1)).astype(f32)[None]

    across_a, along_a = lax.ppermute(first_own, "x", SWAP), lax.ppermute(first_own, "y", SWAP)
    second_own = deal(order_b)
    across_a, along_a, second_own = tie((across_a, along_a, second_own))
    near_a = this_core(first_own, across_a, along_a, corner(across_a, along_a))
    far_a = lax.ppermute(near_a, "c", SWAP)
    near_a, second_own = tie((near_a, second_own))
    across_b, along_b = lax.ppermute(second_own, "x", SWAP), lax.ppermute(second_own, "y", SWAP)

    w_outer, w_inner, w_output, head_all_done = tie((w_outer, w_inner, w_output, head_pack))
    vectors = (b_output, ln1_gain, ln1_shift, b_outer, ln2_gain, ln2_shift)
    layer_pack = jnp.concatenate(
        [w_outer] + [w_inner[:, n * width:(n + 1) * width] for n in range(4)] + [w_output]
        + [pad(b_inner)] + [pad(v) for v in vectors] + [jnp.zeros((25, width), bf16)], axis=0)
    layer_all = lax.all_gather(quarter(layer_pack), ALL, axis=0, tiled=True).reshape(shards, 9 * per + 32, width)
    layer_weights = canonical(layer_all, shards)
    inner_bias = layer_all[:, 9 * per, :4 * per].reshape(1, 4 * width).astype(f32)
    vector_rows = jnp.concatenate(
        [layer_all[:, 9 * per + 1 + n, :per].reshape(1, width) for n in range(6)] + [jnp.zeros((2, width), bf16)],
        axis=0).astype(f32)
    back_pack = jnp.concatenate([w_query, w_key, w_value, jnp.zeros((32, width), bf16)], axis=0)
    back_all = lax.all_gather(quarter(back_pack), ALL, axis=0, tiled=True).reshape(shards, 3 * per + 32, width)

    slots = lax.dynamic_slice_in_dim(deal_order, lax.axis_index("z") * 2, 2)
    matches = slots[:, None] == jnp.arange(seq_count, dtype=jnp.int32)[None, :]
    lens = jnp.sum(jnp.where(matches, lengths[None, :], 0), axis=1).astype(jnp.int32)
    infos = [jnp.stack([lens[n], x, y, c]).astype(jnp.int32) for n in range(2)]

    def swap(array):
        flat = array.reshape((8,) + array.shape[2:])
        return lax.all_to_all(flat, PAIR, split_axis=0, concat_axis=0, tiled=True)

    def to_tokens(array):
        return swap(array).reshape((4, 2) + array.shape[2:])

    def to_heads(array):
        return swap(array).reshape((2, 4) + array.shape[2:])

    heads_a = project(near_a, far_a, head_weight, bias_row, infos[0])
    heads_a, across_b, along_b = tie((heads_a, across_b, along_b))
    near_b = this_core(second_own, across_b, along_b, corner(across_b, along_b))
    own_first, lse_own_a = attend_forward(False, 0, *heads_a, infos[0], None)
    own_first, near_b = tie((own_first, near_b))
    far_b = lax.ppermute(near_b, "c", SWAP)
    sh_first, lse_sh_a = attend_forward(True, 0, *heads_a, infos[0], None)
    sh_first, far_b = tie((sh_first, far_b))
    heads_b = project(near_b, far_b, head_weight, bias_row, infos[1])
    own, lse_own_b = attend_forward(False, 1, *heads_b, infos[1], own_first)
    own_t = to_tokens(own)
    own, info_later = tie((own, infos[1]))
    sh, lse_sh_b = attend_forward(True, 1, *heads_b, info_later, sh_first)
    sh_sent, own_t = tie((sh, own_t))
    sh_t = to_tokens(sh_sent)
    mine_rows = jnp.where(x == 0, jnp.stack([first_own, across_a]), jnp.stack([second_own, across_b]))[None]

    (act, resid, g_own, g_sh, active, d_inner, normed, d_outer, d_branch, vec_sums, bin_sums) = feed_forward(
        mine_rows, own_t, sh_t, cotangent.reshape(-1, width), layer_weights, inner_bias, vector_rows, infos[0])
    g_own_h, g_sh_h = to_heads(g_own), to_heads(g_sh)
    active, back_all = tie((active, back_all))
    packed = weight_grads(scale, active, d_outer, normed, d_inner, own_t, sh_t, d_branch)
    sums = jnp.concatenate([bin_sums.reshape(4, width), vec_sums, jnp.zeros((20, width), f32)], axis=0) * scale
    ready = from_canonical(packed, sums.astype(bf16), shards)
    _, g_own_h = tie((ready, g_own_h))
    back_weights = canonical_heads(back_all, shards, 3)
    layer_part = lax.psum_scatter(ready.reshape(-1, width), ("z", "x", "c"), scatter_dimension=0, tiled=True)

    qkv_a, qkv_b = heads_a[:3], heads_b[:3]
    first = attend_backward(False, 0, *qkv_a, lse_own_a, own, g_own_h, infos[0], None)
    dqkv_own, = attend_backward(False, 1, *qkv_b, lse_own_b, own, g_own_h, infos[1], first)
    back_own = to_tokens(dqkv_own)
    dqkv_own, info_a, info_b = tie((dqkv_own, *infos))
    first = attend_backward(True, 0, *qkv_a, lse_sh_a, sh, g_sh_h, info_a, None)
    dq_sh, dkv_sh = attend_backward(True, 1, *qkv_b, lse_sh_b, sh, g_sh_h, info_b, first)
    kept = lax.dynamic_index_in_dim(dkv_sh, c, axis=0, keepdims=False)
    given = lax.dynamic_index_in_dim(dkv_sh, 1 - c, axis=0, keepdims=False)
    taken = lax.ppermute(given, "c", SWAP)
    shared_out = jnp.concatenate([dq_sh, (kept.astype(f32) + taken.astype(f32)).astype(bf16)], axis=2)
    shared_out, back_own, dqkv_own = tie((shared_out, back_own, dqkv_own))
    back_shared = to_tokens(shared_out.reshape(2, 4, 3, 32, -1))
    d_heads, d_bias = head_grads(scale, (near_a, far_a, near_b, far_b), dqkv_own, dq_sh, dkv_sh, infos[0])

    head_ready = jnp.concatenate([
        d_heads.reshape(zs, 2, per, 384),
        jnp.broadcast_to(d_bias[:1].astype(bf16)[None, None], (zs, 2, 16, 384))], axis=2)
    head_ready, _ = tie((head_ready, back_shared))
    if zs == 4:
        group = lax.axis_index("z")
        head_sum = lax.dynamic_index_in_dim(head_ready, group, axis=0, keepdims=False).astype(f32)
        for k in range(1, zs):
            sent = lax.dynamic_index_in_dim(head_ready, (group + k) % zs, axis=0, keepdims=False)
            head_sum = head_sum + lax.ppermute(sent, "z", [(i, (i + k) % zs) for i in range(zs)]).astype(f32)
        head_sum = head_sum.astype(bf16)
    else:
        head_sum = lax.psum_scatter(
            head_ready.reshape(-1, 384), "z", scatter_dimension=0, tiled=True).reshape(2, per + 16, 384)
    head_mine = lax.dynamic_index_in_dim(head_sum, x, axis=0, keepdims=False)
    head_other = lax.dynamic_index_in_dim(head_sum, 1 - x, axis=0, keepdims=False)

    d_rows = token_grad(back_own, back_shared, back_weights, resid)
    layer_part, _, head_mine, head_other = tie((layer_part, d_rows, head_mine, head_other))
    returned = lax.all_to_all(
        d_rows.reshape(shards, stretch, width), SHARD, split_axis=0, concat_axis=0, tiled=True)

    head_pair = jnp.stack([head_mine, lax.ppermute(head_other, "x", SWAP)])
    head_four = jnp.stack([head_pair, lax.ppermute(head_pair, "y", SWAP)])
    head_eight = jnp.stack([head_four, lax.ppermute(head_four, "c", SWAP)]).reshape(2, 2, 2, per + 16, 6, HD)
    cores = flipped(flipped(flipped(head_eight, 2, x), 1, y), 0, c).astype(f32)

    def full(kind):
        joined = jnp.stack([cores[0, :, :, :, 2 * kind], cores[0, :, :, :, 2 * kind + 1] + cores[1, :, :, :, 2 * kind + 1],
                            cores[1, :, :, :, 2 * kind]], axis=0)
        return joined.transpose(3, 2, 1, 0, 4).reshape(per + 16, width)
    d_wq, d_wk, d_wv = (full(kind) for kind in range(3))
    place = lax.axis_index("z") * 2 + x
    own_slice = lambda row, n: lax.dynamic_slice_in_dim(row, place * n, n)
    d_bq, d_bv = own_slice(d_wq[per], per), own_slice(d_wv[per], per)
    d_wq, d_wk, d_wv = d_wq[:per], d_wk[:per], d_wv[:per]

    layer_sum = (layer_part.astype(f32) + lax.ppermute(layer_part, "y", SWAP).astype(f32)).astype(bf16)
    layer_grads = flipped(jnp.stack([layer_sum, lax.ppermute(layer_sum, "c", SWAP)]), 0, c)
    layer_grads = layer_grads.reshape(9 * per + 32, width).astype(f32)
    d_wouter = layer_grads[:4 * per]
    d_winner = jnp.concatenate([layer_grads[(4 + n) * per:(5 + n) * per] for n in range(4)], axis=1)
    d_woutput = layer_grads[8 * per:9 * per]
    d_binner = own_slice(layer_grads[9 * per:9 * per + 4].reshape(-1), 4 * per)
    d_bo, d_g1, d_s1, d_bout, d_g2, d_s2 = (own_slice(layer_grads[9 * per + 4 + n], per) for n in range(6))
    returned, d_wouter, d_winner, d_woutput, d_wq, d_wk, d_wv = tie(
        (returned, d_wouter, d_winner, d_woutput, d_wq, d_wk, d_wv))
    d_tokens = jnp.zeros_like(returned).at[deal_order].set(returned)[:, None]
    return (act.reshape(1, shards, stretch, width), d_tokens, d_wq, d_wk, d_wv, d_woutput, d_bq, d_bv, d_bo,
            d_g1, d_s1, d_winner, d_binner, d_wouter, d_bout, d_g2, d_s2)


def solution(mesh):
    shards, splits = mesh.devices.shape
    fine = Mesh(mesh.devices.reshape(shards // 2, 2, splits // 2, 2), ALL)
    S, Q = SHARD, ("y", "c")
    row, mat = P(S), P(S, None)
    return jax.shard_map(
        body, mesh=fine,
        in_specs=(P(None, S, Q, None), P(), P(), mat, mat, mat, mat, row, row, row, row, row, mat, row, mat, row, row, row,
                  P(S, None, Q, None)),
        out_specs=(P(S, None, Q, None), P(None, S, Q, None), mat, mat, mat, mat, row, row, row, row, row, mat, row, mat,
                   row, row, row),
        check_vma=False)
```

```python
import functools, math
import jax
import jax.numpy as jnp
from jax import lax
from jax.experimental import pallas as pl
from jax.experimental.pallas import tpu as pltpu
from jax.sharding import Mesh, PartitionSpec as P

f32, bf16 = jnp.float32, jnp.bfloat16
LOG2E = 1.4426950408889634
LN2 = 0.6931471805599453
CH = 512
BQ = 1024
RB = 256
HD = 64
FAR = -1.0e30

def dg(a, b, ca, cb):
    return lax.dot_general(a, b, (((ca,), (cb,)), ((), ())), preferred_element_type=f32)


def three_parts(row):
    hi = row.astype(bf16).astype(f32)
    rest = row - hi
    mid = rest.astype(bf16).astype(f32)
    return hi, mid, rest - mid


def with_shift(top, shift):
    hi, mid, low = three_parts(shift)
    row = lax.broadcasted_iota(jnp.int32, (HD, top.shape[1]), 0)
    tail = jnp.where(row == 0, -hi, jnp.where(row == 1, -mid, jnp.where(row == 2, -low, jnp.where(row == 3, 1.0, 0.0))))
    return jnp.concatenate([top.astype(f32), tail], axis=0)


def load_rows(rows, ref, spans, x):
    stretch = ref.shape[3]
    for z in range(spans):
        for a in range(2):
            at = (2 * z + a) * stretch
            rows[at:at + stretch] = ref[0, a ^ x, z]


def qkv_kernel(stretch, spans, info, near_ref, far_ref, w_ref, b_ref, q_out, k_out, v_out, size_out, rows):
    away, half = pl.program_id(0), pl.program_id(2)
    owner = ((pl.program_id(1) ^ info[2]) << 1) | (away ^ info[3])

    @pl.when(away == 0)
    def _():
        load_rows(rows, near_ref, spans, info[1])

    @pl.when(away == 1)
    def _():
        load_rows(rows, far_ref, spans, info[1])
    weight = w_ref[...].reshape(rows.shape[1], 384)
    made = dg(rows[...], weight, 1, 0) + b_ref[...]
    count = rows.shape[0]
    q_t = (made[:, :128] * (LOG2E / 8.0)).T
    q_out[0, 0] = q_t[:HD].astype(bf16)
    q_out[1, 0] = q_t[HD:].astype(bf16)
    lane = lax.broadcasted_iota(jnp.int32, (count, 128), 1)
    row = lax.broadcasted_iota(jnp.int32, (count, 128), 0) + half * count
    shift = int(math.log2(stretch))
    position = lax.shift_left(lax.shift_right_logical(row, shift), shift + 2) + owner * stretch + (row & (stretch - 1))
    hidden = jnp.where(position < info[0], 0.0, FAR)
    tail = jnp.where(lane == HD + 3, hidden, jnp.where(lane < HD + 3, 1.0, 0.0))
    keys = made[:, 128:256]
    picks = lax.broadcasted_iota(jnp.int32, (128, 128), 0) // HD == lax.broadcasted_iota(jnp.int32, (128, 128), 1)
    sizes = dg((keys * keys).astype(bf16), jnp.where(picks, 1.0, 0.0).astype(bf16), 1, 0)
    size_out[0, 0] = jnp.max(sizes, axis=0, keepdims=True)
    for head in range(2):
        turned = keys if head == 0 else pltpu.roll(keys, HD, 1)
        full = jnp.where(lane < HD, turned, tail).astype(bf16)
        for j in range(count // 128):
            k_out[head, j] = full[j * 128:(j + 1) * 128]
    v_t = made[:, 256:384].T
    ones = jnp.where(lax.broadcasted_iota(jnp.int32, (HD, count), 0) < 3, 1.0, 0.0)
    for head in range(2):
        full = jnp.concatenate([v_t[head * HD:(head + 1) * HD], ones], axis=0).astype(bf16)
        for j in range(count // 128):
            v_out[head, j] = full[:, j * 128:(j + 1) * 128]


def owner_of(away, across, info):
    return ((across ^ info[2]) << 1) | (away ^ info[3])


def project(near, far, weight, bias, info):
    _, _, zs, stretch, width = near.shape
    local = 2 * zs * stretch
    spans = 512 // (2 * stretch)
    halves = local // 512
    chunks = 4 * local // CH
    per = chunks // halves
    block = (1, 2, spans, stretch, width)
    return pl.pallas_call(
        functools.partial(qkv_kernel, stretch, spans),
        grid_spec=pltpu.PrefetchScalarGridSpec(
            num_scalar_prefetch=1, grid=(2, 2, halves),
            in_specs=[
                pl.BlockSpec(block, lambda a, o, h, n: (jnp.where(a == 0, o, 1), 0, jnp.where(a == 0, h, halves - 1), 0, 0)),
                pl.BlockSpec(block, lambda a, o, h, n: (jnp.where(a == 0, 0, o), 0, jnp.where(a == 0, 0, h), 0, 0)),
                pl.BlockSpec((8, width // 8, 384), lambda a, o, h, n: (0, 0, n[1])),
                pl.BlockSpec((1, 384), lambda a, o, h, n: (0, 0)),
            ],
            out_specs=[
                pl.BlockSpec((2, 1, HD, 512), lambda a, o, h, n: (0, owner_of(a, o, n), 0, h)),
                pl.BlockSpec((2, per, 128, 128), lambda a, o, h, n: (0, h, owner_of(a, o, n), 0)),
                pl.BlockSpec((2, per, 128, 128), lambda a, o, h, n: (0, h, 0, owner_of(a, o, n))),
                pl.BlockSpec((1, 1, 1, 128), lambda a, o, h, n: (owner_of(a, o, n), h, 0, 0)),
            ],
            scratch_shapes=[pltpu.VMEM((512, width), bf16)]),
        out_shape=[
            jax.ShapeDtypeStruct((2, 4, HD, local), bf16),
            jax.ShapeDtypeStruct((2, chunks, CH, 128), bf16),
            jax.ShapeDtypeStruct((2, chunks, 128, CH), bf16),
            jax.ShapeDtypeStruct((4, halves, 1, 128), f32),
        ],
        compiler_params=pltpu.CompilerParams(vmem_limit_bytes=60 << 20),
        name="qkv",
        cost_estimate=cost(4 * near.size * 384, near.size * 8),
    )(info, near, far, weight, bias)


def step_on(q, j, count):
    last = j + 1 == count
    return jnp.where(last, q + 1, q), jnp.where(last, 0, j + 1)


def assemble(ref, q, shared, core):
    if not shared:
        return ref[0, q]
    at = pl.multiple_of(core * 512, 512)
    return jnp.concatenate([ref[0, 2 * q, :, pl.ds(at, 512)], ref[0, 2 * q + 1, :, pl.ds(at, 512)]], axis=1)


def fwd_kernel(shared, info, q_ref, k_ref, v_ref, size_ref, held_ref, out_ref, lse_ref, acc, probs, qa, shifts):
    count = lax.div(info[0] + (CH - 1), CH)
    parts = 2 if shared else 4
    lane = lax.broadcasted_iota(jnp.int32, (1, 128), 1)
    sizes = functools.reduce(jnp.maximum, [size_ref[o, h] for o in range(size_ref.shape[0]) for h in range(size_ref.shape[1])])
    widest = jnp.sqrt(jnp.max(jnp.where(lane == int(shared), sizes, 0.0), axis=1, keepdims=True))

    for part in range(parts):
        q_t = assemble(q_ref, part, shared, info[3])
        wide = q_t.astype(f32)
        shift = jnp.sqrt(jnp.sum(wide * wide, axis=0, keepdims=True)) * widest
        shifts[part] = shift
        qa[part] = with_shift(q_t, shift).astype(bf16)

    def raised(part, j):
        return jnp.exp2(dg(k_ref[0, j], qa[part], 1, 0)).astype(bf16)

    probs[0] = raised(0, 0)

    def body(t, carry):
        part, j = carry
        now = t & 1
        part_next, j_next = step_on(part, j, count)
        before = jnp.where(j == 0, 0.0, acc[...])
        acc[...] = before + dg(v_ref[0, j], probs[now], 1, 0)
        probs[1 - now] = raised(jnp.minimum(part_next, parts - 1), j_next)

        @pl.when(j + 1 == count)
        def _():
            total = acc[HD:HD + 1]
            fine = (jnp.min(total) > 2.0 ** -90) & (jnp.max(total) < 2.0 ** 60)

            @pl.when(jnp.logical_not(fine))
            def _():
                plain = qa[part].astype(f32)
                row = lax.broadcasted_iota(jnp.int32, plain.shape, 0)
                qa[part] = jnp.where((row >= HD) & (row < HD + 3), 0.0, plain).astype(bf16)

                def peak(i, top):
                    return jnp.maximum(top, jnp.max(dg(k_ref[0, i], qa[part], 1, 0), axis=0, keepdims=True))
                shift = lax.fori_loop(0, count, peak, jnp.full((1, BQ), FAR, f32))
                shifts[part] = shift
                qa[part] = with_shift(plain[:HD], shift).astype(bf16)
                acc[...] = jnp.zeros_like(acc)

                def again(i, carry):
                    acc[...] += dg(v_ref[0, i], raised(part, i), 1, 0)
                    return carry
                lax.fori_loop(0, count, again, 0)

            total = acc[HD:HD + 1]
            mixed = (acc[:HD] * (1.0 / total)).astype(bf16)
            lse_ref[part] = shifts[part] + jnp.log2(total)
            if shared:
                out_ref[0, 2 * part] = mixed[:, :512]
                out_ref[0, 2 * part + 1] = mixed[:, 512:]
            else:
                out_ref[0, part] = mixed
        return part_next, j_next

    lax.fori_loop(0, parts * count, body, (0, 0))


def head_spec(shared, *dims):
    zeros = (0,) * len(dims)
    return pl.BlockSpec((1,) + dims, lambda i, n: (int(shared),) + zeros)


def whole_spec(*dims):
    return pl.BlockSpec(dims, lambda i, n: (0,) * len(dims))


def cost(flops, moved, exps=0):
    return pl.CostEstimate(flops=int(flops), bytes_accessed=int(moved), transcendentals=int(exps))


def attend_forward(shared, seq, q, k, v, sizes, info, held):
    _, owners, _, local = q.shape
    chunks = k.shape[1]
    wide = local // 2 if shared else local
    parts = owners * wide // BQ
    pairs = parts * BQ * chunks * CH * 0.6
    shape = jax.ShapeDtypeStruct((2, owners, HD, wide), bf16)
    first = held is None
    if first:
        kernel = lambda info, q, k, v, size, *rest: fwd_kernel(shared, info, q, k, v, size, None, *rest)
    else:
        kernel = functools.partial(fwd_kernel, shared)
    return pl.pallas_call(
        kernel,
        grid_spec=pltpu.PrefetchScalarGridSpec(
            num_scalar_prefetch=1, grid=(1,),
            in_specs=[
                head_spec(shared, owners, HD, local), head_spec(shared, chunks, CH, 128), head_spec(shared, chunks, 128, CH),
                whole_spec(*sizes.shape),
            ] + ([] if first else [pl.BlockSpec(memory_space=pl.ANY)]),
            out_specs=[pl.BlockSpec((1, owners, HD, wide), lambda i, n: (seq, 0, 0, 0)), whole_spec(parts, 1, BQ)],
            scratch_shapes=[
                pltpu.VMEM((128, BQ), f32), pltpu.VMEM((2, CH, BQ), bf16), pltpu.VMEM((parts, 128, BQ), bf16),
                pltpu.VMEM((parts, 1, BQ), f32),
            ]),
        out_shape=[shape, jax.ShapeDtypeStruct((parts, 1, BQ), f32)],
        input_output_aliases={} if first else {5: 0},
        compiler_params=pltpu.CompilerParams(vmem_limit_bytes=60 << 20),
        cost_estimate=cost(pairs * 1024, chunks * CH * 512, pairs),
        name="attend_forward_shared" if shared else "attend_forward_own",
    )(*((info, q, k, v, sizes) + (() if first else (held,))))


def bwd_kernel(shared, first, info, q_ref, k_ref, v_ref, lse_ref, out_ref, gout_ref, *rest):
    rest = rest if first else rest[3 if shared else 1:]
    if shared:
        dq_ref, kept_ref, given_ref, dk_acc, dv_acc, dq_acc, qa, qat, ga, gat, pb, db = rest
    else:
        dqkv_ref, dk_acc, dv_acc, dq_acc, qa, qat, ga, gat, pb, db = rest
    count = lax.div(info[0] + (CH - 1), CH)
    chunks = k_ref.shape[1]
    parts = 2 if shared else 4
    dk_acc[...] = jnp.zeros_like(dk_acc)
    dv_acc[...] = jnp.zeros_like(dv_acc)

    def piece(ref, part):
        if shared:
            return jnp.concatenate([ref[0, 2 * part], ref[0, 2 * part + 1]], axis=1)
        return ref[0, part]

    for part in range(parts):
        q_full = with_shift(assemble(q_ref, part, shared, info[3]), lse_ref[part])
        qat[part] = q_full.astype(bf16)
        qa[part] = q_full.T.astype(bf16)
        g_t = piece(gout_ref, part)
        meet = jnp.sum(g_t.astype(f32) * piece(out_ref, part).astype(f32), axis=0, keepdims=True)
        g_full = with_shift(g_t, meet)
        gat[part] = g_full.astype(bf16)
        ga[part] = g_full.T.astype(bf16)

    def ahead(part, j, slot):
        raised = jnp.exp2(dg(qa[part], k_ref[0, j], 1, 1))
        pb[slot] = raised.astype(bf16)
        db[slot] = (raised * dg(ga[part], v_ref[0, j], 1, 0)).astype(bf16)

    ahead(0, 0, 0)

    def body(t, carry):
        part, j = carry
        now = t & 1
        part_next, j_next = step_on(part, j, count)
        dv_acc[j] += dg(gat[part], pb[now], 1, 0)[:HD]
        dk_acc[j] += dg(qat[part], db[now], 1, 0)[:HD]
        before = jnp.where(j == 0, 0.0, dq_acc[...])
        dq_acc[...] = before + dg(db[now], k_ref[0, j], 1, 0)
        ahead(jnp.minimum(part_next, parts - 1), j_next, 1 - now)

        @pl.when(j + 1 == count)
        def _():
            dq_t = (dq_acc[...] * 0.125).T[:HD].astype(bf16)
            if shared:
                for a in range(2):
                    dq_ref[0, 2 * part + a, :, :512] = dq_t[:32, a * 512:(a + 1) * 512]
                    dq_ref[0, 2 * part + a, :, 512:] = dq_t[32:, a * 512:(a + 1) * 512]
            else:
                dqkv_ref[0, part, 0] = dq_t
        return part_next, j_next

    lax.fori_loop(0, parts * count, body, (0, 0))
    for j in range(chunks):
        for owner in range(4):
            cols = slice(owner * 128, (owner + 1) * 128)
            dk_wide, dv_wide = dk_acc[j, :, cols] * LN2, dv_acc[j, :, cols]
            dk, dv = dk_wide.astype(bf16), dv_wide.astype(bf16)
            if shared:
                here = info[3] == 0
                kept_ref[0, owner, :, j * 128:(j + 1) * 128] = jnp.where(here, dk_wide, dv_wide).astype(bf16)
                given_ref[0, owner, :, j * 128:(j + 1) * 128] = jnp.where(here, dv_wide, dk_wide).astype(bf16)
            else:
                dqkv_ref[0, owner, 1, :, j * 128:(j + 1) * 128] = dk
                dqkv_ref[0, owner, 2, :, j * 128:(j + 1) * 128] = dv


def attend_backward(shared, seq, q, k, v, lse, out, g_out, info, held):
    _, owners, _, local = q.shape
    chunks = k.shape[1]
    wide = out.shape[3]
    parts = owners * wide // BQ
    pairs = parts * BQ * chunks * CH * 0.6
    shape = jax.ShapeDtypeStruct
    first = held is None
    if shared:
        out_specs = [pl.BlockSpec((1, owners, rows, local), lambda i, n: (seq, 0, 0, 0)) for rows in (32, HD, HD)]
        out_shape = [shape((2, owners, rows, local), bf16) for rows in (32, HD, HD)]
    else:
        out_specs = [pl.BlockSpec((1, owners, 3, HD, local), lambda i, n: (seq, 0, 0, 0, 0))]
        out_shape = [shape((2, owners, 3, HD, local), bf16)]
    kept = () if first else tuple(held)
    of_seq = pl.BlockSpec((1, owners, HD, wide), lambda i, n: (seq, 0, 0, 0))
    return pl.pallas_call(
        functools.partial(bwd_kernel, shared, first),
        grid_spec=pltpu.PrefetchScalarGridSpec(
            num_scalar_prefetch=1, grid=(1,),
            in_specs=[
                head_spec(shared, owners, HD, local), head_spec(shared, chunks, CH, 128), head_spec(shared, chunks, 128, CH),
                whole_spec(parts, 1, BQ), of_seq, of_seq,
            ] + [pl.BlockSpec(memory_space=pl.ANY)] * len(kept),
            out_specs=out_specs,
            scratch_shapes=[
                pltpu.VMEM((chunks, HD, CH), f32), pltpu.VMEM((chunks, HD, CH), f32), pltpu.VMEM((BQ, 128), f32),
                pltpu.VMEM((parts, BQ, 128), bf16), pltpu.VMEM((parts, 128, BQ), bf16),
                pltpu.VMEM((parts, BQ, 128), bf16), pltpu.VMEM((parts, 128, BQ), bf16),
                pltpu.VMEM((2, BQ, CH), bf16), pltpu.VMEM((2, BQ, CH), bf16),
            ]),
        out_shape=out_shape,
        input_output_aliases={7 + n: n for n in range(len(kept))},
        compiler_params=pltpu.CompilerParams(vmem_limit_bytes=60 << 20),
        cost_estimate=cost(pairs * 100, chunks * CH * 2048),
        name="attend_backward_shared" if shared else "attend_backward_own",
    )(info, q, k, v, lse, out, g_out, *kept)


def gelu_pair(u):
    half = 0.5 * (1.0 + lax.erf(u * 0.7071067811865476))
    return u * half, half + u * (0.3989422804014327 * jnp.exp2(u * u * (-0.5 * LOG2E)))


def norm_stats(v):
    mean = jnp.mean(v, axis=-1, keepdims=True)
    centred = v - mean
    inverse = lax.rsqrt(jnp.mean(centred * centred, axis=-1, keepdims=True) + 1e-12)
    return centred * inverse, inverse


def norm_back(grad, xhat, inverse, gain):
    g = grad * gain
    return (g - jnp.mean(g, axis=-1, keepdims=True) - xhat * jnp.mean(g * xhat, axis=-1, keepdims=True)) * inverse


def weight_part(ref, first, rows):
    part = ref[:, first:first + rows, :]
    return part.reshape(part.shape[0] * rows, part.shape[2])


def ffn_kernel(spans, info, x_ref, own_ref, sh_ref, cot_ref, w_ref, bin_ref, vec_ref,
               act_out, resid_out, gown_out, gsh_out, active_out, dinner_out, normed_out, douter_out, dbranch_out,
               vec_sum, bin_sum, slope, row_block):
    step = pl.program_id(0)
    width = x_ref.shape[-1]
    load_rows(row_block, x_ref, spans, info[1])
    rows = row_block[...].astype(f32)
    mixed_t = jnp.concatenate(
        [part for p in range(4) for part in (own_ref[p, 0], sh_ref[p, 0], own_ref[p, 1])], axis=0)
    vec = vec_ref[...]
    branch = dg(mixed_t, weight_part(w_ref, 768, 96), 0, 0) + vec[0:1]
    xhat1, inv1 = norm_stats(rows + branch)
    normed = xhat1 * vec[1:2] + vec[2:3]
    low = normed.astype(bf16)
    normed_out[...] = low
    outer = normed + vec[3:4]
    for n in range(4):
        cols = slice(n * 768, (n + 1) * 768)
        inner = dg(low, weight_part(w_ref, 384 + 96 * n, 96), 1, 0) + bin_ref[:, cols]
        value, bend = gelu_pair(inner)
        active_out[:, cols] = value.astype(bf16)
        slope[:, cols] = bend.astype(bf16)
    outer = outer + dg(active_out[...], weight_part(w_ref, 0, 384), 1, 0)
    xhat2, inv2 = norm_stats(outer)
    act_out[...] = (xhat2 * vec[4:5] + vec[5:6]).astype(bf16)
    cot = cot_ref[...].astype(f32)
    d2 = norm_back(cot, xhat2, inv2, vec[4:5])
    d_outer = d2.astype(bf16)
    douter_out[...] = d_outer
    d_normed = d2
    sums_in = []
    for n in range(4):
        cols = slice(n * 768, (n + 1) * 768)
        d_active = dg(d_outer, weight_part(w_ref.at[2 * n:2 * n + 2], 0, 384), 1, 1)
        d_inner = (d_active * slope[:, cols].astype(f32)).astype(bf16)
        dinner_out[:, cols] = d_inner
        sums_in.append(jnp.sum(d_inner.astype(f32), axis=0, keepdims=True))
        d_normed = d_normed + dg(d_inner, weight_part(w_ref, 384 + 96 * n, 96), 1, 1)
    d1 = norm_back(d_normed, xhat1, inv1, vec[1:2])
    resid_out[...] = d1
    d_branch = d1.astype(bf16)
    dbranch_out[...] = d_branch
    g_t = dg(weight_part(w_ref, 768, 96), d_branch, 1, 1).astype(bf16)
    for p in range(4):
        gown_out[p, 0] = g_t[192 * p:192 * p + 64]
        gsh_out[p, 0] = g_t[192 * p + 64:192 * p + 128]
        gown_out[p, 1] = g_t[192 * p + 128:192 * p + 192]
    total = lambda a: jnp.sum(a, axis=0, keepdims=True)
    sums = jnp.concatenate([
        total(d_branch.astype(f32)), total(d_normed * xhat1), total(d_normed),
        total(d_outer.astype(f32)), total(cot * xhat2), total(cot), jnp.zeros((2, width), f32)], axis=0)

    @pl.when(step == 0)
    def _():
        vec_sum[...] = sums
        for n in range(4):
            bin_sum[:, n * 768:(n + 1) * 768] = sums_in[n]

    @pl.when(step > 0)
    def _():
        vec_sum[...] += sums
        for n in range(4):
            bin_sum[:, n * 768:(n + 1) * 768] += sums_in[n]


def feed_forward(rows_in, own, sh, cotangent, weights, inner_bias, vectors, info):
    _, _, _, stretch, width = rows_in.shape
    local = cotangent.shape[0]
    spans = RB // (2 * stretch)
    steps = local // RB
    half_steps = steps // 2
    wide = inner_bias.shape[1]
    rows = lambda n: pl.BlockSpec((RB, n), lambda r, a: (r, 0))
    fixed = lambda *dims: pl.BlockSpec(dims, lambda r, a: (0,) * len(dims))
    own_spec = pl.BlockSpec((4, 2, HD, RB), lambda r, a: (0, 0, 0, r))
    sh_spec = pl.BlockSpec((4, 1, HD, RB), lambda r, a: (0, r // half_steps, 0, r % half_steps))
    shape = jax.ShapeDtypeStruct
    return pl.pallas_call(
        functools.partial(ffn_kernel, spans),
        grid_spec=pltpu.PrefetchScalarGridSpec(
            num_scalar_prefetch=1, grid=(steps,),
            in_specs=[
                pl.BlockSpec((1, 2, spans, stretch, width), lambda r, a: (0, 0, r, 0, 0)),
                own_spec, sh_spec, rows(width),
                pl.BlockSpec(weights.shape, lambda r, a: (0, 0, 0), pipeline_mode=pl.Buffered(1)),
                fixed(1, wide), fixed(8, width),
            ],
            out_specs=[
                rows(width), rows(width), own_spec, sh_spec, rows(wide), rows(wide), rows(width), rows(width), rows(width),
                fixed(8, width), fixed(1, wide),
            ],
            scratch_shapes=[pltpu.VMEM((RB, wide), bf16), pltpu.VMEM((RB, width), bf16)]),
        out_shape=[
            shape((local, width), bf16), shape((local, width), f32), shape(own.shape, bf16), shape(sh.shape, bf16),
            shape((local, wide), bf16), shape((local, wide), bf16), shape((local, width), bf16),
            shape((local, width), bf16), shape((local, width), bf16), shape((8, width), f32), shape((1, wide), f32),
        ],
        compiler_params=pltpu.CompilerParams(vmem_limit_bytes=60 << 20),
        name="feed_forward",
        cost_estimate=cost(local * width * (width + 2 * wide) * 4, local * wide * 20),
    )(info, rows_in, own, sh, cotangent, weights, inner_bias, vectors)


def outer_grad_kernel(scale, active_ref, douter_ref, out_ref):
    made = (dg(active_ref[...], douter_ref[...], 0, 0) * scale).astype(bf16)
    out_ref[...] = made.reshape(out_ref.shape)


def inner_grad_kernel(scale, packed_ref, normed_ref, dinner_ref, own_ref, sh_ref, dbranch_ref, out_ref):
    step = pl.program_id(0)

    @pl.when(step < 4)
    def _():
        out_ref[...] = (dg(normed_ref[...], dinner_ref[...], 0, 0) * scale).astype(bf16).reshape(out_ref.shape)

    @pl.when(step == 4)
    def _():
        mixed_t = jnp.concatenate([
            part for p in range(4)
            for part in (own_ref[p, 0], jnp.concatenate([sh_ref[p, 0], sh_ref[p, 1]], axis=1), own_ref[p, 1])], axis=0)
        out_ref[...] = (dg(mixed_t, dbranch_ref[...], 1, 0) * scale).astype(bf16).reshape(out_ref.shape)


def weight_grads(scale, active, d_outer, normed, d_inner, own, sh, d_branch):
    local, wide = active.shape
    width = normed.shape[1]
    packed = pl.pallas_call(
        functools.partial(outer_grad_kernel, scale), grid=(4,),
        in_specs=[pl.BlockSpec((local, width), lambda m: (0, m)), pl.BlockSpec((local, width), lambda m: (0, 0))],
        out_specs=pl.BlockSpec((2, 384, width), lambda m: (m, 0, 0)),
        out_shape=jax.ShapeDtypeStruct((8, 896, width), bf16),
        compiler_params=pltpu.CompilerParams(vmem_limit_bytes=60 << 20), name="outer_grad",
        cost_estimate=cost(2 * local * wide * width, 2 * wide * (local + width)),
    )(active, d_outer)
    fixed = lambda a: pl.BlockSpec(a.shape, lambda n: (0,) * a.ndim)
    return pl.pallas_call(
        functools.partial(inner_grad_kernel, scale), grid=(5,),
        in_specs=[
            pl.BlockSpec(memory_space=pl.ANY), fixed(normed),
            pl.BlockSpec((local, width), lambda n: (0, jnp.minimum(n, 3))), fixed(own), fixed(sh), fixed(d_branch)],
        out_specs=pl.BlockSpec((8, 96, width), lambda n: (0, 4 + n, 0)),
        out_shape=jax.ShapeDtypeStruct((8, 896, width), bf16), input_output_aliases={0: 0},
        compiler_params=pltpu.CompilerParams(vmem_limit_bytes=60 << 20), name="inner_grad",
        cost_estimate=cost(2 * local * (wide + width) * width, 2 * (wide + width) * (local + width)),
    )(packed, normed, d_inner, own, sh, d_branch)


def head_grad_kernel(scale, spans, info, *refs):
    x_refs, (own_ref, dq_ref, kept_ref, given_ref, out_ref, bias_out, acc, bias_acc, rows) = refs[:4], refs[4:]
    seq, away, half = pl.program_id(0), pl.program_id(1), pl.program_id(3)
    last = (seq == 1) & (away == 1) & (pl.program_id(2) == 1) & (half == pl.num_programs(3) - 1)
    for n in range(4):
        @pl.when(seq * 2 + away == n)
        def _(n=n):
            load_rows(rows, x_refs[n], spans, info[1])
    dq_t = jnp.where(half == info[3], jnp.concatenate([dq_ref[0, 0, :, :512], dq_ref[0, 0, :, 512:]], axis=0).astype(f32), 0.0)
    kept, given = kept_ref[0, 0].astype(f32), given_ref[0, 0].astype(f32)
    here = info[3] == 0
    d_t = jnp.concatenate([
        own_ref[0, 0, 0], dq_t.astype(bf16), own_ref[0, 0, 1], jnp.where(here, kept, given).astype(bf16),
        own_ref[0, 0, 2], jnp.where(here, given, kept).astype(bf16)], axis=0)

    @pl.when((seq == 0) & (away == 0) & (pl.program_id(2) == 0) & (half == 0))
    def _():
        acc[...] = jnp.zeros_like(acc)
        bias_acc[...] = jnp.zeros_like(bias_acc)
    acc[...] += dg(d_t, rows[...], 1, 0)
    bias_acc[...] += dg(jnp.ones((8, d_t.shape[1]), bf16), d_t, 1, 1)

    @pl.when(last)
    def _():
        out_ref[...] = (acc[...] * scale).T.astype(bf16)
        bias_out[...] = bias_acc[...] * scale


def head_grads(scale, sources, dqkv_own, dq_sh, kept, given, info):
    _, _, zs, stretch, width = sources[0].shape
    local = 2 * zs * stretch
    spans = 512 // (2 * stretch)
    halves = local // 512

    def source_spec(n):
        def index(s, a, o, h, i):
            now = 2 * s + a
            across = jnp.where(now == n, o, jnp.where(now < n, 0, 1))
            return (across, 0, jnp.where(now == n, h, jnp.where(now < n, 0, halves - 1)), 0, 0)
        return pl.BlockSpec((1, 2, spans, stretch, width), index)
    return pl.pallas_call(
        functools.partial(head_grad_kernel, scale, spans),
        grid_spec=pltpu.PrefetchScalarGridSpec(
            num_scalar_prefetch=1, grid=(2, 2, 2, halves),
            in_specs=[source_spec(n) for n in range(4)] + [
                pl.BlockSpec((1, 1, 3, HD, 512), lambda s, a, o, h, i: (s, owner_of(a, o, i), 0, 0, h)),
                pl.BlockSpec((1, 1, 32, local), lambda s, a, o, h, i: (s, owner_of(a, o, i), 0, 0)),
            ] + [pl.BlockSpec((1, 1, HD, 512), lambda s, a, o, h, i: (s, owner_of(a, o, i), 0, h))] * 2,
            out_specs=[pl.BlockSpec((width, 384), lambda s, a, o, h, i: (0, 0)), pl.BlockSpec((8, 384), lambda s, a, o, h, i: (0, 0))],
            scratch_shapes=[pltpu.VMEM((384, width), f32), pltpu.VMEM((8, 384), f32), pltpu.VMEM((512, width), bf16)]),
        out_shape=[jax.ShapeDtypeStruct((width, 384), bf16), jax.ShapeDtypeStruct((8, 384), f32)],
        compiler_params=pltpu.CompilerParams(vmem_limit_bytes=60 << 20), name="head_grads",
        cost_estimate=cost(8 * local * 768 * width, 8 * local * width * 2),
    )(info, *sources, dqkv_own, dq_sh, kept, given)


def token_grad_kernel(own_ref, low_ref, high_ref, dkv_ref, w_ref, resid_ref, out_ref):
    total = resid_ref[...]
    for kind in range(3):
        made = []
        for p in range(4):
            if kind == 0:
                middle = jnp.concatenate([low_ref[p, 0], high_ref[p, 0]], axis=0)
            else:
                middle = jnp.concatenate([dkv_ref[p, kind - 1, n] for n in range(2)], axis=0)
            made += [own_ref[p, 0, kind], middle, own_ref[p, 1, kind]]
        total = total + dg(jnp.concatenate(made, axis=0), weight_part(w_ref, 96 * kind, 96), 0, 1)
    out_ref[...] = total.astype(bf16)


def token_grad(own, shared, weights, resid):
    local, width = resid.shape
    steps = local // RB
    half_steps = steps // 2
    rows = pl.BlockSpec((RB, width), lambda r: (r, 0))
    return pl.pallas_call(
        token_grad_kernel, grid=(steps,),
        in_specs=[
            pl.BlockSpec((4, 2, 3, HD, RB), lambda r: (0, 0, 0, 0, r)),
            pl.BlockSpec((4, 1, None, 32, RB), lambda r: (0, r // half_steps, 2, 0, r % half_steps)),
            pl.BlockSpec((4, 1, None, 32, RB), lambda r: (0, r // half_steps, 2, 0, half_steps + r % half_steps)),
            pl.BlockSpec((4, 2, 2, 32, RB), lambda r: (0, 0, 0, 0, r)),
            pl.BlockSpec(weights.shape, lambda r: (0, 0, 0)), rows],
        out_specs=rows, out_shape=jax.ShapeDtypeStruct((local, width), bf16),
        compiler_params=pltpu.CompilerParams(vmem_limit_bytes=60 << 20), name="token_grad",
        cost_estimate=cost(local * width * width * 6, local * width * 12),
    )(own, shared, shared, shared, weights, resid)


SWAP = [(0, 1), (1, 0)]
def settle_kernel(*refs):
    refs[-1][...] = sum(ref[...].astype(f32) for ref in refs[:-2]).astype(bf16)


def settle(parts, after):
    whole = pl.BlockSpec(memory_space=pltpu.VMEM)
    return pl.pallas_call(
        settle_kernel, in_specs=[whole] * len(parts) + [pl.BlockSpec(memory_space=pl.ANY)], out_specs=whole,
        out_shape=jax.ShapeDtypeStruct(parts[0].shape, bf16), name="settle",
        cost_estimate=cost(5e10, 1e8),
    )(*parts, after)


PAIR = ("x", "y", "c")
ALL = ("z", "x", "y", "c")
SHARD = ("z", "x")


def canonical(packed, shards):
    if shards == 8:
        return packed
    width = packed.shape[2]
    per, keep = 96 * 8 // shards, shards // 8
    outer = packed[:, :4 * per].reshape(8, 384, width)
    inner = packed[:, 4 * per:8 * per].reshape(8, keep, 4, per, width).transpose(0, 2, 1, 3, 4).reshape(8, 384, width)
    output = packed[:, 8 * per:9 * per].reshape(8, 96, width)
    return jnp.concatenate([outer, inner, output, jnp.zeros((8, 32, width), packed.dtype)], axis=1)


def from_canonical(packed, last, shards):
    width = packed.shape[2]
    if shards == 8:
        return packed.at[:, 864:].set(jnp.broadcast_to(last[None], (8, 32, width)))
    per, keep = 96 * 8 // shards, shards // 8
    outer = packed[:, :384].reshape(shards, 4 * per, width)
    inner = packed[:, 384:768].reshape(8, 4, keep, per, width).transpose(0, 2, 1, 3, 4).reshape(shards, 4 * per, width)
    output = packed[:, 768:864].reshape(shards, per, width)
    return jnp.concatenate([outer, inner, output, jnp.broadcast_to(last[None], (shards, 32, width))], axis=1)


def canonical_heads(packed, shards, parts):
    if shards == 8:
        return packed
    width = packed.shape[2]
    per = 96 * 8 // shards
    made = [packed[:, k * per:(k + 1) * per].reshape(8, 96, width) for k in range(parts)]
    return jnp.concatenate(made + [jnp.zeros((8, 32, width), packed.dtype)], axis=1)


def quarter(rows):
    place = lax.axis_index("y") * 2 + lax.axis_index("c")
    part = rows.shape[0] // 4
    return lax.dynamic_slice_in_dim(rows, place * part, part)


def flipped(array, axis, here):
    return jnp.where(here == 0, array, jnp.flip(array, axis))


def body(tokens, lengths, deal_order, w_query, w_key, w_value, w_output, b_query, b_value, b_output,
         ln1_gain, ln1_shift, w_inner, b_inner, w_outer, b_outer, ln2_gain, ln2_shift, cotangent):
    tie = lax.optimization_barrier
    zs = lax.axis_size("z")
    shards = 2 * zs
    scale = 1.0 / (shards * 4)
    seq_count, _, stretch, width = tokens.shape
    per = w_query.shape[0]
    half = zs // 2
    x, y, c = lax.axis_index("x"), lax.axis_index("y"), lax.axis_index("c")

    def deal(ordered):
        return lax.all_to_all(ordered, "z", split_axis=0, concat_axis=0, tiled=True)

    def corner(across, along):
        return [lax.ppermute(across[:half], "y", SWAP), lax.ppermute(along[half:], "x", SWAP)]

    def this_core(own, across, along, corner):
        return jnp.concatenate([own, across, along] + corner, axis=0).reshape(2, 2, zs, stretch, width)

    ordered_a = jnp.take(tokens[:, 0], deal_order[0::2], axis=0)
    first_own = deal(ordered_a)
    (_, tokens, w_query, w_key, w_value, b_query, b_value, w_outer, w_inner, w_output, b_inner, deal_order) = tie(
        (ordered_a, tokens, w_query, w_key, w_value, b_query, b_value, w_outer, w_inner, w_output, b_inner, deal_order))
    ordered_b = jnp.take(tokens[:, 0], deal_order[1::2], axis=0)

    def head_columns(matrix):
        heads = matrix.reshape(per, 2, 2, 3, HD)
        mine = lax.dynamic_index_in_dim(heads, y, axis=2, keepdims=False)
        own = lax.dynamic_index_in_dim(mine, 2 * c, axis=2, keepdims=False)
        return [own, mine[:, :, 1]]
    pad = lambda v: jnp.pad(v, (0, width - v.shape[0]))[None]
    columns = jnp.concatenate(
        [col for matrix in (w_query, w_key, w_value) for col in head_columns(matrix)], axis=2).reshape(per, width)
    head_pack = jnp.concatenate([columns, pad(b_query), pad(b_value), jnp.zeros((14, width), bf16)], axis=0)
    vectors = (b_output, ln1_gain, ln1_shift, b_outer, ln2_gain, ln2_shift)
    layer_pack = jnp.concatenate(
        [w_outer] + [w_inner[:, n * width:(n + 1) * width] for n in range(4)] + [w_output]
        + [pad(b_inner)] + [pad(v) for v in vectors] + [jnp.zeros((25, width), bf16)], axis=0)
    layer_quarter = quarter(layer_pack)
    back_quarter = quarter(jnp.concatenate([w_query, w_key, w_value, jnp.zeros((32, width), bf16)], axis=0))
    first_own, ordered_b, head_pack, layer_quarter, back_quarter = tie(
        (first_own, ordered_b, head_pack, layer_quarter, back_quarter))
    head_all = lax.all_gather(head_pack, SHARD, axis=0, tiled=False)
    head_weight = canonical_heads(head_all, shards, 1)

    def head_bias(row):
        heads = head_all[:, per + row, :per].reshape(2, 2, 3, HD)
        mine = lax.dynamic_slice(heads, (x, y, 0, 0), (1, 1, 3, HD))[0, 0]
        return [lax.dynamic_index_in_dim(mine, 2 * c, axis=0, keepdims=False), mine[1]]
    bias_row = jnp.concatenate(head_bias(0) + [jnp.zeros((2 * HD,), bf16)] + head_bias(1)).astype(f32)[None]

    across_a, along_a = lax.ppermute(first_own, "x", SWAP), lax.ppermute(first_own, "y", SWAP)
    second_own = deal(ordered_b)
    across_a, along_a, second_own = tie((across_a, along_a, second_own))
    corner_a = corner(across_a, along_a)
    second_own, *corner_a = tie((second_own, *corner_a))
    near_a = this_core(first_own, across_a, along_a, corner_a)
    far_a = lax.ppermute(near_a, "c", SWAP)
    across_b, along_b = lax.ppermute(second_own, "x", SWAP), lax.ppermute(second_own, "y", SWAP)
    far_a, across_b, along_b = tie((far_a, across_b, along_b))
    corner_b = corner(across_b, along_b)

    layer_all = lax.all_gather(layer_quarter, ALL, axis=0, tiled=True).reshape(shards, 9 * per + 32, width)
    layer_weights = canonical(layer_all, shards)
    inner_bias = layer_all[:, 9 * per, :4 * per].reshape(1, 4 * width).astype(f32)
    vector_rows = jnp.concatenate(
        [layer_all[:, 9 * per + 1 + n, :per].reshape(1, width) for n in range(6)] + [jnp.zeros((2, width), bf16)],
        axis=0).astype(f32)
    back_all = lax.all_gather(back_quarter, ALL, axis=0, tiled=True).reshape(shards, 3 * per + 32, width)

    slots = lax.dynamic_slice_in_dim(deal_order, lax.axis_index("z") * 2, 2)
    matches = slots[:, None] == jnp.arange(seq_count, dtype=jnp.int32)[None, :]
    lens = jnp.sum(jnp.where(matches, lengths[None, :], 0), axis=1).astype(jnp.int32)
    infos = [jnp.stack([lens[n], x, y, c]).astype(jnp.int32) for n in range(2)]

    def swap(array):
        flat = array.reshape((8,) + array.shape[2:])
        return lax.all_to_all(flat, PAIR, split_axis=0, concat_axis=0, tiled=True)

    def to_tokens(array):
        return swap(array).reshape((4, 2) + array.shape[2:])

    def to_heads(array):
        return swap(array).reshape((2, 4) + array.shape[2:])

    heads_a = project(near_a, far_a, head_weight, bias_row, infos[0])
    heads_a, *corner_b = tie((heads_a, *corner_b))
    near_b = this_core(second_own, across_b, along_b, corner_b)
    far_b = lax.ppermute(near_b, "c", SWAP)
    own_first, lse_own_a = attend_forward(False, 0, *heads_a, infos[0], None)
    own_first, far_b = tie((own_first, far_b))
    heads_b = project(near_b, far_b, head_weight, bias_row, infos[1])
    own, lse_own_b = attend_forward(False, 1, *heads_b, infos[1], own_first)
    own_t = to_tokens(own)
    own, info_a, info_b = tie((own, *infos))
    sh_first, lse_sh_a = attend_forward(True, 0, *heads_a, info_a, None)
    sh, lse_sh_b = attend_forward(True, 1, *heads_b, info_b, sh_first)
    sh_sent, own_t = tie((sh, own_t))
    sh_t = to_tokens(sh_sent)
    mine_rows = jnp.where(x == 0, jnp.stack([first_own, across_a]), jnp.stack([second_own, across_b]))[None]

    (act, resid, g_own, g_sh, active, d_inner, normed, d_outer, d_branch, vec_sums, bin_sums) = feed_forward(
        mine_rows, own_t, sh_t, cotangent.reshape(-1, width), layer_weights, inner_bias, vector_rows, infos[0])
    g_own_h, g_sh_h = to_heads(g_own), to_heads(g_sh)
    active, back_all = tie((active, back_all))
    packed = weight_grads(scale, active, d_outer, normed, d_inner, own_t, sh_t, d_branch)
    sums = jnp.concatenate([bin_sums.reshape(4, width), vec_sums, jnp.zeros((20, width), f32)], axis=0) * scale
    ready = from_canonical(packed, sums.astype(bf16), shards)
    ready, g_own_h = tie((ready, g_own_h))
    back_weights = canonical_heads(back_all, shards, 3)
    layer_part = lax.psum_scatter(ready.reshape(-1, width), ("z", "x", "c"), scatter_dimension=0, tiled=True)

    qkv_a, qkv_b = heads_a[:3], heads_b[:3]
    first = attend_backward(False, 0, *qkv_a, lse_own_a, own, g_own_h, infos[0], None)
    dqkv_own, = attend_backward(False, 1, *qkv_b, lse_own_b, own, g_own_h, infos[1], first)
    back_own = to_tokens(dqkv_own)
    dqkv_own, info_a, info_b = tie((dqkv_own, *infos))
    first = attend_backward(True, 0, *qkv_a, lse_sh_a, sh, g_sh_h, info_a, None)
    dq_sh, kept, given = attend_backward(True, 1, *qkv_b, lse_sh_b, sh, g_sh_h, info_b, first)
    taken = lax.ppermute(given, "c", SWAP)
    shared_out = jnp.concatenate([(kept.astype(f32) + taken.astype(f32)).astype(bf16), dq_sh], axis=2)
    shared_out, back_own, dqkv_own = tie((shared_out, back_own, dqkv_own))
    back_shared = to_tokens(shared_out.reshape(2, 4, 3, 32, -1))
    d_heads, d_bias = head_grads(scale, (near_a, far_a, near_b, far_b), dqkv_own, dq_sh, kept, given, infos[0])

    head_ready = jnp.concatenate([
        d_heads.reshape(zs, 2, per, 384),
        jnp.broadcast_to(d_bias[:1].astype(bf16)[None, None], (zs, 2, 16, 384))], axis=2)
    head_ready, _ = tie((head_ready, back_shared))
    d_rows = token_grad(back_own, back_shared, back_weights, resid)
    if zs == 4:
        group = lax.axis_index("z")
        parts = [lax.dynamic_index_in_dim(head_ready, (group + k) % zs, axis=0, keepdims=False) for k in range(zs)]
        parts = parts[:1] + [
            lax.ppermute(parts[k], "z", [(i, (i + k) % zs) for i in range(zs)]) for k in range(1, zs)]
        head_sum = settle(parts, d_rows)
    else:
        head_sum = lax.psum_scatter(
            head_ready.reshape(-1, 384), "z", scatter_dimension=0, tiled=True).reshape(2, per + 16, 384)
    layer_part, _ = tie((layer_part, head_sum))
    returned = lax.all_to_all(
        d_rows.reshape(shards, stretch, width), SHARD, split_axis=0, concat_axis=0, tiled=True)

    def apart(array, bits):
        return lax.ppermute(array, PAIR, [(i, i ^ bits) for i in range(8)]) if bits else array

    halves = [lax.dynamic_index_in_dim(head_sum, x ^ k, axis=0, keepdims=False) for k in range(2)]
    head_eight = jnp.stack([apart(halves[bits >> 2], bits) for bits in range(8)]).reshape(2, 2, 2, per + 16, 6, HD)
    cores = flipped(flipped(flipped(head_eight, 0, x), 1, y), 2, c).astype(f32)

    def full(kind):
        joined = jnp.stack([cores[:, :, 0, :, 2 * kind], cores[:, :, 0, :, 2 * kind + 1] + cores[:, :, 1, :, 2 * kind + 1],
                            cores[:, :, 1, :, 2 * kind]], axis=2)
        return joined.transpose(3, 0, 1, 2, 4).reshape(per + 16, width)
    d_wq, d_wk, d_wv = (full(kind) for kind in range(3))
    place = lax.axis_index("z") * 2 + x
    own_slice = lambda row, n: lax.dynamic_slice_in_dim(row, place * n, n)
    d_bq, d_bv = own_slice(d_wq[per], per), own_slice(d_wv[per], per)
    d_wq, d_wk, d_wv = d_wq[:per], d_wk[:per], d_wv[:per]

    near_sum = layer_part.astype(f32) + apart(layer_part, 2).astype(f32)
    far_sum = apart(layer_part, 1).astype(f32) + apart(layer_part, 3).astype(f32)
    layer_grads = flipped(jnp.stack([near_sum, far_sum]), 0, c).reshape(9 * per + 32, width)
    d_wouter = layer_grads[:4 * per]
    d_winner = jnp.concatenate([layer_grads[(4 + n) * per:(5 + n) * per] for n in range(4)], axis=1)
    d_woutput = layer_grads[8 * per:9 * per]
    d_binner = own_slice(layer_grads[9 * per:9 * per + 4].reshape(-1), 4 * per)
    d_bo, d_g1, d_s1, d_bout, d_g2, d_s2 = (own_slice(layer_grads[9 * per + 4 + n], per) for n in range(6))
    small = (d_bq, d_bv, d_binner, d_bo, d_g1, d_s1, d_bout, d_g2, d_s2)
    returned = tie((returned, d_wouter, d_winner, d_woutput, d_wq, d_wk, d_wv) + small)[0]
    steps = jnp.arange(seq_count, dtype=jnp.int32)
    slot_of = jnp.sum(jnp.where(deal_order[:, None] == steps[None, :], steps[:, None], 0), axis=0)
    d_tokens = jnp.take(returned, slot_of, axis=0)[:, None]
    return (act.reshape(1, shards, stretch, width), d_tokens, d_wq, d_wk, d_wv, d_woutput, d_bq, d_bv, d_bo,
            d_g1, d_s1, d_winner, d_binner, d_wouter, d_bout, d_g2, d_s2)


def solution(mesh):
    shards, splits = mesh.devices.shape
    fine = Mesh(mesh.devices.reshape(shards // 2, 2, splits // 2, 2), ALL)
    S, Q = SHARD, ("y", "c")
    row, mat = P(S), P(S, None)
    return jax.shard_map(
        body, mesh=fine,
        in_specs=(P(None, S, Q, None), P(), P(), mat, mat, mat, mat, row, row, row, row, row, mat, row, mat, row, row, row,
                  P(S, None, Q, None)),
        out_specs=(P(S, None, Q, None), P(None, S, Q, None), mat, mat, mat, mat, row, row, row, row, row, mat, row, mat,
                   row, row, row),
        check_vma=False)
```

```python
import functools, math
import jax
import jax.numpy as jnp
from jax import lax
from jax.experimental import pallas as pl
from jax.experimental.pallas import tpu as pltpu
from jax.sharding import Mesh, PartitionSpec as P

f32, bf16 = jnp.float32, jnp.bfloat16
LOG2E = 1.4426950408889634
LN2 = 0.6931471805599453
CH = 512
BQ = 1024
RB = 256
HD = 64
FAR = -1.0e30

def dg(a, b, ca, cb):
    return lax.dot_general(a, b, (((ca,), (cb,)), ((), ())), preferred_element_type=f32)


def three_parts(row):
    hi = row.astype(bf16).astype(f32)
    rest = row - hi
    mid = rest.astype(bf16).astype(f32)
    return hi, mid, rest - mid


def with_shift(top, shift):
    hi, mid, low = three_parts(shift)
    row = lax.broadcasted_iota(jnp.int32, (HD, top.shape[1]), 0)
    tail = jnp.where(row == 0, -hi, jnp.where(row == 1, -mid, jnp.where(row == 2, -low, jnp.where(row == 3, 1.0, 0.0))))
    return jnp.concatenate([top.astype(f32), tail], axis=0)


def load_rows(rows, ref, spans, x):
    stretch = ref.shape[3]
    for z in range(spans):
        for a in range(2):
            at = (2 * z + a) * stretch
            rows[at:at + stretch] = ref[0, a ^ x, z]


def qkv_kernel(stretch, spans, info, near_ref, far_ref, w_ref, b_ref, q_out, k_out, v_out, size_out, rows):
    away, half = pl.program_id(0), pl.program_id(2)
    owner = ((pl.program_id(1) ^ info[2]) << 1) | (away ^ info[3])

    @pl.when(away == 0)
    def _():
        load_rows(rows, near_ref, spans, info[1])

    @pl.when(away == 1)
    def _():
        load_rows(rows, far_ref, spans, info[1])
    weight = w_ref[...].reshape(rows.shape[1], 384)
    made = dg(rows[...], weight, 1, 0) + b_ref[...]
    count = rows.shape[0]
    q_t = (made[:, :128] * (LOG2E / 8.0)).T
    q_out[0, 0] = q_t[:HD].astype(bf16)
    q_out[1, 0] = q_t[HD:].astype(bf16)
    lane = lax.broadcasted_iota(jnp.int32, (count, 128), 1)
    row = lax.broadcasted_iota(jnp.int32, (count, 128), 0) + half * count
    shift = int(math.log2(stretch))
    position = lax.shift_left(lax.shift_right_logical(row, shift), shift + 2) + owner * stretch + (row & (stretch - 1))
    hidden = jnp.where(position < info[0], 0.0, FAR)
    tail = jnp.where(lane == HD + 3, hidden, jnp.where(lane < HD + 3, 1.0, 0.0))
    keys = made[:, 128:256]
    picks = lax.broadcasted_iota(jnp.int32, (128, 128), 0) // HD == lax.broadcasted_iota(jnp.int32, (128, 128), 1)
    sizes = dg((keys * keys).astype(bf16), jnp.where(picks, 1.0, 0.0).astype(bf16), 1, 0)
    size_out[0, 0] = jnp.max(sizes, axis=0, keepdims=True)
    for head in range(2):
        turned = keys if head == 0 else pltpu.roll(keys, HD, 1)
        full = jnp.where(lane < HD, turned, tail).astype(bf16)
        for j in range(count // 128):
            k_out[head, j] = full[j * 128:(j + 1) * 128]
    v_t = made[:, 256:384].T
    ones = jnp.where(lax.broadcasted_iota(jnp.int32, (HD, count), 0) < 3, 1.0, 0.0)
    for head in range(2):
        full = jnp.concatenate([v_t[head * HD:(head + 1) * HD], ones], axis=0).astype(bf16)
        for j in range(count // 128):
            v_out[head, j] = full[:, j * 128:(j + 1) * 128]


def owner_of(away, across, info):
    return ((across ^ info[2]) << 1) | (away ^ info[3])


def project(near, far, weight, bias, info):
    _, _, zs, stretch, width = near.shape
    local = 2 * zs * stretch
    spans = 512 // (2 * stretch)
    halves = local // 512
    chunks = 4 * local // CH
    per = chunks // halves
    block = (1, 2, spans, stretch, width)
    return pl.pallas_call(
        functools.partial(qkv_kernel, stretch, spans),
        grid_spec=pltpu.PrefetchScalarGridSpec(
            num_scalar_prefetch=1, grid=(2, 2, halves),
            in_specs=[
                pl.BlockSpec(block, lambda a, o, h, n: (jnp.where(a == 0, o, 1), 0, jnp.where(a == 0, h, halves - 1), 0, 0)),
                pl.BlockSpec(block, lambda a, o, h, n: (jnp.where(a == 0, 0, o), 0, jnp.where(a == 0, 0, h), 0, 0)),
                pl.BlockSpec((8, width // 8, 384), lambda a, o, h, n: (0, 0, n[1])),
                pl.BlockSpec((1, 384), lambda a, o, h, n: (0, 0)),
            ],
            out_specs=[
                pl.BlockSpec((2, 1, HD, 512), lambda a, o, h, n: (0, owner_of(a, o, n), 0, h)),
                pl.BlockSpec((2, per, 128, 128), lambda a, o, h, n: (0, h, owner_of(a, o, n), 0)),
                pl.BlockSpec((2, per, 128, 128), lambda a, o, h, n: (0, h, 0, owner_of(a, o, n))),
                pl.BlockSpec((1, 1, 1, 128), lambda a, o, h, n: (owner_of(a, o, n), h, 0, 0)),
            ],
            scratch_shapes=[pltpu.VMEM((512, width), bf16)]),
        out_shape=[
            jax.ShapeDtypeStruct((2, 4, HD, local), bf16),
            jax.ShapeDtypeStruct((2, chunks, CH, 128), bf16),
            jax.ShapeDtypeStruct((2, chunks, 128, CH), bf16),
            jax.ShapeDtypeStruct((4, halves, 1, 128), f32),
        ],
        compiler_params=pltpu.CompilerParams(vmem_limit_bytes=40 << 20),
        name="qkv",
        cost_estimate=cost(4 * near.size * 384, near.size * 8),
    )(info, near, far, weight, bias)


def step_on(q, j, count):
    last = j + 1 == count
    return jnp.where(last, q + 1, q), jnp.where(last, 0, j + 1)


def assemble(ref, q, shared, core):
    if not shared:
        return ref[0, q]
    at = pl.multiple_of(core * 512, 512)
    return jnp.concatenate([ref[0, 2 * q, :, pl.ds(at, 512)], ref[0, 2 * q + 1, :, pl.ds(at, 512)]], axis=1)


def fwd_kernel(shared, info, q_ref, k_ref, v_ref, size_ref, held_ref, out_ref, lse_ref, acc, probs, qa, shifts):
    count = lax.div(info[0] + (CH - 1), CH)
    parts = 2 if shared else 4
    lane = lax.broadcasted_iota(jnp.int32, (1, 128), 1)
    sizes = functools.reduce(jnp.maximum, [size_ref[o, h] for o in range(size_ref.shape[0]) for h in range(size_ref.shape[1])])
    widest = jnp.sqrt(jnp.max(jnp.where(lane == int(shared), sizes, 0.0), axis=1, keepdims=True))

    for part in range(parts):
        q_t = assemble(q_ref, part, shared, info[3])
        wide = q_t.astype(f32)
        shift = jnp.sqrt(jnp.sum(wide * wide, axis=0, keepdims=True)) * widest
        shifts[part] = shift
        qa[part] = with_shift(q_t, shift).astype(bf16)

    def raised(part, j):
        return jnp.exp2(dg(k_ref[0, j], qa[part], 1, 0)).astype(bf16)

    probs[0] = raised(0, 0)

    def body(t, carry):
        part, j = carry
        now = t & 1
        part_next, j_next = step_on(part, j, count)
        before = jnp.where(j == 0, 0.0, acc[...])
        acc[...] = before + dg(v_ref[0, j], probs[now], 1, 0)
        probs[1 - now] = raised(jnp.minimum(part_next, parts - 1), j_next)

        @pl.when(j + 1 == count)
        def _():
            total = acc[HD:HD + 1]
            fine = (jnp.min(total) > 2.0 ** -90) & (jnp.max(total) < 2.0 ** 60)

            @pl.when(jnp.logical_not(fine))
            def _():
                plain = qa[part].astype(f32)
                row = lax.broadcasted_iota(jnp.int32, plain.shape, 0)
                qa[part] = jnp.where((row >= HD) & (row < HD + 3), 0.0, plain).astype(bf16)

                def peak(i, top):
                    return jnp.maximum(top, jnp.max(dg(k_ref[0, i], qa[part], 1, 0), axis=0, keepdims=True))
                shift = lax.fori_loop(0, count, peak, jnp.full((1, BQ), FAR, f32))
                shifts[part] = shift
                qa[part] = with_shift(plain[:HD], shift).astype(bf16)
                acc[...] = jnp.zeros_like(acc)

                def again(i, carry):
                    acc[...] += dg(v_ref[0, i], raised(part, i), 1, 0)
                    return carry
                lax.fori_loop(0, count, again, 0)

            total = acc[HD:HD + 1]
            mixed = (acc[:HD] * (1.0 / total)).astype(bf16)
            lse_ref[part] = shifts[part] + jnp.log2(total)
            if shared:
                out_ref[0, 2 * part] = mixed[:, :512]
                out_ref[0, 2 * part + 1] = mixed[:, 512:]
            else:
                out_ref[0, part] = mixed
        return part_next, j_next

    lax.fori_loop(0, parts * count, body, (0, 0))


def head_spec(shared, *dims):
    zeros = (0,) * len(dims)
    return pl.BlockSpec((1,) + dims, lambda i, n: (int(shared),) + zeros)


def whole_spec(*dims):
    return pl.BlockSpec(dims, lambda i, n: (0,) * len(dims))


def cost(flops, moved, exps=0):
    return pl.CostEstimate(flops=int(flops), bytes_accessed=int(moved), transcendentals=int(exps))


def attend_forward(shared, seq, q, k, v, sizes, info, held):
    _, owners, _, local = q.shape
    chunks = k.shape[1]
    wide = local // 2 if shared else local
    parts = owners * wide // BQ
    pairs = parts * BQ * chunks * CH * 0.6
    shape = jax.ShapeDtypeStruct((2, owners, HD, wide), bf16)
    first = held is None
    if first:
        kernel = lambda info, q, k, v, size, *rest: fwd_kernel(shared, info, q, k, v, size, None, *rest)
    else:
        kernel = functools.partial(fwd_kernel, shared)
    return pl.pallas_call(
        kernel,
        grid_spec=pltpu.PrefetchScalarGridSpec(
            num_scalar_prefetch=1, grid=(1,),
            in_specs=[
                head_spec(shared, owners, HD, local), head_spec(shared, chunks, CH, 128), head_spec(shared, chunks, 128, CH),
                whole_spec(*sizes.shape),
            ] + ([] if first else [pl.BlockSpec(memory_space=pl.ANY)]),
            out_specs=[pl.BlockSpec((1, owners, HD, wide), lambda i, n: (seq, 0, 0, 0)), whole_spec(parts, 1, BQ)],
            scratch_shapes=[
                pltpu.VMEM((128, BQ), f32), pltpu.VMEM((2, CH, BQ), bf16), pltpu.VMEM((parts, 128, BQ), bf16),
                pltpu.VMEM((parts, 1, BQ), f32),
            ]),
        out_shape=[shape, jax.ShapeDtypeStruct((parts, 1, BQ), f32)],
        input_output_aliases={} if first else {5: 0},
        compiler_params=pltpu.CompilerParams(vmem_limit_bytes=48 << 20),
        cost_estimate=cost(pairs * 1024, chunks * CH * 512, pairs),
        name="attend_forward_shared" if shared else "attend_forward_own",
    )(*((info, q, k, v, sizes) + (() if first else (held,))))


def bwd_kernel(shared, first, info, q_ref, k_ref, v_ref, lse_ref, out_ref, gout_ref, *rest):
    rest = rest if first else rest[3 if shared else 1:]
    if shared:
        dq_ref, kept_ref, given_ref, dk_acc, dv_acc, dq_acc, qa, qat, ga, gat, pb, db = rest
    else:
        dqkv_ref, dk_acc, dv_acc, dq_acc, qa, qat, ga, gat, pb, db = rest
    count = lax.div(info[0] + (CH - 1), CH)
    chunks = k_ref.shape[1]
    parts = 2 if shared else 4
    dk_acc[...] = jnp.zeros_like(dk_acc)
    dv_acc[...] = jnp.zeros_like(dv_acc)

    def piece(ref, part):
        if shared:
            return jnp.concatenate([ref[0, 2 * part], ref[0, 2 * part + 1]], axis=1)
        return ref[0, part]

    for part in range(parts):
        q_full = with_shift(assemble(q_ref, part, shared, info[3]), lse_ref[part])
        qat[part] = q_full.astype(bf16)
        qa[part] = q_full.T.astype(bf16)
        g_t = piece(gout_ref, part)
        meet = jnp.sum(g_t.astype(f32) * piece(out_ref, part).astype(f32), axis=0, keepdims=True)
        g_full = with_shift(g_t, meet)
        gat[part] = g_full.astype(bf16)
        ga[part] = g_full.T.astype(bf16)

    def ahead(part, j, slot):
        raised = jnp.exp2(dg(qa[part], k_ref[0, j], 1, 1))
        pb[slot] = raised.astype(bf16)
        db[slot] = (raised * dg(ga[part], v_ref[0, j], 1, 0)).astype(bf16)

    ahead(0, 0, 0)

    def body(t, carry):
        part, j = carry
        now = t & 1
        part_next, j_next = step_on(part, j, count)
        dv_acc[j] += dg(gat[part], pb[now], 1, 0)[:HD]
        dk_acc[j] += dg(qat[part], db[now], 1, 0)[:HD]
        before = jnp.where(j == 0, 0.0, dq_acc[...])
        dq_acc[...] = before + dg(db[now], k_ref[0, j], 1, 0)
        ahead(jnp.minimum(part_next, parts - 1), j_next, 1 - now)

        @pl.when(j + 1 == count)
        def _():
            dq_t = (dq_acc[...] * 0.125).T[:HD].astype(bf16)
            if shared:
                for a in range(2):
                    dq_ref[0, 2 * part + a, :, :512] = dq_t[:32, a * 512:(a + 1) * 512]
                    dq_ref[0, 2 * part + a, :, 512:] = dq_t[32:, a * 512:(a + 1) * 512]
            else:
                dqkv_ref[0, part, 0] = dq_t
        return part_next, j_next

    lax.fori_loop(0, parts * count, body, (0, 0))
    for j in range(chunks):
        for owner in range(4):
            cols = slice(owner * 128, (owner + 1) * 128)
            dk_wide, dv_wide = dk_acc[j, :, cols] * LN2, dv_acc[j, :, cols]
            dk, dv = dk_wide.astype(bf16), dv_wide.astype(bf16)
            if shared:
                here = info[3] == 0
                kept_ref[0, owner, :, j * 128:(j + 1) * 128] = jnp.where(here, dk_wide, dv_wide).astype(bf16)
                given_ref[0, owner, :, j * 128:(j + 1) * 128] = jnp.where(here, dv_wide, dk_wide).astype(bf16)
            else:
                dqkv_ref[0, owner, 1, :, j * 128:(j + 1) * 128] = dk
                dqkv_ref[0, owner, 2, :, j * 128:(j + 1) * 128] = dv


def attend_backward(shared, seq, q, k, v, lse, out, g_out, info, held):
    _, owners, _, local = q.shape
    chunks = k.shape[1]
    wide = out.shape[3]
    parts = owners * wide // BQ
    pairs = parts * BQ * chunks * CH * 0.6
    shape = jax.ShapeDtypeStruct
    first = held is None
    if shared:
        out_specs = [pl.BlockSpec((1, owners, rows, local), lambda i, n: (seq, 0, 0, 0)) for rows in (32, HD, HD)]
        out_shape = [shape((2, owners, rows, local), bf16) for rows in (32, HD, HD)]
    else:
        out_specs = [pl.BlockSpec((1, owners, 3, HD, local), lambda i, n: (seq, 0, 0, 0, 0))]
        out_shape = [shape((2, owners, 3, HD, local), bf16)]
    kept = () if first else tuple(held)
    of_seq = pl.BlockSpec((1, owners, HD, wide), lambda i, n: (seq, 0, 0, 0))
    return pl.pallas_call(
        functools.partial(bwd_kernel, shared, first),
        grid_spec=pltpu.PrefetchScalarGridSpec(
            num_scalar_prefetch=1, grid=(1,),
            in_specs=[
                head_spec(shared, owners, HD, local), head_spec(shared, chunks, CH, 128), head_spec(shared, chunks, 128, CH),
                whole_spec(parts, 1, BQ), of_seq, of_seq,
            ] + [pl.BlockSpec(memory_space=pl.ANY)] * len(kept),
            out_specs=out_specs,
            scratch_shapes=[
                pltpu.VMEM((chunks, HD, CH), f32), pltpu.VMEM((chunks, HD, CH), f32), pltpu.VMEM((BQ, 128), f32),
                pltpu.VMEM((parts, BQ, 128), bf16), pltpu.VMEM((parts, 128, BQ), bf16),
                pltpu.VMEM((parts, BQ, 128), bf16), pltpu.VMEM((parts, 128, BQ), bf16),
                pltpu.VMEM((2, BQ, CH), bf16), pltpu.VMEM((2, BQ, CH), bf16),
            ]),
        out_shape=out_shape,
        input_output_aliases={7 + n: n for n in range(len(kept))},
        compiler_params=pltpu.CompilerParams(vmem_limit_bytes=56 << 20),
        cost_estimate=cost(pairs * 100, chunks * CH * 2048),
        name="attend_backward_shared" if shared else "attend_backward_own",
    )(info, q, k, v, lse, out, g_out, *kept)


def gelu_pair(u):
    half = 0.5 * (1.0 + lax.erf(u * 0.7071067811865476))
    return u * half, half + u * (0.3989422804014327 * jnp.exp2(u * u * (-0.5 * LOG2E)))


def norm_stats(v):
    mean = jnp.mean(v, axis=-1, keepdims=True)
    centred = v - mean
    inverse = lax.rsqrt(jnp.mean(centred * centred, axis=-1, keepdims=True) + 1e-12)
    return centred * inverse, inverse


def norm_back(grad, xhat, inverse, gain):
    g = grad * gain
    return (g - jnp.mean(g, axis=-1, keepdims=True) - xhat * jnp.mean(g * xhat, axis=-1, keepdims=True)) * inverse


def weight_part(ref, first, rows):
    part = ref[:, first:first + rows, :]
    return part.reshape(part.shape[0] * rows, part.shape[2])


def ffn_kernel(spans, info, x_ref, own_ref, sh_ref, cot_ref, w_ref, bin_ref, vec_ref,
               act_out, resid_out, gown_out, gsh_out, active_out, dinner_out, normed_out, douter_out, dbranch_out,
               vec_sum, bin_sum, slope, row_block):
    step = pl.program_id(0)
    width = x_ref.shape[-1]
    load_rows(row_block, x_ref, spans, info[1])
    rows = row_block[...].astype(f32)
    mixed_t = jnp.concatenate(
        [part for p in range(4) for part in (own_ref[p, 0], sh_ref[p, 0], own_ref[p, 1])], axis=0)
    vec = vec_ref[...]
    branch = dg(mixed_t, weight_part(w_ref, 768, 96), 0, 0) + vec[0:1]
    xhat1, inv1 = norm_stats(rows + branch)
    normed = xhat1 * vec[1:2] + vec[2:3]
    low = normed.astype(bf16)
    normed_out[...] = low
    outer = normed + vec[3:4]
    for n in range(4):
        cols = slice(n * 768, (n + 1) * 768)
        inner = dg(low, weight_part(w_ref, 384 + 96 * n, 96), 1, 0) + bin_ref[:, cols]
        value, bend = gelu_pair(inner)
        active_out[:, cols] = value.astype(bf16)
        slope[:, cols] = bend.astype(bf16)
    outer = outer + dg(active_out[...], weight_part(w_ref, 0, 384), 1, 0)
    xhat2, inv2 = norm_stats(outer)
    act_out[...] = (xhat2 * vec[4:5] + vec[5:6]).astype(bf16)
    cot = cot_ref[...].astype(f32)
    d2 = norm_back(cot, xhat2, inv2, vec[4:5])
    d_outer = d2.astype(bf16)
    douter_out[...] = d_outer
    d_normed = d2
    sums_in = []
    for n in range(4):
        cols = slice(n * 768, (n + 1) * 768)
        d_active = dg(d_outer, weight_part(w_ref.at[2 * n:2 * n + 2], 0, 384), 1, 1)
        d_inner = (d_active * slope[:, cols].astype(f32)).astype(bf16)
        dinner_out[:, cols] = d_inner
        sums_in.append(jnp.sum(d_inner.astype(f32), axis=0, keepdims=True))
        d_normed = d_normed + dg(d_inner, weight_part(w_ref, 384 + 96 * n, 96), 1, 1)
    d1 = norm_back(d_normed, xhat1, inv1, vec[1:2])
    resid_out[...] = d1
    d_branch = d1.astype(bf16)
    dbranch_out[...] = d_branch
    g_t = dg(weight_part(w_ref, 768, 96), d_branch, 1, 1).astype(bf16)
    for p in range(4):
        gown_out[p, 0] = g_t[192 * p:192 * p + 64]
        gsh_out[p, 0] = g_t[192 * p + 64:192 * p + 128]
        gown_out[p, 1] = g_t[192 * p + 128:192 * p + 192]
    total = lambda a: jnp.sum(a, axis=0, keepdims=True)
    sums = jnp.concatenate([
        total(d_branch.astype(f32)), total(d_normed * xhat1), total(d_normed),
        total(d_outer.astype(f32)), total(cot * xhat2), total(cot), jnp.zeros((2, width), f32)], axis=0)

    @pl.when(step == 0)
    def _():
        vec_sum[...] = sums
        for n in range(4):
            bin_sum[:, n * 768:(n + 1) * 768] = sums_in[n]

    @pl.when(step > 0)
    def _():
        vec_sum[...] += sums
        for n in range(4):
            bin_sum[:, n * 768:(n + 1) * 768] += sums_in[n]


def feed_forward(rows_in, own, sh, cotangent, weights, inner_bias, vectors, info):
    _, _, _, stretch, width = rows_in.shape
    local = cotangent.shape[0]
    spans = RB // (2 * stretch)
    steps = local // RB
    half_steps = steps // 2
    wide = inner_bias.shape[1]
    rows = lambda n: pl.BlockSpec((RB, n), lambda r, a: (r, 0))
    fixed = lambda *dims: pl.BlockSpec(dims, lambda r, a: (0,) * len(dims))
    own_spec = pl.BlockSpec((4, 2, HD, RB), lambda r, a: (0, 0, 0, r))
    sh_spec = pl.BlockSpec((4, 1, HD, RB), lambda r, a: (0, r // half_steps, 0, r % half_steps))
    shape = jax.ShapeDtypeStruct
    return pl.pallas_call(
        functools.partial(ffn_kernel, spans),
        grid_spec=pltpu.PrefetchScalarGridSpec(
            num_scalar_prefetch=1, grid=(steps,),
            in_specs=[
                pl.BlockSpec((1, 2, spans, stretch, width), lambda r, a: (0, 0, r, 0, 0)),
                own_spec, sh_spec, rows(width),
                pl.BlockSpec(weights.shape, lambda r, a: (0, 0, 0), pipeline_mode=pl.Buffered(1)),
                fixed(1, wide), fixed(8, width),
            ],
            out_specs=[
                rows(width), rows(width), own_spec, sh_spec, rows(wide), rows(wide), rows(width), rows(width), rows(width),
                fixed(8, width), fixed(1, wide),
            ],
            scratch_shapes=[pltpu.VMEM((RB, wide), bf16), pltpu.VMEM((RB, width), bf16)]),
        out_shape=[
            shape((local, width), bf16), shape((local, width), f32), shape(own.shape, bf16), shape(sh.shape, bf16),
            shape((local, wide), bf16), shape((local, wide), bf16), shape((local, width), bf16),
            shape((local, width), bf16), shape((local, width), bf16), shape((8, width), f32), shape((1, wide), f32),
        ],
        compiler_params=pltpu.CompilerParams(vmem_limit_bytes=60 << 20),
        name="feed_forward",
        cost_estimate=cost(local * width * (width + 2 * wide) * 4, local * wide * 20),
    )(info, rows_in, own, sh, cotangent, weights, inner_bias, vectors)


def outer_grad_kernel(scale, active_ref, douter_ref, out_ref):
    made = (dg(active_ref[...], douter_ref[...], 0, 0) * scale).astype(bf16)
    out_ref[...] = made.reshape(out_ref.shape)


def inner_grad_kernel(scale, packed_ref, normed_ref, dinner_ref, own_ref, sh_ref, dbranch_ref, out_ref):
    step = pl.program_id(0)

    @pl.when(step < 4)
    def _():
        out_ref[...] = (dg(normed_ref[...], dinner_ref[...], 0, 0) * scale).astype(bf16).reshape(out_ref.shape)

    @pl.when(step == 4)
    def _():
        mixed_t = jnp.concatenate([
            part for p in range(4)
            for part in (own_ref[p, 0], jnp.concatenate([sh_ref[p, 0], sh_ref[p, 1]], axis=1), own_ref[p, 1])], axis=0)
        out_ref[...] = (dg(mixed_t, dbranch_ref[...], 1, 0) * scale).astype(bf16).reshape(out_ref.shape)


def weight_grads(scale, active, d_outer, normed, d_inner, own, sh, d_branch):
    local, wide = active.shape
    width = normed.shape[1]
    packed = pl.pallas_call(
        functools.partial(outer_grad_kernel, scale), grid=(4,),
        in_specs=[pl.BlockSpec((local, width), lambda m: (0, m)), pl.BlockSpec((local, width), lambda m: (0, 0))],
        out_specs=pl.BlockSpec((2, 384, width), lambda m: (m, 0, 0)),
        out_shape=jax.ShapeDtypeStruct((8, 896, width), bf16),
        compiler_params=pltpu.CompilerParams(vmem_limit_bytes=40 << 20), name="outer_grad",
        cost_estimate=cost(2 * local * wide * width, 2 * wide * (local + width)),
    )(active, d_outer)
    fixed = lambda a: pl.BlockSpec(a.shape, lambda n: (0,) * a.ndim)
    return pl.pallas_call(
        functools.partial(inner_grad_kernel, scale), grid=(5,),
        in_specs=[
            pl.BlockSpec(memory_space=pl.ANY), fixed(normed),
            pl.BlockSpec((local, width), lambda n: (0, jnp.minimum(n, 3))), fixed(own), fixed(sh), fixed(d_branch)],
        out_specs=pl.BlockSpec((8, 96, width), lambda n: (0, 4 + n, 0)),
        out_shape=jax.ShapeDtypeStruct((8, 896, width), bf16), input_output_aliases={0: 0},
        compiler_params=pltpu.CompilerParams(vmem_limit_bytes=40 << 20), name="inner_grad",
        cost_estimate=cost(2 * local * (wide + width) * width, 2 * (wide + width) * (local + width)),
    )(packed, normed, d_inner, own, sh, d_branch)


def head_grad_kernel(scale, spans, info, *refs):
    x_refs, (own_ref, dq_ref, kept_ref, given_ref, out_ref, bias_out, acc, bias_acc, rows) = refs[:4], refs[4:]
    seq, away, half = pl.program_id(0), pl.program_id(1), pl.program_id(3)
    last = (seq == 1) & (away == 1) & (pl.program_id(2) == 1) & (half == pl.num_programs(3) - 1)
    for n in range(4):
        @pl.when(seq * 2 + away == n)
        def _(n=n):
            load_rows(rows, x_refs[n], spans, info[1])
    dq_t = jnp.where(half == info[3], jnp.concatenate([dq_ref[0, 0, :, :512], dq_ref[0, 0, :, 512:]], axis=0).astype(f32), 0.0)
    kept, given = kept_ref[0, 0].astype(f32), given_ref[0, 0].astype(f32)
    here = info[3] == 0
    d_t = jnp.concatenate([
        own_ref[0, 0, 0], dq_t.astype(bf16), own_ref[0, 0, 1], jnp.where(here, kept, given).astype(bf16),
        own_ref[0, 0, 2], jnp.where(here, given, kept).astype(bf16)], axis=0)

    @pl.when((seq == 0) & (away == 0) & (pl.program_id(2) == 0) & (half == 0))
    def _():
        acc[...] = jnp.zeros_like(acc)
        bias_acc[...] = jnp.zeros_like(bias_acc)
    acc[...] += dg(d_t, rows[...], 1, 0)
    bias_acc[...] += dg(jnp.ones((8, d_t.shape[1]), bf16), d_t, 1, 1)

    @pl.when(last)
    def _():
        out_ref[...] = (acc[...] * scale).T.astype(bf16)
        bias_out[...] = bias_acc[...] * scale


def head_grads(scale, sources, dqkv_own, dq_sh, kept, given, info):
    _, _, zs, stretch, width = sources[0].shape
    local = 2 * zs * stretch
    spans = 512 // (2 * stretch)
    halves = local // 512

    def source_spec(n):
        def index(s, a, o, h, i):
            now = 2 * s + a
            across = jnp.where(now == n, o, jnp.where(now < n, 0, 1))
            return (across, 0, jnp.where(now == n, h, jnp.where(now < n, 0, halves - 1)), 0, 0)
        return pl.BlockSpec((1, 2, spans, stretch, width), index)
    return pl.pallas_call(
        functools.partial(head_grad_kernel, scale, spans),
        grid_spec=pltpu.PrefetchScalarGridSpec(
            num_scalar_prefetch=1, grid=(2, 2, 2, halves),
            in_specs=[source_spec(n) for n in range(4)] + [
                pl.BlockSpec((1, 1, 3, HD, 512), lambda s, a, o, h, i: (s, owner_of(a, o, i), 0, 0, h)),
                pl.BlockSpec((1, 1, 32, local), lambda s, a, o, h, i: (s, owner_of(a, o, i), 0, 0)),
            ] + [pl.BlockSpec((1, 1, HD, 512), lambda s, a, o, h, i: (s, owner_of(a, o, i), 0, h))] * 2,
            out_specs=[pl.BlockSpec((width, 384), lambda s, a, o, h, i: (0, 0)), pl.BlockSpec((8, 384), lambda s, a, o, h, i: (0, 0))],
            scratch_shapes=[pltpu.VMEM((384, width), f32), pltpu.VMEM((8, 384), f32), pltpu.VMEM((512, width), bf16)]),
        out_shape=[jax.ShapeDtypeStruct((width, 384), bf16), jax.ShapeDtypeStruct((8, 384), f32)],
        compiler_params=pltpu.CompilerParams(vmem_limit_bytes=40 << 20), name="head_grads",
        cost_estimate=cost(8 * local * 768 * width, 8 * local * width * 2),
    )(info, *sources, dqkv_own, dq_sh, kept, given)


def token_grad_kernel(own_ref, low_ref, high_ref, dkv_ref, w_ref, resid_ref, out_ref):
    total = resid_ref[...]
    for kind in range(3):
        made = []
        for p in range(4):
            if kind == 0:
                middle = jnp.concatenate([low_ref[p, 0], high_ref[p, 0]], axis=0)
            else:
                middle = jnp.concatenate([dkv_ref[p, kind - 1, n] for n in range(2)], axis=0)
            made += [own_ref[p, 0, kind], middle, own_ref[p, 1, kind]]
        total = total + dg(jnp.concatenate(made, axis=0), weight_part(w_ref, 96 * kind, 96), 0, 1)
    out_ref[...] = total.astype(bf16)


def token_grad(own, shared, weights, resid):
    local, width = resid.shape
    steps = local // RB
    half_steps = steps // 2
    rows = pl.BlockSpec((RB, width), lambda r: (r, 0))
    return pl.pallas_call(
        token_grad_kernel, grid=(steps,),
        in_specs=[
            pl.BlockSpec((4, 2, 3, HD, RB), lambda r: (0, 0, 0, 0, r)),
            pl.BlockSpec((4, 1, None, 32, RB), lambda r: (0, r // half_steps, 2, 0, r % half_steps)),
            pl.BlockSpec((4, 1, None, 32, RB), lambda r: (0, r // half_steps, 2, 0, half_steps + r % half_steps)),
            pl.BlockSpec((4, 2, 2, 32, RB), lambda r: (0, 0, 0, 0, r)),
            pl.BlockSpec(weights.shape, lambda r: (0, 0, 0)), rows],
        out_specs=rows, out_shape=jax.ShapeDtypeStruct((local, width), bf16),
        compiler_params=pltpu.CompilerParams(vmem_limit_bytes=40 << 20), name="token_grad",
        cost_estimate=cost(local * width * width * 6, local * width * 12),
    )(own, shared, shared, shared, weights, resid)


SWAP = [(0, 1), (1, 0)]
def settle_kernel(*refs):
    refs[-1][...] = sum(ref[...].astype(f32) for ref in refs[:-2]).astype(bf16)


def settle(parts, after):
    whole = pl.BlockSpec(memory_space=pltpu.VMEM)
    return pl.pallas_call(
        settle_kernel, in_specs=[whole] * len(parts) + [pl.BlockSpec(memory_space=pl.ANY)], out_specs=whole,
        out_shape=jax.ShapeDtypeStruct(parts[0].shape, bf16), name="settle",
        cost_estimate=cost(5e10, 1e8),
    )(*parts, after)


PAIR = ("x", "y", "c")
ALL = ("z", "x", "y", "c")
SHARD = ("z", "x")


def canonical(packed, shards):
    if shards == 8:
        return packed
    width = packed.shape[2]
    per, keep = 96 * 8 // shards, shards // 8
    outer = packed[:, :4 * per].reshape(8, 384, width)
    inner = packed[:, 4 * per:8 * per].reshape(8, keep, 4, per, width).transpose(0, 2, 1, 3, 4).reshape(8, 384, width)
    output = packed[:, 8 * per:9 * per].reshape(8, 96, width)
    return jnp.concatenate([outer, inner, output, jnp.zeros((8, 32, width), packed.dtype)], axis=1)


def from_canonical(packed, last, shards):
    width = packed.shape[2]
    if shards == 8:
        return packed.at[:, 864:].set(jnp.broadcast_to(last[None], (8, 32, width)))
    per, keep = 96 * 8 // shards, shards // 8
    outer = packed[:, :384].reshape(shards, 4 * per, width)
    inner = packed[:, 384:768].reshape(8, 4, keep, per, width).transpose(0, 2, 1, 3, 4).reshape(shards, 4 * per, width)
    output = packed[:, 768:864].reshape(shards, per, width)
    return jnp.concatenate([outer, inner, output, jnp.broadcast_to(last[None], (shards, 32, width))], axis=1)


def canonical_heads(packed, shards, parts):
    if shards == 8:
        return packed
    width = packed.shape[2]
    per = 96 * 8 // shards
    made = [packed[:, k * per:(k + 1) * per].reshape(8, 96, width) for k in range(parts)]
    return jnp.concatenate(made + [jnp.zeros((8, 32, width), packed.dtype)], axis=1)


def quarter(rows):
    place = lax.axis_index("y") * 2 + lax.axis_index("c")
    part = rows.shape[0] // 4
    return lax.dynamic_slice_in_dim(rows, place * part, part)


def flipped(array, axis, here):
    return jnp.where(here == 0, array, jnp.flip(array, axis))


def body(tokens, lengths, deal_order, w_query, w_key, w_value, w_output, b_query, b_value, b_output,
         ln1_gain, ln1_shift, w_inner, b_inner, w_outer, b_outer, ln2_gain, ln2_shift, cotangent):
    tie = lax.optimization_barrier
    zs = lax.axis_size("z")
    shards = 2 * zs
    scale = 1.0 / (shards * 4)
    seq_count, _, stretch, width = tokens.shape
    per = w_query.shape[0]
    half = zs // 2
    x, y, c = lax.axis_index("x"), lax.axis_index("y"), lax.axis_index("c")

    def deal(ordered):
        return lax.all_to_all(ordered, "z", split_axis=0, concat_axis=0, tiled=True)

    def corner(across, along):
        return [lax.ppermute(across[:half], "y", SWAP), lax.ppermute(along[half:], "x", SWAP)]

    def this_core(own, across, along, corner):
        return jnp.concatenate([own, across, along] + corner, axis=0).reshape(2, 2, zs, stretch, width)

    ordered_a = jnp.take(tokens[:, 0], deal_order[0::2], axis=0)
    first_own = deal(ordered_a)
    (_, tokens, w_query, w_key, w_value, b_query, b_value, w_outer, w_inner, w_output, b_inner, deal_order) = tie(
        (ordered_a, tokens, w_query, w_key, w_value, b_query, b_value, w_outer, w_inner, w_output, b_inner, deal_order))
    ordered_b = jnp.take(tokens[:, 0], deal_order[1::2], axis=0)

    def head_columns(matrix):
        heads = matrix.reshape(per, 2, 2, 3, HD)
        mine = lax.dynamic_index_in_dim(heads, y, axis=2, keepdims=False)
        own = lax.dynamic_index_in_dim(mine, 2 * c, axis=2, keepdims=False)
        return [own, mine[:, :, 1]]
    pad = lambda v: jnp.pad(v, (0, width - v.shape[0]))[None]
    columns = jnp.concatenate(
        [col for matrix in (w_query, w_key, w_value) for col in head_columns(matrix)], axis=2).reshape(per, width)
    head_pack = jnp.concatenate([columns, pad(b_query), pad(b_value), jnp.zeros((14, width), bf16)], axis=0)
    vectors = (b_output, ln1_gain, ln1_shift, b_outer, ln2_gain, ln2_shift)
    layer_pack = jnp.concatenate(
        [w_outer] + [w_inner[:, n * width:(n + 1) * width] for n in range(4)] + [w_output]
        + [pad(b_inner)] + [pad(v) for v in vectors] + [jnp.zeros((25, width), bf16)], axis=0)
    layer_quarter = quarter(layer_pack)
    back_quarter = quarter(jnp.concatenate([w_query, w_key, w_value, jnp.zeros((32, width), bf16)], axis=0))
    first_own, ordered_b, head_pack, layer_quarter, back_quarter = tie(
        (first_own, ordered_b, head_pack, layer_quarter, back_quarter))
    head_all = lax.all_gather(head_pack, SHARD, axis=0, tiled=False)
    head_weight = canonical_heads(head_all, shards, 1)

    def head_bias(row):
        heads = head_all[:, per + row, :per].reshape(2, 2, 3, HD)
        mine = lax.dynamic_slice(heads, (x, y, 0, 0), (1, 1, 3, HD))[0, 0]
        return [lax.dynamic_index_in_dim(mine, 2 * c, axis=0, keepdims=False), mine[1]]
    bias_row = jnp.concatenate(head_bias(0) + [jnp.zeros((2 * HD,), bf16)] + head_bias(1)).astype(f32)[None]

    across_a, along_a = lax.ppermute(first_own, "x", SWAP), lax.ppermute(first_own, "y", SWAP)
    second_own = deal(ordered_b)
    across_a, along_a, second_own = tie((across_a, along_a, second_own))
    corner_a = corner(across_a, along_a)
    second_own, *corner_a = tie((second_own, *corner_a))
    near_a = this_core(first_own, across_a, along_a, corner_a)
    far_a = lax.ppermute(near_a, "c", SWAP)
    across_b, along_b = lax.ppermute(second_own, "x", SWAP), lax.ppermute(second_own, "y", SWAP)

    layer_all = lax.all_gather(layer_quarter, ALL, axis=0, tiled=True).reshape(shards, 9 * per + 32, width)
    layer_weights = canonical(layer_all, shards)
    inner_bias = layer_all[:, 9 * per, :4 * per].reshape(1, 4 * width).astype(f32)
    vector_rows = jnp.concatenate(
        [layer_all[:, 9 * per + 1 + n, :per].reshape(1, width) for n in range(6)] + [jnp.zeros((2, width), bf16)],
        axis=0).astype(f32)
    back_all = lax.all_gather(back_quarter, ALL, axis=0, tiled=True).reshape(shards, 3 * per + 32, width)

    slots = lax.dynamic_slice_in_dim(deal_order, lax.axis_index("z") * 2, 2)
    matches = slots[:, None] == jnp.arange(seq_count, dtype=jnp.int32)[None, :]
    lens = jnp.sum(jnp.where(matches, lengths[None, :], 0), axis=1).astype(jnp.int32)
    infos = [jnp.stack([lens[n], x, y, c]).astype(jnp.int32) for n in range(2)]

    def swap(array):
        flat = array.reshape((8,) + array.shape[2:])
        return lax.all_to_all(flat, PAIR, split_axis=0, concat_axis=0, tiled=True)

    def to_tokens(array):
        return swap(array).reshape((4, 2) + array.shape[2:])

    def to_heads(array):
        return swap(array).reshape((2, 4) + array.shape[2:])

    heads_a = project(near_a, far_a, head_weight, bias_row, infos[0])
    heads_a, across_b, along_b = tie((heads_a, across_b, along_b))
    near_b = this_core(second_own, across_b, along_b, corner(across_b, along_b))
    own_first, lse_own_a = attend_forward(False, 0, *heads_a, infos[0], None)
    own_first, near_b = tie((own_first, near_b))
    far_b = lax.ppermute(near_b, "c", SWAP)
    heads_b = project(near_b, far_b, head_weight, bias_row, infos[1])
    own, lse_own_b = attend_forward(False, 1, *heads_b, infos[1], own_first)
    own_t = to_tokens(own)
    own, info_a, info_b = tie((own, *infos))
    sh_first, lse_sh_a = attend_forward(True, 0, *heads_a, info_a, None)
    sh, lse_sh_b = attend_forward(True, 1, *heads_b, info_b, sh_first)
    sh_sent, own_t = tie((sh, own_t))
    sh_t = to_tokens(sh_sent)
    mine_rows = jnp.where(x == 0, jnp.stack([first_own, across_a]), jnp.stack([second_own, across_b]))[None]

    (act, resid, g_own, g_sh, active, d_inner, normed, d_outer, d_branch, vec_sums, bin_sums) = feed_forward(
        mine_rows, own_t, sh_t, cotangent.reshape(-1, width), layer_weights, inner_bias, vector_rows, infos[0])
    g_own_h, g_sh_h = to_heads(g_own), to_heads(g_sh)
    active, back_all = tie((active, back_all))
    packed = weight_grads(scale, active, d_outer, normed, d_inner, own_t, sh_t, d_branch)
    sums = jnp.concatenate([bin_sums.reshape(4, width), vec_sums, jnp.zeros((20, width), f32)], axis=0) * scale
    ready = from_canonical(packed, sums.astype(bf16), shards)
    ready, g_own_h = tie((ready, g_own_h))
    back_weights = canonical_heads(back_all, shards, 3)
    layer_part = lax.psum_scatter(ready.reshape(-1, width), ("z", "x", "c"), scatter_dimension=0, tiled=True)

    qkv_a, qkv_b = heads_a[:3], heads_b[:3]
    first = attend_backward(False, 0, *qkv_a, lse_own_a, own, g_own_h, infos[0], None)
    dqkv_own, = attend_backward(False, 1, *qkv_b, lse_own_b, own, g_own_h, infos[1], first)
    back_own = to_tokens(dqkv_own)
    dqkv_own, info_a, info_b = tie((dqkv_own, *infos))
    first = attend_backward(True, 0, *qkv_a, lse_sh_a, sh, g_sh_h, info_a, None)
    dq_sh, kept, given = attend_backward(True, 1, *qkv_b, lse_sh_b, sh, g_sh_h, info_b, first)
    taken = lax.ppermute(given, "c", SWAP)
    shared_out = jnp.concatenate([(kept.astype(f32) + taken.astype(f32)).astype(bf16), dq_sh], axis=2)
    shared_out, back_own, dqkv_own = tie((shared_out, back_own, dqkv_own))
    back_shared = to_tokens(shared_out.reshape(2, 4, 3, 32, -1))
    d_heads, d_bias = head_grads(scale, (near_a, far_a, near_b, far_b), dqkv_own, dq_sh, kept, given, infos[0])

    head_ready = jnp.concatenate([
        d_heads.reshape(zs, 2, per, 384),
        jnp.broadcast_to(d_bias[:1].astype(bf16)[None, None], (zs, 2, 16, 384))], axis=2)
    layer_sum = (layer_part.astype(f32) + lax.ppermute(layer_part, "y", SWAP).astype(f32)).astype(bf16)
    head_ready, back_shared, layer_sum = tie((head_ready, back_shared, layer_sum))
    d_rows = token_grad(back_own, back_shared, back_weights, resid)
    if zs == 4:
        group = lax.axis_index("z")
        parts = [lax.dynamic_index_in_dim(head_ready, (group + k) % zs, axis=0, keepdims=False) for k in range(zs)]
        parts = parts[:1] + [
            lax.ppermute(parts[k], "z", [(i, (i + k) % zs) for i in range(zs)]) for k in range(1, zs)]
        head_sum = settle(parts, d_rows)
    else:
        head_sum = lax.psum_scatter(
            head_ready.reshape(-1, 384), "z", scatter_dimension=0, tiled=True).reshape(2, per + 16, 384)
    returned = lax.all_to_all(
        d_rows.reshape(shards, stretch, width), SHARD, split_axis=0, concat_axis=0, tiled=True)

    def apart(array, bits):
        return lax.ppermute(array, PAIR, [(i, i ^ bits) for i in range(8)]) if bits else array

    halves = [lax.dynamic_index_in_dim(head_sum, x ^ k, axis=0, keepdims=False) for k in range(2)]
    head_eight = jnp.stack([apart(halves[bits >> 2], bits) for bits in range(8)]).reshape(2, 2, 2, per + 16, 6, HD)
    cores = flipped(flipped(flipped(head_eight, 0, x), 1, y), 2, c).astype(f32)

    def full(kind):
        joined = jnp.stack([cores[:, :, 0, :, 2 * kind], cores[:, :, 0, :, 2 * kind + 1] + cores[:, :, 1, :, 2 * kind + 1],
                            cores[:, :, 1, :, 2 * kind]], axis=2)
        return joined.transpose(3, 0, 1, 2, 4).reshape(per + 16, width)
    d_wq, d_wk, d_wv = (full(kind) for kind in range(3))
    place = lax.axis_index("z") * 2 + x
    own_slice = lambda row, n: lax.dynamic_slice_in_dim(row, place * n, n)
    d_bq, d_bv = own_slice(d_wq[per], per), own_slice(d_wv[per], per)
    d_wq, d_wk, d_wv = d_wq[:per], d_wk[:per], d_wv[:per]

    layer_grads = flipped(jnp.stack([layer_sum, lax.ppermute(layer_sum, "c", SWAP)]), 0, c)
    layer_grads = layer_grads.reshape(9 * per + 32, width).astype(f32)
    d_wouter = layer_grads[:4 * per]
    d_winner = jnp.concatenate([layer_grads[(4 + n) * per:(5 + n) * per] for n in range(4)], axis=1)
    d_woutput = layer_grads[8 * per:9 * per]
    d_binner = own_slice(layer_grads[9 * per:9 * per + 4].reshape(-1), 4 * per)
    d_bo, d_g1, d_s1, d_bout, d_g2, d_s2 = (own_slice(layer_grads[9 * per + 4 + n], per) for n in range(6))
    small = (d_bq, d_bv, d_binner, d_bo, d_g1, d_s1, d_bout, d_g2, d_s2)
    returned = tie((returned, d_wouter, d_winner, d_woutput, d_wq, d_wk, d_wv) + small)[0]
    steps = jnp.arange(seq_count, dtype=jnp.int32)
    slot_of = jnp.sum(jnp.where(deal_order[:, None] == steps[None, :], steps[:, None], 0), axis=0)
    d_tokens = jnp.take(returned, slot_of, axis=0)[:, None]
    return (act.reshape(1, shards, stretch, width), d_tokens, d_wq, d_wk, d_wv, d_woutput, d_bq, d_bv, d_bo,
            d_g1, d_s1, d_winner, d_binner, d_wouter, d_bout, d_g2, d_s2)


def solution(mesh):
    shards, splits = mesh.devices.shape
    fine = Mesh(mesh.devices.reshape(shards // 2, 2, splits // 2, 2), ALL)
    S, Q = SHARD, ("y", "c")
    row, mat = P(S), P(S, None)
    return jax.shard_map(
        body, mesh=fine,
        in_specs=(P(None, S, Q, None), P(), P(), mat, mat, mat, mat, row, row, row, row, row, mat, row, mat, row, row, row,
                  P(S, None, Q, None)),
        out_specs=(P(S, None, Q, None), P(None, S, Q, None), mat, mat, mat, mat, row, row, row, row, row, mat, row, mat,
                   row, row, row),
        check_vma=False)
```

```python
import functools, math
import jax
import jax.numpy as jnp
from jax import lax
from jax.experimental import pallas as pl
from jax.experimental.pallas import tpu as pltpu
from jax.sharding import Mesh, PartitionSpec as P

f32, bf16 = jnp.float32, jnp.bfloat16
LOG2E = 1.4426950408889634
LN2 = 0.6931471805599453
CH = 256
BQ = 2048
RB = 256
FB = 512
PARTS = 2
HD = 64
FAR = -1.0e30

def dg(a, b, ca, cb):
    return lax.dot_general(a, b, (((ca,), (cb,)), ((), ())), preferred_element_type=f32)


def three_parts(row):
    hi = row.astype(bf16).astype(f32)
    rest = row - hi
    mid = rest.astype(bf16).astype(f32)
    return hi, mid, rest - mid


def with_shift(top, shift):
    hi, mid, low = three_parts(shift)
    row = lax.broadcasted_iota(jnp.int32, (HD, top.shape[1]), 0)
    tail = jnp.where(row == 0, -hi, jnp.where(row == 1, -mid, jnp.where(row == 2, -low, jnp.where(row == 3, 1.0, 0.0))))
    return jnp.concatenate([top.astype(f32), tail], axis=0)


def load_rows(rows, ref, spans, x):
    stretch = ref.shape[3]
    for z in range(spans):
        for a in range(2):
            at = (2 * z + a) * stretch
            rows[at:at + stretch] = ref[0, a ^ x, z]


def qkv_kernel(stretch, spans, info, near_ref, far_ref, w_ref, b_ref, q_out, k_out, v_out, size_out, rows):
    away, half = pl.program_id(0), pl.program_id(2)
    owner = ((pl.program_id(1) ^ info[2]) << 1) | (away ^ info[3])

    @pl.when(away == 0)
    def _():
        load_rows(rows, near_ref, spans, info[1])

    @pl.when(away == 1)
    def _():
        load_rows(rows, far_ref, spans, info[1])
    weight = w_ref[...].reshape(rows.shape[1], 384)
    made = dg(rows[...], weight, 1, 0) + b_ref[...]
    count = rows.shape[0]
    q_t = (made[:, :128] * (LOG2E / 8.0)).T
    q_out[0, 0] = q_t[:HD].astype(bf16)
    q_out[1, 0] = q_t[HD:].astype(bf16)
    lane = lax.broadcasted_iota(jnp.int32, (count, 128), 1)
    row = lax.broadcasted_iota(jnp.int32, (count, 128), 0) + half * count
    shift = int(math.log2(stretch))
    position = lax.shift_left(lax.shift_right_logical(row, shift), shift + 2) + owner * stretch + (row & (stretch - 1))
    hidden = jnp.where(position < info[0], 0.0, FAR)
    tail = jnp.where(lane == HD + 3, hidden, jnp.where(lane < HD + 3, 1.0, 0.0))
    keys = made[:, 128:256]
    picks = lax.broadcasted_iota(jnp.int32, (128, 128), 0) // HD == lax.broadcasted_iota(jnp.int32, (128, 128), 1)
    sizes = dg((keys * keys).astype(bf16), jnp.where(picks, 1.0, 0.0).astype(bf16), 1, 0)
    size_out[0, 0] = jnp.max(sizes, axis=0, keepdims=True)
    for head in range(2):
        turned = keys if head == 0 else pltpu.roll(keys, HD, 1)
        full = jnp.where(lane < HD, turned, tail).astype(bf16)
        for j in range(count // 128):
            k_out[head, j, 0] = full[j * 128:(j + 1) * 128]
    v_t = made[:, 256:384].T
    ones = jnp.where(lax.broadcasted_iota(jnp.int32, (HD, count), 0) < 3, 1.0, 0.0)
    for head in range(2):
        full = jnp.concatenate([v_t[head * HD:(head + 1) * HD], ones], axis=0).astype(bf16)
        for j in range(count // 128):
            v_out[head, j, 0] = full[:, j * 128:(j + 1) * 128]


def owner_of(away, across, info):
    return ((across ^ info[2]) << 1) | (away ^ info[3])


def project(near, far, weight, bias, info):
    _, _, zs, stretch, width = near.shape
    local = 2 * zs * stretch
    spans = 512 // (2 * stretch)
    halves = local // 512
    spans_of_rows = local // 128
    per = spans_of_rows // halves
    block = (1, 2, spans, stretch, width)
    q, k, v, sizes = pl.pallas_call(
        functools.partial(qkv_kernel, stretch, spans),
        grid_spec=pltpu.PrefetchScalarGridSpec(
            num_scalar_prefetch=1, grid=(2, 2, halves),
            in_specs=[
                pl.BlockSpec(block, lambda a, o, h, n: (jnp.where(a == 0, o, 1), 0, jnp.where(a == 0, h, halves - 1), 0, 0)),
                pl.BlockSpec(block, lambda a, o, h, n: (jnp.where(a == 0, 0, o), 0, jnp.where(a == 0, 0, h), 0, 0)),
                pl.BlockSpec((8, width // 8, 384), lambda a, o, h, n: (0, 0, n[1])),
                pl.BlockSpec((1, 384), lambda a, o, h, n: (0, 0)),
            ],
            out_specs=[
                pl.BlockSpec((2, 1, HD, 512), lambda a, o, h, n: (0, owner_of(a, o, n), 0, h)),
                pl.BlockSpec((2, per, 1, 128, 128), lambda a, o, h, n: (0, h, o ^ n[2], a ^ n[3], 0)),
                pl.BlockSpec((2, per, 1, 128, 128), lambda a, o, h, n: (0, h, o ^ n[2], 0, a ^ n[3])),
                pl.BlockSpec((1, 1, 1, 128), lambda a, o, h, n: (owner_of(a, o, n), h, 0, 0)),
            ],
            scratch_shapes=[pltpu.VMEM((512, width), bf16)]),
        out_shape=[
            jax.ShapeDtypeStruct((2, 4, HD, local), bf16),
            jax.ShapeDtypeStruct((2, spans_of_rows, 2, CH, 128), bf16),
            jax.ShapeDtypeStruct((2, spans_of_rows, 2, 128, CH), bf16),
            jax.ShapeDtypeStruct((4, halves, 1, 128), f32),
        ],
        compiler_params=pltpu.CompilerParams(vmem_limit_bytes=40 << 20),
        name="qkv",
        cost_estimate=cost(4 * near.size * 384, near.size * 8),
    )(info, near, far, weight, bias)
    return q, k.reshape(2, -1, CH, 128), v.reshape(2, -1, 128, CH), sizes


def step_on(q, j, count):
    last = j + 1 == count
    return jnp.where(last, q + 1, q), jnp.where(last, 0, j + 1)


def assemble(ref, part, shared, core):
    if not shared:
        return jnp.concatenate([ref[0, 2 * part], ref[0, 2 * part + 1]], axis=1)
    at = pl.multiple_of(core * 512, 512)
    return jnp.concatenate([ref[0, n, :, pl.ds(at, 512)] for n in range(4)], axis=1)


def fwd_kernel(shared, info, q_ref, k_ref, v_ref, size_ref, held_ref, out_ref, lse_ref, acc, probs, qa, shifts):
    count = info[4]
    parts = 1 if shared else 2
    lane = lax.broadcasted_iota(jnp.int32, (1, 128), 1)
    sizes = functools.reduce(jnp.maximum, [size_ref[o, h] for o in range(size_ref.shape[0]) for h in range(size_ref.shape[1])])
    widest = jnp.sqrt(jnp.max(jnp.where(lane == int(shared), sizes, 0.0), axis=1, keepdims=True))

    for part in range(parts):
        q_t = assemble(q_ref, part, shared, info[3])
        wide = q_t.astype(f32)
        shift = jnp.sqrt(jnp.sum(wide * wide, axis=0, keepdims=True)) * widest
        shifts[part] = shift
        qa[part] = with_shift(q_t, shift).astype(bf16)

    def raised(part, j):
        return jnp.exp2(dg(k_ref[0, j], qa[part], 1, 0)).astype(bf16)

    probs[0] = raised(0, 0)

    def body(t, carry):
        part, j = carry
        now = t & 1
        part_next, j_next = step_on(part, j, count)
        before = jnp.where(j == 0, 0.0, acc[...])
        acc[...] = before + dg(v_ref[0, j], probs[now], 1, 0)
        probs[1 - now] = raised(jnp.minimum(part_next, parts - 1), j_next)

        @pl.when(j + 1 == count)
        def _():
            total = acc[HD:HD + 1]
            fine = (jnp.min(total) > 2.0 ** -90) & (jnp.max(total) < 2.0 ** 60)

            @pl.when(jnp.logical_not(fine))
            def _():
                plain = qa[part].astype(f32)
                row = lax.broadcasted_iota(jnp.int32, plain.shape, 0)
                qa[part] = jnp.where((row >= HD) & (row < HD + 3), 0.0, plain).astype(bf16)

                def peak(i, top):
                    return jnp.maximum(top, jnp.max(dg(k_ref[0, i], qa[part], 1, 0), axis=0, keepdims=True))
                shift = lax.fori_loop(0, count, peak, jnp.full((1, BQ), FAR, f32))
                shifts[part] = shift
                qa[part] = with_shift(plain[:HD], shift).astype(bf16)
                acc[...] = jnp.zeros_like(acc)

                def again(i, carry):
                    acc[...] += dg(v_ref[0, i], raised(part, i), 1, 0)
                    return carry
                lax.fori_loop(0, count, again, 0)

            total = acc[HD:HD + 1]
            mixed = (acc[:HD] * (1.0 / total)).astype(bf16)
            lse_ref[part] = shifts[part] + jnp.log2(total)
            if shared:
                for n in range(4):
                    out_ref[0, n] = mixed[:, n * 512:(n + 1) * 512]
            else:
                for n in range(2):
                    out_ref[0, 2 * part + n] = mixed[:, n * 1024:(n + 1) * 1024]
        return part_next, j_next

    lax.fori_loop(0, parts * count, body, (0, 0))


def head_spec(shared, *dims):
    zeros = (0,) * len(dims)
    return pl.BlockSpec((1,) + dims, lambda i, n: (int(shared),) + zeros)


def whole_spec(*dims):
    return pl.BlockSpec(dims, lambda i, n: (0,) * len(dims))


def cost(flops, moved, exps=0):
    return pl.CostEstimate(flops=int(flops), bytes_accessed=int(moved), transcendentals=int(exps))


def attend_forward(shared, seq, q, k, v, sizes, info, held):
    _, owners, _, local = q.shape
    chunks = k.shape[1]
    wide = local // 2 if shared else local
    parts = owners * wide // BQ
    pairs = parts * BQ * chunks * CH * 0.6
    shape = jax.ShapeDtypeStruct((2, owners, HD, wide), bf16)
    first = held is None
    if first:
        kernel = lambda info, q, k, v, size, *rest: fwd_kernel(shared, info, q, k, v, size, None, *rest)
    else:
        kernel = functools.partial(fwd_kernel, shared)
    return pl.pallas_call(
        kernel,
        grid_spec=pltpu.PrefetchScalarGridSpec(
            num_scalar_prefetch=1, grid=(1,),
            in_specs=[
                head_spec(shared, owners, HD, local), head_spec(shared, chunks, CH, 128), head_spec(shared, chunks, 128, CH),
                whole_spec(*sizes.shape),
            ] + ([] if first else [pl.BlockSpec(memory_space=pl.ANY)]),
            out_specs=[pl.BlockSpec((1, owners, HD, wide), lambda i, n: (seq, 0, 0, 0)), whole_spec(parts, 1, BQ)],
            scratch_shapes=[
                pltpu.VMEM((128, BQ), f32), pltpu.VMEM((2, CH, BQ), bf16), pltpu.VMEM((parts, 128, BQ), bf16),
                pltpu.VMEM((parts, 1, BQ), f32),
            ]),
        out_shape=[shape, jax.ShapeDtypeStruct((parts, 1, BQ), f32)],
        input_output_aliases={} if first else {5: 0},
        compiler_params=pltpu.CompilerParams(vmem_limit_bytes=48 << 20),
        cost_estimate=cost(pairs * 1024, chunks * CH * 512, pairs),
        name="attend_forward_shared" if shared else "attend_forward_own",
    )(*((info, q, k, v, sizes) + (() if first else (held,))))


def bwd_kernel(shared, first, info, q_ref, k_ref, v_ref, lse_ref, out_ref, gout_ref, *rest):
    rest = rest if first else rest[3 if shared else 1:]
    if shared:
        dq_ref, kept_ref, given_ref, dk_acc, dv_acc, dq_acc, qa, qat, ga, gat, pb, db = rest
    else:
        dqkv_ref, dk_acc, dv_acc, dq_acc, qa, qat, ga, gat, pb, db = rest
    count = info[4]
    chunks = k_ref.shape[1]
    parts = 1 if shared else 2
    dk_acc[...] = jnp.zeros_like(dk_acc)
    dv_acc[...] = jnp.zeros_like(dv_acc)

    def piece(ref, part):
        return jnp.concatenate([ref[0, n] for n in (range(4) if shared else (2 * part, 2 * part + 1))], axis=1)

    for part in range(parts):
        q_full = with_shift(assemble(q_ref, part, shared, info[3]), lse_ref[part])
        qat[part] = q_full.astype(bf16)
        qa[part] = q_full.T.astype(bf16)
        g_t = piece(gout_ref, part)
        meet = jnp.sum(g_t.astype(f32) * piece(out_ref, part).astype(f32), axis=0, keepdims=True)
        g_full = with_shift(g_t, meet)
        gat[part] = g_full.astype(bf16)
        ga[part] = g_full.T.astype(bf16)

    def ahead(part, j, slot):
        raised = jnp.exp2(dg(qa[part], k_ref[0, j], 1, 1))
        pb[slot] = raised.astype(bf16)
        db[slot] = (raised * dg(ga[part], v_ref[0, j], 1, 0)).astype(bf16)

    ahead(0, 0, 0)

    def body(t, carry):
        part, j = carry
        now = t & 1
        part_next, j_next = step_on(part, j, count)
        dv_acc[j] += dg(gat[part], pb[now], 1, 0)[:HD]
        dk_acc[j] += dg(qat[part], db[now], 1, 0)[:HD]
        before = jnp.where(j == 0, 0.0, dq_acc[...])
        dq_acc[...] = before + dg(db[now], k_ref[0, j], 1, 0)
        ahead(jnp.minimum(part_next, parts - 1), j_next, 1 - now)

        @pl.when(j + 1 == count)
        def _():
            dq_t = (dq_acc[...] * 0.125).T[:HD].astype(bf16)
            if shared:
                for n in range(4):
                    dq_ref[0, n, :, :512] = dq_t[:32, n * 512:(n + 1) * 512]
                    dq_ref[0, n, :, 512:] = dq_t[32:, n * 512:(n + 1) * 512]
            else:
                for n in range(2):
                    dqkv_ref[0, 2 * part + n, 0] = dq_t[:, n * 1024:(n + 1) * 1024]
        return part_next, j_next

    lax.fori_loop(0, parts * count, body, (0, 0))
    for block in range(chunks):
        j, across = block // 2, block % 2
        for owner in (2 * across, 2 * across + 1):
            cols = slice((owner - 2 * across) * 128, (owner - 2 * across + 1) * 128)
            dk_wide, dv_wide = dk_acc[block, :, cols] * LN2, dv_acc[block, :, cols]
            dk, dv = dk_wide.astype(bf16), dv_wide.astype(bf16)
            if shared:
                here = info[3] == 0
                kept_ref[0, owner, :, j * 128:(j + 1) * 128] = jnp.where(here, dk_wide, dv_wide).astype(bf16)
                given_ref[0, owner, :, j * 128:(j + 1) * 128] = jnp.where(here, dv_wide, dk_wide).astype(bf16)
            else:
                dqkv_ref[0, owner, 1, :, j * 128:(j + 1) * 128] = dk
                dqkv_ref[0, owner, 2, :, j * 128:(j + 1) * 128] = dv


def attend_backward(shared, seq, q, k, v, lse, out, g_out, info, held):
    _, owners, _, local = q.shape
    chunks = k.shape[1]
    wide = out.shape[3]
    parts = owners * wide // BQ
    pairs = parts * BQ * chunks * CH * 0.6
    shape = jax.ShapeDtypeStruct
    first = held is None
    if shared:
        out_specs = [pl.BlockSpec((1, owners, rows, local), lambda i, n: (seq, 0, 0, 0)) for rows in (32, HD, HD)]
        out_shape = [shape((2, owners, rows, local), bf16) for rows in (32, HD, HD)]
    else:
        out_specs = [pl.BlockSpec((1, owners, 3, HD, local), lambda i, n: (seq, 0, 0, 0, 0))]
        out_shape = [shape((2, owners, 3, HD, local), bf16)]
    kept = () if first else tuple(held)
    of_seq = pl.BlockSpec((1, owners, HD, wide), lambda i, n: (seq, 0, 0, 0))
    return pl.pallas_call(
        functools.partial(bwd_kernel, shared, first),
        grid_spec=pltpu.PrefetchScalarGridSpec(
            num_scalar_prefetch=1, grid=(1,),
            in_specs=[
                head_spec(shared, owners, HD, local), head_spec(shared, chunks, CH, 128), head_spec(shared, chunks, 128, CH),
                whole_spec(parts, 1, BQ), of_seq, of_seq,
            ] + [pl.BlockSpec(memory_space=pl.ANY)] * len(kept),
            out_specs=out_specs,
            scratch_shapes=[
                pltpu.VMEM((chunks, HD, CH), f32), pltpu.VMEM((chunks, HD, CH), f32), pltpu.VMEM((BQ, 128), f32),
                pltpu.VMEM((parts, BQ, 128), bf16), pltpu.VMEM((parts, 128, BQ), bf16),
                pltpu.VMEM((parts, BQ, 128), bf16), pltpu.VMEM((parts, 128, BQ), bf16),
                pltpu.VMEM((2, BQ, CH), bf16), pltpu.VMEM((2, BQ, CH), bf16),
            ]),
        out_shape=out_shape,
        input_output_aliases={7 + n: n for n in range(len(kept))},
        compiler_params=pltpu.CompilerParams(vmem_limit_bytes=56 << 20),
        cost_estimate=cost(pairs * 100, chunks * CH * 2048),
        name="attend_backward_shared" if shared else "attend_backward_own",
    )(info, q, k, v, lse, out, g_out, *kept)


def gelu_pair(u):
    half = 0.5 * (1.0 + lax.erf(u * 0.7071067811865476))
    return u * half, half + u * (0.3989422804014327 * jnp.exp2(u * u * (-0.5 * LOG2E)))


def norm_stats(v):
    mean = jnp.mean(v, axis=-1, keepdims=True)
    centred = v - mean
    inverse = lax.rsqrt(jnp.mean(centred * centred, axis=-1, keepdims=True) + 1e-12)
    return centred * inverse, inverse


def norm_back(grad, xhat, inverse, gain):
    g = grad * gain
    return (g - jnp.mean(g, axis=-1, keepdims=True) - xhat * jnp.mean(g * xhat, axis=-1, keepdims=True)) * inverse


def weight_part(ref, first, rows):
    part = ref[:, first:first + rows, :]
    return part.reshape(part.shape[0] * rows, part.shape[2])


def ffn_kernel(spans, info, x_ref, own_ref, sh_ref, cot_ref, w_ref, bin_ref, vec_ref,
               act_out, resid_out, gown_out, gsh_out, active_out, dinner_out, normed_out, douter_out, dbranch_out,
               vec_sum, bin_sum, slope, row_block):
    step = pl.program_id(0)
    load_rows(row_block, x_ref, spans, info[1])
    count = row_block.shape[0] // PARTS
    vec = vec_ref[...]
    total = lambda a: jnp.sum(a, axis=0, keepdims=True)
    held = [{"at": slice(n * count, (n + 1) * count)} for n in range(PARTS)]

    def branch(h):
        at = h["at"]
        mixed_t = jnp.concatenate(
            [part for p in range(4) for part in (own_ref[p, 0, :, at], sh_ref[p, 0, :, at], own_ref[p, 1, :, at])], axis=0)
        h["sum1"] = row_block[at].astype(f32) + (dg(mixed_t, weight_part(w_ref, 768, 96), 0, 0) + vec[0:1])

    def first_norm(h):
        h["xhat1"], h["inv1"] = norm_stats(h["sum1"])
        normed = h["xhat1"] * vec[1:2] + vec[2:3]
        normed_out[h["at"]] = normed.astype(bf16)
        h["outer"] = normed + vec[3:4]

    def widen(h):
        at = h["at"]
        for n in range(4):
            cols = slice(n * 768, (n + 1) * 768)
            value, bend = gelu_pair(dg(normed_out[at], weight_part(w_ref, 384 + 96 * n, 96), 1, 0) + bin_ref[:, cols])
            active_out[at, cols] = value.astype(bf16)
            slope[at, cols] = bend.astype(bf16)

    def narrow(h):
        h["outer"] = h["outer"] + dg(active_out[h["at"]], weight_part(w_ref, 0, 384), 1, 0)

    def second_norm(h):
        at = h["at"]
        xhat2, inv2 = norm_stats(h["outer"])
        act_out[at] = (xhat2 * vec[4:5] + vec[5:6]).astype(bf16)
        cot = cot_ref[at].astype(f32)
        d2 = norm_back(cot, xhat2, inv2, vec[4:5])
        d_outer = d2.astype(bf16)
        douter_out[at] = d_outer
        h["d_normed"] = d2
        h["sums"] = [total(d_outer.astype(f32)), total(cot * xhat2), total(cot)]

    def back(h):
        at = h["at"]
        h["inner_sums"] = []
        for n in range(4):
            cols = slice(n * 768, (n + 1) * 768)
            d_active = dg(douter_out[at], weight_part(w_ref.at[2 * n:2 * n + 2], 0, 384), 1, 1)
            d_inner = (d_active * slope[at, cols].astype(f32)).astype(bf16)
            dinner_out[at, cols] = d_inner
            h["inner_sums"].append(total(d_inner.astype(f32)))
            h["d_normed"] = h["d_normed"] + dg(d_inner, weight_part(w_ref, 384 + 96 * n, 96), 1, 1)

    def first_back(h):
        at = h["at"]
        d_normed = h["d_normed"]
        d1 = norm_back(d_normed, h["xhat1"], h["inv1"], vec[1:2])
        resid_out[at] = d1
        d_branch = d1.astype(bf16)
        dbranch_out[at] = d_branch
        h["sums"] = [total(d_branch.astype(f32)), total(d_normed * h["xhat1"]), total(d_normed)] + h["sums"]

    def mix_back(h):
        at = h["at"]
        g_t = dg(weight_part(w_ref, 768, 96), dbranch_out[at], 1, 1).astype(bf16)
        for p in range(4):
            gown_out[p, 0, :, at] = g_t[192 * p:192 * p + 64]
            gsh_out[p, 0, :, at] = g_t[192 * p + 64:192 * p + 128]
            gown_out[p, 1, :, at] = g_t[192 * p + 128:192 * p + 192]

    for products, norm in ((branch, first_norm), (widen, None), (narrow, second_norm), (back, first_back), (mix_back, None)):
        for h in held:
            products(h)
            if norm is not None:
                norm(h)
    sums = jnp.concatenate([
        functools.reduce(jnp.add, [h["sums"][n] for h in held]) for n in range(6)] + [jnp.zeros((2, vec.shape[1]), f32)], axis=0)
    inner_sums = [functools.reduce(jnp.add, [h["inner_sums"][n] for h in held]) for n in range(4)]

    @pl.when(step == 0)
    def _():
        vec_sum[...] = sums
        for n in range(4):
            bin_sum[:, n * 768:(n + 1) * 768] = inner_sums[n]

    @pl.when(step > 0)
    def _():
        vec_sum[...] += sums
        for n in range(4):
            bin_sum[:, n * 768:(n + 1) * 768] += inner_sums[n]


def feed_forward(rows_in, own, sh, cotangent, weights, inner_bias, vectors, info):
    _, _, _, stretch, width = rows_in.shape
    local = cotangent.shape[0]
    spans = FB // (2 * stretch)
    steps = local // FB
    half_steps = steps // 2
    wide = inner_bias.shape[1]
    rows = lambda n: pl.BlockSpec((FB, n), lambda r, a: (r, 0))
    fixed = lambda *dims: pl.BlockSpec(dims, lambda r, a: (0,) * len(dims))
    own_spec = pl.BlockSpec((4, 2, HD, FB), lambda r, a: (0, 0, 0, r))
    sh_spec = pl.BlockSpec((4, 1, HD, FB), lambda r, a: (0, r // half_steps, 0, r % half_steps))
    shape = jax.ShapeDtypeStruct
    return pl.pallas_call(
        functools.partial(ffn_kernel, spans),
        grid_spec=pltpu.PrefetchScalarGridSpec(
            num_scalar_prefetch=1, grid=(steps,),
            in_specs=[
                pl.BlockSpec((1, 2, spans, stretch, width), lambda r, a: (0, 0, r, 0, 0)),
                own_spec, sh_spec, rows(width),
                pl.BlockSpec(weights.shape, lambda r, a: (0, 0, 0), pipeline_mode=pl.Buffered(1)),
                fixed(1, wide), fixed(8, width),
            ],
            out_specs=[
                rows(width), rows(width), own_spec, sh_spec, rows(wide), rows(wide), rows(width), rows(width), rows(width),
                fixed(8, width), fixed(1, wide),
            ],
            scratch_shapes=[pltpu.VMEM((FB, wide), bf16), pltpu.VMEM((FB, width), bf16)]),
        out_shape=[
            shape((local, width), bf16), shape((local, width), f32), shape(own.shape, bf16), shape(sh.shape, bf16),
            shape((local, wide), bf16), shape((local, wide), bf16), shape((local, width), bf16),
            shape((local, width), bf16), shape((local, width), bf16), shape((8, width), f32), shape((1, wide), f32),
        ],
        compiler_params=pltpu.CompilerParams(vmem_limit_bytes=60 << 20),
        name="feed_forward",
        cost_estimate=cost(local * width * (width + 2 * wide) * 4, local * wide * 20),
    )(info, rows_in, own, sh, cotangent, weights, inner_bias, vectors)


def outer_grad_kernel(scale, active_ref, douter_ref, out_ref):
    made = (dg(active_ref[...], douter_ref[...], 0, 0) * scale).astype(bf16)
    out_ref[...] = made.reshape(out_ref.shape)


def inner_grad_kernel(scale, packed_ref, normed_ref, dinner_ref, own_ref, sh_ref, dbranch_ref, out_ref):
    step = pl.program_id(0)

    @pl.when(step < 4)
    def _():
        out_ref[...] = (dg(normed_ref[...], dinner_ref[...], 0, 0) * scale).astype(bf16).reshape(out_ref.shape)

    @pl.when(step == 4)
    def _():
        mixed_t = jnp.concatenate([
            part for p in range(4)
            for part in (own_ref[p, 0], jnp.concatenate([sh_ref[p, 0], sh_ref[p, 1]], axis=1), own_ref[p, 1])], axis=0)
        out_ref[...] = (dg(mixed_t, dbranch_ref[...], 1, 0) * scale).astype(bf16).reshape(out_ref.shape)


def weight_grads(scale, active, d_outer, normed, d_inner, own, sh, d_branch):
    local, wide = active.shape
    width = normed.shape[1]
    packed = pl.pallas_call(
        functools.partial(outer_grad_kernel, scale), grid=(4,),
        in_specs=[pl.BlockSpec((local, width), lambda m: (0, m)), pl.BlockSpec((local, width), lambda m: (0, 0))],
        out_specs=pl.BlockSpec((2, 384, width), lambda m: (m, 0, 0)),
        out_shape=jax.ShapeDtypeStruct((8, 896, width), bf16),
        compiler_params=pltpu.CompilerParams(vmem_limit_bytes=40 << 20), name="outer_grad",
        cost_estimate=cost(2 * local * wide * width, 2 * wide * (local + width)),
    )(active, d_outer)
    fixed = lambda a: pl.BlockSpec(a.shape, lambda n: (0,) * a.ndim)
    return pl.pallas_call(
        functools.partial(inner_grad_kernel, scale), grid=(5,),
        in_specs=[
            pl.BlockSpec(memory_space=pl.ANY), fixed(normed),
            pl.BlockSpec((local, width), lambda n: (0, jnp.minimum(n, 3))), fixed(own), fixed(sh), fixed(d_branch)],
        out_specs=pl.BlockSpec((8, 96, width), lambda n: (0, 4 + n, 0)),
        out_shape=jax.ShapeDtypeStruct((8, 896, width), bf16), input_output_aliases={0: 0},
        compiler_params=pltpu.CompilerParams(vmem_limit_bytes=40 << 20), name="inner_grad",
        cost_estimate=cost(2 * local * (wide + width) * width, 2 * (wide + width) * (local + width)),
    )(packed, normed, d_inner, own, sh, d_branch)


def head_grad_kernel(scale, spans, info, *refs):
    x_refs, (own_ref, dq_ref, kept_ref, given_ref, out_ref, bias_out, acc, bias_acc, rows) = refs[:4], refs[4:]
    seq, away, half = pl.program_id(0), pl.program_id(1), pl.program_id(3)
    last = (seq == 1) & (away == 1) & (pl.program_id(2) == 1) & (half == pl.num_programs(3) - 1)
    for n in range(4):
        @pl.when(seq * 2 + away == n)
        def _(n=n):
            load_rows(rows, x_refs[n], spans, info[1])
    dq_t = jnp.where(half == info[3], jnp.concatenate([dq_ref[0, 0, :, :512], dq_ref[0, 0, :, 512:]], axis=0).astype(f32), 0.0)
    kept, given = kept_ref[0, 0].astype(f32), given_ref[0, 0].astype(f32)
    here = info[3] == 0
    d_t = jnp.concatenate([
        own_ref[0, 0, 0], dq_t.astype(bf16), own_ref[0, 0, 1], jnp.where(here, kept, given).astype(bf16),
        own_ref[0, 0, 2], jnp.where(here, given, kept).astype(bf16)], axis=0)

    @pl.when((seq == 0) & (away == 0) & (pl.program_id(2) == 0) & (half == 0))
    def _():
        acc[...] = jnp.zeros_like(acc)
        bias_acc[...] = jnp.zeros_like(bias_acc)
    acc[...] += dg(d_t, rows[...], 1, 0)
    bias_acc[...] += dg(jnp.ones((8, d_t.shape[1]), bf16), d_t, 1, 1)

    @pl.when(last)
    def _():
        out_ref[...] = (acc[...] * scale).T.astype(bf16)
        bias_out[...] = bias_acc[...] * scale


def head_grads(scale, sources, dqkv_own, dq_sh, kept, given, info):
    _, _, zs, stretch, width = sources[0].shape
    local = 2 * zs * stretch
    spans = 512 // (2 * stretch)
    halves = local // 512

    def source_spec(n):
        def index(s, a, o, h, i):
            now = 2 * s + a
            across = jnp.where(now == n, o, jnp.where(now < n, 0, 1))
            return (across, 0, jnp.where(now == n, h, jnp.where(now < n, 0, halves - 1)), 0, 0)
        return pl.BlockSpec((1, 2, spans, stretch, width), index)
    return pl.pallas_call(
        functools.partial(head_grad_kernel, scale, spans),
        grid_spec=pltpu.PrefetchScalarGridSpec(
            num_scalar_prefetch=1, grid=(2, 2, 2, halves),
            in_specs=[source_spec(n) for n in range(4)] + [
                pl.BlockSpec((1, 1, 3, HD, 512), lambda s, a, o, h, i: (s, owner_of(a, o, i), 0, 0, h)),
                pl.BlockSpec((1, 1, 32, local), lambda s, a, o, h, i: (s, owner_of(a, o, i), 0, 0)),
            ] + [pl.BlockSpec((1, 1, HD, 512), lambda s, a, o, h, i: (s, owner_of(a, o, i), 0, h))] * 2,
            out_specs=[pl.BlockSpec((width, 384), lambda s, a, o, h, i: (0, 0)), pl.BlockSpec((8, 384), lambda s, a, o, h, i: (0, 0))],
            scratch_shapes=[pltpu.VMEM((384, width), f32), pltpu.VMEM((8, 384), f32), pltpu.VMEM((512, width), bf16)]),
        out_shape=[jax.ShapeDtypeStruct((width, 384), bf16), jax.ShapeDtypeStruct((8, 384), f32)],
        compiler_params=pltpu.CompilerParams(vmem_limit_bytes=40 << 20), name="head_grads",
        cost_estimate=cost(8 * local * 768 * width, 8 * local * width * 2),
    )(info, *sources, dqkv_own, dq_sh, kept, given)


def token_grad_kernel(half, own_ref, low_ref, high_ref, dkv_ref, w_ref, resid_ref, out_ref):
    total = resid_ref[...]
    for kind in range(3):
        made = []
        for p in range(4):
            if kind == 0:
                middle = jnp.concatenate([low_ref[p, 0], high_ref[p, 0]], axis=0)
            else:
                middle = jnp.concatenate([dkv_ref[p, kind - 1, n] for n in range(2)], axis=0)
            made += [own_ref[p, 0, kind], middle, own_ref[p, 1, kind]]
        rows = out_ref.shape[1]
        weight = w_ref[half * 4:half * 4 + 4, 96 * kind:96 * kind + 96].reshape(rows, w_ref.shape[2])
        total = total + dg(jnp.concatenate(made, axis=0), weight, 0, 1)
    out_ref[...] = total.astype(bf16)


def token_grad(half, own, shared, weights, resid):
    local, width = resid.shape
    part = width // 2
    steps = local // RB
    half_steps = steps // 2
    return pl.pallas_call(
        functools.partial(token_grad_kernel, half), grid=(steps,),
        in_specs=[
            pl.BlockSpec((4, 2, 3, HD, RB), lambda r: (0, 0, 0, 0, r)),
            pl.BlockSpec((4, 1, None, 32, RB), lambda r: (0, r // half_steps, 2, 0, r % half_steps)),
            pl.BlockSpec((4, 1, None, 32, RB), lambda r: (0, r // half_steps, 2, 0, half_steps + r % half_steps)),
            pl.BlockSpec((4, 2, 2, 32, RB), lambda r: (0, 0, 0, 0, r)),
            pl.BlockSpec(weights.shape, lambda r: (0, 0, 0)), pl.BlockSpec((RB, part), lambda r: (r, half))],
        out_specs=pl.BlockSpec((RB, part), lambda r: (r, 0)), out_shape=jax.ShapeDtypeStruct((local, part), bf16),
        compiler_params=pltpu.CompilerParams(vmem_limit_bytes=60 << 20), name="token_grad",
        cost_estimate=cost(local * width * width * 3, local * width * 10),
    )(own, shared, shared, shared, weights, resid)


SWAP = [(0, 1), (1, 0)]
PAIR = ("x", "y", "c")
ALL = ("z", "x", "y", "c")
SHARD = ("z", "x")


def canonical(packed, shards):
    if shards == 8:
        return packed
    width = packed.shape[2]
    per, keep = 96 * 8 // shards, shards // 8
    outer = packed[:, :4 * per].reshape(8, 384, width)
    inner = packed[:, 4 * per:8 * per].reshape(8, keep, 4, per, width).transpose(0, 2, 1, 3, 4).reshape(8, 384, width)
    output = packed[:, 8 * per:9 * per].reshape(8, 96, width)
    return jnp.concatenate([outer, inner, output, jnp.zeros((8, 32, width), packed.dtype)], axis=1)


def from_canonical(packed, last, shards):
    width = packed.shape[2]
    if shards == 8:
        return packed.at[:, 864:].set(jnp.broadcast_to(last[None], (8, 32, width)))
    per, keep = 96 * 8 // shards, shards // 8
    outer = packed[:, :384].reshape(shards, 4 * per, width)
    inner = packed[:, 384:768].reshape(8, 4, keep, per, width).transpose(0, 2, 1, 3, 4).reshape(shards, 4 * per, width)
    output = packed[:, 768:864].reshape(shards, per, width)
    return jnp.concatenate([outer, inner, output, jnp.broadcast_to(last[None], (shards, 32, width))], axis=1)


def canonical_heads(packed, shards, parts):
    if shards == 8:
        return packed
    width = packed.shape[2]
    per = 96 * 8 // shards
    made = [packed[:, k * per:(k + 1) * per].reshape(8, 96, width) for k in range(parts)]
    return jnp.concatenate(made + [jnp.zeros((8, 32, width), packed.dtype)], axis=1)


def quarter(rows):
    place = lax.axis_index("y") * 2 + lax.axis_index("c")
    part = rows.shape[0] // 4
    return lax.dynamic_slice_in_dim(rows, place * part, part)


def flipped(array, axis, here):
    return jnp.where(here == 0, array, jnp.flip(array, axis))


def body(tokens, lengths, deal_order, w_query, w_key, w_value, w_output, b_query, b_value, b_output,
         ln1_gain, ln1_shift, w_inner, b_inner, w_outer, b_outer, ln2_gain, ln2_shift, cotangent):
    tie = lax.optimization_barrier
    zs = lax.axis_size("z")
    shards = 2 * zs
    scale = 1.0 / (shards * 4)
    seq_count, _, stretch, width = tokens.shape
    per = w_query.shape[0]
    half = zs // 2
    x, y, c = lax.axis_index("x"), lax.axis_index("y"), lax.axis_index("c")

    def deal(ordered):
        return lax.all_to_all(ordered, "z", split_axis=0, concat_axis=0, tiled=True)

    def corner(across, along):
        return [lax.ppermute(across[:half], "y", SWAP), lax.ppermute(along[half:], "x", SWAP)]

    def this_core(own, across, along, corner):
        return jnp.concatenate([own, across, along] + corner, axis=0).reshape(2, 2, zs, stretch, width)

    ordered_a = jnp.take(tokens[:, 0], deal_order[0::2], axis=0)
    first_own = deal(ordered_a)
    (_, tokens, w_query, w_key, w_value, b_query, b_value, w_outer, w_inner, w_output, b_inner, deal_order) = tie(
        (ordered_a, tokens, w_query, w_key, w_value, b_query, b_value, w_outer, w_inner, w_output, b_inner, deal_order))
    ordered_b = jnp.take(tokens[:, 0], deal_order[1::2], axis=0)

    def head_columns(matrix):
        heads = matrix.reshape(per, 2, 2, 3, HD)
        mine = lax.dynamic_index_in_dim(heads, y, axis=2, keepdims=False)
        own = lax.dynamic_index_in_dim(mine, 2 * c, axis=2, keepdims=False)
        return [own, mine[:, :, 1]]
    pad = lambda v: jnp.pad(v, (0, width - v.shape[0]))[None]
    columns = jnp.concatenate(
        [col for matrix in (w_query, w_key, w_value) for col in head_columns(matrix)], axis=2).reshape(per, width)
    head_pack = jnp.concatenate([columns, pad(b_query), pad(b_value), jnp.zeros((14, width), bf16)], axis=0)
    vectors = (b_output, ln1_gain, ln1_shift, b_outer, ln2_gain, ln2_shift)
    layer_pack = jnp.concatenate(
        [w_outer] + [w_inner[:, n * width:(n + 1) * width] for n in range(4)] + [w_output]
        + [pad(b_inner)] + [pad(v) for v in vectors] + [jnp.zeros((25, width), bf16)], axis=0)
    layer_quarter = quarter(layer_pack)
    back_quarter = quarter(jnp.concatenate([w_query, w_key, w_value, jnp.zeros((32, width), bf16)], axis=0))
    first_own, ordered_b, head_pack, layer_quarter, back_quarter = tie(
        (first_own, ordered_b, head_pack, layer_quarter, back_quarter))
    head_all = lax.all_gather(head_pack, SHARD, axis=0, tiled=False)
    head_weight = canonical_heads(head_all, shards, 1)

    def head_bias(row):
        heads = head_all[:, per + row, :per].reshape(2, 2, 3, HD)
        mine = lax.dynamic_slice(heads, (x, y, 0, 0), (1, 1, 3, HD))[0, 0]
        return [lax.dynamic_index_in_dim(mine, 2 * c, axis=0, keepdims=False), mine[1]]
    bias_row = jnp.concatenate(head_bias(0) + [jnp.zeros((2 * HD,), bf16)] + head_bias(1)).astype(f32)[None]

    across_a, along_a = lax.ppermute(first_own, "x", SWAP), lax.ppermute(first_own, "y", SWAP)
    second_own = deal(ordered_b)
    across_a, along_a, second_own = tie((across_a, along_a, second_own))
    corner_a = corner(across_a, along_a)
    second_own, *corner_a = tie((second_own, *corner_a))
    near_a = this_core(first_own, across_a, along_a, corner_a)
    far_a = lax.ppermute(near_a, "c", SWAP)
    across_b, along_b = lax.ppermute(second_own, "x", SWAP), lax.ppermute(second_own, "y", SWAP)

    layer_all = lax.all_gather(layer_quarter, ALL, axis=0, tiled=True).reshape(shards, 9 * per + 32, width)
    layer_weights = canonical(layer_all, shards)
    inner_bias = layer_all[:, 9 * per, :4 * per].reshape(1, 4 * width).astype(f32)
    vector_rows = jnp.concatenate(
        [layer_all[:, 9 * per + 1 + n, :per].reshape(1, width) for n in range(6)] + [jnp.zeros((2, width), bf16)],
        axis=0).astype(f32)
    back_all = lax.all_gather(back_quarter, ALL, axis=0, tiled=True).reshape(shards, 3 * per + 32, width)

    slots = lax.dynamic_slice_in_dim(deal_order, lax.axis_index("z") * 2, 2)
    matches = slots[:, None] == jnp.arange(seq_count, dtype=jnp.int32)[None, :]
    lens = jnp.sum(jnp.where(matches, lengths[None, :], 0), axis=1).astype(jnp.int32)
    last = (lens + 511) // 512 - 1
    counts = 2 * last + 1 + (lens > 512 * last + 2 * stretch).astype(jnp.int32)
    infos = [jnp.stack([lens[n], x, y, c, counts[n]]).astype(jnp.int32) for n in range(2)]

    def swap(array):
        flat = array.reshape((8,) + array.shape[2:])
        return lax.all_to_all(flat, PAIR, split_axis=0, concat_axis=0, tiled=True)

    def to_tokens(array):
        return swap(array).reshape((4, 2) + array.shape[2:])

    def to_heads(array):
        return swap(array).reshape((2, 4) + array.shape[2:])

    heads_a = project(near_a, far_a, head_weight, bias_row, infos[0])
    heads_a, across_b, along_b = tie((heads_a, across_b, along_b))
    near_b = this_core(second_own, across_b, along_b, corner(across_b, along_b))
    own_first, lse_own_a = attend_forward(False, 0, *heads_a, infos[0], None)
    own_first, near_b = tie((own_first, near_b))
    far_b = lax.ppermute(near_b, "c", SWAP)
    heads_b = project(near_b, far_b, head_weight, bias_row, infos[1])
    own, lse_own_b = attend_forward(False, 1, *heads_b, infos[1], own_first)
    own_t = to_tokens(own)
    own, info_a, info_b = tie((own, *infos))
    sh_first, lse_sh_a = attend_forward(True, 0, *heads_a, info_a, None)
    sh, lse_sh_b = attend_forward(True, 1, *heads_b, info_b, sh_first)
    sh_sent, own_t = tie((sh, own_t))
    sh_t = to_tokens(sh_sent)
    mine_rows = jnp.where(x == 0, jnp.stack([first_own, across_a]), jnp.stack([second_own, across_b]))[None]

    (act, resid, g_own, g_sh, active, d_inner, normed, d_outer, d_branch, vec_sums, bin_sums) = feed_forward(
        mine_rows, own_t, sh_t, cotangent.reshape(-1, width), layer_weights, inner_bias, vector_rows, infos[0])
    g_own_h, g_sh_h = to_heads(g_own), to_heads(g_sh)
    active, back_all = tie((active, back_all))
    packed = weight_grads(scale, active, d_outer, normed, d_inner, own_t, sh_t, d_branch)
    sums = jnp.concatenate([bin_sums.reshape(4, width), vec_sums, jnp.zeros((20, width), f32)], axis=0) * scale
    ready = from_canonical(packed, sums.astype(bf16), shards)
    ready, g_own_h = tie((ready, g_own_h))
    back_weights = canonical_heads(back_all, shards, 3)
    layer_part = lax.psum_scatter(ready.reshape(-1, width), ("z", "x", "c"), scatter_dimension=0, tiled=True)

    qkv_a, qkv_b = heads_a[:3], heads_b[:3]
    first = attend_backward(False, 0, *qkv_a, lse_own_a, own, g_own_h, infos[0], None)
    dqkv_own, = attend_backward(False, 1, *qkv_b, lse_own_b, own, g_own_h, infos[1], first)
    back_own = to_tokens(dqkv_own)
    dqkv_own, info_a, info_b = tie((dqkv_own, *infos))
    first = attend_backward(True, 0, *qkv_a, lse_sh_a, sh, g_sh_h, info_a, None)
    dq_sh, kept, given = attend_backward(True, 1, *qkv_b, lse_sh_b, sh, g_sh_h, info_b, first)
    taken = lax.ppermute(given, "c", SWAP)
    shared_out = jnp.concatenate([(kept.astype(f32) + taken.astype(f32)).astype(bf16), dq_sh], axis=2)
    shared_out, back_own, dqkv_own = tie((shared_out, back_own, dqkv_own))
    back_shared = to_tokens(shared_out.reshape(2, 4, 3, 32, -1))
    d_heads, d_bias = head_grads(scale, (near_a, far_a, near_b, far_b), dqkv_own, dq_sh, kept, given, infos[0])

    head_ready = jnp.concatenate([
        d_heads.reshape(zs, 2, per, 384),
        jnp.broadcast_to(d_bias[:1].astype(bf16)[None, None], (zs, 2, 16, 384))], axis=2)
    head_ready, _, layer_part = tie((head_ready, back_shared, layer_part))
    head_sum = lax.psum_scatter(head_ready.reshape(-1, 384), "z", scatter_dimension=0, tiled=True)
    d_rows = [token_grad(n, back_own, back_shared, back_weights, resid).reshape(shards, stretch, -1) for n in range(2)]

    def give_back(rows):
        return lax.all_to_all(rows, SHARD, split_axis=0, concat_axis=0, tiled=True)
    returned = [give_back(d_rows[0])]
    head_sum, late_rows, returned[0] = tie((head_sum, d_rows[1], returned[0]))
    returned.append(give_back(late_rows))
    head_eight = lax.all_gather(head_sum, PAIR, axis=0, tiled=False).reshape(2, 2, 2, 2, per + 16, 6, HD)
    cores = lax.dynamic_index_in_dim(head_eight, x, axis=3, keepdims=False).astype(f32)
    layer_part, _ = tie((layer_part, d_rows[0]))
    layer_sum = (layer_part.astype(f32) + lax.ppermute(layer_part, "y", SWAP).astype(f32)).astype(bf16)
    def full(kind):
        joined = jnp.stack([cores[:, :, 0, :, 2 * kind], cores[:, :, 0, :, 2 * kind + 1] + cores[:, :, 1, :, 2 * kind + 1],
                            cores[:, :, 1, :, 2 * kind]], axis=2)
        return joined.transpose(3, 0, 1, 2, 4).reshape(per + 16, width)
    d_wq, d_wk, d_wv = (full(kind) for kind in range(3))
    place = lax.axis_index("z") * 2 + x
    own_slice = lambda row, n: lax.dynamic_slice_in_dim(row, place * n, n)
    d_bq, d_bv = own_slice(d_wq[per], per), own_slice(d_wv[per], per)
    d_wq, d_wk, d_wv = d_wq[:per], d_wk[:per], d_wv[:per]

    layer_grads = flipped(jnp.stack([layer_sum, lax.ppermute(layer_sum, "c", SWAP)]), 0, c)
    layer_grads = layer_grads.reshape(9 * per + 32, width).astype(f32)
    d_wouter = layer_grads[:4 * per]
    d_winner = jnp.concatenate([layer_grads[(4 + n) * per:(5 + n) * per] for n in range(4)], axis=1)
    d_woutput = layer_grads[8 * per:9 * per]
    d_binner = own_slice(layer_grads[9 * per:9 * per + 4].reshape(-1), 4 * per)
    d_bo, d_g1, d_s1, d_bout, d_g2, d_s2 = (own_slice(layer_grads[9 * per + 4 + n], per) for n in range(6))
    small = (d_bq, d_bv, d_binner, d_bo, d_g1, d_s1, d_bout, d_g2, d_s2)
    returned = tie(tuple(returned) + (d_wouter, d_winner, d_woutput, d_wq, d_wk, d_wv) + small)[:2]
    steps = jnp.arange(seq_count, dtype=jnp.int32)
    slot_of = jnp.sum(jnp.where(deal_order[:, None] == steps[None, :], steps[:, None], 0), axis=0)
    d_tokens = jnp.concatenate([jnp.take(rows, slot_of, axis=0) for rows in returned], axis=2)[:, None]
    return (act.reshape(1, shards, stretch, width), d_tokens, d_wq, d_wk, d_wv, d_woutput, d_bq, d_bv, d_bo,
            d_g1, d_s1, d_winner, d_binner, d_wouter, d_bout, d_g2, d_s2)


def solution(mesh):
    shards, splits = mesh.devices.shape
    fine = Mesh(mesh.devices.reshape(shards // 2, 2, splits // 2, 2), ALL)
    S, Q = SHARD, ("y", "c")
    row, mat = P(S), P(S, None)
    return jax.shard_map(
        body, mesh=fine,
        in_specs=(P(None, S, Q, None), P(), P(), mat, mat, mat, mat, row, row, row, row, row, mat, row, mat, row, row, row,
                  P(S, None, Q, None)),
        out_specs=(P(S, None, Q, None), P(None, S, Q, None), mat, mat, mat, mat, row, row, row, row, row, mat, row, mat,
                   row, row, row),
        check_vma=False)
```

```python
import functools, math
import jax
import jax.numpy as jnp
from jax import lax
from jax.experimental import pallas as pl
from jax.experimental.pallas import tpu as pltpu
from jax.sharding import Mesh, PartitionSpec as P

f32, bf16 = jnp.float32, jnp.bfloat16
LOG2E = 1.4426950408889634
LN2 = 0.6931471805599453
CH = 256
BQ = 2048
RB = 256
FB = 512
PARTS = 2
HD = 64
FAR = -1.0e30

def dg(a, b, ca, cb):
    return lax.dot_general(a, b, (((ca,), (cb,)), ((), ())), preferred_element_type=f32)


def three_parts(row):
    hi = row.astype(bf16).astype(f32)
    rest = row - hi
    mid = rest.astype(bf16).astype(f32)
    return hi, mid, rest - mid


def with_shift(top, shift):
    hi, mid, low = three_parts(shift)
    row = lax.broadcasted_iota(jnp.int32, (HD, top.shape[1]), 0)
    tail = jnp.where(row == 0, -hi, jnp.where(row == 1, -mid, jnp.where(row == 2, -low, jnp.where(row == 3, 1.0, 0.0))))
    return jnp.concatenate([top.astype(f32), tail], axis=0)


def load_rows(rows, ref, spans, x):
    stretch = ref.shape[3]
    for z in range(spans):
        for a in range(2):
            at = (2 * z + a) * stretch
            rows[at:at + stretch] = ref[0, a ^ x, z]


def qkv_kernel(stretch, spans, info, near_ref, far_ref, w_ref, b_ref, q_out, k_out, v_out, size_out, rows):
    away, half = pl.program_id(0), pl.program_id(2)
    owner = ((pl.program_id(1) ^ info[2]) << 1) | (away ^ info[3])

    @pl.when(away == 0)
    def _():
        load_rows(rows, near_ref, spans, info[1])

    @pl.when(away == 1)
    def _():
        load_rows(rows, far_ref, spans, info[1])
    weight = w_ref[...].reshape(rows.shape[1], 384)
    made = dg(rows[...], weight, 1, 0) + b_ref[...]
    count = rows.shape[0]
    q_t = (made[:, :128] * (LOG2E / 8.0)).T
    q_out[0, 0] = q_t[:HD].astype(bf16)
    q_out[1, 0] = q_t[HD:].astype(bf16)
    lane = lax.broadcasted_iota(jnp.int32, (count, 128), 1)
    row = lax.broadcasted_iota(jnp.int32, (count, 128), 0) + half * count
    shift = int(math.log2(stretch))
    position = lax.shift_left(lax.shift_right_logical(row, shift), shift + 2) + owner * stretch + (row & (stretch - 1))
    hidden = jnp.where(position < info[0], 0.0, FAR)
    tail = jnp.where(lane == HD + 3, hidden, jnp.where(lane < HD + 3, 1.0, 0.0))
    keys = made[:, 128:256]
    picks = lax.broadcasted_iota(jnp.int32, (128, 128), 0) // HD == lax.broadcasted_iota(jnp.int32, (128, 128), 1)
    sizes = dg((keys * keys).astype(bf16), jnp.where(picks, 1.0, 0.0).astype(bf16), 1, 0)
    size_out[0, 0] = jnp.max(sizes, axis=0, keepdims=True)
    for head in range(2):
        turned = keys if head == 0 else pltpu.roll(keys, HD, 1)
        full = jnp.where(lane < HD, turned, tail).astype(bf16)
        for j in range(count // 128):
            k_out[head, j, 0] = full[j * 128:(j + 1) * 128]
    v_t = made[:, 256:384].T
    ones = jnp.where(lax.broadcasted_iota(jnp.int32, (HD, count), 0) < 3, 1.0, 0.0)
    for head in range(2):
        full = jnp.concatenate([v_t[head * HD:(head + 1) * HD], ones], axis=0).astype(bf16)
        for j in range(count // 128):
            v_out[head, j, 0] = full[:, j * 128:(j + 1) * 128]


def owner_of(away, across, info):
    return ((across ^ info[2]) << 1) | (away ^ info[3])


def project(near, far, weight, bias, info):
    _, _, zs, stretch, width = near.shape
    local = 2 * zs * stretch
    spans = 512 // (2 * stretch)
    halves = local // 512
    spans_of_rows = local // 128
    per = spans_of_rows // halves
    block = (1, 2, spans, stretch, width)
    q, k, v, sizes = pl.pallas_call(
        functools.partial(qkv_kernel, stretch, spans),
        grid_spec=pltpu.PrefetchScalarGridSpec(
            num_scalar_prefetch=1, grid=(2, 2, halves),
            in_specs=[
                pl.BlockSpec(block, lambda a, o, h, n: (jnp.where(a == 0, o, 1), 0, jnp.where(a == 0, h, halves - 1), 0, 0)),
                pl.BlockSpec(block, lambda a, o, h, n: (jnp.where(a == 0, 0, o), 0, jnp.where(a == 0, 0, h), 0, 0)),
                pl.BlockSpec((8, width // 8, 384), lambda a, o, h, n: (0, 0, n[1])),
                pl.BlockSpec((1, 384), lambda a, o, h, n: (0, 0)),
            ],
            out_specs=[
                pl.BlockSpec((2, 1, HD, 512), lambda a, o, h, n: (0, owner_of(a, o, n), 0, h)),
                pl.BlockSpec((2, per, 1, 128, 128), lambda a, o, h, n: (0, h, o ^ n[2], a ^ n[3], 0)),
                pl.BlockSpec((2, per, 1, 128, 128), lambda a, o, h, n: (0, h, o ^ n[2], 0, a ^ n[3])),
                pl.BlockSpec((1, 1, 1, 128), lambda a, o, h, n: (owner_of(a, o, n), h, 0, 0)),
            ],
            scratch_shapes=[pltpu.VMEM((512, width), bf16)]),
        out_shape=[
            jax.ShapeDtypeStruct((2, 4, HD, local), bf16),
            jax.ShapeDtypeStruct((2, spans_of_rows, 2, CH, 128), bf16),
            jax.ShapeDtypeStruct((2, spans_of_rows, 2, 128, CH), bf16),
            jax.ShapeDtypeStruct((4, halves, 1, 128), f32),
        ],
        compiler_params=pltpu.CompilerParams(vmem_limit_bytes=60 << 20),
        name="qkv",
        cost_estimate=cost(4 * near.size * 384, near.size * 8),
    )(info, near, far, weight, bias)
    return q, k.reshape(2, -1, CH, 128), v.reshape(2, -1, 128, CH), sizes


def step_on(q, j, count):
    last = j + 1 == count
    return jnp.where(last, q + 1, q), jnp.where(last, 0, j + 1)


def assemble(ref, part, shared, core):
    if not shared:
        return jnp.concatenate([ref[0, 2 * part], ref[0, 2 * part + 1]], axis=1)
    at = pl.multiple_of(core * 512, 512)
    return jnp.concatenate([ref[0, n, :, pl.ds(at, 512)] for n in range(4)], axis=1)


def fwd_kernel(shared, info, q_ref, k_ref, v_ref, size_ref, held_ref, out_ref, lse_ref, acc, probs, qa, shifts):
    count = info[4]
    parts = 1 if shared else 2
    lane = lax.broadcasted_iota(jnp.int32, (1, 128), 1)
    sizes = functools.reduce(jnp.maximum, [size_ref[o, h] for o in range(size_ref.shape[0]) for h in range(size_ref.shape[1])])
    widest = jnp.sqrt(jnp.max(jnp.where(lane == int(shared), sizes, 0.0), axis=1, keepdims=True))

    for part in range(parts):
        q_t = assemble(q_ref, part, shared, info[3])
        wide = q_t.astype(f32)
        shift = jnp.sqrt(jnp.sum(wide * wide, axis=0, keepdims=True)) * widest
        shifts[part] = shift
        qa[part] = with_shift(q_t, shift).astype(bf16)

    def raised(part, j):
        return jnp.exp2(dg(k_ref[0, j], qa[part], 1, 0)).astype(bf16)

    probs[0] = raised(0, 0)

    def body(t, carry):
        part, j = carry
        now = t & 1
        part_next, j_next = step_on(part, j, count)
        before = jnp.where(j == 0, 0.0, acc[...])
        acc[...] = before + dg(v_ref[0, j], probs[now], 1, 0)
        probs[1 - now] = raised(jnp.minimum(part_next, parts - 1), j_next)

        @pl.when(j + 1 == count)
        def _():
            total = acc[HD:HD + 1]
            fine = (jnp.min(total) > 2.0 ** -90) & (jnp.max(total) < 2.0 ** 60)

            @pl.when(jnp.logical_not(fine))
            def _():
                plain = qa[part].astype(f32)
                row = lax.broadcasted_iota(jnp.int32, plain.shape, 0)
                qa[part] = jnp.where((row >= HD) & (row < HD + 3), 0.0, plain).astype(bf16)

                def peak(i, top):
                    return jnp.maximum(top, jnp.max(dg(k_ref[0, i], qa[part], 1, 0), axis=0, keepdims=True))
                shift = lax.fori_loop(0, count, peak, jnp.full((1, BQ), FAR, f32))
                shifts[part] = shift
                qa[part] = with_shift(plain[:HD], shift).astype(bf16)
                acc[...] = jnp.zeros_like(acc)

                def again(i, carry):
                    acc[...] += dg(v_ref[0, i], raised(part, i), 1, 0)
                    return carry
                lax.fori_loop(0, count, again, 0)

            total = acc[HD:HD + 1]
            mixed = (acc[:HD] * (1.0 / total)).astype(bf16)
            lse_ref[part] = shifts[part] + jnp.log2(total)
            if shared:
                for n in range(4):
                    out_ref[0, n] = mixed[:, n * 512:(n + 1) * 512]
            else:
                for n in range(2):
                    out_ref[0, 2 * part + n] = mixed[:, n * 1024:(n + 1) * 1024]
        return part_next, j_next

    lax.fori_loop(0, parts * count, body, (0, 0))


def head_spec(shared, *dims):
    zeros = (0,) * len(dims)
    return pl.BlockSpec((1,) + dims, lambda i, n: (int(shared),) + zeros)


def whole_spec(*dims):
    return pl.BlockSpec(dims, lambda i, n: (0,) * len(dims))


def cost(flops, moved, exps=0):
    return pl.CostEstimate(flops=int(flops), bytes_accessed=int(moved), transcendentals=int(exps))


def attend_forward(shared, seq, q, k, v, sizes, info, held):
    _, owners, _, local = q.shape
    chunks = k.shape[1]
    wide = local // 2 if shared else local
    parts = owners * wide // BQ
    pairs = parts * BQ * chunks * CH * 0.6
    shape = jax.ShapeDtypeStruct((2, owners, HD, wide), bf16)
    first = held is None
    if first:
        kernel = lambda info, q, k, v, size, *rest: fwd_kernel(shared, info, q, k, v, size, None, *rest)
    else:
        kernel = functools.partial(fwd_kernel, shared)
    return pl.pallas_call(
        kernel,
        grid_spec=pltpu.PrefetchScalarGridSpec(
            num_scalar_prefetch=1, grid=(1,),
            in_specs=[
                head_spec(shared, owners, HD, local), head_spec(shared, chunks, CH, 128), head_spec(shared, chunks, 128, CH),
                whole_spec(*sizes.shape),
            ] + ([] if first else [pl.BlockSpec(memory_space=pl.ANY)]),
            out_specs=[pl.BlockSpec((1, owners, HD, wide), lambda i, n: (seq, 0, 0, 0)), whole_spec(parts, 1, BQ)],
            scratch_shapes=[
                pltpu.VMEM((128, BQ), f32), pltpu.VMEM((2, CH, BQ), bf16), pltpu.VMEM((parts, 128, BQ), bf16),
                pltpu.VMEM((parts, 1, BQ), f32),
            ]),
        out_shape=[shape, jax.ShapeDtypeStruct((parts, 1, BQ), f32)],
        input_output_aliases={} if first else {5: 0},
        compiler_params=pltpu.CompilerParams(vmem_limit_bytes=48 << 20),
        cost_estimate=cost(pairs * 1024, chunks * CH * 512, pairs),
        name="attend_forward_shared" if shared else "attend_forward_own",
    )(*((info, q, k, v, sizes) + (() if first else (held,))))


def bwd_kernel(shared, first, info, q_ref, k_ref, v_ref, lse_ref, out_ref, gout_ref, *rest):
    rest = rest if first else rest[3 if shared else 1:]
    if shared:
        dq_ref, kept_ref, given_ref, dk_acc, dv_acc, dq_acc, qa, qat, ga, gat, pb, db = rest
    else:
        dqkv_ref, dk_acc, dv_acc, dq_acc, qa, qat, ga, gat, pb, db = rest
    count = info[4]
    chunks = k_ref.shape[1]
    parts = 1 if shared else 2
    dk_acc[...] = jnp.zeros_like(dk_acc)
    dv_acc[...] = jnp.zeros_like(dv_acc)

    def piece(ref, part):
        return jnp.concatenate([ref[0, n] for n in (range(4) if shared else (2 * part, 2 * part + 1))], axis=1)

    for part in range(parts):
        q_full = with_shift(assemble(q_ref, part, shared, info[3]), lse_ref[part])
        qat[part] = q_full.astype(bf16)
        qa[part] = q_full.T.astype(bf16)
        g_t = piece(gout_ref, part)
        meet = jnp.sum(g_t.astype(f32) * piece(out_ref, part).astype(f32), axis=0, keepdims=True)
        g_full = with_shift(g_t, meet)
        gat[part] = g_full.astype(bf16)
        ga[part] = g_full.T.astype(bf16)

    def ahead(part, j, slot):
        raised = jnp.exp2(dg(qa[part], k_ref[0, j], 1, 1))
        pb[slot] = raised.astype(bf16)
        db[slot] = (raised * dg(ga[part], v_ref[0, j], 1, 0)).astype(bf16)

    ahead(0, 0, 0)

    def body(t, carry):
        part, j = carry
        now = t & 1
        part_next, j_next = step_on(part, j, count)
        dv_acc[j] += dg(gat[part], pb[now], 1, 0)[:HD]
        dk_acc[j] += dg(qat[part], db[now], 1, 0)[:HD]
        before = jnp.where(j == 0, 0.0, dq_acc[...])
        dq_acc[...] = before + dg(db[now], k_ref[0, j], 1, 0)
        ahead(jnp.minimum(part_next, parts - 1), j_next, 1 - now)

        @pl.when(j + 1 == count)
        def _():
            dq_t = (dq_acc[...] * 0.125).T[:HD].astype(bf16)
            if shared:
                for n in range(4):
                    dq_ref[0, n, :, :512] = dq_t[:32, n * 512:(n + 1) * 512]
                    dq_ref[0, n, :, 512:] = dq_t[32:, n * 512:(n + 1) * 512]
            else:
                for n in range(2):
                    dqkv_ref[0, 2 * part + n, 0] = dq_t[:, n * 1024:(n + 1) * 1024]
        return part_next, j_next

    lax.fori_loop(0, parts * count, body, (0, 0))
    for block in range(chunks):
        j, across = block // 2, block % 2
        for owner in (2 * across, 2 * across + 1):
            cols = slice((owner - 2 * across) * 128, (owner - 2 * across + 1) * 128)
            dk_wide, dv_wide = dk_acc[block, :, cols] * LN2, dv_acc[block, :, cols]
            dk, dv = dk_wide.astype(bf16), dv_wide.astype(bf16)
            if shared:
                here = info[3] == 0
                kept_ref[0, owner, :, j * 128:(j + 1) * 128] = jnp.where(here, dk_wide, dv_wide).astype(bf16)
                given_ref[0, owner, :, j * 128:(j + 1) * 128] = jnp.where(here, dv_wide, dk_wide).astype(bf16)
            else:
                dqkv_ref[0, owner, 1, :, j * 128:(j + 1) * 128] = dk
                dqkv_ref[0, owner, 2, :, j * 128:(j + 1) * 128] = dv


def attend_backward(shared, seq, q, k, v, lse, out, g_out, info, held):
    _, owners, _, local = q.shape
    chunks = k.shape[1]
    wide = out.shape[3]
    parts = owners * wide // BQ
    pairs = parts * BQ * chunks * CH * 0.6
    shape = jax.ShapeDtypeStruct
    first = held is None
    if shared:
        out_specs = [pl.BlockSpec((1, owners, rows, local), lambda i, n: (seq, 0, 0, 0)) for rows in (32, HD, HD)]
        out_shape = [shape((2, owners, rows, local), bf16) for rows in (32, HD, HD)]
    else:
        out_specs = [pl.BlockSpec((1, owners, 3, HD, local), lambda i, n: (seq, 0, 0, 0, 0))]
        out_shape = [shape((2, owners, 3, HD, local), bf16)]
    kept = () if first else tuple(held)
    of_seq = pl.BlockSpec((1, owners, HD, wide), lambda i, n: (seq, 0, 0, 0))
    return pl.pallas_call(
        functools.partial(bwd_kernel, shared, first),
        grid_spec=pltpu.PrefetchScalarGridSpec(
            num_scalar_prefetch=1, grid=(1,),
            in_specs=[
                head_spec(shared, owners, HD, local), head_spec(shared, chunks, CH, 128), head_spec(shared, chunks, 128, CH),
                whole_spec(parts, 1, BQ), of_seq, of_seq,
            ] + [pl.BlockSpec(memory_space=pl.ANY)] * len(kept),
            out_specs=out_specs,
            scratch_shapes=[
                pltpu.VMEM((chunks, HD, CH), f32), pltpu.VMEM((chunks, HD, CH), f32), pltpu.VMEM((BQ, 128), f32),
                pltpu.VMEM((parts, BQ, 128), bf16), pltpu.VMEM((parts, 128, BQ), bf16),
                pltpu.VMEM((parts, BQ, 128), bf16), pltpu.VMEM((parts, 128, BQ), bf16),
                pltpu.VMEM((2, BQ, CH), bf16), pltpu.VMEM((2, BQ, CH), bf16),
            ]),
        out_shape=out_shape,
        input_output_aliases={7 + n: n for n in range(len(kept))},
        compiler_params=pltpu.CompilerParams(vmem_limit_bytes=56 << 20),
        cost_estimate=cost(pairs * 100, chunks * CH * 2048),
        name="attend_backward_shared" if shared else "attend_backward_own",
    )(info, q, k, v, lse, out, g_out, *kept)


def gelu_pair(u):
    half = 0.5 * (1.0 + lax.erf(u * 0.7071067811865476))
    return u * half, half + u * (0.3989422804014327 * jnp.exp2(u * u * (-0.5 * LOG2E)))


def norm_stats(v):
    mean = jnp.mean(v, axis=-1, keepdims=True)
    centred = v - mean
    inverse = lax.rsqrt(jnp.mean(centred * centred, axis=-1, keepdims=True) + 1e-12)
    return centred * inverse, inverse


def norm_back(grad, xhat, inverse, gain):
    g = grad * gain
    return (g - jnp.mean(g, axis=-1, keepdims=True) - xhat * jnp.mean(g * xhat, axis=-1, keepdims=True)) * inverse


def weight_part(ref, first, rows):
    part = ref[:, first:first + rows, :]
    return part.reshape(part.shape[0] * rows, part.shape[2])


def ffn_kernel(spans, info, x_ref, own_ref, sh_ref, cot_ref, w_ref, bin_ref, vec_ref,
               act_out, resid_out, gown_out, gsh_out, active_out, dinner_out, normed_out, douter_out, dbranch_out,
               vec_sum, bin_sum, slope, row_block):
    step = pl.program_id(0)
    load_rows(row_block, x_ref, spans, info[1])
    count = row_block.shape[0] // PARTS
    vec = vec_ref[...]
    total = lambda a: jnp.sum(a, axis=0, keepdims=True)
    held = [{"at": slice(n * count, (n + 1) * count)} for n in range(PARTS)]

    def branch(h):
        at = h["at"]
        mixed_t = jnp.concatenate(
            [part for p in range(4) for part in (own_ref[p, 0, :, at], sh_ref[p, 0, :, at], own_ref[p, 1, :, at])], axis=0)
        h["sum1"] = row_block[at].astype(f32) + (dg(mixed_t, weight_part(w_ref, 768, 96), 0, 0) + vec[0:1])

    def first_norm(h):
        h["xhat1"], h["inv1"] = norm_stats(h["sum1"])
        normed = h["xhat1"] * vec[1:2] + vec[2:3]
        normed_out[h["at"]] = normed.astype(bf16)
        h["outer"] = normed + vec[3:4]

    def widen(h):
        at = h["at"]
        for n in range(4):
            cols = slice(n * 768, (n + 1) * 768)
            value, bend = gelu_pair(dg(normed_out[at], weight_part(w_ref, 384 + 96 * n, 96), 1, 0) + bin_ref[:, cols])
            active_out[at, cols] = value.astype(bf16)
            slope[at, cols] = bend.astype(bf16)

    def narrow(h):
        h["outer"] = h["outer"] + dg(active_out[h["at"]], weight_part(w_ref, 0, 384), 1, 0)

    def second_norm(h):
        at = h["at"]
        xhat2, inv2 = norm_stats(h["outer"])
        act_out[at] = (xhat2 * vec[4:5] + vec[5:6]).astype(bf16)
        cot = cot_ref[at].astype(f32)
        d2 = norm_back(cot, xhat2, inv2, vec[4:5])
        d_outer = d2.astype(bf16)
        douter_out[at] = d_outer
        h["d_normed"] = d2
        h["sums"] = [total(d_outer.astype(f32)), total(cot * xhat2), total(cot)]

    def back(h):
        at = h["at"]
        h["inner_sums"] = []
        for n in range(4):
            cols = slice(n * 768, (n + 1) * 768)
            d_active = dg(douter_out[at], weight_part(w_ref.at[2 * n:2 * n + 2], 0, 384), 1, 1)
            d_inner = (d_active * slope[at, cols].astype(f32)).astype(bf16)
            dinner_out[at, cols] = d_inner
            h["inner_sums"].append(total(d_inner.astype(f32)))
            h["d_normed"] = h["d_normed"] + dg(d_inner, weight_part(w_ref, 384 + 96 * n, 96), 1, 1)

    def first_back(h):
        at = h["at"]
        d_normed = h["d_normed"]
        d1 = norm_back(d_normed, h["xhat1"], h["inv1"], vec[1:2])
        resid_out[at] = d1
        d_branch = d1.astype(bf16)
        dbranch_out[at] = d_branch
        h["sums"] = [total(d_branch.astype(f32)), total(d_normed * h["xhat1"]), total(d_normed)] + h["sums"]

    def mix_back(h):
        at = h["at"]
        g_t = dg(weight_part(w_ref, 768, 96), dbranch_out[at], 1, 1).astype(bf16)
        for p in range(4):
            gown_out[p, 0, :, at] = g_t[192 * p:192 * p + 64]
            gsh_out[p, 0, :, at] = g_t[192 * p + 64:192 * p + 128]
            gown_out[p, 1, :, at] = g_t[192 * p + 128:192 * p + 192]

    for products, norm in ((branch, first_norm), (widen, None), (narrow, second_norm), (back, first_back), (mix_back, None)):
        for h in held:
            products(h)
            if norm is not None:
                norm(h)
    sums = jnp.concatenate([
        functools.reduce(jnp.add, [h["sums"][n] for h in held]) for n in range(6)] + [jnp.zeros((2, vec.shape[1]), f32)], axis=0)
    inner_sums = [functools.reduce(jnp.add, [h["inner_sums"][n] for h in held]) for n in range(4)]

    @pl.when(step == 0)
    def _():
        vec_sum[...] = sums
        for n in range(4):
            bin_sum[:, n * 768:(n + 1) * 768] = inner_sums[n]

    @pl.when(step > 0)
    def _():
        vec_sum[...] += sums
        for n in range(4):
            bin_sum[:, n * 768:(n + 1) * 768] += inner_sums[n]


def feed_forward(rows_in, own, sh, cotangent, weights, inner_bias, vectors, info):
    _, _, _, stretch, width = rows_in.shape
    local = cotangent.shape[0]
    spans = FB // (2 * stretch)
    steps = local // FB
    half_steps = steps // 2
    wide = inner_bias.shape[1]
    rows = lambda n: pl.BlockSpec((FB, n), lambda r, a: (r, 0))
    fixed = lambda *dims: pl.BlockSpec(dims, lambda r, a: (0,) * len(dims))
    own_spec = pl.BlockSpec((4, 2, HD, FB), lambda r, a: (0, 0, 0, r))
    sh_spec = pl.BlockSpec((4, 1, HD, FB), lambda r, a: (0, r // half_steps, 0, r % half_steps))
    shape = jax.ShapeDtypeStruct
    return pl.pallas_call(
        functools.partial(ffn_kernel, spans),
        grid_spec=pltpu.PrefetchScalarGridSpec(
            num_scalar_prefetch=1, grid=(steps,),
            in_specs=[
                pl.BlockSpec((1, 2, spans, stretch, width), lambda r, a: (0, 0, r, 0, 0)),
                own_spec, sh_spec, rows(width),
                pl.BlockSpec(weights.shape, lambda r, a: (0, 0, 0), pipeline_mode=pl.Buffered(1)),
                fixed(1, wide), fixed(8, width),
            ],
            out_specs=[
                rows(width), rows(width), own_spec, sh_spec, rows(wide), rows(wide), rows(width), rows(width), rows(width),
                fixed(8, width), fixed(1, wide),
            ],
            scratch_shapes=[pltpu.VMEM((FB, wide), bf16), pltpu.VMEM((FB, width), bf16)]),
        out_shape=[
            shape((local, width), bf16), shape((local, width), f32), shape(own.shape, bf16), shape(sh.shape, bf16),
            shape((local, wide), bf16), shape((local, wide), bf16), shape((local, width), bf16),
            shape((local, width), bf16), shape((local, width), bf16), shape((8, width), f32), shape((1, wide), f32),
        ],
        compiler_params=pltpu.CompilerParams(vmem_limit_bytes=60 << 20),
        name="feed_forward",
        cost_estimate=cost(local * width * (width + 2 * wide) * 4, local * wide * 20),
    )(info, rows_in, own, sh, cotangent, weights, inner_bias, vectors)


def outer_grad_kernel(scale, active_ref, douter_ref, out_ref):
    made = (dg(active_ref[...], douter_ref[...], 0, 0) * scale).astype(bf16)
    out_ref[...] = made.reshape(out_ref.shape)


def inner_grad_kernel(scale, packed_ref, normed_ref, dinner_ref, own_ref, sh_ref, dbranch_ref, out_ref):
    step = pl.program_id(0)

    @pl.when(step < 4)
    def _():
        out_ref[...] = (dg(normed_ref[...], dinner_ref[...], 0, 0) * scale).astype(bf16).reshape(out_ref.shape)

    @pl.when(step == 4)
    def _():
        mixed_t = jnp.concatenate([
            part for p in range(4)
            for part in (own_ref[p, 0], jnp.concatenate([sh_ref[p, 0], sh_ref[p, 1]], axis=1), own_ref[p, 1])], axis=0)
        out_ref[...] = (dg(mixed_t, dbranch_ref[...], 1, 0) * scale).astype(bf16).reshape(out_ref.shape)


def weight_grads(scale, active, d_outer, normed, d_inner, own, sh, d_branch):
    local, wide = active.shape
    width = normed.shape[1]
    packed = pl.pallas_call(
        functools.partial(outer_grad_kernel, scale), grid=(4,),
        in_specs=[pl.BlockSpec((local, width), lambda m: (0, m)), pl.BlockSpec((local, width), lambda m: (0, 0))],
        out_specs=pl.BlockSpec((2, 384, width), lambda m: (m, 0, 0)),
        out_shape=jax.ShapeDtypeStruct((8, 896, width), bf16),
        compiler_params=pltpu.CompilerParams(vmem_limit_bytes=40 << 20), name="outer_grad",
        cost_estimate=cost(2 * local * wide * width, 2 * wide * (local + width)),
    )(active, d_outer)
    fixed = lambda a: pl.BlockSpec(a.shape, lambda n: (0,) * a.ndim)
    return pl.pallas_call(
        functools.partial(inner_grad_kernel, scale), grid=(5,),
        in_specs=[
            pl.BlockSpec(memory_space=pl.ANY), fixed(normed),
            pl.BlockSpec((local, width), lambda n: (0, jnp.minimum(n, 3))), fixed(own), fixed(sh), fixed(d_branch)],
        out_specs=pl.BlockSpec((8, 96, width), lambda n: (0, 4 + n, 0)),
        out_shape=jax.ShapeDtypeStruct((8, 896, width), bf16), input_output_aliases={0: 0},
        compiler_params=pltpu.CompilerParams(vmem_limit_bytes=40 << 20), name="inner_grad",
        cost_estimate=cost(2 * local * (wide + width) * width, 2 * (wide + width) * (local + width)),
    )(packed, normed, d_inner, own, sh, d_branch)


def head_grad_kernel(scale, spans, info, *refs):
    x_refs, (own_ref, dq_ref, kept_ref, given_ref, out_ref, bias_out, acc, bias_acc, rows) = refs[:4], refs[4:]
    seq, away, half = pl.program_id(0), pl.program_id(1), pl.program_id(3)
    last = (seq == 1) & (away == 1) & (pl.program_id(2) == 1) & (half == pl.num_programs(3) - 1)
    for n in range(4):
        @pl.when(seq * 2 + away == n)
        def _(n=n):
            load_rows(rows, x_refs[n], spans, info[1])
    dq_t = jnp.where(half == info[3], jnp.concatenate([dq_ref[0, 0, :, :512], dq_ref[0, 0, :, 512:]], axis=0).astype(f32), 0.0)
    kept, given = kept_ref[0, 0].astype(f32), given_ref[0, 0].astype(f32)
    here = info[3] == 0
    d_t = jnp.concatenate([
        own_ref[0, 0, 0], dq_t.astype(bf16), own_ref[0, 0, 1], jnp.where(here, kept, given).astype(bf16),
        own_ref[0, 0, 2], jnp.where(here, given, kept).astype(bf16)], axis=0)

    @pl.when((seq == 0) & (away == 0) & (pl.program_id(2) == 0) & (half == 0))
    def _():
        acc[...] = jnp.zeros_like(acc)
        bias_acc[...] = jnp.zeros_like(bias_acc)
    acc[...] += dg(d_t, rows[...], 1, 0)
    bias_acc[...] += dg(jnp.ones((8, d_t.shape[1]), bf16), d_t, 1, 1)

    @pl.when(last)
    def _():
        out_ref[...] = (acc[...] * scale).T.astype(bf16)
        bias_out[...] = bias_acc[...] * scale


def head_grads(scale, sources, dqkv_own, dq_sh, kept, given, info):
    _, _, zs, stretch, width = sources[0].shape
    local = 2 * zs * stretch
    spans = 512 // (2 * stretch)
    halves = local // 512

    def source_spec(n):
        def index(s, a, o, h, i):
            now = 2 * s + a
            across = jnp.where(now == n, o, jnp.where(now < n, 0, 1))
            return (across, 0, jnp.where(now == n, h, jnp.where(now < n, 0, halves - 1)), 0, 0)
        return pl.BlockSpec((1, 2, spans, stretch, width), index)
    return pl.pallas_call(
        functools.partial(head_grad_kernel, scale, spans),
        grid_spec=pltpu.PrefetchScalarGridSpec(
            num_scalar_prefetch=1, grid=(2, 2, 2, halves),
            in_specs=[source_spec(n) for n in range(4)] + [
                pl.BlockSpec((1, 1, 3, HD, 512), lambda s, a, o, h, i: (s, owner_of(a, o, i), 0, 0, h)),
                pl.BlockSpec((1, 1, 32, local), lambda s, a, o, h, i: (s, owner_of(a, o, i), 0, 0)),
            ] + [pl.BlockSpec((1, 1, HD, 512), lambda s, a, o, h, i: (s, owner_of(a, o, i), 0, h))] * 2,
            out_specs=[pl.BlockSpec((width, 384), lambda s, a, o, h, i: (0, 0)), pl.BlockSpec((8, 384), lambda s, a, o, h, i: (0, 0))],
            scratch_shapes=[pltpu.VMEM((384, width), f32), pltpu.VMEM((8, 384), f32), pltpu.VMEM((512, width), bf16)]),
        out_shape=[jax.ShapeDtypeStruct((width, 384), bf16), jax.ShapeDtypeStruct((8, 384), f32)],
        compiler_params=pltpu.CompilerParams(vmem_limit_bytes=40 << 20), name="head_grads",
        cost_estimate=cost(8 * local * 768 * width, 8 * local * width * 2),
    )(info, *sources, dqkv_own, dq_sh, kept, given)


def token_grad_kernel(own_ref, low_ref, high_ref, dkv_ref, w_ref, resid_ref, out_ref):
    total = resid_ref[...]
    for kind in range(3):
        made = []
        for p in range(4):
            if kind == 0:
                middle = jnp.concatenate([low_ref[p, 0], high_ref[p, 0]], axis=0)
            else:
                middle = jnp.concatenate([dkv_ref[p, kind - 1, n] for n in range(2)], axis=0)
            made += [own_ref[p, 0, kind], middle, own_ref[p, 1, kind]]
        total = total + dg(jnp.concatenate(made, axis=0), weight_part(w_ref, 96 * kind, 96), 0, 1)
    out_ref[...] = total.astype(bf16)


def token_grad(own, shared, weights, resid):
    local, width = resid.shape
    steps = local // RB
    half_steps = steps // 2
    rows = pl.BlockSpec((RB, width), lambda r: (r, 0))
    return pl.pallas_call(
        token_grad_kernel, grid=(steps,),
        in_specs=[
            pl.BlockSpec((4, 2, 3, HD, RB), lambda r: (0, 0, 0, 0, r)),
            pl.BlockSpec((4, 1, None, 32, RB), lambda r: (0, r // half_steps, 2, 0, r % half_steps)),
            pl.BlockSpec((4, 1, None, 32, RB), lambda r: (0, r // half_steps, 2, 0, half_steps + r % half_steps)),
            pl.BlockSpec((4, 2, 2, 32, RB), lambda r: (0, 0, 0, 0, r)),
            pl.BlockSpec(weights.shape, lambda r: (0, 0, 0)), rows],
        out_specs=rows, out_shape=jax.ShapeDtypeStruct((local, width), bf16),
        compiler_params=pltpu.CompilerParams(vmem_limit_bytes=60 << 20), name="token_grad",
        cost_estimate=cost(local * width * width * 6, local * width * 12),
    )(own, shared, shared, shared, weights, resid)


def head_unpack_kernel(per, info, src_ref, q_out, k_out, v_out, bias_out):
    low = lax.broadcasted_iota(jnp.int32, (src_ref.shape[1], 128), 1) < HD

    def rows_of(p, core, cols):
        at = (((p >> 1) ^ info[1]) << 2) | (((p & 1) ^ info[2]) << 1) | (core ^ info[3])
        return src_ref[at, :, cols].astype(f32)
    for kind, out in enumerate((q_out, k_out, v_out)):
        cols = slice(128 * kind, 128 * kind + 128)
        tiles = []
        for pair in range(2):
            first, second = [], []
            for p in (2 * pair, 2 * pair + 1):
                near, far = rows_of(p, 0, cols), rows_of(p, 1, cols)
                first.append(near + jnp.where(low, 0.0, far))
                second.append(far)
            turned = pltpu.roll(first[1], HD, 1)
            tiles += [first[0], jnp.where(low, second[0], turned), jnp.where(low, turned, pltpu.roll(second[1], HD, 1))]
        made = jnp.concatenate(tiles, axis=1)
        out[...] = made[:per]
        if kind != 1:
            bias_out[kind // 2:kind // 2 + 1] = made[per:per + 1]


def head_unpack(source, per, width, info):
    shape = jax.ShapeDtypeStruct
    full = lambda n: pl.BlockSpec((n, width), lambda i, f: (0, 0))
    return pl.pallas_call(
        functools.partial(head_unpack_kernel, per),
        grid_spec=pltpu.PrefetchScalarGridSpec(
            num_scalar_prefetch=1, grid=(1,),
            in_specs=[pl.BlockSpec(source.shape, lambda i, f: (0, 0, 0))],
            out_specs=[full(per)] * 3 + [full(2)]),
        out_shape=[shape((per, width), f32)] * 3 + [shape((2, width), f32)], name="head_unpack",
    )(info, source)


SWAP = [(0, 1), (1, 0)]
def settle_kernel(*refs):
    refs[-1][...] = sum(ref[...].astype(f32) for ref in refs[:-2]).astype(bf16)


def settle(parts, after):
    whole = pl.BlockSpec(memory_space=pltpu.VMEM)
    return pl.pallas_call(
        settle_kernel, in_specs=[whole] * len(parts) + [pl.BlockSpec(memory_space=pl.ANY)], out_specs=whole,
        out_shape=jax.ShapeDtypeStruct(parts[0].shape, bf16), name="settle",
        cost_estimate=cost(1e9, 1e6),
    )(*parts, after)


PAIR = ("x", "y", "c")
ALL = ("z", "x", "y", "c")
SHARD = ("z", "x")


def canonical(packed, shards):
    if shards == 8:
        return packed
    width = packed.shape[2]
    per, keep = 96 * 8 // shards, shards // 8
    outer = packed[:, :4 * per].reshape(8, 384, width)
    inner = packed[:, 4 * per:8 * per].reshape(8, keep, 4, per, width).transpose(0, 2, 1, 3, 4).reshape(8, 384, width)
    output = packed[:, 8 * per:9 * per].reshape(8, 96, width)
    return jnp.concatenate([outer, inner, output, jnp.zeros((8, 32, width), packed.dtype)], axis=1)


def from_canonical(packed, last, shards):
    width = packed.shape[2]
    if shards == 8:
        return packed.at[:, 864:].set(jnp.broadcast_to(last[None], (8, 32, width)))
    per, keep = 96 * 8 // shards, shards // 8
    outer = packed[:, :384].reshape(shards, 4 * per, width)
    inner = packed[:, 384:768].reshape(8, 4, keep, per, width).transpose(0, 2, 1, 3, 4).reshape(shards, 4 * per, width)
    output = packed[:, 768:864].reshape(shards, per, width)
    return jnp.concatenate([outer, inner, output, jnp.broadcast_to(last[None], (shards, 32, width))], axis=1)


def canonical_heads(packed, shards, parts):
    if shards == 8:
        return packed
    width = packed.shape[2]
    per = 96 * 8 // shards
    made = [packed[:, k * per:(k + 1) * per].reshape(8, 96, width) for k in range(parts)]
    return jnp.concatenate(made + [jnp.zeros((8, 32, width), packed.dtype)], axis=1)


def quarter(rows):
    place = lax.axis_index("y") * 2 + lax.axis_index("c")
    part = rows.shape[0] // 4
    return lax.dynamic_slice_in_dim(rows, place * part, part)


def flipped(array, axis, here):
    return jnp.where(here == 0, array, jnp.flip(array, axis))


def body(tokens, lengths, deal_order, w_query, w_key, w_value, w_output, b_query, b_value, b_output,
         ln1_gain, ln1_shift, w_inner, b_inner, w_outer, b_outer, ln2_gain, ln2_shift, cotangent):
    tie = lax.optimization_barrier
    zs = lax.axis_size("z")
    shards = 2 * zs
    scale = 1.0 / (shards * 4)
    seq_count, _, stretch, width = tokens.shape
    per = w_query.shape[0]
    half = zs // 2
    x, y, c = lax.axis_index("x"), lax.axis_index("y"), lax.axis_index("c")

    def deal(ordered):
        return lax.all_to_all(ordered, "z", split_axis=0, concat_axis=0, tiled=True)

    def corner(across, along):
        return [lax.ppermute(across[:half], "y", SWAP), lax.ppermute(along[half:], "x", SWAP)]

    def this_core(own, across, along, corner):
        return jnp.concatenate([own, across, along] + corner, axis=0).reshape(2, 2, zs, stretch, width)

    ordered_a = tokens[:, 0].at[deal_order[0::2]].get(mode="promise_in_bounds")
    first_own = deal(ordered_a)
    (_, tokens, w_query, w_key, w_value, b_query, b_value, w_outer, w_inner, w_output, b_inner, deal_order) = tie(
        (ordered_a, tokens, w_query, w_key, w_value, b_query, b_value, w_outer, w_inner, w_output, b_inner, deal_order))
    ordered_b = tokens[:, 0].at[deal_order[1::2]].get(mode="promise_in_bounds")

    def head_columns(matrix):
        heads = matrix.reshape(per, 2, 2, 3, HD)
        mine = lax.dynamic_index_in_dim(heads, y, axis=2, keepdims=False)
        own = lax.dynamic_index_in_dim(mine, 2 * c, axis=2, keepdims=False)
        return [own, mine[:, :, 1]]
    pad = lambda v: jnp.pad(v, (0, width - v.shape[0]))[None]
    columns = jnp.concatenate(
        [col for matrix in (w_query, w_key, w_value) for col in head_columns(matrix)], axis=2).reshape(per, width)
    head_pack = jnp.concatenate([columns, pad(b_query), pad(b_value), jnp.zeros((14, width), bf16)], axis=0)
    vectors = (b_output, ln1_gain, ln1_shift, b_outer, ln2_gain, ln2_shift)
    layer_pack = jnp.concatenate(
        [w_outer] + [w_inner[:, n * width:(n + 1) * width] for n in range(4)] + [w_output]
        + [pad(b_inner)] + [pad(v) for v in vectors] + [jnp.zeros((25, width), bf16)], axis=0)
    layer_quarter = quarter(layer_pack)
    back_quarter = quarter(jnp.concatenate([w_query, w_key, w_value, jnp.zeros((32, width), bf16)], axis=0))
    first_own, ordered_b, head_pack, layer_quarter, back_quarter = tie(
        (first_own, ordered_b, head_pack, layer_quarter, back_quarter))
    head_all = lax.all_gather(head_pack, SHARD, axis=0, tiled=False)
    head_weight = canonical_heads(head_all, shards, 1)

    def head_bias(row):
        heads = head_all[:, per + row, :per].reshape(2, 2, 3, HD)
        mine = lax.dynamic_slice(heads, (x, y, 0, 0), (1, 1, 3, HD))[0, 0]
        return [lax.dynamic_index_in_dim(mine, 2 * c, axis=0, keepdims=False), mine[1]]
    bias_row = jnp.concatenate(head_bias(0) + [jnp.zeros((2 * HD,), bf16)] + head_bias(1)).astype(f32)[None]

    across_a, along_a = lax.ppermute(first_own, "x", SWAP), lax.ppermute(first_own, "y", SWAP)
    second_own = deal(ordered_b)
    across_a, along_a, second_own = tie((across_a, along_a, second_own))
    corner_a = corner(across_a, along_a)
    second_own, *corner_a = tie((second_own, *corner_a))
    near_a = this_core(first_own, across_a, along_a, corner_a)
    far_a = lax.ppermute(near_a, "c", SWAP)
    across_b, along_b = lax.ppermute(second_own, "x", SWAP), lax.ppermute(second_own, "y", SWAP)

    layer_all = lax.all_gather(layer_quarter, ALL, axis=0, tiled=True).reshape(shards, 9 * per + 32, width)
    layer_weights = canonical(layer_all, shards)
    inner_bias = layer_all[:, 9 * per, :4 * per].reshape(1, 4 * width).astype(f32)
    vector_rows = jnp.concatenate(
        [layer_all[:, 9 * per + 1 + n, :per].reshape(1, width) for n in range(6)] + [jnp.zeros((2, width), bf16)],
        axis=0).astype(f32)
    back_all = lax.all_gather(back_quarter, ALL, axis=0, tiled=True).reshape(shards, 3 * per + 32, width)

    slots = lax.dynamic_slice_in_dim(deal_order, lax.axis_index("z") * 2, 2)
    matches = slots[:, None] == jnp.arange(seq_count, dtype=jnp.int32)[None, :]
    lens = jnp.sum(jnp.where(matches, lengths[None, :], 0), axis=1).astype(jnp.int32)
    last = (lens + 511) // 512 - 1
    counts = 2 * last + 1 + (lens > 512 * last + 2 * stretch).astype(jnp.int32)
    infos = [jnp.stack([lens[n], x, y, c, counts[n]]).astype(jnp.int32) for n in range(2)]

    def swap(array):
        flat = array.reshape((8,) + array.shape[2:])
        return lax.all_to_all(flat, PAIR, split_axis=0, concat_axis=0, tiled=True)

    def to_tokens(array):
        return swap(array).reshape((4, 2) + array.shape[2:])

    def to_heads(array):
        return swap(array).reshape((2, 4) + array.shape[2:])

    heads_a = project(near_a, far_a, head_weight, bias_row, infos[0])
    heads_a, across_b, along_b = tie((heads_a, across_b, along_b))
    near_b = this_core(second_own, across_b, along_b, corner(across_b, along_b))
    own_first, lse_own_a = attend_forward(False, 0, *heads_a, infos[0], None)
    own_first, near_b = tie((own_first, near_b))
    far_b = lax.ppermute(near_b, "c", SWAP)
    heads_b = project(near_b, far_b, head_weight, bias_row, infos[1])
    own, lse_own_b = attend_forward(False, 1, *heads_b, infos[1], own_first)
    own_t = to_tokens(own)
    own, info_a, info_b = tie((own, *infos))
    sh_first, lse_sh_a = attend_forward(True, 0, *heads_a, info_a, None)
    sh, lse_sh_b = attend_forward(True, 1, *heads_b, info_b, sh_first)
    sh_sent, own_t = tie((sh, own_t))
    sh_t = to_tokens(sh_sent)
    mine_rows = jnp.where(x == 0, jnp.stack([first_own, across_a]), jnp.stack([second_own, across_b]))[None]

    (act, resid, g_own, g_sh, active, d_inner, normed, d_outer, d_branch, vec_sums, bin_sums) = feed_forward(
        mine_rows, own_t, sh_t, cotangent.reshape(-1, width), layer_weights, inner_bias, vector_rows, infos[0])
    g_own_h, g_sh_h = to_heads(g_own), to_heads(g_sh)
    active, back_all = tie((active, back_all))
    packed = weight_grads(scale, active, d_outer, normed, d_inner, own_t, sh_t, d_branch)
    sums = jnp.concatenate([bin_sums.reshape(4, width), vec_sums, jnp.zeros((20, width), f32)], axis=0) * scale
    ready = from_canonical(packed, sums.astype(bf16), shards)
    ready, g_own_h = tie((ready, g_own_h))
    back_weights = canonical_heads(back_all, shards, 3)
    layer_part = lax.psum_scatter(ready.reshape(-1, width), ("z", "x", "c"), scatter_dimension=0, tiled=True)

    qkv_a, qkv_b = heads_a[:3], heads_b[:3]
    first = attend_backward(False, 0, *qkv_a, lse_own_a, own, g_own_h, infos[0], None)
    dqkv_own, = attend_backward(False, 1, *qkv_b, lse_own_b, own, g_own_h, infos[1], first)
    back_own = to_tokens(dqkv_own)
    dqkv_own, info_a, info_b = tie((dqkv_own, *infos))
    first = attend_backward(True, 0, *qkv_a, lse_sh_a, sh, g_sh_h, info_a, None)
    dq_sh, kept, given = attend_backward(True, 1, *qkv_b, lse_sh_b, sh, g_sh_h, info_b, first)
    taken = lax.ppermute(given, "c", SWAP)
    shared_out = jnp.concatenate([(kept.astype(f32) + taken.astype(f32)).astype(bf16), dq_sh], axis=2)
    shared_out, back_own, dqkv_own = tie((shared_out, back_own, dqkv_own))
    back_shared = to_tokens(shared_out.reshape(2, 4, 3, 32, -1))
    d_heads, d_bias = head_grads(scale, (near_a, far_a, near_b, far_b), dqkv_own, dq_sh, kept, given, infos[0])

    head_ready = jnp.concatenate([
        d_heads.reshape(zs, 2, per, 384),
        jnp.broadcast_to(d_bias[:1].astype(bf16)[None, None], (zs, 2, 16, 384))], axis=2)
    head_ready, back_shared = tie((head_ready, back_shared))
    d_rows = token_grad(back_own, back_shared, back_weights, resid)
    if zs == 4:
        group = lax.axis_index("z")
        parts = [lax.dynamic_index_in_dim(head_ready, (group + k) % zs, axis=0, keepdims=False) for k in range(zs)]
        parts = parts[:1] + [
            lax.ppermute(parts[k], "z", [(i, (i + k) % zs) for i in range(zs)]) for k in range(1, zs)]
        head_sum = settle(parts, d_rows)
    else:
        head_sum = lax.psum_scatter(
            head_ready.reshape(-1, 384), "z", scatter_dimension=0, tiled=True).reshape(2, per + 16, 384)
    layer_part, _ = tie((layer_part, d_rows))
    layer_sum = (layer_part.astype(f32) + lax.ppermute(layer_part, "y", SWAP).astype(f32)).astype(bf16)
    returned = lax.all_to_all(
        d_rows.reshape(shards, stretch, width), SHARD, split_axis=0, concat_axis=0, tiled=True)

    def apart(array, bits):
        return lax.ppermute(array, PAIR, [(i, i ^ bits) for i in range(8)]) if bits else array

    halves = [lax.dynamic_index_in_dim(head_sum, x ^ k, axis=0, keepdims=False) for k in range(2)]
    head_eight = jnp.stack([apart(halves[bits >> 2], bits) for bits in range(8)])
    d_wq, d_wk, d_wv, d_bias_rows = head_unpack(head_eight, per, width, infos[0])
    place = lax.axis_index("z") * 2 + x
    own_slice = lambda row, n: lax.dynamic_slice_in_dim(row, place * n, n)
    d_bq, d_bv = own_slice(d_bias_rows[0], per), own_slice(d_bias_rows[1], per)

    layer_grads = flipped(jnp.stack([layer_sum, lax.ppermute(layer_sum, "c", SWAP)]), 0, c)
    layer_grads = layer_grads.reshape(9 * per + 32, width).astype(f32)
    d_wouter = layer_grads[:4 * per]
    d_winner = jnp.concatenate([layer_grads[(4 + n) * per:(5 + n) * per] for n in range(4)], axis=1)
    d_woutput = layer_grads[8 * per:9 * per]
    d_binner = own_slice(layer_grads[9 * per:9 * per + 4].reshape(-1), 4 * per)
    d_bo, d_g1, d_s1, d_bout, d_g2, d_s2 = (own_slice(layer_grads[9 * per + 4 + n], per) for n in range(6))
    small = (d_bq, d_bv, d_binner, d_bo, d_g1, d_s1, d_bout, d_g2, d_s2)
    returned = tie((returned, d_wouter, d_winner, d_woutput, d_wq, d_wk, d_wv) + small)[0]
    steps = jnp.arange(seq_count, dtype=jnp.int32)
    slot_of = jnp.sum(jnp.where(deal_order[:, None] == steps[None, :], steps[:, None], 0), axis=0)
    d_tokens = returned.at[slot_of].get(mode="promise_in_bounds")[:, None]
    return (act.reshape(1, shards, stretch, width), d_tokens, d_wq, d_wk, d_wv, d_woutput, d_bq, d_bv, d_bo,
            d_g1, d_s1, d_winner, d_binner, d_wouter, d_bout, d_g2, d_s2)


def solution(mesh):
    shards, splits = mesh.devices.shape
    fine = Mesh(mesh.devices.reshape(shards // 2, 2, splits // 2, 2), ALL)
    S, Q = SHARD, ("y", "c")
    row, mat = P(S), P(S, None)
    return jax.shard_map(
        body, mesh=fine,
        in_specs=(P(None, S, Q, None), P(), P(), mat, mat, mat, mat, row, row, row, row, row, mat, row, mat, row, row, row,
                  P(S, None, Q, None)),
        out_specs=(P(S, None, Q, None), P(None, S, Q, None), mat, mat, mat, mat, row, row, row, row, row, mat, row, mat,
                   row, row, row),
        check_vma=False)
```

```python
import functools, math
import jax
import jax.numpy as jnp
from jax import lax
from jax.experimental import pallas as pl
from jax.experimental.pallas import tpu as pltpu
from jax.sharding import Mesh, PartitionSpec as P

f32, bf16 = jnp.float32, jnp.bfloat16
LOG2E = 1.4426950408889634
LN2 = 0.6931471805599453
CH = 256
BQ = 2048
RB = 256
FB = 512
PARTS = 2
HD = 64
FAR = -1.0e30

def dg(a, b, ca, cb):
    return lax.dot_general(a, b, (((ca,), (cb,)), ((), ())), preferred_element_type=f32)


def three_parts(row):
    hi = row.astype(bf16).astype(f32)
    rest = row - hi
    mid = rest.astype(bf16).astype(f32)
    return hi, mid, rest - mid


def with_shift(top, shift):
    hi, mid, low = three_parts(shift)
    row = lax.broadcasted_iota(jnp.int32, (HD, top.shape[1]), 0)
    tail = jnp.where(row == 0, -hi, jnp.where(row == 1, -mid, jnp.where(row == 2, -low, jnp.where(row == 3, 1.0, 0.0))))
    return jnp.concatenate([top.astype(f32), tail], axis=0)


def load_rows(rows, ref, spans, x):
    stretch = ref.shape[3]
    for z in range(spans):
        for a in range(2):
            at = (2 * z + a) * stretch
            rows[at:at + stretch] = ref[0, a ^ x, z]


def qkv_kernel(stretch, spans, info, near_ref, far_ref, w_ref, b_ref, q_out, k_out, v_out, size_out, rows):
    away, half = pl.program_id(0), pl.program_id(2)
    owner = ((pl.program_id(1) ^ info[2]) << 1) | (away ^ info[3])

    @pl.when(away == 0)
    def _():
        load_rows(rows, near_ref, spans, info[1])

    @pl.when(away == 1)
    def _():
        load_rows(rows, far_ref, spans, info[1])
    weight = w_ref[...].reshape(rows.shape[1], 384)
    made = dg(rows[...], weight, 1, 0) + b_ref[...]
    count = rows.shape[0]
    q_t = (made[:, :128] * (LOG2E / 8.0)).T
    q_out[0, 0] = q_t[:HD].astype(bf16)
    q_out[1, 0] = q_t[HD:].astype(bf16)
    lane = lax.broadcasted_iota(jnp.int32, (count, 128), 1)
    row = lax.broadcasted_iota(jnp.int32, (count, 128), 0) + half * count
    shift = int(math.log2(stretch))
    position = lax.shift_left(lax.shift_right_logical(row, shift), shift + 2) + owner * stretch + (row & (stretch - 1))
    hidden = jnp.where(position < info[0], 0.0, FAR)
    tail = jnp.where(lane == HD + 3, hidden, jnp.where(lane < HD + 3, 1.0, 0.0))
    keys = made[:, 128:256]
    picks = lax.broadcasted_iota(jnp.int32, (128, 128), 0) // HD == lax.broadcasted_iota(jnp.int32, (128, 128), 1)
    sizes = dg((keys * keys).astype(bf16), jnp.where(picks, 1.0, 0.0).astype(bf16), 1, 0)
    size_out[0, 0] = jnp.max(sizes, axis=0, keepdims=True)
    for head in range(2):
        turned = keys if head == 0 else pltpu.roll(keys, HD, 1)
        full = jnp.where(lane < HD, turned, tail).astype(bf16)
        for j in range(count // 128):
            k_out[head, j, 0] = full[j * 128:(j + 1) * 128]
    v_t = made[:, 256:384].T
    ones = jnp.where(lax.broadcasted_iota(jnp.int32, (HD, count), 0) < 3, 1.0, 0.0)
    for head in range(2):
        full = jnp.concatenate([v_t[head * HD:(head + 1) * HD], ones], axis=0).astype(bf16)
        for j in range(count // 128):
            v_out[head, j, 0] = full[:, j * 128:(j + 1) * 128]


def owner_of(away, across, info):
    return ((across ^ info[2]) << 1) | (away ^ info[3])


def project(near, far, weight, bias, info):
    _, _, zs, stretch, width = near.shape
    local = 2 * zs * stretch
    spans = 1024 // (2 * stretch)
    halves = local // 1024
    spans_of_rows = local // 128
    per = spans_of_rows // halves
    block = (1, 2, spans, stretch, width)
    q, k, v, sizes = pl.pallas_call(
        functools.partial(qkv_kernel, stretch, spans),
        grid_spec=pltpu.PrefetchScalarGridSpec(
            num_scalar_prefetch=1, grid=(2, 2, halves),
            in_specs=[
                pl.BlockSpec(block, lambda a, o, h, n: (jnp.where(a == 0, o, 1), 0, jnp.where(a == 0, h, halves - 1), 0, 0)),
                pl.BlockSpec(block, lambda a, o, h, n: (jnp.where(a == 0, 0, o), 0, jnp.where(a == 0, 0, h), 0, 0)),
                pl.BlockSpec((8, width // 8, 384), lambda a, o, h, n: (0, 0, n[1])),
                pl.BlockSpec((1, 384), lambda a, o, h, n: (0, 0)),
            ],
            out_specs=[
                pl.BlockSpec((2, 1, HD, 1024), lambda a, o, h, n: (0, owner_of(a, o, n), 0, h)),
                pl.BlockSpec((2, per, 1, 128, 128), lambda a, o, h, n: (0, h, o ^ n[2], a ^ n[3], 0)),
                pl.BlockSpec((2, per, 1, 128, 128), lambda a, o, h, n: (0, h, o ^ n[2], 0, a ^ n[3])),
                pl.BlockSpec((1, 1, 1, 128), lambda a, o, h, n: (owner_of(a, o, n), h, 0, 0)),
            ],
            scratch_shapes=[pltpu.VMEM((1024, width), bf16)]),
        out_shape=[
            jax.ShapeDtypeStruct((2, 4, HD, local), bf16),
            jax.ShapeDtypeStruct((2, spans_of_rows, 2, CH, 128), bf16),
            jax.ShapeDtypeStruct((2, spans_of_rows, 2, 128, CH), bf16),
            jax.ShapeDtypeStruct((4, halves, 1, 128), f32),
        ],
        compiler_params=pltpu.CompilerParams(vmem_limit_bytes=60 << 20),
        name="qkv",
        cost_estimate=cost(4 * near.size * 384, near.size * 8),
    )(info, near, far, weight, bias)
    return q, k.reshape(2, -1, CH, 128), v.reshape(2, -1, 128, CH), sizes


def step_on(q, j, count):
    last = j + 1 == count
    return jnp.where(last, q + 1, q), jnp.where(last, 0, j + 1)


def assemble(ref, part, shared, core):
    if not shared:
        return jnp.concatenate([ref[0, 2 * part], ref[0, 2 * part + 1]], axis=1)
    at = pl.multiple_of(core * 512, 512)
    return jnp.concatenate([ref[0, n, :, pl.ds(at, 512)] for n in range(4)], axis=1)


def fwd_kernel(shared, info, q_ref, k_ref, v_ref, size_ref, held_ref, out_ref, lse_ref, acc, probs, qa, shifts):
    count = info[4]
    parts = 1 if shared else 2
    lane = lax.broadcasted_iota(jnp.int32, (1, 128), 1)
    sizes = functools.reduce(jnp.maximum, [size_ref[o, h] for o in range(size_ref.shape[0]) for h in range(size_ref.shape[1])])
    widest = jnp.sqrt(jnp.max(jnp.where(lane == int(shared), sizes, 0.0), axis=1, keepdims=True))

    for part in range(parts):
        q_t = assemble(q_ref, part, shared, info[3])
        wide = q_t.astype(f32)
        shift = jnp.sqrt(jnp.sum(wide * wide, axis=0, keepdims=True)) * widest
        shifts[part] = shift
        qa[part] = with_shift(q_t, shift).astype(bf16)

    def raised(part, j):
        return jnp.exp2(dg(k_ref[0, j], qa[part], 1, 0)).astype(bf16)

    probs[0] = raised(0, 0)

    def body(t, carry, ahead_too=True):
        part, j = carry
        now = t & 1
        part_next, j_next = step_on(part, j, count)
        before = jnp.where(j == 0, 0.0, acc[...])
        acc[...] = before + dg(v_ref[0, j], probs[now], 1, 0)
        if ahead_too:
            probs[1 - now] = raised(part_next, j_next)

        @pl.when(j + 1 == count)
        def _():
            total = acc[HD:HD + 1]
            fine = (jnp.min(total) > 2.0 ** -90) & (jnp.max(total) < 2.0 ** 60)

            @pl.when(jnp.logical_not(fine))
            def _():
                plain = qa[part].astype(f32)
                row = lax.broadcasted_iota(jnp.int32, plain.shape, 0)
                qa[part] = jnp.where((row >= HD) & (row < HD + 3), 0.0, plain).astype(bf16)

                def peak(i, top):
                    return jnp.maximum(top, jnp.max(dg(k_ref[0, i], qa[part], 1, 0), axis=0, keepdims=True))
                shift = lax.fori_loop(0, count, peak, jnp.full((1, BQ), FAR, f32))
                shifts[part] = shift
                qa[part] = with_shift(plain[:HD], shift).astype(bf16)
                acc[...] = jnp.zeros_like(acc)

                def again(i, carry):
                    acc[...] += dg(v_ref[0, i], raised(part, i), 1, 0)
                    return carry
                lax.fori_loop(0, count, again, 0)

            total = acc[HD:HD + 1]
            mixed = (acc[:HD] * (1.0 / total)).astype(bf16)
            lse_ref[part] = shifts[part] + jnp.log2(total)
            if shared:
                for n in range(4):
                    out_ref[0, n] = mixed[:, n * 512:(n + 1) * 512]
            else:
                for n in range(2):
                    out_ref[0, 2 * part + n] = mixed[:, n * 1024:(n + 1) * 1024]
        return part_next, j_next

    turns = parts * count
    body(turns - 1, lax.fori_loop(0, turns - 1, body, (0, 0)), False)


def head_spec(shared, *dims):
    zeros = (0,) * len(dims)
    return pl.BlockSpec((1,) + dims, lambda i, n: (int(shared),) + zeros)


def whole_spec(*dims):
    return pl.BlockSpec(dims, lambda i, n: (0,) * len(dims))


def cost(flops, moved, exps=0):
    return pl.CostEstimate(flops=int(flops), bytes_accessed=int(moved), transcendentals=int(exps))


def attend_forward(shared, seq, q, k, v, sizes, info, held):
    _, owners, _, local = q.shape
    chunks = k.shape[1]
    wide = local // 2 if shared else local
    parts = owners * wide // BQ
    pairs = parts * BQ * chunks * CH * 0.6
    shape = jax.ShapeDtypeStruct((2, owners, HD, wide), bf16)
    first = held is None
    if first:
        kernel = lambda info, q, k, v, size, *rest: fwd_kernel(shared, info, q, k, v, size, None, *rest)
    else:
        kernel = functools.partial(fwd_kernel, shared)
    return pl.pallas_call(
        kernel,
        grid_spec=pltpu.PrefetchScalarGridSpec(
            num_scalar_prefetch=1, grid=(1,),
            in_specs=[
                head_spec(shared, owners, HD, local), head_spec(shared, chunks, CH, 128), head_spec(shared, chunks, 128, CH),
                whole_spec(*sizes.shape),
            ] + ([] if first else [pl.BlockSpec(memory_space=pl.ANY)]),
            out_specs=[pl.BlockSpec((1, owners, HD, wide), lambda i, n: (seq, 0, 0, 0)), whole_spec(parts, 1, BQ)],
            scratch_shapes=[
                pltpu.VMEM((128, BQ), f32), pltpu.VMEM((2, CH, BQ), bf16), pltpu.VMEM((parts, 128, BQ), bf16),
                pltpu.VMEM((parts, 1, BQ), f32),
            ]),
        out_shape=[shape, jax.ShapeDtypeStruct((parts, 1, BQ), f32)],
        input_output_aliases={} if first else {5: 0},
        compiler_params=pltpu.CompilerParams(vmem_limit_bytes=48 << 20),
        cost_estimate=cost(pairs * 1024, chunks * CH * 512, pairs),
        name="attend_forward_shared" if shared else "attend_forward_own",
    )(*((info, q, k, v, sizes) + (() if first else (held,))))


def bwd_kernel(shared, first, info, q_ref, k_ref, v_ref, lse_ref, out_ref, gout_ref, *rest):
    rest = rest if first else rest[3 if shared else 1:]
    if shared:
        dq_ref, kept_ref, given_ref, dk_acc, dv_acc, dq_acc, qa, qat, ga, gat, pb, db = rest
    else:
        dqkv_ref, dk_acc, dv_acc, dq_acc, qa, qat, ga, gat, pb, db = rest
    count = info[4]
    chunks = k_ref.shape[1]
    parts = 1 if shared else 2
    dk_acc[...] = jnp.zeros_like(dk_acc)
    dv_acc[...] = jnp.zeros_like(dv_acc)

    def piece(ref, part):
        return jnp.concatenate([ref[0, n] for n in (range(4) if shared else (2 * part, 2 * part + 1))], axis=1)

    for part in range(parts):
        q_full = with_shift(assemble(q_ref, part, shared, info[3]), lse_ref[part])
        qat[part] = q_full.astype(bf16)
        qa[part] = q_full.T.astype(bf16)
        g_t = piece(gout_ref, part)
        meet = jnp.sum(g_t.astype(f32) * piece(out_ref, part).astype(f32), axis=0, keepdims=True)
        g_full = with_shift(g_t, meet)
        gat[part] = g_full.astype(bf16)
        ga[part] = g_full.T.astype(bf16)

    def ahead(part, j, slot):
        raised = jnp.exp2(dg(qa[part], k_ref[0, j], 1, 1))
        pb[slot] = raised.astype(bf16)
        db[slot] = (raised * dg(ga[part], v_ref[0, j], 1, 0)).astype(bf16)

    ahead(0, 0, 0)

    def body(t, carry, ahead_too=True):
        part, j = carry
        now = t & 1
        part_next, j_next = step_on(part, j, count)
        dv_acc[j] += dg(gat[part], pb[now], 1, 0)[:HD]
        dk_acc[j] += dg(qat[part], db[now], 1, 0)[:HD]
        before = jnp.where(j == 0, 0.0, dq_acc[...])
        dq_acc[...] = before + dg(db[now], k_ref[0, j], 1, 0)
        if ahead_too:
            ahead(part_next, j_next, 1 - now)

        @pl.when(j + 1 == count)
        def _():
            dq_t = (dq_acc[...] * 0.125).T[:HD].astype(bf16)
            if shared:
                for n in range(4):
                    dq_ref[0, n, :, :512] = dq_t[:32, n * 512:(n + 1) * 512]
                    dq_ref[0, n, :, 512:] = dq_t[32:, n * 512:(n + 1) * 512]
            else:
                for n in range(2):
                    dqkv_ref[0, 2 * part + n, 0] = dq_t[:, n * 1024:(n + 1) * 1024]
        return part_next, j_next

    turns = parts * count
    body(turns - 1, lax.fori_loop(0, turns - 1, body, (0, 0)), False)
    for block in range(chunks):
        j, across = block // 2, block % 2
        for owner in (2 * across, 2 * across + 1):
            cols = slice((owner - 2 * across) * 128, (owner - 2 * across + 1) * 128)
            dk_wide, dv_wide = dk_acc[block, :, cols] * LN2, dv_acc[block, :, cols]
            dk, dv = dk_wide.astype(bf16), dv_wide.astype(bf16)
            if shared:
                here = info[3] == 0
                kept_ref[0, owner, :, j * 128:(j + 1) * 128] = jnp.where(here, dk_wide, dv_wide).astype(bf16)
                given_ref[0, owner, :, j * 128:(j + 1) * 128] = jnp.where(here, dv_wide, dk_wide).astype(bf16)
            else:
                dqkv_ref[0, owner, 1, :, j * 128:(j + 1) * 128] = dk
                dqkv_ref[0, owner, 2, :, j * 128:(j + 1) * 128] = dv


def attend_backward(shared, seq, q, k, v, lse, out, g_out, info, held):
    _, owners, _, local = q.shape
    chunks = k.shape[1]
    wide = out.shape[3]
    parts = owners * wide // BQ
    pairs = parts * BQ * chunks * CH * 0.6
    shape = jax.ShapeDtypeStruct
    first = held is None
    if shared:
        out_specs = [pl.BlockSpec((1, owners, rows, local), lambda i, n: (seq, 0, 0, 0)) for rows in (32, HD, HD)]
        out_shape = [shape((2, owners, rows, local), bf16) for rows in (32, HD, HD)]
    else:
        out_specs = [pl.BlockSpec((1, owners, 3, HD, local), lambda i, n: (seq, 0, 0, 0, 0))]
        out_shape = [shape((2, owners, 3, HD, local), bf16)]
    kept = () if first else tuple(held)
    of_seq = pl.BlockSpec((1, owners, HD, wide), lambda i, n: (seq, 0, 0, 0))
    return pl.pallas_call(
        functools.partial(bwd_kernel, shared, first),
        grid_spec=pltpu.PrefetchScalarGridSpec(
            num_scalar_prefetch=1, grid=(1,),
            in_specs=[
                head_spec(shared, owners, HD, local), head_spec(shared, chunks, CH, 128), head_spec(shared, chunks, 128, CH),
                whole_spec(parts, 1, BQ), of_seq, of_seq,
            ] + [pl.BlockSpec(memory_space=pl.ANY)] * len(kept),
            out_specs=out_specs,
            scratch_shapes=[
                pltpu.VMEM((chunks, HD, CH), f32), pltpu.VMEM((chunks, HD, CH), f32), pltpu.VMEM((BQ, 128), f32),
                pltpu.VMEM((parts, BQ, 128), bf16), pltpu.VMEM((parts, 128, BQ), bf16),
                pltpu.VMEM((parts, BQ, 128), bf16), pltpu.VMEM((parts, 128, BQ), bf16),
                pltpu.VMEM((2, BQ, CH), bf16), pltpu.VMEM((2, BQ, CH), bf16),
            ]),
        out_shape=out_shape,
        input_output_aliases={7 + n: n for n in range(len(kept))},
        compiler_params=pltpu.CompilerParams(vmem_limit_bytes=56 << 20),
        cost_estimate=cost(pairs * 100, chunks * CH * 2048),
        name="attend_backward_shared" if shared else "attend_backward_own",
    )(info, q, k, v, lse, out, g_out, *kept)


def gelu_pair(u):
    half = 0.5 * (1.0 + lax.erf(u * 0.7071067811865476))
    return u * half, half + u * (0.3989422804014327 * jnp.exp2(u * u * (-0.5 * LOG2E)))


def norm_stats(v):
    mean = jnp.mean(v, axis=-1, keepdims=True)
    centred = v - mean
    inverse = lax.rsqrt(jnp.mean(centred * centred, axis=-1, keepdims=True) + 1e-12)
    return centred * inverse, inverse


def norm_back(grad, xhat, inverse, gain):
    g = grad * gain
    return (g - jnp.mean(g, axis=-1, keepdims=True) - xhat * jnp.mean(g * xhat, axis=-1, keepdims=True)) * inverse


def weight_part(ref, first, rows):
    part = ref[:, first:first + rows, :]
    return part.reshape(part.shape[0] * rows, part.shape[2])


def ffn_kernel(spans, info, x_ref, own_ref, sh_ref, cot_ref, w_ref, bin_ref, vec_ref,
               act_out, resid_out, gown_out, gsh_out, active_out, dinner_out, normed_out, douter_out, dbranch_out,
               vec_sum, bin_sum, slope, row_block):
    step = pl.program_id(0)
    load_rows(row_block, x_ref, spans, info[1])
    count = row_block.shape[0] // PARTS
    vec = vec_ref[...]
    total = lambda a: jnp.sum(a, axis=0, keepdims=True)
    held = [{"at": slice(n * count, (n + 1) * count)} for n in range(PARTS)]

    def branch(h):
        at = h["at"]
        mixed_t = jnp.concatenate(
            [part for p in range(4) for part in (own_ref[p, 0, :, at], sh_ref[p, 0, :, at], own_ref[p, 1, :, at])], axis=0)
        h["sum1"] = row_block[at].astype(f32) + (dg(mixed_t, weight_part(w_ref, 768, 96), 0, 0) + vec[0:1])

    def first_norm(h):
        h["xhat1"], h["inv1"] = norm_stats(h["sum1"])
        normed = h["xhat1"] * vec[1:2] + vec[2:3]
        normed_out[h["at"]] = normed.astype(bf16)
        h["outer"] = normed + vec[3:4]

    def widen(h):
        at = h["at"]
        for n in range(4):
            cols = slice(n * 768, (n + 1) * 768)
            value, bend = gelu_pair(dg(normed_out[at], weight_part(w_ref, 384 + 96 * n, 96), 1, 0) + bin_ref[:, cols])
            active_out[at, cols] = value.astype(bf16)
            slope[at, cols] = bend.astype(bf16)

    def narrow(h):
        h["outer"] = h["outer"] + dg(active_out[h["at"]], weight_part(w_ref, 0, 384), 1, 0)

    def second_norm(h):
        at = h["at"]
        xhat2, inv2 = norm_stats(h["outer"])
        act_out[at] = (xhat2 * vec[4:5] + vec[5:6]).astype(bf16)
        cot = cot_ref[at].astype(f32)
        d2 = norm_back(cot, xhat2, inv2, vec[4:5])
        d_outer = d2.astype(bf16)
        douter_out[at] = d_outer
        h["d_normed"] = d2
        h["sums"] = [total(d_outer.astype(f32)), total(cot * xhat2), total(cot)]

    def back(h):
        at = h["at"]
        h["inner_sums"] = []
        for n in range(4):
            cols = slice(n * 768, (n + 1) * 768)
            d_active = dg(douter_out[at], weight_part(w_ref.at[2 * n:2 * n + 2], 0, 384), 1, 1)
            d_inner = (d_active * slope[at, cols].astype(f32)).astype(bf16)
            dinner_out[at, cols] = d_inner
            h["inner_sums"].append(total(d_inner.astype(f32)))
            h["d_normed"] = h["d_normed"] + dg(d_inner, weight_part(w_ref, 384 + 96 * n, 96), 1, 1)

    def first_back(h):
        at = h["at"]
        d_normed = h["d_normed"]
        d1 = norm_back(d_normed, h["xhat1"], h["inv1"], vec[1:2])
        resid_out[at] = d1
        d_branch = d1.astype(bf16)
        dbranch_out[at] = d_branch
        h["sums"] = [total(d_branch.astype(f32)), total(d_normed * h["xhat1"]), total(d_normed)] + h["sums"]

    def mix_back(h):
        at = h["at"]
        g_t = dg(weight_part(w_ref, 768, 96), dbranch_out[at], 1, 1).astype(bf16)
        for p in range(4):
            gown_out[p, 0, :, at] = g_t[192 * p:192 * p + 64]
            gsh_out[p, 0, :, at] = g_t[192 * p + 64:192 * p + 128]
            gown_out[p, 1, :, at] = g_t[192 * p + 128:192 * p + 192]

    for products, norm in ((branch, first_norm), (widen, None), (narrow, second_norm), (back, first_back), (mix_back, None)):
        for h in held:
            products(h)
            if norm is not None:
                norm(h)
    sums = jnp.concatenate([
        functools.reduce(jnp.add, [h["sums"][n] for h in held]) for n in range(6)] + [jnp.zeros((2, vec.shape[1]), f32)], axis=0)
    inner_sums = [functools.reduce(jnp.add, [h["inner_sums"][n] for h in held]) for n in range(4)]

    @pl.when(step == 0)
    def _():
        vec_sum[...] = sums
        for n in range(4):
            bin_sum[:, n * 768:(n + 1) * 768] = inner_sums[n]

    @pl.when(step > 0)
    def _():
        vec_sum[...] += sums
        for n in range(4):
            bin_sum[:, n * 768:(n + 1) * 768] += inner_sums[n]


def feed_forward(rows_in, own, sh, cotangent, weights, inner_bias, vectors, info):
    _, _, _, stretch, width = rows_in.shape
    local = cotangent.shape[0]
    spans = FB // (2 * stretch)
    steps = local // FB
    half_steps = steps // 2
    wide = inner_bias.shape[1]
    rows = lambda n: pl.BlockSpec((FB, n), lambda r, a: (r, 0))
    fixed = lambda *dims: pl.BlockSpec(dims, lambda r, a: (0,) * len(dims))
    own_spec = pl.BlockSpec((4, 2, HD, FB), lambda r, a: (0, 0, 0, r))
    sh_spec = pl.BlockSpec((4, 1, HD, FB), lambda r, a: (0, r // half_steps, 0, r % half_steps))
    shape = jax.ShapeDtypeStruct
    return pl.pallas_call(
        functools.partial(ffn_kernel, spans),
        grid_spec=pltpu.PrefetchScalarGridSpec(
            num_scalar_prefetch=1, grid=(steps,),
            in_specs=[
                pl.BlockSpec((1, 2, spans, stretch, width), lambda r, a: (0, 0, r, 0, 0)),
                own_spec, sh_spec, rows(width),
                pl.BlockSpec(weights.shape, lambda r, a: (0, 0, 0), pipeline_mode=pl.Buffered(1)),
                fixed(1, wide), fixed(8, width),
            ],
            out_specs=[
                rows(width), rows(width), own_spec, sh_spec, rows(wide), rows(wide), rows(width), rows(width), rows(width),
                fixed(8, width), fixed(1, wide),
            ],
            scratch_shapes=[pltpu.VMEM((FB, wide), bf16), pltpu.VMEM((FB, width), bf16)]),
        out_shape=[
            shape((local, width), bf16), shape((local, width), f32), shape(own.shape, bf16), shape(sh.shape, bf16),
            shape((local, wide), bf16), shape((local, wide), bf16), shape((local, width), bf16),
            shape((local, width), bf16), shape((local, width), bf16), shape((8, width), f32), shape((1, wide), f32),
        ],
        compiler_params=pltpu.CompilerParams(vmem_limit_bytes=60 << 20),
        name="feed_forward",
        cost_estimate=cost(local * width * (width + 2 * wide) * 4, local * wide * 20),
    )(info, rows_in, own, sh, cotangent, weights, inner_bias, vectors)


def outer_grad_kernel(scale, active_ref, douter_ref, out_ref):
    made = (dg(active_ref[...], douter_ref[...], 0, 0) * scale).astype(bf16)
    out_ref[...] = made.reshape(out_ref.shape)


def inner_grad_kernel(scale, packed_ref, normed_ref, dinner_ref, own_ref, sh_ref, dbranch_ref, out_ref):
    step = pl.program_id(0)

    @pl.when(step < 4)
    def _():
        out_ref[...] = (dg(normed_ref[...], dinner_ref[...], 0, 0) * scale).astype(bf16).reshape(out_ref.shape)

    @pl.when(step == 4)
    def _():
        mixed_t = jnp.concatenate([
            part for p in range(4)
            for part in (own_ref[p, 0], jnp.concatenate([sh_ref[p, 0], sh_ref[p, 1]], axis=1), own_ref[p, 1])], axis=0)
        out_ref[...] = (dg(mixed_t, dbranch_ref[...], 1, 0) * scale).astype(bf16).reshape(out_ref.shape)


def weight_grads(scale, active, d_outer, normed, d_inner, own, sh, d_branch):
    local, wide = active.shape
    width = normed.shape[1]
    packed = pl.pallas_call(
        functools.partial(outer_grad_kernel, scale), grid=(4,),
        in_specs=[pl.BlockSpec((local, width), lambda m: (0, m)), pl.BlockSpec((local, width), lambda m: (0, 0))],
        out_specs=pl.BlockSpec((2, 384, width), lambda m: (m, 0, 0)),
        out_shape=jax.ShapeDtypeStruct((8, 896, width), bf16),
        compiler_params=pltpu.CompilerParams(vmem_limit_bytes=40 << 20), name="outer_grad",
        cost_estimate=cost(2 * local * wide * width, 2 * wide * (local + width)),
    )(active, d_outer)
    fixed = lambda a: pl.BlockSpec(a.shape, lambda n: (0,) * a.ndim)
    return pl.pallas_call(
        functools.partial(inner_grad_kernel, scale), grid=(5,),
        in_specs=[
            pl.BlockSpec(memory_space=pl.ANY), fixed(normed),
            pl.BlockSpec((local, width), lambda n: (0, jnp.minimum(n, 3))), fixed(own), fixed(sh), fixed(d_branch)],
        out_specs=pl.BlockSpec((8, 96, width), lambda n: (0, 4 + n, 0)),
        out_shape=jax.ShapeDtypeStruct((8, 896, width), bf16), input_output_aliases={0: 0},
        compiler_params=pltpu.CompilerParams(vmem_limit_bytes=40 << 20), name="inner_grad",
        cost_estimate=cost(2 * local * (wide + width) * width, 2 * (wide + width) * (local + width)),
    )(packed, normed, d_inner, own, sh, d_branch)


def head_grad_kernel(scale, spans, info, *refs):
    x_refs, (own_ref, dq_ref, kept_ref, given_ref, out_ref, bias_out, acc, bias_acc, rows) = refs[:4], refs[4:]
    seq, away, half = pl.program_id(0), pl.program_id(1), pl.program_id(3)
    last = (seq == 1) & (away == 1) & (pl.program_id(2) == 1) & (half == pl.num_programs(3) - 1)
    for n in range(4):
        @pl.when(seq * 2 + away == n)
        def _(n=n):
            load_rows(rows, x_refs[n], spans, info[1])
    dq_t = jnp.where(half == info[3], jnp.concatenate([dq_ref[0, 0, :, :512], dq_ref[0, 0, :, 512:]], axis=0).astype(f32), 0.0)
    kept, given = kept_ref[0, 0].astype(f32), given_ref[0, 0].astype(f32)
    here = info[3] == 0
    d_t = jnp.concatenate([
        own_ref[0, 0, 0], dq_t.astype(bf16), own_ref[0, 0, 1], jnp.where(here, kept, given).astype(bf16),
        own_ref[0, 0, 2], jnp.where(here, given, kept).astype(bf16)], axis=0)

    @pl.when((seq == 0) & (away == 0) & (pl.program_id(2) == 0) & (half == 0))
    def _():
        acc[...] = jnp.zeros_like(acc)
        bias_acc[...] = jnp.zeros_like(bias_acc)
    acc[...] += dg(d_t, rows[...], 1, 0)
    bias_acc[...] += dg(jnp.ones((8, d_t.shape[1]), bf16), d_t, 1, 1)

    @pl.when(last)
    def _():
        out_ref[...] = (acc[...] * scale).T.astype(bf16)
        bias_out[...] = bias_acc[...] * scale


def head_grads(scale, sources, dqkv_own, dq_sh, kept, given, info):
    _, _, zs, stretch, width = sources[0].shape
    local = 2 * zs * stretch
    spans = 512 // (2 * stretch)
    halves = local // 512

    def source_spec(n):
        def index(s, a, o, h, i):
            now = 2 * s + a
            across = jnp.where(now == n, o, jnp.where(now < n, 0, 1))
            return (across, 0, jnp.where(now == n, h, jnp.where(now < n, 0, halves - 1)), 0, 0)
        return pl.BlockSpec((1, 2, spans, stretch, width), index)
    return pl.pallas_call(
        functools.partial(head_grad_kernel, scale, spans),
        grid_spec=pltpu.PrefetchScalarGridSpec(
            num_scalar_prefetch=1, grid=(2, 2, 2, halves),
            in_specs=[source_spec(n) for n in range(4)] + [
                pl.BlockSpec((1, 1, 3, HD, 512), lambda s, a, o, h, i: (s, owner_of(a, o, i), 0, 0, h)),
                pl.BlockSpec((1, 1, 32, local), lambda s, a, o, h, i: (s, owner_of(a, o, i), 0, 0)),
            ] + [pl.BlockSpec((1, 1, HD, 512), lambda s, a, o, h, i: (s, owner_of(a, o, i), 0, h))] * 2,
            out_specs=[pl.BlockSpec((width, 384), lambda s, a, o, h, i: (0, 0)), pl.BlockSpec((8, 384), lambda s, a, o, h, i: (0, 0))],
            scratch_shapes=[pltpu.VMEM((384, width), f32), pltpu.VMEM((8, 384), f32), pltpu.VMEM((512, width), bf16)]),
        out_shape=[jax.ShapeDtypeStruct((width, 384), bf16), jax.ShapeDtypeStruct((8, 384), f32)],
        compiler_params=pltpu.CompilerParams(vmem_limit_bytes=40 << 20), name="head_grads",
        cost_estimate=cost(8 * local * 768 * width, 8 * local * width * 2),
    )(info, *sources, dqkv_own, dq_sh, kept, given)


def token_grad_kernel(own_ref, low_ref, high_ref, dkv_ref, w_ref, resid_ref, out_ref):
    total = resid_ref[...]
    for kind in range(3):
        made = []
        for p in range(4):
            if kind == 0:
                middle = jnp.concatenate([low_ref[p, 0], high_ref[p, 0]], axis=0)
            else:
                middle = jnp.concatenate([dkv_ref[p, kind - 1, n] for n in range(2)], axis=0)
            made += [own_ref[p, 0, kind], middle, own_ref[p, 1, kind]]
        total = total + dg(jnp.concatenate(made, axis=0), weight_part(w_ref, 96 * kind, 96), 0, 1)
    out_ref[...] = total.astype(bf16)


def token_grad(own, shared, weights, resid):
    local, width = resid.shape
    steps = local // RB
    half_steps = steps // 2
    rows = pl.BlockSpec((RB, width), lambda r: (r, 0))
    return pl.pallas_call(
        token_grad_kernel, grid=(steps,),
        in_specs=[
            pl.BlockSpec((4, 2, 3, HD, RB), lambda r: (0, 0, 0, 0, r)),
            pl.BlockSpec((4, 1, None, 32, RB), lambda r: (0, r // half_steps, 2, 0, r % half_steps)),
            pl.BlockSpec((4, 1, None, 32, RB), lambda r: (0, r // half_steps, 2, 0, half_steps + r % half_steps)),
            pl.BlockSpec((4, 2, 2, 32, RB), lambda r: (0, 0, 0, 0, r)),
            pl.BlockSpec(weights.shape, lambda r: (0, 0, 0)), rows],
        out_specs=rows, out_shape=jax.ShapeDtypeStruct((local, width), bf16),
        compiler_params=pltpu.CompilerParams(vmem_limit_bytes=60 << 20), name="token_grad",
        cost_estimate=cost(local * width * width * 6, local * width * 12),
    )(own, shared, shared, shared, weights, resid)


def head_unpack_kernel(per, info, src_ref, q_out, k_out, v_out, bias_out):
    low = lax.broadcasted_iota(jnp.int32, (src_ref.shape[1], 128), 1) < HD

    def rows_of(p, core, cols):
        at = (((p >> 1) ^ info[1]) << 2) | (((p & 1) ^ info[2]) << 1) | (core ^ info[3])
        return src_ref[at, :, cols].astype(f32)
    for kind, out in enumerate((q_out, k_out, v_out)):
        cols = slice(128 * kind, 128 * kind + 128)
        tiles = []
        for pair in range(2):
            first, second = [], []
            for p in (2 * pair, 2 * pair + 1):
                near, far = rows_of(p, 0, cols), rows_of(p, 1, cols)
                first.append(near + jnp.where(low, 0.0, far))
                second.append(far)
            turned = pltpu.roll(first[1], HD, 1)
            tiles += [first[0], jnp.where(low, second[0], turned), jnp.where(low, turned, pltpu.roll(second[1], HD, 1))]
        made = jnp.concatenate(tiles, axis=1)
        out[...] = made[:per]
        if kind != 1:
            bias_out[kind // 2:kind // 2 + 1] = made[per:per + 1]


def head_unpack(source, per, width, info):
    shape = jax.ShapeDtypeStruct
    full = lambda n: pl.BlockSpec((n, width), lambda i, f: (0, 0))
    return pl.pallas_call(
        functools.partial(head_unpack_kernel, per),
        grid_spec=pltpu.PrefetchScalarGridSpec(
            num_scalar_prefetch=1, grid=(1,),
            in_specs=[pl.BlockSpec(source.shape, lambda i, f: (0, 0, 0))],
            out_specs=[full(per)] * 3 + [full(2)]),
        out_shape=[shape((per, width), f32)] * 3 + [shape((2, width), f32)], name="head_unpack",
    )(info, source)


SWAP = [(0, 1), (1, 0)]
def settle_kernel(*refs):
    refs[-1][...] = sum(ref[...].astype(f32) for ref in refs[:-2]).astype(bf16)


def settle(parts, after):
    whole = pl.BlockSpec(memory_space=pltpu.VMEM)
    return pl.pallas_call(
        settle_kernel, in_specs=[whole] * len(parts) + [pl.BlockSpec(memory_space=pl.ANY)], out_specs=whole,
        out_shape=jax.ShapeDtypeStruct(parts[0].shape, bf16), name="settle",
        cost_estimate=cost(1e9, 1e6),
    )(*parts, after)


PAIR = ("x", "y", "c")
ALL = ("z", "x", "y", "c")
SHARD = ("z", "x")


def canonical(packed, shards):
    if shards == 8:
        return packed
    width = packed.shape[2]
    per, keep = 96 * 8 // shards, shards // 8
    outer = packed[:, :4 * per].reshape(8, 384, width)
    inner = packed[:, 4 * per:8 * per].reshape(8, keep, 4, per, width).transpose(0, 2, 1, 3, 4).reshape(8, 384, width)
    output = packed[:, 8 * per:9 * per].reshape(8, 96, width)
    return jnp.concatenate([outer, inner, output, jnp.zeros((8, 32, width), packed.dtype)], axis=1)


def from_canonical(packed, last, shards):
    width = packed.shape[2]
    if shards == 8:
        return packed.at[:, 864:].set(jnp.broadcast_to(last[None], (8, 32, width)))
    per, keep = 96 * 8 // shards, shards // 8
    outer = packed[:, :384].reshape(shards, 4 * per, width)
    inner = packed[:, 384:768].reshape(8, 4, keep, per, width).transpose(0, 2, 1, 3, 4).reshape(shards, 4 * per, width)
    output = packed[:, 768:864].reshape(shards, per, width)
    return jnp.concatenate([outer, inner, output, jnp.broadcast_to(last[None], (shards, 32, width))], axis=1)


def canonical_heads(packed, shards, parts):
    if shards == 8:
        return packed
    width = packed.shape[2]
    per = 96 * 8 // shards
    made = [packed[:, k * per:(k + 1) * per].reshape(8, 96, width) for k in range(parts)]
    return jnp.concatenate(made + [jnp.zeros((8, 32, width), packed.dtype)], axis=1)


def quarter(rows):
    place = lax.axis_index("y") * 2 + lax.axis_index("c")
    part = rows.shape[0] // 4
    return lax.dynamic_slice_in_dim(rows, place * part, part)


def flipped(array, axis, here):
    return jnp.where(here == 0, array, jnp.flip(array, axis))


def body(tokens, lengths, deal_order, w_query, w_key, w_value, w_output, b_query, b_value, b_output,
         ln1_gain, ln1_shift, w_inner, b_inner, w_outer, b_outer, ln2_gain, ln2_shift, cotangent):
    tie = lax.optimization_barrier
    zs = lax.axis_size("z")
    shards = 2 * zs
    scale = 1.0 / (shards * 4)
    seq_count, _, stretch, width = tokens.shape
    per = w_query.shape[0]
    half = zs // 2
    x, y, c = lax.axis_index("x"), lax.axis_index("y"), lax.axis_index("c")

    def deal(ordered):
        return lax.all_to_all(ordered, "z", split_axis=0, concat_axis=0, tiled=True)

    def corner(across, along):
        return [lax.ppermute(across[:half], "y", SWAP), lax.ppermute(along[half:], "x", SWAP)]

    def this_core(own, across, along, corner):
        return jnp.concatenate([own, across, along] + corner, axis=0).reshape(2, 2, zs, stretch, width)

    ordered_a = tokens[:, 0].at[deal_order[0::2]].get(mode="promise_in_bounds")
    first_own = deal(ordered_a)
    _, tokens, w_query, w_key, w_value, b_query, b_value, deal_order = tie(
        (ordered_a, tokens, w_query, w_key, w_value, b_query, b_value, deal_order))
    ordered_b = tokens[:, 0].at[deal_order[1::2]].get(mode="promise_in_bounds")

    def head_columns(matrix):
        heads = matrix.reshape(per, 2, 2, 3, HD)
        mine = lax.dynamic_index_in_dim(heads, y, axis=2, keepdims=False)
        own = lax.dynamic_index_in_dim(mine, 2 * c, axis=2, keepdims=False)
        return [own, mine[:, :, 1]]
    pad = lambda v: jnp.pad(v, (0, width - v.shape[0]))[None]
    columns = jnp.concatenate(
        [col for matrix in (w_query, w_key, w_value) for col in head_columns(matrix)], axis=2).reshape(per, width)
    head_pack = jnp.concatenate([columns, pad(b_query), pad(b_value), jnp.zeros((14, width), bf16)], axis=0)
    first_own, ordered_b, head_pack = tie((first_own, ordered_b, head_pack))
    head_all = lax.all_gather(head_pack, SHARD, axis=0, tiled=False)
    head_weight = canonical_heads(head_all, shards, 1)

    def head_bias(row):
        heads = head_all[:, per + row, :per].reshape(2, 2, 3, HD)
        mine = lax.dynamic_slice(heads, (x, y, 0, 0), (1, 1, 3, HD))[0, 0]
        return [lax.dynamic_index_in_dim(mine, 2 * c, axis=0, keepdims=False), mine[1]]
    bias_row = jnp.concatenate(head_bias(0) + [jnp.zeros((2 * HD,), bf16)] + head_bias(1)).astype(f32)[None]

    across_a, along_a = lax.ppermute(first_own, "x", SWAP), lax.ppermute(first_own, "y", SWAP)
    second_own = deal(ordered_b)
    across_a, along_a, second_own, w_outer, w_inner, w_output, b_inner = tie(
        (across_a, along_a, second_own, w_outer, w_inner, w_output, b_inner))
    corner_a = corner(across_a, along_a)
    second_own, *corner_a = tie((second_own, *corner_a))
    near_a = this_core(first_own, across_a, along_a, corner_a)
    far_a = lax.ppermute(near_a, "c", SWAP)
    across_b, along_b = lax.ppermute(second_own, "x", SWAP), lax.ppermute(second_own, "y", SWAP)

    vectors = (b_output, ln1_gain, ln1_shift, b_outer, ln2_gain, ln2_shift)
    layer_pack = jnp.concatenate(
        [w_outer] + [w_inner[:, n * width:(n + 1) * width] for n in range(4)] + [w_output]
        + [pad(b_inner)] + [pad(v) for v in vectors] + [jnp.zeros((25, width), bf16)], axis=0)
    layer_quarter = quarter(layer_pack)
    back_quarter = quarter(jnp.concatenate([w_query, w_key, w_value, jnp.zeros((32, width), bf16)], axis=0))
    layer_all = lax.all_gather(layer_quarter, ALL, axis=0, tiled=True).reshape(shards, 9 * per + 32, width)
    layer_weights = canonical(layer_all, shards)
    inner_bias = layer_all[:, 9 * per, :4 * per].reshape(1, 4 * width).astype(f32)
    vector_rows = jnp.concatenate(
        [layer_all[:, 9 * per + 1 + n, :per].reshape(1, width) for n in range(6)] + [jnp.zeros((2, width), bf16)],
        axis=0).astype(f32)
    back_all = lax.all_gather(back_quarter, ALL, axis=0, tiled=True).reshape(shards, 3 * per + 32, width)

    slots = lax.dynamic_slice_in_dim(deal_order, lax.axis_index("z") * 2, 2)
    matches = slots[:, None] == jnp.arange(seq_count, dtype=jnp.int32)[None, :]
    lens = jnp.sum(jnp.where(matches, lengths[None, :], 0), axis=1).astype(jnp.int32)
    last = (lens + 511) // 512 - 1
    counts = 2 * last + 1 + (lens > 512 * last + 2 * stretch).astype(jnp.int32)
    infos = [jnp.stack([lens[n], x, y, c, counts[n]]).astype(jnp.int32) for n in range(2)]

    def swap(array):
        flat = array.reshape((8,) + array.shape[2:])
        return lax.all_to_all(flat, PAIR, split_axis=0, concat_axis=0, tiled=True)

    def to_tokens(array):
        return swap(array).reshape((4, 2) + array.shape[2:])

    def to_heads(array):
        return swap(array).reshape((2, 4) + array.shape[2:])

    heads_a = project(near_a, far_a, head_weight, bias_row, infos[0])
    heads_a, across_b, along_b = tie((heads_a, across_b, along_b))
    near_b = this_core(second_own, across_b, along_b, corner(across_b, along_b))
    own_first, lse_own_a = attend_forward(False, 0, *heads_a, infos[0], None)
    own_first, near_b = tie((own_first, near_b))
    far_b = lax.ppermute(near_b, "c", SWAP)
    heads_b = project(near_b, far_b, head_weight, bias_row, infos[1])
    own, lse_own_b = attend_forward(False, 1, *heads_b, infos[1], own_first)
    own_t = to_tokens(own)
    own, info_a, info_b = tie((own, *infos))
    sh_first, lse_sh_a = attend_forward(True, 0, *heads_a, info_a, None)
    sh, lse_sh_b = attend_forward(True, 1, *heads_b, info_b, sh_first)
    sh_sent, own_t = tie((sh, own_t))
    sh_t = to_tokens(sh_sent)
    mine_rows = jnp.where(x == 0, jnp.stack([first_own, across_a]), jnp.stack([second_own, across_b]))[None]

    (act, resid, g_own, g_sh, active, d_inner, normed, d_outer, d_branch, vec_sums, bin_sums) = feed_forward(
        mine_rows, own_t, sh_t, cotangent.reshape(-1, width), layer_weights, inner_bias, vector_rows, infos[0])
    g_own_h, g_sh_h = to_heads(g_own), to_heads(g_sh)
    active, back_all = tie((active, back_all))
    packed = weight_grads(scale, active, d_outer, normed, d_inner, own_t, sh_t, d_branch)
    sums = jnp.concatenate([bin_sums.reshape(4, width), vec_sums, jnp.zeros((20, width), f32)], axis=0) * scale
    ready = from_canonical(packed, sums.astype(bf16), shards)
    ready, g_own_h = tie((ready, g_own_h))
    back_weights = canonical_heads(back_all, shards, 3)
    layer_part = lax.psum_scatter(ready.reshape(-1, width), ("z", "x", "c"), scatter_dimension=0, tiled=True)

    qkv_a, qkv_b = heads_a[:3], heads_b[:3]
    first = attend_backward(False, 0, *qkv_a, lse_own_a, own, g_own_h, infos[0], None)
    dqkv_own, = attend_backward(False, 1, *qkv_b, lse_own_b, own, g_own_h, infos[1], first)
    back_own = to_tokens(dqkv_own)
    dqkv_own, info_a, info_b = tie((dqkv_own, *infos))
    first = attend_backward(True, 0, *qkv_a, lse_sh_a, sh, g_sh_h, info_a, None)
    dq_sh, kept, given = attend_backward(True, 1, *qkv_b, lse_sh_b, sh, g_sh_h, info_b, first)
    taken = lax.ppermute(given, "c", SWAP)
    shared_out = jnp.concatenate([(kept.astype(f32) + taken.astype(f32)).astype(bf16), dq_sh], axis=2)
    shared_out, back_own, dqkv_own = tie((shared_out, back_own, dqkv_own))
    back_shared = to_tokens(shared_out.reshape(2, 4, 3, 32, -1))
    d_heads, d_bias = head_grads(scale, (near_a, far_a, near_b, far_b), dqkv_own, dq_sh, kept, given, infos[0])

    head_ready = jnp.concatenate([
        d_heads.reshape(zs, 2, per, 384),
        jnp.broadcast_to(d_bias[:1].astype(bf16)[None, None], (zs, 2, 16, 384))], axis=2)
    head_ready, back_shared = tie((head_ready, back_shared))
    d_rows = token_grad(back_own, back_shared, back_weights, resid)
    if zs == 4:
        group = lax.axis_index("z")
        parts = [lax.dynamic_index_in_dim(head_ready, (group + k) % zs, axis=0, keepdims=False) for k in range(zs)]
        parts = parts[:1] + [
            lax.ppermute(parts[k], "z", [(i, (i + k) % zs) for i in range(zs)]) for k in range(1, zs)]
        head_sum = settle(parts, d_rows)
    else:
        head_sum = lax.psum_scatter(
            head_ready.reshape(-1, 384), "z", scatter_dimension=0, tiled=True).reshape(2, per + 16, 384)
    layer_part, _ = tie((layer_part, d_rows))
    layer_sum = (layer_part.astype(f32) + lax.ppermute(layer_part, "y", SWAP).astype(f32)).astype(bf16)
    returned = lax.all_to_all(
        d_rows.reshape(shards, stretch, width), SHARD, split_axis=0, concat_axis=0, tiled=True)

    def apart(array, bits):
        return lax.ppermute(array, PAIR, [(i, i ^ bits) for i in range(8)]) if bits else array

    halves = [lax.dynamic_index_in_dim(head_sum, x ^ k, axis=0, keepdims=False) for k in range(2)]
    head_eight = jnp.stack([apart(halves[bits >> 2], bits) for bits in range(8)])
    d_wq, d_wk, d_wv, d_bias_rows = head_unpack(head_eight, per, width, infos[0])
    place = lax.axis_index("z") * 2 + x
    own_slice = lambda row, n: lax.dynamic_slice_in_dim(row, place * n, n)
    d_bq, d_bv = own_slice(d_bias_rows[0], per), own_slice(d_bias_rows[1], per)

    layer_grads = flipped(jnp.stack([layer_sum, lax.ppermute(layer_sum, "c", SWAP)]), 0, c)
    layer_grads = layer_grads.reshape(9 * per + 32, width).astype(f32)
    d_wouter = layer_grads[:4 * per]
    d_winner = jnp.concatenate([layer_grads[(4 + n) * per:(5 + n) * per] for n in range(4)], axis=1)
    d_woutput = layer_grads[8 * per:9 * per]
    d_binner = own_slice(layer_grads[9 * per:9 * per + 4].reshape(-1), 4 * per)
    d_bo, d_g1, d_s1, d_bout, d_g2, d_s2 = (own_slice(layer_grads[9 * per + 4 + n], per) for n in range(6))
    small = (d_bq, d_bv, d_binner, d_bo, d_g1, d_s1, d_bout, d_g2, d_s2)
    returned = tie((returned, d_wouter, d_winner, d_woutput, d_wq, d_wk, d_wv) + small)[0]
    steps = jnp.arange(seq_count, dtype=jnp.int32)
    slot_of = jnp.sum(jnp.where(deal_order[:, None] == steps[None, :], steps[:, None], 0), axis=0)
    d_tokens = returned.at[slot_of].get(mode="promise_in_bounds")[:, None]
    return (act.reshape(1, shards, stretch, width), d_tokens, d_wq, d_wk, d_wv, d_woutput, d_bq, d_bv, d_bo,
            d_g1, d_s1, d_winner, d_binner, d_wouter, d_bout, d_g2, d_s2)


def solution(mesh):
    shards, splits = mesh.devices.shape
    fine = Mesh(mesh.devices.reshape(shards // 2, 2, splits // 2, 2), ALL)
    S, Q = SHARD, ("y", "c")
    row, mat = P(S), P(S, None)
    return jax.shard_map(
        body, mesh=fine,
        in_specs=(P(None, S, Q, None), P(), P(), mat, mat, mat, mat, row, row, row, row, row, mat, row, mat, row, row, row,
                  P(S, None, Q, None)),
        out_specs=(P(S, None, Q, None), P(None, S, Q, None), mat, mat, mat, mat, row, row, row, row, row, mat, row, mat,
                   row, row, row),
        check_vma=False)
```

```python
import functools, math
import jax
import jax.numpy as jnp
from jax import lax
from jax.experimental import pallas as pl
from jax.experimental.pallas import tpu as pltpu
from jax.sharding import Mesh, PartitionSpec as P

f32, bf16 = jnp.float32, jnp.bfloat16
LOG2E = 1.4426950408889634
LN2 = 0.6931471805599453
CH = 256
BQ = 2048
RB = 256
FB = 512
PARTS = 2
HD = 64
FAR = -1.0e30

def dg(a, b, ca, cb):
    return lax.dot_general(a, b, (((ca,), (cb,)), ((), ())), preferred_element_type=f32)


def three_parts(row):
    hi = row.astype(bf16).astype(f32)
    rest = row - hi
    mid = rest.astype(bf16).astype(f32)
    return hi, mid, rest - mid


def with_shift(top, shift):
    hi, mid, low = three_parts(shift)
    row = lax.broadcasted_iota(jnp.int32, (HD, top.shape[1]), 0)
    tail = jnp.where(row == 0, -hi, jnp.where(row == 1, -mid, jnp.where(row == 2, -low, jnp.where(row == 3, 1.0, 0.0))))
    return jnp.concatenate([top.astype(f32), tail], axis=0)


def load_rows(rows, ref, spans, x):
    stretch = ref.shape[3]
    for z in range(spans):
        for a in range(2):
            at = (2 * z + a) * stretch
            rows[at:at + stretch] = ref[0, a ^ x, z]


def qkv_kernel(stretch, spans, info, near_ref, far_ref, w_ref, b_ref, q_out, k_out, v_out, size_out, rows):
    away, half = pl.program_id(0), pl.program_id(2)
    owner = ((pl.program_id(1) ^ info[2]) << 1) | (away ^ info[3])

    @pl.when(away == 0)
    def _():
        load_rows(rows, near_ref, spans, info[1])

    @pl.when(away == 1)
    def _():
        load_rows(rows, far_ref, spans, info[1])
    weight = w_ref[...].reshape(rows.shape[1], 384)
    made = dg(rows[...], weight, 1, 0) + b_ref[...]
    count = rows.shape[0]
    q_t = (made[:, :128] * (LOG2E / 8.0)).T
    q_out[0, 0] = q_t[:HD].astype(bf16)
    q_out[1, 0] = q_t[HD:].astype(bf16)
    lane = lax.broadcasted_iota(jnp.int32, (count, 128), 1)
    row = lax.broadcasted_iota(jnp.int32, (count, 128), 0) + half * count
    shift = int(math.log2(stretch))
    position = lax.shift_left(lax.shift_right_logical(row, shift), shift + 2) + owner * stretch + (row & (stretch - 1))
    hidden = jnp.where(position < info[0], 0.0, FAR)
    tail = jnp.where(lane == HD + 3, hidden, jnp.where(lane < HD + 3, 1.0, 0.0))
    keys = made[:, 128:256]
    picks = lax.broadcasted_iota(jnp.int32, (128, 128), 0) // HD == lax.broadcasted_iota(jnp.int32, (128, 128), 1)
    sizes = dg((keys * keys).astype(bf16), jnp.where(picks, 1.0, 0.0).astype(bf16), 1, 0)
    size_out[0, 0] = jnp.max(sizes, axis=0, keepdims=True)
    for head in range(2):
        turned = keys if head == 0 else pltpu.roll(keys, HD, 1)
        full = jnp.where(lane < HD, turned, tail).astype(bf16)
        for j in range(count // 128):
            k_out[head, j, 0] = full[j * 128:(j + 1) * 128]
    v_t = made[:, 256:384].T
    ones = jnp.where(lax.broadcasted_iota(jnp.int32, (HD, count), 0) < 3, 1.0, 0.0)
    for head in range(2):
        full = jnp.concatenate([v_t[head * HD:(head + 1) * HD], ones], axis=0).astype(bf16)
        for j in range(count // 128):
            v_out[head, j, 0] = full[:, j * 128:(j + 1) * 128]


def owner_of(away, across, info):
    return ((across ^ info[2]) << 1) | (away ^ info[3])


def project(near, far, weight, bias, info):
    _, _, zs, stretch, width = near.shape
    local = 2 * zs * stretch
    spans = 1024 // (2 * stretch)
    halves = local // 1024
    spans_of_rows = local // 128
    per = spans_of_rows // halves
    block = (1, 2, spans, stretch, width)
    q, k, v, sizes = pl.pallas_call(
        functools.partial(qkv_kernel, stretch, spans),
        grid_spec=pltpu.PrefetchScalarGridSpec(
            num_scalar_prefetch=1, grid=(2, 2, halves),
            in_specs=[
                pl.BlockSpec(block, lambda a, o, h, n: (jnp.where(a == 0, o, 1), 0, jnp.where(a == 0, h, halves - 1), 0, 0)),
                pl.BlockSpec(block, lambda a, o, h, n: (jnp.where(a == 0, 0, o), 0, jnp.where(a == 0, 0, h), 0, 0)),
                pl.BlockSpec((8, width // 8, 384), lambda a, o, h, n: (0, 0, n[1])),
                pl.BlockSpec((1, 384), lambda a, o, h, n: (0, 0)),
            ],
            out_specs=[
                pl.BlockSpec((2, 1, HD, 1024), lambda a, o, h, n: (0, owner_of(a, o, n), 0, h)),
                pl.BlockSpec((2, per, 1, 128, 128), lambda a, o, h, n: (0, h, o ^ n[2], a ^ n[3], 0)),
                pl.BlockSpec((2, per, 1, 128, 128), lambda a, o, h, n: (0, h, o ^ n[2], 0, a ^ n[3])),
                pl.BlockSpec((1, 1, 1, 128), lambda a, o, h, n: (owner_of(a, o, n), h, 0, 0)),
            ],
            scratch_shapes=[pltpu.VMEM((1024, width), bf16)]),
        out_shape=[
            jax.ShapeDtypeStruct((2, 4, HD, local), bf16),
            jax.ShapeDtypeStruct((2, spans_of_rows, 2, CH, 128), bf16),
            jax.ShapeDtypeStruct((2, spans_of_rows, 2, 128, CH), bf16),
            jax.ShapeDtypeStruct((4, halves, 1, 128), f32),
        ],
        compiler_params=pltpu.CompilerParams(vmem_limit_bytes=60 << 20),
        name="qkv",
        cost_estimate=cost(4 * near.size * 384, near.size * 8),
    )(info, near, far, weight, bias)
    return q, k.reshape(2, -1, CH, 128), v.reshape(2, -1, 128, CH), sizes


def step_on(q, j, count):
    last = j + 1 == count
    return jnp.where(last, q + 1, q), jnp.where(last, 0, j + 1)


def assemble(ref, part, shared, core):
    if not shared:
        return jnp.concatenate([ref[0, 2 * part], ref[0, 2 * part + 1]], axis=1)
    at = pl.multiple_of(core * 512, 512)
    return jnp.concatenate([ref[0, n, :, pl.ds(at, 512)] for n in range(4)], axis=1)


def fwd_kernel(shared, info, q_ref, k_ref, v_ref, size_ref, held_ref, out_ref, lse_ref, acc, probs, qa, shifts):
    count = info[4]
    parts = 1 if shared else 2
    lane = lax.broadcasted_iota(jnp.int32, (1, 128), 1)
    sizes = functools.reduce(jnp.maximum, [size_ref[o, h] for o in range(size_ref.shape[0]) for h in range(size_ref.shape[1])])
    widest = jnp.sqrt(jnp.max(jnp.where(lane == int(shared), sizes, 0.0), axis=1, keepdims=True))

    for part in range(parts):
        q_t = assemble(q_ref, part, shared, info[3])
        wide = q_t.astype(f32)
        shift = jnp.sqrt(jnp.sum(wide * wide, axis=0, keepdims=True)) * widest
        shifts[part] = shift
        qa[part] = with_shift(q_t, shift).astype(bf16)

    def raised(part, j):
        return jnp.exp2(dg(k_ref[0, j], qa[part], 1, 0)).astype(bf16)

    probs[0] = raised(0, 0)

    def body(t, carry, ahead_too=True):
        part, j = carry
        now = t & 1
        part_next, j_next = step_on(part, j, count)
        before = jnp.where(j == 0, 0.0, acc[...])
        acc[...] = before + dg(v_ref[0, j], probs[now], 1, 0)
        if ahead_too:
            probs[1 - now] = raised(part_next, j_next)

        @pl.when(j + 1 == count)
        def _():
            total = acc[HD:HD + 1]
            fine = (jnp.min(total) > 2.0 ** -90) & (jnp.max(total) < 2.0 ** 60)

            @pl.when(jnp.logical_not(fine))
            def _():
                plain = qa[part].astype(f32)
                row = lax.broadcasted_iota(jnp.int32, plain.shape, 0)
                qa[part] = jnp.where((row >= HD) & (row < HD + 3), 0.0, plain).astype(bf16)

                def peak(i, top):
                    return jnp.maximum(top, jnp.max(dg(k_ref[0, i], qa[part], 1, 0), axis=0, keepdims=True))
                shift = lax.fori_loop(0, count, peak, jnp.full((1, BQ), FAR, f32))
                shifts[part] = shift
                qa[part] = with_shift(plain[:HD], shift).astype(bf16)
                acc[...] = jnp.zeros_like(acc)

                def again(i, carry):
                    acc[...] += dg(v_ref[0, i], raised(part, i), 1, 0)
                    return carry
                lax.fori_loop(0, count, again, 0)

            total = acc[HD:HD + 1]
            mixed = (acc[:HD] * (1.0 / total)).astype(bf16)
            lse_ref[part] = shifts[part] + jnp.log2(total)
            if shared:
                for n in range(4):
                    out_ref[0, n] = mixed[:, n * 512:(n + 1) * 512]
            else:
                for n in range(2):
                    out_ref[0, 2 * part + n] = mixed[:, n * 1024:(n + 1) * 1024]
        return part_next, j_next

    turns = parts * count
    body(turns - 1, lax.fori_loop(0, turns - 1, body, (0, 0)), False)


def head_spec(shared, *dims):
    zeros = (0,) * len(dims)
    return pl.BlockSpec((1,) + dims, lambda i, n: (int(shared),) + zeros)


def whole_spec(*dims):
    return pl.BlockSpec(dims, lambda i, n: (0,) * len(dims))


def cost(flops, moved, exps=0):
    return pl.CostEstimate(flops=int(flops), bytes_accessed=int(moved), transcendentals=int(exps))


def attend_forward(shared, seq, q, k, v, sizes, info, held):
    _, owners, _, local = q.shape
    chunks = k.shape[1]
    wide = local // 2 if shared else local
    parts = owners * wide // BQ
    pairs = parts * BQ * chunks * CH * 0.6
    shape = jax.ShapeDtypeStruct((2, owners, HD, wide), bf16)
    first = held is None
    if first:
        kernel = lambda info, q, k, v, size, *rest: fwd_kernel(shared, info, q, k, v, size, None, *rest)
    else:
        kernel = functools.partial(fwd_kernel, shared)
    return pl.pallas_call(
        kernel,
        grid_spec=pltpu.PrefetchScalarGridSpec(
            num_scalar_prefetch=1, grid=(1,),
            in_specs=[
                head_spec(shared, owners, HD, local), head_spec(shared, chunks, CH, 128), head_spec(shared, chunks, 128, CH),
                whole_spec(*sizes.shape),
            ] + ([] if first else [pl.BlockSpec(memory_space=pl.ANY)]),
            out_specs=[pl.BlockSpec((1, owners, HD, wide), lambda i, n: (seq, 0, 0, 0)), whole_spec(parts, 1, BQ)],
            scratch_shapes=[
                pltpu.VMEM((128, BQ), f32), pltpu.VMEM((2, CH, BQ), bf16), pltpu.VMEM((parts, 128, BQ), bf16),
                pltpu.VMEM((parts, 1, BQ), f32),
            ]),
        out_shape=[shape, jax.ShapeDtypeStruct((parts, 1, BQ), f32)],
        input_output_aliases={} if first else {5: 0},
        compiler_params=pltpu.CompilerParams(vmem_limit_bytes=60 << 20),
        cost_estimate=cost(pairs * 1024, chunks * CH * 512, pairs),
        name="attend_forward_shared" if shared else "attend_forward_own",
    )(*((info, q, k, v, sizes) + (() if first else (held,))))


def bwd_kernel(shared, first, info, q_ref, k_ref, v_ref, lse_ref, out_ref, gout_ref, *rest):
    rest = rest if first else rest[3 if shared else 1:]
    if shared:
        dq_ref, kept_ref, given_ref, dk_acc, dv_acc, dq_acc, qa, qat, ga, gat, pb, db = rest
    else:
        dqkv_ref, dk_acc, dv_acc, dq_acc, qa, qat, ga, gat, pb, db = rest
    count = info[4]
    chunks = k_ref.shape[1]
    parts = 1 if shared else 2
    dk_acc[...] = jnp.zeros_like(dk_acc)
    dv_acc[...] = jnp.zeros_like(dv_acc)

    def piece(ref, part):
        return jnp.concatenate([ref[0, n] for n in (range(4) if shared else (2 * part, 2 * part + 1))], axis=1)

    for part in range(parts):
        q_full = with_shift(assemble(q_ref, part, shared, info[3]), lse_ref[part])
        qat[part] = q_full.astype(bf16)
        qa[part] = q_full.T.astype(bf16)
        g_t = piece(gout_ref, part)
        meet = jnp.sum(g_t.astype(f32) * piece(out_ref, part).astype(f32), axis=0, keepdims=True)
        g_full = with_shift(g_t, meet)
        gat[part] = g_full.astype(bf16)
        ga[part] = g_full.T.astype(bf16)

    def ahead(part, j, slot):
        raised = jnp.exp2(dg(qa[part], k_ref[0, j], 1, 1))
        pb[slot] = raised.astype(bf16)
        db[slot] = (raised * dg(ga[part], v_ref[0, j], 1, 0)).astype(bf16)

    ahead(0, 0, 0)

    def body(t, carry, ahead_too=True):
        part, j = carry
        now = t & 1
        part_next, j_next = step_on(part, j, count)
        dv_acc[j] += dg(gat[part], pb[now], 1, 0)[:HD]
        dk_acc[j] += dg(qat[part], db[now], 1, 0)[:HD]
        before = jnp.where(j == 0, 0.0, dq_acc[...])
        dq_acc[...] = before + dg(db[now], k_ref[0, j], 1, 0)
        if ahead_too:
            ahead(part_next, j_next, 1 - now)

        @pl.when(j + 1 == count)
        def _():
            dq_t = (dq_acc[...] * 0.125).T[:HD].astype(bf16)
            if shared:
                for n in range(4):
                    dq_ref[0, n, :, :512] = dq_t[:32, n * 512:(n + 1) * 512]
                    dq_ref[0, n, :, 512:] = dq_t[32:, n * 512:(n + 1) * 512]
            else:
                for n in range(2):
                    dqkv_ref[0, 2 * part + n, 0] = dq_t[:, n * 1024:(n + 1) * 1024]
        return part_next, j_next

    turns = parts * count
    body(turns - 1, lax.fori_loop(0, turns - 1, body, (0, 0)), False)
    for block in range(chunks):
        j, across = block // 2, block % 2
        for owner in (2 * across, 2 * across + 1):
            cols = slice((owner - 2 * across) * 128, (owner - 2 * across + 1) * 128)
            dk_wide, dv_wide = dk_acc[block, :, cols] * LN2, dv_acc[block, :, cols]
            dk, dv = dk_wide.astype(bf16), dv_wide.astype(bf16)
            if shared:
                here = info[3] == 0
                kept_ref[0, owner, :, j * 128:(j + 1) * 128] = jnp.where(here, dk_wide, dv_wide).astype(bf16)
                given_ref[0, owner, :, j * 128:(j + 1) * 128] = jnp.where(here, dv_wide, dk_wide).astype(bf16)
            else:
                dqkv_ref[0, owner, 1, :, j * 128:(j + 1) * 128] = dk
                dqkv_ref[0, owner, 2, :, j * 128:(j + 1) * 128] = dv


def attend_backward(shared, seq, q, k, v, lse, out, g_out, info, held):
    _, owners, _, local = q.shape
    chunks = k.shape[1]
    wide = out.shape[3]
    parts = owners * wide // BQ
    pairs = parts * BQ * chunks * CH * 0.6
    shape = jax.ShapeDtypeStruct
    first = held is None
    if shared:
        out_specs = [pl.BlockSpec((1, owners, rows, local), lambda i, n: (seq, 0, 0, 0)) for rows in (32, HD, HD)]
        out_shape = [shape((2, owners, rows, local), bf16) for rows in (32, HD, HD)]
    else:
        out_specs = [pl.BlockSpec((1, owners, 3, HD, local), lambda i, n: (seq, 0, 0, 0, 0))]
        out_shape = [shape((2, owners, 3, HD, local), bf16)]
    kept = () if first else tuple(held)
    of_seq = pl.BlockSpec((1, owners, HD, wide), lambda i, n: (seq, 0, 0, 0))
    return pl.pallas_call(
        functools.partial(bwd_kernel, shared, first),
        grid_spec=pltpu.PrefetchScalarGridSpec(
            num_scalar_prefetch=1, grid=(1,),
            in_specs=[
                head_spec(shared, owners, HD, local), head_spec(shared, chunks, CH, 128), head_spec(shared, chunks, 128, CH),
                whole_spec(parts, 1, BQ), of_seq, of_seq,
            ] + [pl.BlockSpec(memory_space=pl.ANY)] * len(kept),
            out_specs=out_specs,
            scratch_shapes=[
                pltpu.VMEM((chunks, HD, CH), f32), pltpu.VMEM((chunks, HD, CH), f32), pltpu.VMEM((BQ, 128), f32),
                pltpu.VMEM((parts, BQ, 128), bf16), pltpu.VMEM((parts, 128, BQ), bf16),
                pltpu.VMEM((parts, BQ, 128), bf16), pltpu.VMEM((parts, 128, BQ), bf16),
                pltpu.VMEM((2, BQ, CH), bf16), pltpu.VMEM((2, BQ, CH), bf16),
            ]),
        out_shape=out_shape,
        input_output_aliases={7 + n: n for n in range(len(kept))},
        compiler_params=pltpu.CompilerParams(vmem_limit_bytes=60 << 20),
        cost_estimate=cost(pairs * 100, chunks * CH * 2048),
        name="attend_backward_shared" if shared else "attend_backward_own",
    )(info, q, k, v, lse, out, g_out, *kept)


def gelu_pair(u):
    half = 0.5 * (1.0 + lax.erf(u * 0.7071067811865476))
    return u * half, half + u * (0.3989422804014327 * jnp.exp2(u * u * (-0.5 * LOG2E)))


def norm_stats(v):
    mean = jnp.mean(v, axis=-1, keepdims=True)
    centred = v - mean
    inverse = lax.rsqrt(jnp.mean(centred * centred, axis=-1, keepdims=True) + 1e-12)
    return centred * inverse, inverse


def norm_back(grad, xhat, inverse, gain):
    g = grad * gain
    return (g - jnp.mean(g, axis=-1, keepdims=True) - xhat * jnp.mean(g * xhat, axis=-1, keepdims=True)) * inverse


def weight_part(ref, first, rows):
    part = ref[:, first:first + rows, :]
    return part.reshape(part.shape[0] * rows, part.shape[2])


def ffn_kernel(spans, info, x_ref, own_ref, sh_ref, cot_ref, w_ref, bin_ref, vec_ref,
               act_out, resid_out, gown_out, gsh_out, active_out, dinner_out, normed_out, douter_out, dbranch_out,
               vec_sum, bin_sum, slope, row_block):
    step = pl.program_id(0)
    load_rows(row_block, x_ref, spans, info[1])
    count = row_block.shape[0] // PARTS
    vec = vec_ref[...]
    total = lambda a: jnp.sum(a, axis=0, keepdims=True)
    held = [{"at": slice(n * count, (n + 1) * count)} for n in range(PARTS)]

    def branch(h):
        at = h["at"]
        mixed_t = jnp.concatenate(
            [part for p in range(4) for part in (own_ref[p, 0, :, at], sh_ref[p, 0, :, at], own_ref[p, 1, :, at])], axis=0)
        h["sum1"] = row_block[at].astype(f32) + (dg(mixed_t, weight_part(w_ref, 768, 96), 0, 0) + vec[0:1])

    def first_norm(h):
        h["xhat1"], h["inv1"] = norm_stats(h["sum1"])
        normed = h["xhat1"] * vec[1:2] + vec[2:3]
        normed_out[h["at"]] = normed.astype(bf16)
        h["outer"] = normed + vec[3:4]

    def widen(h):
        at = h["at"]
        for n in range(4):
            cols = slice(n * 768, (n + 1) * 768)
            value, bend = gelu_pair(dg(normed_out[at], weight_part(w_ref, 384 + 96 * n, 96), 1, 0) + bin_ref[:, cols])
            active_out[at, cols] = value.astype(bf16)
            slope[at, cols] = bend.astype(bf16)

    def narrow(h):
        h["outer"] = h["outer"] + dg(active_out[h["at"]], weight_part(w_ref, 0, 384), 1, 0)

    def second_norm(h):
        at = h["at"]
        xhat2, inv2 = norm_stats(h["outer"])
        act_out[at] = (xhat2 * vec[4:5] + vec[5:6]).astype(bf16)
        cot = cot_ref[at].astype(f32)
        d2 = norm_back(cot, xhat2, inv2, vec[4:5])
        d_outer = d2.astype(bf16)
        douter_out[at] = d_outer
        h["d_normed"] = d2
        h["sums"] = [total(d_outer.astype(f32)), total(cot * xhat2), total(cot)]

    def back(h):
        at = h["at"]
        h["inner_sums"] = []
        for n in range(4):
            cols = slice(n * 768, (n + 1) * 768)
            d_active = dg(douter_out[at], weight_part(w_ref.at[2 * n:2 * n + 2], 0, 384), 1, 1)
            d_inner = (d_active * slope[at, cols].astype(f32)).astype(bf16)
            dinner_out[at, cols] = d_inner
            h["inner_sums"].append(total(d_inner.astype(f32)))
            h["d_normed"] = h["d_normed"] + dg(d_inner, weight_part(w_ref, 384 + 96 * n, 96), 1, 1)

    def first_back(h):
        at = h["at"]
        d_normed = h["d_normed"]
        d1 = norm_back(d_normed, h["xhat1"], h["inv1"], vec[1:2])
        resid_out[at] = d1
        d_branch = d1.astype(bf16)
        dbranch_out[at] = d_branch
        h["sums"] = [total(d_branch.astype(f32)), total(d_normed * h["xhat1"]), total(d_normed)] + h["sums"]

    def mix_back(h):
        at = h["at"]
        g_t = dg(weight_part(w_ref, 768, 96), dbranch_out[at], 1, 1).astype(bf16)
        for p in range(4):
            gown_out[p, 0, :, at] = g_t[192 * p:192 * p + 64]
            gsh_out[p, 0, :, at] = g_t[192 * p + 64:192 * p + 128]
            gown_out[p, 1, :, at] = g_t[192 * p + 128:192 * p + 192]

    for products, norm in ((branch, first_norm), (widen, None), (narrow, second_norm), (back, first_back), (mix_back, None)):
        for h in held:
            products(h)
            if norm is not None:
                norm(h)
    sums = jnp.concatenate([
        functools.reduce(jnp.add, [h["sums"][n] for h in held]) for n in range(6)] + [jnp.zeros((2, vec.shape[1]), f32)], axis=0)
    inner_sums = [functools.reduce(jnp.add, [h["inner_sums"][n] for h in held]) for n in range(4)]

    @pl.when(step == 0)
    def _():
        vec_sum[...] = sums
        for n in range(4):
            bin_sum[:, n * 768:(n + 1) * 768] = inner_sums[n]

    @pl.when(step > 0)
    def _():
        vec_sum[...] += sums
        for n in range(4):
            bin_sum[:, n * 768:(n + 1) * 768] += inner_sums[n]


def feed_forward(rows_in, own, sh, cotangent, weights, inner_bias, vectors, info):
    _, _, _, stretch, width = rows_in.shape
    local = cotangent.shape[0]
    spans = FB // (2 * stretch)
    steps = local // FB
    half_steps = steps // 2
    wide = inner_bias.shape[1]
    rows = lambda n: pl.BlockSpec((FB, n), lambda r, a: (r, 0))
    fixed = lambda *dims: pl.BlockSpec(dims, lambda r, a: (0,) * len(dims))
    own_spec = pl.BlockSpec((4, 2, HD, FB), lambda r, a: (0, 0, 0, r))
    sh_spec = pl.BlockSpec((4, 1, HD, FB), lambda r, a: (0, r // half_steps, 0, r % half_steps))
    shape = jax.ShapeDtypeStruct
    return pl.pallas_call(
        functools.partial(ffn_kernel, spans),
        grid_spec=pltpu.PrefetchScalarGridSpec(
            num_scalar_prefetch=1, grid=(steps,),
            in_specs=[
                pl.BlockSpec((1, 2, spans, stretch, width), lambda r, a: (0, 0, r, 0, 0)),
                own_spec, sh_spec, rows(width),
                pl.BlockSpec(weights.shape, lambda r, a: (0, 0, 0), pipeline_mode=pl.Buffered(1)),
                fixed(1, wide), fixed(8, width),
            ],
            out_specs=[
                rows(width), rows(width), own_spec, sh_spec, rows(wide), rows(wide), rows(width), rows(width), rows(width),
                fixed(8, width), fixed(1, wide),
            ],
            scratch_shapes=[pltpu.VMEM((FB, wide), bf16), pltpu.VMEM((FB, width), bf16)]),
        out_shape=[
            shape((local, width), bf16), shape((local, width), f32), shape(own.shape, bf16), shape(sh.shape, bf16),
            shape((local, wide), bf16), shape((local, wide), bf16), shape((local, width), bf16),
            shape((local, width), bf16), shape((local, width), bf16), shape((8, width), f32), shape((1, wide), f32),
        ],
        compiler_params=pltpu.CompilerParams(vmem_limit_bytes=60 << 20),
        name="feed_forward",
        cost_estimate=cost(local * width * (width + 2 * wide) * 4, local * wide * 20),
    )(info, rows_in, own, sh, cotangent, weights, inner_bias, vectors)


def outer_grad_kernel(scale, active_ref, douter_ref, out_ref):
    made = (dg(active_ref[...], douter_ref[...], 0, 0) * scale).astype(bf16)
    out_ref[...] = made.reshape(out_ref.shape)


def inner_grad_kernel(scale, packed_ref, normed_ref, dinner_ref, own_ref, sh_ref, dbranch_ref, out_ref):
    step = pl.program_id(0)

    @pl.when(step < 4)
    def _():
        out_ref[...] = (dg(normed_ref[...], dinner_ref[...], 0, 0) * scale).astype(bf16).reshape(out_ref.shape)

    @pl.when(step == 4)
    def _():
        mixed_t = jnp.concatenate([
            part for p in range(4)
            for part in (own_ref[p, 0], jnp.concatenate([sh_ref[p, 0], sh_ref[p, 1]], axis=1), own_ref[p, 1])], axis=0)
        out_ref[...] = (dg(mixed_t, dbranch_ref[...], 1, 0) * scale).astype(bf16).reshape(out_ref.shape)


def weight_grads(scale, active, d_outer, normed, d_inner, own, sh, d_branch):
    local, wide = active.shape
    width = normed.shape[1]
    packed = pl.pallas_call(
        functools.partial(outer_grad_kernel, scale), grid=(4,),
        in_specs=[pl.BlockSpec((local, width), lambda m: (0, m)), pl.BlockSpec((local, width), lambda m: (0, 0))],
        out_specs=pl.BlockSpec((2, 384, width), lambda m: (m, 0, 0)),
        out_shape=jax.ShapeDtypeStruct((8, 896, width), bf16),
        compiler_params=pltpu.CompilerParams(vmem_limit_bytes=40 << 20), name="outer_grad",
        cost_estimate=cost(2 * local * wide * width, 2 * wide * (local + width)),
    )(active, d_outer)
    fixed = lambda a: pl.BlockSpec(a.shape, lambda n: (0,) * a.ndim)
    return pl.pallas_call(
        functools.partial(inner_grad_kernel, scale), grid=(5,),
        in_specs=[
            pl.BlockSpec(memory_space=pl.ANY), fixed(normed),
            pl.BlockSpec((local, width), lambda n: (0, jnp.minimum(n, 3))), fixed(own), fixed(sh), fixed(d_branch)],
        out_specs=pl.BlockSpec((8, 96, width), lambda n: (0, 4 + n, 0)),
        out_shape=jax.ShapeDtypeStruct((8, 896, width), bf16), input_output_aliases={0: 0},
        compiler_params=pltpu.CompilerParams(vmem_limit_bytes=40 << 20), name="inner_grad",
        cost_estimate=cost(2 * local * (wide + width) * width, 2 * (wide + width) * (local + width)),
    )(packed, normed, d_inner, own, sh, d_branch)


def head_grad_kernel(scale, spans, info, *refs):
    x_refs, (own_ref, dq_ref, kept_ref, given_ref, out_ref, bias_out, acc, bias_acc, rows) = refs[:4], refs[4:]
    seq, away, half = pl.program_id(0), pl.program_id(1), pl.program_id(3)
    last = (seq == 1) & (away == 1) & (pl.program_id(2) == 1) & (half == pl.num_programs(3) - 1)
    for n in range(4):
        @pl.when(seq * 2 + away == n)
        def _(n=n):
            load_rows(rows, x_refs[n], spans, info[1])
    dq_t = jnp.where(half == info[3], jnp.concatenate([dq_ref[0, 0, :, :512], dq_ref[0, 0, :, 512:]], axis=0).astype(f32), 0.0)
    kept, given = kept_ref[0, 0].astype(f32), given_ref[0, 0].astype(f32)
    here = info[3] == 0
    d_t = jnp.concatenate([
        own_ref[0, 0, 0], dq_t.astype(bf16), own_ref[0, 0, 1], jnp.where(here, kept, given).astype(bf16),
        own_ref[0, 0, 2], jnp.where(here, given, kept).astype(bf16)], axis=0)

    @pl.when((seq == 0) & (away == 0) & (pl.program_id(2) == 0) & (half == 0))
    def _():
        acc[...] = jnp.zeros_like(acc)
        bias_acc[...] = jnp.zeros_like(bias_acc)
    acc[...] += dg(d_t, rows[...], 1, 0)
    bias_acc[...] += dg(jnp.ones((8, d_t.shape[1]), bf16), d_t, 1, 1)

    @pl.when(last)
    def _():
        out_ref[...] = (acc[...] * scale).T.astype(bf16)
        bias_out[...] = bias_acc[...] * scale


def head_grads(scale, sources, dqkv_own, dq_sh, kept, given, info):
    _, _, zs, stretch, width = sources[0].shape
    local = 2 * zs * stretch
    spans = 512 // (2 * stretch)
    halves = local // 512

    def source_spec(n):
        def index(s, a, o, h, i):
            now = 2 * s + a
            across = jnp.where(now == n, o, jnp.where(now < n, 0, 1))
            return (across, 0, jnp.where(now == n, h, jnp.where(now < n, 0, halves - 1)), 0, 0)
        return pl.BlockSpec((1, 2, spans, stretch, width), index)
    return pl.pallas_call(
        functools.partial(head_grad_kernel, scale, spans),
        grid_spec=pltpu.PrefetchScalarGridSpec(
            num_scalar_prefetch=1, grid=(2, 2, 2, halves),
            in_specs=[source_spec(n) for n in range(4)] + [
                pl.BlockSpec((1, 1, 3, HD, 512), lambda s, a, o, h, i: (s, owner_of(a, o, i), 0, 0, h)),
                pl.BlockSpec((1, 1, 32, local), lambda s, a, o, h, i: (s, owner_of(a, o, i), 0, 0)),
            ] + [pl.BlockSpec((1, 1, HD, 512), lambda s, a, o, h, i: (s, owner_of(a, o, i), 0, h))] * 2,
            out_specs=[pl.BlockSpec((width, 384), lambda s, a, o, h, i: (0, 0)), pl.BlockSpec((8, 384), lambda s, a, o, h, i: (0, 0))],
            scratch_shapes=[pltpu.VMEM((384, width), f32), pltpu.VMEM((8, 384), f32), pltpu.VMEM((512, width), bf16)]),
        out_shape=[jax.ShapeDtypeStruct((width, 384), bf16), jax.ShapeDtypeStruct((8, 384), f32)],
        compiler_params=pltpu.CompilerParams(vmem_limit_bytes=40 << 20), name="head_grads",
        cost_estimate=cost(8 * local * 768 * width, 8 * local * width * 2),
    )(info, *sources, dqkv_own, dq_sh, kept, given)


def token_grad_kernel(own_ref, low_ref, high_ref, dkv_ref, w_ref, resid_ref, out_ref):
    total = resid_ref[...]
    for kind in range(3):
        made = []
        for p in range(4):
            if kind == 0:
                middle = jnp.concatenate([low_ref[p, 0], high_ref[p, 0]], axis=0)
            else:
                middle = jnp.concatenate([dkv_ref[p, kind - 1, n] for n in range(2)], axis=0)
            made += [own_ref[p, 0, kind], middle, own_ref[p, 1, kind]]
        total = total + dg(jnp.concatenate(made, axis=0), weight_part(w_ref, 96 * kind, 96), 0, 1)
    out_ref[...] = total.astype(bf16)


def token_grad(own, shared, weights, resid):
    local, width = resid.shape
    steps = local // RB
    half_steps = steps // 2
    rows = pl.BlockSpec((RB, width), lambda r: (r, 0))
    return pl.pallas_call(
        token_grad_kernel, grid=(steps,),
        in_specs=[
            pl.BlockSpec((4, 2, 3, HD, RB), lambda r: (0, 0, 0, 0, r)),
            pl.BlockSpec((4, 1, None, 32, RB), lambda r: (0, r // half_steps, 2, 0, r % half_steps)),
            pl.BlockSpec((4, 1, None, 32, RB), lambda r: (0, r // half_steps, 2, 0, half_steps + r % half_steps)),
            pl.BlockSpec((4, 2, 2, 32, RB), lambda r: (0, 0, 0, 0, r)),
            pl.BlockSpec(weights.shape, lambda r: (0, 0, 0)), rows],
        out_specs=rows, out_shape=jax.ShapeDtypeStruct((local, width), bf16),
        compiler_params=pltpu.CompilerParams(vmem_limit_bytes=60 << 20), name="token_grad",
        cost_estimate=cost(local * width * width * 6, local * width * 12),
    )(own, shared, shared, shared, weights, resid)


def head_unpack_kernel(per, info, src_ref, q_out, k_out, v_out, bias_out):
    low = lax.broadcasted_iota(jnp.int32, (src_ref.shape[1], 128), 1) < HD

    def rows_of(p, core, cols):
        at = (((p >> 1) ^ info[1]) << 2) | (((p & 1) ^ info[2]) << 1) | (core ^ info[3])
        return src_ref[at, :, cols].astype(f32)
    for kind, out in enumerate((q_out, k_out, v_out)):
        cols = slice(128 * kind, 128 * kind + 128)
        tiles = []
        for pair in range(2):
            first, second = [], []
            for p in (2 * pair, 2 * pair + 1):
                near, far = rows_of(p, 0, cols), rows_of(p, 1, cols)
                first.append(near + jnp.where(low, 0.0, far))
                second.append(far)
            turned = pltpu.roll(first[1], HD, 1)
            tiles += [first[0], jnp.where(low, second[0], turned), jnp.where(low, turned, pltpu.roll(second[1], HD, 1))]
        made = jnp.concatenate(tiles, axis=1)
        out[...] = made[:per]
        if kind != 1:
            bias_out[kind // 2:kind // 2 + 1] = made[per:per + 1]


def head_unpack(source, per, width, info):
    shape = jax.ShapeDtypeStruct
    full = lambda n: pl.BlockSpec((n, width), lambda i, f: (0, 0))
    return pl.pallas_call(
        functools.partial(head_unpack_kernel, per),
        grid_spec=pltpu.PrefetchScalarGridSpec(
            num_scalar_prefetch=1, grid=(1,),
            in_specs=[pl.BlockSpec(source.shape, lambda i, f: (0, 0, 0))],
            out_specs=[full(per)] * 3 + [full(2)]),
        out_shape=[shape((per, width), f32)] * 3 + [shape((2, width), f32)], name="head_unpack",
    )(info, source)


SWAP = [(0, 1), (1, 0)]
def settle_kernel(*refs):
    refs[-1][...] = sum(ref[...].astype(f32) for ref in refs[:-2]).astype(bf16)


def settle(parts, after):
    whole = pl.BlockSpec(memory_space=pltpu.VMEM)
    return pl.pallas_call(
        settle_kernel, in_specs=[whole] * len(parts) + [pl.BlockSpec(memory_space=pl.ANY)], out_specs=whole,
        out_shape=jax.ShapeDtypeStruct(parts[0].shape, bf16), name="settle",
        cost_estimate=cost(1e9, 1e6),
    )(*parts, after)


PAIR = ("x", "y", "c")
ALL = ("z", "x", "y", "c")
SHARD = ("z", "x")


def canonical(packed, shards):
    if shards == 8:
        return packed
    width = packed.shape[2]
    per, keep = 96 * 8 // shards, shards // 8
    outer = packed[:, :4 * per].reshape(8, 384, width)
    inner = packed[:, 4 * per:8 * per].reshape(8, keep, 4, per, width).transpose(0, 2, 1, 3, 4).reshape(8, 384, width)
    output = packed[:, 8 * per:9 * per].reshape(8, 96, width)
    return jnp.concatenate([outer, inner, output, jnp.zeros((8, 32, width), packed.dtype)], axis=1)


def from_canonical(packed, last, shards):
    width = packed.shape[2]
    if shards == 8:
        return packed.at[:, 864:].set(jnp.broadcast_to(last[None], (8, 32, width)))
    per, keep = 96 * 8 // shards, shards // 8
    outer = packed[:, :384].reshape(shards, 4 * per, width)
    inner = packed[:, 384:768].reshape(8, 4, keep, per, width).transpose(0, 2, 1, 3, 4).reshape(shards, 4 * per, width)
    output = packed[:, 768:864].reshape(shards, per, width)
    return jnp.concatenate([outer, inner, output, jnp.broadcast_to(last[None], (shards, 32, width))], axis=1)


def canonical_heads(packed, shards, parts):
    if shards == 8:
        return packed
    width = packed.shape[2]
    per = 96 * 8 // shards
    made = [packed[:, k * per:(k + 1) * per].reshape(8, 96, width) for k in range(parts)]
    return jnp.concatenate(made + [jnp.zeros((8, 32, width), packed.dtype)], axis=1)


def quarter(pieces):
    part = sum(piece.shape[0] for piece in pieces) // 4

    def taken(k):
        found, at = [], 0
        for piece in pieces:
            low, high = max(k * part - at, 0), min((k + 1) * part - at, piece.shape[0])
            if low < high:
                found.append(piece[low:high])
            at += piece.shape[0]
        return jnp.concatenate(found, axis=0)
    place = lax.axis_index("y") * 2 + lax.axis_index("c")
    return lax.switch(place, [functools.partial(taken, k) for k in range(4)])


def flipped(array, axis, here):
    return jnp.where(here == 0, array, jnp.flip(array, axis))


def body(tokens, lengths, deal_order, w_query, w_key, w_value, w_output, b_query, b_value, b_output,
         ln1_gain, ln1_shift, w_inner, b_inner, w_outer, b_outer, ln2_gain, ln2_shift, cotangent):
    tie = lax.optimization_barrier
    zs = lax.axis_size("z")
    shards = 2 * zs
    scale = 1.0 / (shards * 4)
    seq_count, _, stretch, width = tokens.shape
    per = w_query.shape[0]
    half = zs // 2
    x, y, c = lax.axis_index("x"), lax.axis_index("y"), lax.axis_index("c")

    def deal(ordered):
        return lax.all_to_all(ordered, "z", split_axis=0, concat_axis=0, tiled=True)

    def corner(across, along):
        return [lax.ppermute(across[:half], "y", SWAP), lax.ppermute(along[half:], "x", SWAP)]

    def this_core(own, across, along, corner):
        return jnp.concatenate([own, across, along] + corner, axis=0).reshape(2, 2, zs, stretch, width)

    ordered_a = tokens[:, 0].at[deal_order[0::2]].get(mode="promise_in_bounds")
    first_own = deal(ordered_a)
    (_, tokens, w_query, w_key, w_value, b_query, b_value, w_outer, w_inner, w_output, b_inner, deal_order) = tie(
        (ordered_a, tokens, w_query, w_key, w_value, b_query, b_value, w_outer, w_inner, w_output, b_inner, deal_order))
    ordered_b = tokens[:, 0].at[deal_order[1::2]].get(mode="promise_in_bounds")

    def head_columns(matrix):
        heads = matrix.reshape(per, 2, 2, 3, HD)
        mine = lax.dynamic_index_in_dim(heads, y, axis=2, keepdims=False)
        own = lax.dynamic_index_in_dim(mine, 2 * c, axis=2, keepdims=False)
        return [own, mine[:, :, 1]]
    pad = lambda v: jnp.pad(v, (0, width - v.shape[0]))[None]
    columns = jnp.concatenate(
        [col for matrix in (w_query, w_key, w_value) for col in head_columns(matrix)], axis=2).reshape(per, width)
    head_pack = jnp.concatenate([columns, pad(b_query), pad(b_value), jnp.zeros((14, width), bf16)], axis=0)
    vectors = (b_output, ln1_gain, ln1_shift, b_outer, ln2_gain, ln2_shift)
    vector_pack = jnp.concatenate([pad(b_inner)] + [pad(v) for v in vectors] + [jnp.zeros((25, width), bf16)], axis=0)
    layer_quarter = quarter(
        [w_outer] + [w_inner[:, n * width:(n + 1) * width] for n in range(4)] + [w_output, vector_pack])
    back_quarter = quarter([w_query, w_key, w_value, jnp.zeros((32, width), bf16)])
    slots = lax.dynamic_slice_in_dim(deal_order, lax.axis_index("z") * 2, 2)
    matches = slots[:, None] == jnp.arange(seq_count, dtype=jnp.int32)[None, :]
    lens = jnp.sum(jnp.where(matches, lengths[None, :], 0), axis=1).astype(jnp.int32)
    last = (lens + 511) // 512 - 1
    counts = 2 * last + 1 + (lens > 512 * last + 2 * stretch).astype(jnp.int32)
    infos = [jnp.stack([lens[n], x, y, c, counts[n]]).astype(jnp.int32) for n in range(2)]
    first_own, ordered_b, head_pack, layer_quarter, back_quarter, *infos = tie(
        (first_own, ordered_b, head_pack, layer_quarter, back_quarter, *infos))
    head_all = lax.all_gather(head_pack, SHARD, axis=0, tiled=False)
    head_weight = canonical_heads(head_all, shards, 1)

    def head_bias(row):
        heads = head_all[:, per + row, :per].reshape(2, 2, 3, HD)
        mine = lax.dynamic_slice(heads, (x, y, 0, 0), (1, 1, 3, HD))[0, 0]
        return [lax.dynamic_index_in_dim(mine, 2 * c, axis=0, keepdims=False), mine[1]]
    bias_row = jnp.concatenate(head_bias(0) + [jnp.zeros((2 * HD,), bf16)] + head_bias(1)).astype(f32)[None]

    across_a, along_a = lax.ppermute(first_own, "x", SWAP), lax.ppermute(first_own, "y", SWAP)
    second_own = deal(ordered_b)
    across_a, along_a, second_own = tie((across_a, along_a, second_own))
    corner_a = corner(across_a, along_a)
    second_own, *corner_a = tie((second_own, *corner_a))
    near_a = this_core(first_own, across_a, along_a, corner_a)
    far_a = lax.ppermute(near_a, "c", SWAP)
    across_b, along_b = lax.ppermute(second_own, "x", SWAP), lax.ppermute(second_own, "y", SWAP)

    layer_all = lax.all_gather(layer_quarter, ALL, axis=0, tiled=True).reshape(shards, 9 * per + 32, width)
    layer_weights = canonical(layer_all, shards)
    inner_bias = layer_all[:, 9 * per, :4 * per].reshape(1, 4 * width).astype(f32)
    vector_rows = jnp.concatenate(
        [layer_all[:, 9 * per + 1 + n, :per].reshape(1, width) for n in range(6)] + [jnp.zeros((2, width), bf16)],
        axis=0).astype(f32)
    back_all = lax.all_gather(back_quarter, ALL, axis=0, tiled=True).reshape(shards, 3 * per + 32, width)

    def swap(array):
        flat = array.reshape((8,) + array.shape[2:])
        return lax.all_to_all(flat, PAIR, split_axis=0, concat_axis=0, tiled=True)

    def to_tokens(array):
        return swap(array).reshape((4, 2) + array.shape[2:])

    def to_heads(array):
        return swap(array).reshape((2, 4) + array.shape[2:])

    heads_a = project(near_a, far_a, head_weight, bias_row, infos[0])
    heads_a, across_b, along_b = tie((heads_a, across_b, along_b))
    near_b = this_core(second_own, across_b, along_b, corner(across_b, along_b))
    own_first, lse_own_a = attend_forward(False, 0, *heads_a, infos[0], None)
    own_first, near_b = tie((own_first, near_b))
    far_b = lax.ppermute(near_b, "c", SWAP)
    heads_b = project(near_b, far_b, head_weight, bias_row, infos[1])
    own, lse_own_b = attend_forward(False, 1, *heads_b, infos[1], own_first)
    own_t = to_tokens(own)
    own, info_a, info_b = tie((own, *infos))
    sh_first, lse_sh_a = attend_forward(True, 0, *heads_a, info_a, None)
    sh, lse_sh_b = attend_forward(True, 1, *heads_b, info_b, sh_first)
    sh_sent, own_t = tie((sh, own_t))
    sh_t = to_tokens(sh_sent)
    mine_rows = jnp.where(x == 0, jnp.stack([first_own, across_a]), jnp.stack([second_own, across_b]))[None]

    (act, resid, g_own, g_sh, active, d_inner, normed, d_outer, d_branch, vec_sums, bin_sums) = feed_forward(
        mine_rows, own_t, sh_t, cotangent.reshape(-1, width), layer_weights, inner_bias, vector_rows, infos[0])
    g_own_h, g_sh_h = to_heads(g_own), to_heads(g_sh)
    active, back_all = tie((active, back_all))
    packed = weight_grads(scale, active, d_outer, normed, d_inner, own_t, sh_t, d_branch)
    sums = jnp.concatenate([bin_sums.reshape(4, width), vec_sums, jnp.zeros((20, width), f32)], axis=0) * scale
    ready = from_canonical(packed, sums.astype(bf16), shards)
    ready, g_own_h = tie((ready, g_own_h))
    back_weights = canonical_heads(back_all, shards, 3)
    layer_part = lax.psum_scatter(ready.reshape(-1, width), ("z", "x", "c"), scatter_dimension=0, tiled=True)

    qkv_a, qkv_b = heads_a[:3], heads_b[:3]
    first = attend_backward(False, 0, *qkv_a, lse_own_a, own, g_own_h, infos[0], None)
    dqkv_own, = attend_backward(False, 1, *qkv_b, lse_own_b, own, g_own_h, infos[1], first)
    back_own = to_tokens(dqkv_own)
    dqkv_own, info_a, info_b = tie((dqkv_own, *infos))
    first = attend_backward(True, 0, *qkv_a, lse_sh_a, sh, g_sh_h, info_a, None)
    dq_sh, kept, given = attend_backward(True, 1, *qkv_b, lse_sh_b, sh, g_sh_h, info_b, first)
    taken = lax.ppermute(given, "c", SWAP)
    shared_out = jnp.concatenate([(kept.astype(f32) + taken.astype(f32)).astype(bf16), dq_sh], axis=2)
    shared_out, back_own, dqkv_own = tie((shared_out, back_own, dqkv_own))
    back_shared = to_tokens(shared_out.reshape(2, 4, 3, 32, -1))
    d_heads, d_bias = head_grads(scale, (near_a, far_a, near_b, far_b), dqkv_own, dq_sh, kept, given, infos[0])

    head_ready = jnp.concatenate([
        d_heads.reshape(zs, 2, per, 384),
        jnp.broadcast_to(d_bias[:1].astype(bf16)[None, None], (zs, 2, 16, 384))], axis=2)
    head_ready, back_shared = tie((head_ready, back_shared))
    d_rows = token_grad(back_own, back_shared, back_weights, resid)
    if zs == 4:
        group = lax.axis_index("z")
        parts = [lax.dynamic_index_in_dim(head_ready, (group + k) % zs, axis=0, keepdims=False) for k in range(zs)]
        parts = parts[:1] + [
            lax.ppermute(parts[k], "z", [(i, (i + k) % zs) for i in range(zs)]) for k in range(1, zs)]
        head_sum = settle(parts, d_rows)
    else:
        head_sum = lax.psum_scatter(
            head_ready.reshape(-1, 384), "z", scatter_dimension=0, tiled=True).reshape(2, per + 16, 384)
    layer_part, _ = tie((layer_part, d_rows))
    layer_sum = (layer_part.astype(f32) + lax.ppermute(layer_part, "y", SWAP).astype(f32)).astype(bf16)
    returned = lax.all_to_all(
        d_rows.reshape(shards, stretch, width), SHARD, split_axis=0, concat_axis=0, tiled=True)

    def apart(array, bits):
        return lax.ppermute(array, PAIR, [(i, i ^ bits) for i in range(8)]) if bits else array

    halves = [lax.dynamic_index_in_dim(head_sum, x ^ k, axis=0, keepdims=False) for k in range(2)]
    head_eight = jnp.stack([apart(halves[bits >> 2], bits) for bits in range(8)])
    d_wq, d_wk, d_wv, d_bias_rows = head_unpack(head_eight, per, width, infos[0])
    place = lax.axis_index("z") * 2 + x
    own_slice = lambda row, n: lax.dynamic_slice_in_dim(row, place * n, n)
    d_bq, d_bv = own_slice(d_bias_rows[0], per), own_slice(d_bias_rows[1], per)

    layer_grads = flipped(jnp.stack([layer_sum, lax.ppermute(layer_sum, "c", SWAP)]), 0, c)
    layer_grads = layer_grads.reshape(9 * per + 32, width).astype(f32)
    d_wouter = layer_grads[:4 * per]
    d_winner = jnp.concatenate([layer_grads[(4 + n) * per:(5 + n) * per] for n in range(4)], axis=1)
    d_woutput = layer_grads[8 * per:9 * per]
    d_binner = own_slice(layer_grads[9 * per:9 * per + 4].reshape(-1), 4 * per)
    d_bo, d_g1, d_s1, d_bout, d_g2, d_s2 = (own_slice(layer_grads[9 * per + 4 + n], per) for n in range(6))
    small = (d_bq, d_bv, d_binner, d_bo, d_g1, d_s1, d_bout, d_g2, d_s2)
    returned = tie((returned, d_wouter, d_winner, d_woutput, d_wq, d_wk, d_wv) + small)[0]
    steps = jnp.arange(seq_count, dtype=jnp.int32)
    slot_of = jnp.sum(jnp.where(deal_order[:, None] == steps[None, :], steps[:, None], 0), axis=0)
    d_tokens = returned.at[slot_of].get(mode="promise_in_bounds")[:, None]
    return (act.reshape(1, shards, stretch, width), d_tokens, d_wq, d_wk, d_wv, d_woutput, d_bq, d_bv, d_bo,
            d_g1, d_s1, d_winner, d_binner, d_wouter, d_bout, d_g2, d_s2)


def solution(mesh):
    shards, splits = mesh.devices.shape
    fine = Mesh(mesh.devices.reshape(shards // 2, 2, splits // 2, 2), ALL)
    S, Q = SHARD, ("y", "c")
    row, mat = P(S), P(S, None)
    return jax.shard_map(
        body, mesh=fine,
        in_specs=(P(None, S, Q, None), P(), P(), mat, mat, mat, mat, row, row, row, row, row, mat, row, mat, row, row, row,
                  P(S, None, Q, None)),
        out_specs=(P(S, None, Q, None), P(None, S, Q, None), mat, mat, mat, mat, row, row, row, row, row, mat, row, mat,
                   row, row, row),
        check_vma=False)
```

```python
import functools, math
import jax
import jax.numpy as jnp
from jax import lax
from jax.experimental import pallas as pl
from jax.experimental.pallas import tpu as pltpu
from jax.sharding import Mesh, PartitionSpec as P

f32, bf16 = jnp.float32, jnp.bfloat16
LOG2E = 1.4426950408889634
LN2 = 0.6931471805599453
CH = 256
BQ = 2048
RB = 256
FB = 512
PARTS = 2
HD = 64
FAR = -1.0e30

def dg(a, b, ca, cb):
    return lax.dot_general(a, b, (((ca,), (cb,)), ((), ())), preferred_element_type=f32)


def three_parts(row):
    hi = row.astype(bf16).astype(f32)
    rest = row - hi
    mid = rest.astype(bf16).astype(f32)
    return hi, mid, rest - mid


def with_shift(top, shift):
    hi, mid, low = three_parts(shift)
    row = lax.broadcasted_iota(jnp.int32, (HD, top.shape[1]), 0)
    tail = jnp.where(row == 0, -hi, jnp.where(row == 1, -mid, jnp.where(row == 2, -low, jnp.where(row == 3, 1.0, 0.0))))
    return jnp.concatenate([top.astype(f32), tail], axis=0)


def load_rows(rows, ref, spans, x):
    stretch = ref.shape[3]
    for z in range(spans):
        for a in range(2):
            at = (2 * z + a) * stretch
            rows[at:at + stretch] = ref[0, a ^ x, z]


def qkv_kernel(stretch, spans, info, near_ref, far_ref, w_ref, b_ref, q_out, k_out, v_out, size_out, rows):
    away, half = pl.program_id(0), pl.program_id(2)
    owner = ((pl.program_id(1) ^ info[2]) << 1) | (away ^ info[3])

    @pl.when(away == 0)
    def _():
        load_rows(rows, near_ref, spans, info[1])

    @pl.when(away == 1)
    def _():
        load_rows(rows, far_ref, spans, info[1])
    weight = w_ref[...].reshape(rows.shape[1], 384)
    made = dg(rows[...], weight, 1, 0) + b_ref[...]
    count = rows.shape[0]
    q_t = (made[:, :128] * (LOG2E / 8.0)).T
    q_out[0, 0] = q_t[:HD].astype(bf16)
    q_out[1, 0] = q_t[HD:].astype(bf16)
    lane = lax.broadcasted_iota(jnp.int32, (count, 128), 1)
    row = lax.broadcasted_iota(jnp.int32, (count, 128), 0) + half * count
    shift = int(math.log2(stretch))
    position = lax.shift_left(lax.shift_right_logical(row, shift), shift + 2) + owner * stretch + (row & (stretch - 1))
    hidden = jnp.where(position < info[0], 0.0, FAR)
    tail = jnp.where(lane == HD + 3, hidden, jnp.where(lane < HD + 3, 1.0, 0.0))
    keys = made[:, 128:256]
    picks = lax.broadcasted_iota(jnp.int32, (128, 128), 0) // HD == lax.broadcasted_iota(jnp.int32, (128, 128), 1)
    sizes = dg((keys * keys).astype(bf16), jnp.where(picks, 1.0, 0.0).astype(bf16), 1, 0)
    size_out[0, 0] = jnp.max(sizes, axis=0, keepdims=True)
    for head in range(2):
        turned = keys if head == 0 else pltpu.roll(keys, HD, 1)
        full = jnp.where(lane < HD, turned, tail).astype(bf16)
        for j in range(count // 128):
            k_out[head, j, 0] = full[j * 128:(j + 1) * 128]
    v_t = made[:, 256:384].T
    ones = jnp.where(lax.broadcasted_iota(jnp.int32, (HD, count), 0) < 3, 1.0, 0.0)
    for head in range(2):
        full = jnp.concatenate([v_t[head * HD:(head + 1) * HD], ones], axis=0).astype(bf16)
        for j in range(count // 128):
            v_out[head, j, 0] = full[:, j * 128:(j + 1) * 128]


def owner_of(away, across, info):
    return ((across ^ info[2]) << 1) | (away ^ info[3])


def project(near, far, weight, bias, info):
    _, _, zs, stretch, width = near.shape
    local = 2 * zs * stretch
    spans = 1024 // (2 * stretch)
    halves = local // 1024
    spans_of_rows = local // 128
    per = spans_of_rows // halves
    block = (1, 2, spans, stretch, width)
    q, k, v, sizes = pl.pallas_call(
        functools.partial(qkv_kernel, stretch, spans),
        grid_spec=pltpu.PrefetchScalarGridSpec(
            num_scalar_prefetch=1, grid=(2, 2, halves),
            in_specs=[
                pl.BlockSpec(block, lambda a, o, h, n: (jnp.where(a == 0, o, 1), 0, jnp.where(a == 0, h, halves - 1), 0, 0)),
                pl.BlockSpec(block, lambda a, o, h, n: (jnp.where(a == 0, 0, o), 0, jnp.where(a == 0, 0, h), 0, 0)),
                pl.BlockSpec((8, width // 8, 384), lambda a, o, h, n: (0, 0, n[1])),
                pl.BlockSpec((1, 384), lambda a, o, h, n: (0, 0)),
            ],
            out_specs=[
                pl.BlockSpec((2, 1, HD, 1024), lambda a, o, h, n: (0, owner_of(a, o, n), 0, h)),
                pl.BlockSpec((2, per, 1, 128, 128), lambda a, o, h, n: (0, h, o ^ n[2], a ^ n[3], 0)),
                pl.BlockSpec((2, per, 1, 128, 128), lambda a, o, h, n: (0, h, o ^ n[2], 0, a ^ n[3])),
                pl.BlockSpec((1, 1, 1, 128), lambda a, o, h, n: (owner_of(a, o, n), h, 0, 0)),
            ],
            scratch_shapes=[pltpu.VMEM((1024, width), bf16)]),
        out_shape=[
            jax.ShapeDtypeStruct((2, 4, HD, local), bf16),
            jax.ShapeDtypeStruct((2, spans_of_rows, 2, CH, 128), bf16),
            jax.ShapeDtypeStruct((2, spans_of_rows, 2, 128, CH), bf16),
            jax.ShapeDtypeStruct((4, halves, 1, 128), f32),
        ],
        compiler_params=pltpu.CompilerParams(vmem_limit_bytes=60 << 20),
        name="qkv",
        cost_estimate=cost(4 * near.size * 384, near.size * 8),
    )(info, near, far, weight, bias)
    return q, k.reshape(2, -1, CH, 128), v.reshape(2, -1, 128, CH), sizes


def step_on(q, j, count):
    last = j + 1 == count
    return jnp.where(last, q + 1, q), jnp.where(last, 0, j + 1)


def assemble(ref, part, shared, core):
    if not shared:
        return jnp.concatenate([ref[0, 2 * part], ref[0, 2 * part + 1]], axis=1)
    at = pl.multiple_of(core * 512, 512)
    return jnp.concatenate([ref[0, n, :, pl.ds(at, 512)] for n in range(4)], axis=1)


def fwd_kernel(shared, info, q_ref, k_ref, v_ref, size_ref, held_ref, out_ref, lse_ref, acc, probs, qa, shifts):
    count = info[4]
    parts = 1 if shared else 2
    lane = lax.broadcasted_iota(jnp.int32, (1, 128), 1)
    sizes = functools.reduce(jnp.maximum, [size_ref[o, h] for o in range(size_ref.shape[0]) for h in range(size_ref.shape[1])])
    widest = jnp.sqrt(jnp.max(jnp.where(lane == int(shared), sizes, 0.0), axis=1, keepdims=True))

    for part in range(parts):
        q_t = assemble(q_ref, part, shared, info[3])
        wide = q_t.astype(f32)
        shift = jnp.sqrt(jnp.sum(wide * wide, axis=0, keepdims=True)) * widest
        shifts[part] = shift
        qa[part] = with_shift(q_t, shift).astype(bf16)

    def raised(part, j):
        return jnp.exp2(dg(k_ref[0, j], qa[part], 1, 0)).astype(bf16)

    probs[0] = raised(0, 0)

    def body(t, carry, ahead_too=True):
        part, j = carry
        now = t & 1
        part_next, j_next = step_on(part, j, count)
        before = jnp.where(j == 0, 0.0, acc[...])
        acc[...] = before + dg(v_ref[0, j], probs[now], 1, 0)
        if ahead_too:
            probs[1 - now] = raised(part_next, j_next)

        @pl.when(j + 1 == count)
        def _():
            total = acc[HD:HD + 1]
            fine = (jnp.min(total) > 2.0 ** -90) & (jnp.max(total) < 2.0 ** 60)

            @pl.when(jnp.logical_not(fine))
            def _():
                plain = qa[part].astype(f32)
                row = lax.broadcasted_iota(jnp.int32, plain.shape, 0)
                qa[part] = jnp.where((row >= HD) & (row < HD + 3), 0.0, plain).astype(bf16)

                def peak(i, top):
                    return jnp.maximum(top, jnp.max(dg(k_ref[0, i], qa[part], 1, 0), axis=0, keepdims=True))
                shift = lax.fori_loop(0, count, peak, jnp.full((1, BQ), FAR, f32))
                shifts[part] = shift
                qa[part] = with_shift(plain[:HD], shift).astype(bf16)
                acc[...] = jnp.zeros_like(acc)

                def again(i, carry):
                    acc[...] += dg(v_ref[0, i], raised(part, i), 1, 0)
                    return carry
                lax.fori_loop(0, count, again, 0)

            total = acc[HD:HD + 1]
            mixed = (acc[:HD] * (1.0 / total)).astype(bf16)
            lse_ref[part] = shifts[part] + jnp.log2(total)
            if shared:
                for n in range(4):
                    out_ref[0, n] = mixed[:, n * 512:(n + 1) * 512]
            else:
                for n in range(2):
                    out_ref[0, 2 * part + n] = mixed[:, n * 1024:(n + 1) * 1024]
        return part_next, j_next

    turns = parts * count
    body(turns - 1, lax.fori_loop(0, turns - 1, body, (0, 0)), False)


def head_spec(shared, *dims):
    zeros = (0,) * len(dims)
    return pl.BlockSpec((1,) + dims, lambda i, n: (int(shared),) + zeros)


def whole_spec(*dims):
    return pl.BlockSpec(dims, lambda i, n: (0,) * len(dims))


def cost(flops, moved, exps=0):
    return pl.CostEstimate(flops=int(flops), bytes_accessed=int(moved), transcendentals=int(exps))


def attend_forward(shared, seq, q, k, v, sizes, info, held):
    _, owners, _, local = q.shape
    chunks = k.shape[1]
    wide = local // 2 if shared else local
    parts = owners * wide // BQ
    pairs = parts * BQ * chunks * CH * 0.6
    shape = jax.ShapeDtypeStruct((2, owners, HD, wide), bf16)
    first = held is None
    if first:
        kernel = lambda info, q, k, v, size, *rest: fwd_kernel(shared, info, q, k, v, size, None, *rest)
    else:
        kernel = functools.partial(fwd_kernel, shared)
    return pl.pallas_call(
        kernel,
        grid_spec=pltpu.PrefetchScalarGridSpec(
            num_scalar_prefetch=1, grid=(1,),
            in_specs=[
                head_spec(shared, owners, HD, local), head_spec(shared, chunks, CH, 128), head_spec(shared, chunks, 128, CH),
                whole_spec(*sizes.shape),
            ] + ([] if first else [pl.BlockSpec(memory_space=pl.ANY)]),
            out_specs=[pl.BlockSpec((1, owners, HD, wide), lambda i, n: (seq, 0, 0, 0)), whole_spec(parts, 1, BQ)],
            scratch_shapes=[
                pltpu.VMEM((128, BQ), f32), pltpu.VMEM((2, CH, BQ), bf16), pltpu.VMEM((parts, 128, BQ), bf16),
                pltpu.VMEM((parts, 1, BQ), f32),
            ]),
        out_shape=[shape, jax.ShapeDtypeStruct((parts, 1, BQ), f32)],
        input_output_aliases={} if first else {5: 0},
        compiler_params=pltpu.CompilerParams(vmem_limit_bytes=60 << 20),
        cost_estimate=cost(pairs * 1024, chunks * CH * 512, pairs),
        name="attend_forward_shared" if shared else "attend_forward_own",
    )(*((info, q, k, v, sizes) + (() if first else (held,))))


def bwd_kernel(shared, first, info, q_ref, k_ref, v_ref, lse_ref, out_ref, gout_ref, *rest):
    rest = rest if first else rest[3 if shared else 1:]
    if shared:
        dq_ref, kept_ref, given_ref, dk_acc, dv_acc, dq_acc, qa, qat, ga, gat, pb, db = rest
    else:
        dqkv_ref, dk_acc, dv_acc, dq_acc, qa, qat, ga, gat, pb, db = rest
    count = info[4]
    chunks = k_ref.shape[1]
    parts = 1 if shared else 2
    dk_acc[...] = jnp.zeros_like(dk_acc)
    dv_acc[...] = jnp.zeros_like(dv_acc)

    def piece(ref, part):
        return jnp.concatenate([ref[0, n] for n in (range(4) if shared else (2 * part, 2 * part + 1))], axis=1)

    for part in range(parts):
        q_full = with_shift(assemble(q_ref, part, shared, info[3]), lse_ref[part])
        qat[part] = q_full.astype(bf16)
        qa[part] = q_full.T.astype(bf16)
        g_t = piece(gout_ref, part)
        meet = jnp.sum(g_t.astype(f32) * piece(out_ref, part).astype(f32), axis=0, keepdims=True)
        g_full = with_shift(g_t, meet)
        gat[part] = g_full.astype(bf16)
        ga[part] = g_full.T.astype(bf16)

    def ahead(part, j, slot):
        raised = jnp.exp2(dg(qa[part], k_ref[0, j], 1, 1))
        pb[slot] = raised.astype(bf16)
        db[slot] = (raised * dg(ga[part], v_ref[0, j], 1, 0)).astype(bf16)

    ahead(0, 0, 0)

    def body(t, carry, ahead_too=True):
        part, j = carry
        now = t & 1
        part_next, j_next = step_on(part, j, count)
        dv_acc[j] += dg(gat[part], pb[now], 1, 0)[:HD]
        dk_acc[j] += dg(qat[part], db[now], 1, 0)[:HD]
        before = jnp.where(j == 0, 0.0, dq_acc[...])
        dq_acc[...] = before + dg(db[now], k_ref[0, j], 1, 0)
        if ahead_too:
            ahead(part_next, j_next, 1 - now)

        @pl.when(j + 1 == count)
        def _():
            dq_t = (dq_acc[...] * 0.125).T[:HD].astype(bf16)
            if shared:
                for n in range(4):
                    dq_ref[0, n, :, :512] = dq_t[:32, n * 512:(n + 1) * 512]
                    dq_ref[0, n, :, 512:] = dq_t[32:, n * 512:(n + 1) * 512]
            else:
                for n in range(2):
                    dqkv_ref[0, 2 * part + n, 0] = dq_t[:, n * 1024:(n + 1) * 1024]
        return part_next, j_next

    turns = parts * count
    body(turns - 1, lax.fori_loop(0, turns - 1, body, (0, 0)), False)
    for block in range(chunks):
        j, across = block // 2, block % 2
        for owner in (2 * across, 2 * across + 1):
            cols = slice((owner - 2 * across) * 128, (owner - 2 * across + 1) * 128)
            dk_wide, dv_wide = dk_acc[block, :, cols] * LN2, dv_acc[block, :, cols]
            dk, dv = dk_wide.astype(bf16), dv_wide.astype(bf16)
            if shared:
                here = info[3] == 0
                kept_ref[0, owner, :, j * 128:(j + 1) * 128] = jnp.where(here, dk_wide, dv_wide).astype(bf16)
                given_ref[0, owner, :, j * 128:(j + 1) * 128] = jnp.where(here, dv_wide, dk_wide).astype(bf16)
            else:
                dqkv_ref[0, owner, 1, :, j * 128:(j + 1) * 128] = dk
                dqkv_ref[0, owner, 2, :, j * 128:(j + 1) * 128] = dv


def attend_backward(shared, seq, q, k, v, lse, out, g_out, info, held):
    _, owners, _, local = q.shape
    chunks = k.shape[1]
    wide = out.shape[3]
    parts = owners * wide // BQ
    pairs = parts * BQ * chunks * CH * 0.6
    shape = jax.ShapeDtypeStruct
    first = held is None
    if shared:
        out_specs = [pl.BlockSpec((1, owners, rows, local), lambda i, n: (seq, 0, 0, 0)) for rows in (32, HD, HD)]
        out_shape = [shape((2, owners, rows, local), bf16) for rows in (32, HD, HD)]
    else:
        out_specs = [pl.BlockSpec((1, owners, 3, HD, local), lambda i, n: (seq, 0, 0, 0, 0))]
        out_shape = [shape((2, owners, 3, HD, local), bf16)]
    kept = () if first else tuple(held)
    of_seq = pl.BlockSpec((1, owners, HD, wide), lambda i, n: (seq, 0, 0, 0))
    return pl.pallas_call(
        functools.partial(bwd_kernel, shared, first),
        grid_spec=pltpu.PrefetchScalarGridSpec(
            num_scalar_prefetch=1, grid=(1,),
            in_specs=[
                head_spec(shared, owners, HD, local), head_spec(shared, chunks, CH, 128), head_spec(shared, chunks, 128, CH),
                whole_spec(parts, 1, BQ), of_seq, of_seq,
            ] + [pl.BlockSpec(memory_space=pl.ANY)] * len(kept),
            out_specs=out_specs,
            scratch_shapes=[
                pltpu.VMEM((chunks, HD, CH), f32), pltpu.VMEM((chunks, HD, CH), f32), pltpu.VMEM((BQ, 128), f32),
                pltpu.VMEM((parts, BQ, 128), bf16), pltpu.VMEM((parts, 128, BQ), bf16),
                pltpu.VMEM((parts, BQ, 128), bf16), pltpu.VMEM((parts, 128, BQ), bf16),
                pltpu.VMEM((2, BQ, CH), bf16), pltpu.VMEM((2, BQ, CH), bf16),
            ]),
        out_shape=out_shape,
        input_output_aliases={7 + n: n for n in range(len(kept))},
        compiler_params=pltpu.CompilerParams(vmem_limit_bytes=60 << 20),
        cost_estimate=cost(pairs * 100, chunks * CH * 2048),
        name="attend_backward_shared" if shared else "attend_backward_own",
    )(info, q, k, v, lse, out, g_out, *kept)


def gelu_pair(u):
    half = 0.5 * (1.0 + lax.erf(u * 0.7071067811865476))
    return u * half, half + u * (0.3989422804014327 * jnp.exp2(u * u * (-0.5 * LOG2E)))


def norm_stats(v):
    mean = jnp.mean(v, axis=-1, keepdims=True)
    centred = v - mean
    inverse = lax.rsqrt(jnp.mean(centred * centred, axis=-1, keepdims=True) + 1e-12)
    return centred * inverse, inverse


def norm_back(grad, xhat, inverse, gain):
    g = grad * gain
    return (g - jnp.mean(g, axis=-1, keepdims=True) - xhat * jnp.mean(g * xhat, axis=-1, keepdims=True)) * inverse


def weight_part(ref, first, rows):
    part = ref[:, first:first + rows, :]
    return part.reshape(part.shape[0] * rows, part.shape[2])


def ffn_kernel(spans, info, x_ref, own_ref, sh_ref, cot_ref, w_ref, bin_ref, vec_ref,
               act_out, resid_out, gown_out, gsh_out, active_out, dinner_out, normed_out, douter_out, dbranch_out,
               vec_sum, bin_sum, slope, row_block):
    step = pl.program_id(0)
    load_rows(row_block, x_ref, spans, info[1])
    count = row_block.shape[0] // PARTS
    vec = vec_ref[...]
    total = lambda a: jnp.sum(a, axis=0, keepdims=True)
    held = [{"at": slice(n * count, (n + 1) * count)} for n in range(PARTS)]

    def branch(h):
        at = h["at"]
        mixed_t = jnp.concatenate(
            [part for p in range(4) for part in (own_ref[p, 0, :, at], sh_ref[p, 0, :, at], own_ref[p, 1, :, at])], axis=0)
        h["sum1"] = row_block[at].astype(f32) + (dg(mixed_t, weight_part(w_ref, 768, 96), 0, 0) + vec[0:1])

    def first_norm(h):
        h["xhat1"], h["inv1"] = norm_stats(h["sum1"])
        normed = h["xhat1"] * vec[1:2] + vec[2:3]
        normed_out[h["at"]] = normed.astype(bf16)
        h["outer"] = normed + vec[3:4]

    def widen(h):
        at = h["at"]
        for n in range(4):
            cols = slice(n * 768, (n + 1) * 768)
            value, bend = gelu_pair(dg(normed_out[at], weight_part(w_ref, 384 + 96 * n, 96), 1, 0) + bin_ref[:, cols])
            active_out[at, cols] = value.astype(bf16)
            slope[at, cols] = bend.astype(bf16)

    def narrow(h):
        h["outer"] = h["outer"] + dg(active_out[h["at"]], weight_part(w_ref, 0, 384), 1, 0)

    def second_norm(h):
        at = h["at"]
        xhat2, inv2 = norm_stats(h["outer"])
        act_out[at] = (xhat2 * vec[4:5] + vec[5:6]).astype(bf16)
        cot = cot_ref[at].astype(f32)
        d2 = norm_back(cot, xhat2, inv2, vec[4:5])
        d_outer = d2.astype(bf16)
        douter_out[at] = d_outer
        h["d_normed"] = d2
        h["sums"] = [total(d_outer.astype(f32)), total(cot * xhat2), total(cot)]

    def back(h):
        at = h["at"]
        h["inner_sums"] = []
        for n in range(4):
            cols = slice(n * 768, (n + 1) * 768)
            d_active = dg(douter_out[at], weight_part(w_ref.at[2 * n:2 * n + 2], 0, 384), 1, 1)
            d_inner = (d_active * slope[at, cols].astype(f32)).astype(bf16)
            dinner_out[at, cols] = d_inner
            h["inner_sums"].append(total(d_inner.astype(f32)))
            h["d_normed"] = h["d_normed"] + dg(d_inner, weight_part(w_ref, 384 + 96 * n, 96), 1, 1)

    def first_back(h):
        at = h["at"]
        d_normed = h["d_normed"]
        d1 = norm_back(d_normed, h["xhat1"], h["inv1"], vec[1:2])
        resid_out[at] = d1
        d_branch = d1.astype(bf16)
        dbranch_out[at] = d_branch
        h["sums"] = [total(d_branch.astype(f32)), total(d_normed * h["xhat1"]), total(d_normed)] + h["sums"]

    def mix_back(h):
        at = h["at"]
        g_t = dg(weight_part(w_ref, 768, 96), dbranch_out[at], 1, 1).astype(bf16)
        for p in range(4):
            gown_out[p, 0, :, at] = g_t[192 * p:192 * p + 64]
            gsh_out[p, 0, :, at] = g_t[192 * p + 64:192 * p + 128]
            gown_out[p, 1, :, at] = g_t[192 * p + 128:192 * p + 192]

    for products, norm in ((branch, first_norm), (widen, None), (narrow, second_norm), (back, first_back), (mix_back, None)):
        for h in held:
            products(h)
            if norm is not None:
                norm(h)
    sums = jnp.concatenate([
        functools.reduce(jnp.add, [h["sums"][n] for h in held]) for n in range(6)] + [jnp.zeros((2, vec.shape[1]), f32)], axis=0)
    inner_sums = [functools.reduce(jnp.add, [h["inner_sums"][n] for h in held]) for n in range(4)]

    @pl.when(step == 0)
    def _():
        vec_sum[...] = sums
        for n in range(4):
            bin_sum[:, n * 768:(n + 1) * 768] = inner_sums[n]

    @pl.when(step > 0)
    def _():
        vec_sum[...] += sums
        for n in range(4):
            bin_sum[:, n * 768:(n + 1) * 768] += inner_sums[n]


def feed_forward(rows_in, own, sh, cotangent, weights, inner_bias, vectors, info):
    _, _, _, stretch, width = rows_in.shape
    local = cotangent.shape[0]
    spans = FB // (2 * stretch)
    steps = local // FB
    half_steps = steps // 2
    wide = inner_bias.shape[1]
    rows = lambda n: pl.BlockSpec((FB, n), lambda r, a: (r, 0))
    fixed = lambda *dims: pl.BlockSpec(dims, lambda r, a: (0,) * len(dims))
    own_spec = pl.BlockSpec((4, 2, HD, FB), lambda r, a: (0, 0, 0, r))
    sh_spec = pl.BlockSpec((4, 1, HD, FB), lambda r, a: (0, r // half_steps, 0, r % half_steps))
    shape = jax.ShapeDtypeStruct
    return pl.pallas_call(
        functools.partial(ffn_kernel, spans),
        grid_spec=pltpu.PrefetchScalarGridSpec(
            num_scalar_prefetch=1, grid=(steps,),
            in_specs=[
                pl.BlockSpec((1, 2, spans, stretch, width), lambda r, a: (0, 0, r, 0, 0)),
                own_spec, sh_spec, rows(width),
                pl.BlockSpec(weights.shape, lambda r, a: (0, 0, 0), pipeline_mode=pl.Buffered(1)),
                fixed(1, wide), fixed(8, width),
            ],
            out_specs=[
                rows(width), rows(width), own_spec, sh_spec, rows(wide), rows(wide), rows(width), rows(width), rows(width),
                fixed(8, width), fixed(1, wide),
            ],
            scratch_shapes=[pltpu.VMEM((FB, wide), bf16), pltpu.VMEM((FB, width), bf16)]),
        out_shape=[
            shape((local, width), bf16), shape((local, width), f32), shape(own.shape, bf16), shape(sh.shape, bf16),
            shape((local, wide), bf16), shape((local, wide), bf16), shape((local, width), bf16),
            shape((local, width), bf16), shape((local, width), bf16), shape((8, width), f32), shape((1, wide), f32),
        ],
        compiler_params=pltpu.CompilerParams(vmem_limit_bytes=60 << 20),
        name="feed_forward",
        cost_estimate=cost(local * width * (width + 2 * wide) * 4, local * wide * 20),
    )(info, rows_in, own, sh, cotangent, weights, inner_bias, vectors)


def outer_grad_kernel(scale, active_ref, douter_ref, out_ref):
    made = (dg(active_ref[...], douter_ref[...], 0, 0) * scale).astype(bf16)
    out_ref[...] = made.reshape(out_ref.shape)


def inner_grad_kernel(scale, packed_ref, normed_ref, dinner_ref, own_ref, sh_ref, dbranch_ref, out_ref):
    step = pl.program_id(0)

    @pl.when(step < 4)
    def _():
        out_ref[...] = (dg(normed_ref[...], dinner_ref[...], 0, 0) * scale).astype(bf16).reshape(out_ref.shape)

    @pl.when(step == 4)
    def _():
        mixed_t = jnp.concatenate([
            part for p in range(4)
            for part in (own_ref[p, 0], jnp.concatenate([sh_ref[p, 0], sh_ref[p, 1]], axis=1), own_ref[p, 1])], axis=0)
        out_ref[...] = (dg(mixed_t, dbranch_ref[...], 1, 0) * scale).astype(bf16).reshape(out_ref.shape)


def weight_grads(scale, active, d_outer, normed, d_inner, own, sh, d_branch):
    local, wide = active.shape
    width = normed.shape[1]
    packed = pl.pallas_call(
        functools.partial(outer_grad_kernel, scale), grid=(4,),
        in_specs=[pl.BlockSpec((local, width), lambda m: (0, m)), pl.BlockSpec((local, width), lambda m: (0, 0))],
        out_specs=pl.BlockSpec((2, 384, width), lambda m: (m, 0, 0)),
        out_shape=jax.ShapeDtypeStruct((8, 896, width), bf16),
        compiler_params=pltpu.CompilerParams(vmem_limit_bytes=40 << 20), name="outer_grad",
        cost_estimate=cost(2 * local * wide * width, 2 * wide * (local + width)),
    )(active, d_outer)
    fixed = lambda a: pl.BlockSpec(a.shape, lambda n: (0,) * a.ndim)
    return pl.pallas_call(
        functools.partial(inner_grad_kernel, scale), grid=(5,),
        in_specs=[
            pl.BlockSpec(memory_space=pl.ANY), fixed(normed),
            pl.BlockSpec((local, width), lambda n: (0, jnp.minimum(n, 3))), fixed(own), fixed(sh), fixed(d_branch)],
        out_specs=pl.BlockSpec((8, 96, width), lambda n: (0, 4 + n, 0)),
        out_shape=jax.ShapeDtypeStruct((8, 896, width), bf16), input_output_aliases={0: 0},
        compiler_params=pltpu.CompilerParams(vmem_limit_bytes=40 << 20), name="inner_grad",
        cost_estimate=cost(2 * local * (wide + width) * width, 2 * (wide + width) * (local + width)),
    )(packed, normed, d_inner, own, sh, d_branch)


def head_grad_kernel(scale, spans, info, *refs):
    x_refs, (own_ref, dq_ref, kept_ref, given_ref, out_ref, bias_out, acc, bias_acc, rows) = refs[:4], refs[4:]
    seq, away, half = pl.program_id(0), pl.program_id(1), pl.program_id(3)
    last = (seq == 1) & (away == 1) & (pl.program_id(2) == 1) & (half == pl.num_programs(3) - 1)
    for n in range(4):
        @pl.when(seq * 2 + away == n)
        def _(n=n):
            load_rows(rows, x_refs[n], spans, info[1])
    dq_t = jnp.where(half == info[3], jnp.concatenate([dq_ref[0, 0, :, :512], dq_ref[0, 0, :, 512:]], axis=0).astype(f32), 0.0)
    kept, given = kept_ref[0, 0].astype(f32), given_ref[0, 0].astype(f32)
    here = info[3] == 0
    d_t = jnp.concatenate([
        own_ref[0, 0, 0], dq_t.astype(bf16), own_ref[0, 0, 1], jnp.where(here, kept, given).astype(bf16),
        own_ref[0, 0, 2], jnp.where(here, given, kept).astype(bf16)], axis=0)

    @pl.when((seq == 0) & (away == 0) & (pl.program_id(2) == 0) & (half == 0))
    def _():
        acc[...] = jnp.zeros_like(acc)
        bias_acc[...] = jnp.zeros_like(bias_acc)
    acc[...] += dg(d_t, rows[...], 1, 0)
    bias_acc[...] += dg(jnp.ones((8, d_t.shape[1]), bf16), d_t, 1, 1)

    @pl.when(last)
    def _():
        out_ref[...] = (acc[...] * scale).T.astype(bf16)
        bias_out[...] = bias_acc[...] * scale


def head_grads(scale, sources, dqkv_own, dq_sh, kept, given, info):
    _, _, zs, stretch, width = sources[0].shape
    local = 2 * zs * stretch
    spans = 512 // (2 * stretch)
    halves = local // 512

    def source_spec(n):
        def index(s, a, o, h, i):
            now = 2 * s + a
            across = jnp.where(now == n, o, jnp.where(now < n, 0, 1))
            return (across, 0, jnp.where(now == n, h, jnp.where(now < n, 0, halves - 1)), 0, 0)
        return pl.BlockSpec((1, 2, spans, stretch, width), index)
    return pl.pallas_call(
        functools.partial(head_grad_kernel, scale, spans),
        grid_spec=pltpu.PrefetchScalarGridSpec(
            num_scalar_prefetch=1, grid=(2, 2, 2, halves),
            in_specs=[source_spec(n) for n in range(4)] + [
                pl.BlockSpec((1, 1, 3, HD, 512), lambda s, a, o, h, i: (s, owner_of(a, o, i), 0, 0, h)),
                pl.BlockSpec((1, 1, 32, local), lambda s, a, o, h, i: (s, owner_of(a, o, i), 0, 0)),
            ] + [pl.BlockSpec((1, 1, HD, 512), lambda s, a, o, h, i: (s, owner_of(a, o, i), 0, h))] * 2,
            out_specs=[pl.BlockSpec((width, 384), lambda s, a, o, h, i: (0, 0)), pl.BlockSpec((8, 384), lambda s, a, o, h, i: (0, 0))],
            scratch_shapes=[pltpu.VMEM((384, width), f32), pltpu.VMEM((8, 384), f32), pltpu.VMEM((512, width), bf16)]),
        out_shape=[jax.ShapeDtypeStruct((width, 384), bf16), jax.ShapeDtypeStruct((8, 384), f32)],
        compiler_params=pltpu.CompilerParams(vmem_limit_bytes=40 << 20), name="head_grads",
        cost_estimate=cost(8 * local * 768 * width, 8 * local * width * 2),
    )(info, *sources, dqkv_own, dq_sh, kept, given)


def token_grad_kernel(own_ref, low_ref, high_ref, dkv_ref, w_ref, resid_ref, out_ref):
    total = resid_ref[...]
    for kind in range(3):
        made = []
        for p in range(4):
            if kind == 0:
                middle = jnp.concatenate([low_ref[p, 0], high_ref[p, 0]], axis=0)
            else:
                middle = jnp.concatenate([dkv_ref[p, kind - 1, n] for n in range(2)], axis=0)
            made += [own_ref[p, 0, kind], middle, own_ref[p, 1, kind]]
        total = total + dg(jnp.concatenate(made, axis=0), weight_part(w_ref, 96 * kind, 96), 0, 1)
    out_ref[...] = total.astype(bf16)


def token_grad(own, shared, weights, resid):
    local, width = resid.shape
    steps = local // RB
    half_steps = steps // 2
    rows = pl.BlockSpec((RB, width), lambda r: (r, 0))
    return pl.pallas_call(
        token_grad_kernel, grid=(steps,),
        in_specs=[
            pl.BlockSpec((4, 2, 3, HD, RB), lambda r: (0, 0, 0, 0, r)),
            pl.BlockSpec((4, 1, None, 32, RB), lambda r: (0, r // half_steps, 2, 0, r % half_steps)),
            pl.BlockSpec((4, 1, None, 32, RB), lambda r: (0, r // half_steps, 2, 0, half_steps + r % half_steps)),
            pl.BlockSpec((4, 2, 2, 32, RB), lambda r: (0, 0, 0, 0, r)),
            pl.BlockSpec(weights.shape, lambda r: (0, 0, 0)), rows],
        out_specs=rows, out_shape=jax.ShapeDtypeStruct((local, width), bf16),
        compiler_params=pltpu.CompilerParams(vmem_limit_bytes=60 << 20), name="token_grad",
        cost_estimate=cost(local * width * width * 6, local * width * 12),
    )(own, shared, shared, shared, weights, resid)


def head_unpack_kernel(per, info, src_ref, q_out, k_out, v_out, bias_out):
    low = lax.broadcasted_iota(jnp.int32, (src_ref.shape[1], 128), 1) < HD

    def rows_of(p, core, cols):
        at = (((p >> 1) ^ info[1]) << 2) | (((p & 1) ^ info[2]) << 1) | (core ^ info[3])
        return src_ref[at, :, cols].astype(f32)
    for kind, out in enumerate((q_out, k_out, v_out)):
        cols = slice(128 * kind, 128 * kind + 128)
        tiles = []
        for pair in range(2):
            first, second = [], []
            for p in (2 * pair, 2 * pair + 1):
                near, far = rows_of(p, 0, cols), rows_of(p, 1, cols)
                first.append(near + jnp.where(low, 0.0, far))
                second.append(far)
            turned = pltpu.roll(first[1], HD, 1)
            tiles += [first[0], jnp.where(low, second[0], turned), jnp.where(low, turned, pltpu.roll(second[1], HD, 1))]
        made = jnp.concatenate(tiles, axis=1)
        out[...] = made[:per]
        if kind != 1:
            bias_out[kind // 2:kind // 2 + 1] = made[per:per + 1]


def head_unpack(source, per, width, info):
    shape = jax.ShapeDtypeStruct
    full = lambda n: pl.BlockSpec((n, width), lambda i, f: (0, 0))
    return pl.pallas_call(
        functools.partial(head_unpack_kernel, per),
        grid_spec=pltpu.PrefetchScalarGridSpec(
            num_scalar_prefetch=1, grid=(1,),
            in_specs=[pl.BlockSpec(source.shape, lambda i, f: (0, 0, 0))],
            out_specs=[full(per)] * 3 + [full(2)]),
        out_shape=[shape((per, width), f32)] * 3 + [shape((2, width), f32)], name="head_unpack",
    )(info, source)


SWAP = [(0, 1), (1, 0)]
def settle_kernel(*refs):
    refs[-1][...] = sum(ref[...].astype(f32) for ref in refs[:-2]).astype(bf16)


def settle(parts, after):
    whole = pl.BlockSpec(memory_space=pltpu.VMEM)
    return pl.pallas_call(
        settle_kernel, in_specs=[whole] * len(parts) + [pl.BlockSpec(memory_space=pl.ANY)], out_specs=whole,
        out_shape=jax.ShapeDtypeStruct(parts[0].shape, bf16), name="settle",
        cost_estimate=cost(1e9, 1e6),
    )(*parts, after)


PAIR = ("x", "y", "c")
ALL = ("z", "x", "y", "c")
SHARD = ("z", "x")


def canonical(packed, shards):
    if shards == 8:
        return packed
    width = packed.shape[2]
    per, keep = 96 * 8 // shards, shards // 8
    outer = packed[:, :4 * per].reshape(8, 384, width)
    inner = packed[:, 4 * per:8 * per].reshape(8, keep, 4, per, width).transpose(0, 2, 1, 3, 4).reshape(8, 384, width)
    output = packed[:, 8 * per:9 * per].reshape(8, 96, width)
    return jnp.concatenate([outer, inner, output, jnp.zeros((8, 32, width), packed.dtype)], axis=1)


def from_canonical(packed, last, shards):
    width = packed.shape[2]
    if shards == 8:
        return packed.at[:, 864:].set(jnp.broadcast_to(last[None], (8, 32, width)))
    per, keep = 96 * 8 // shards, shards // 8
    outer = packed[:, :384].reshape(shards, 4 * per, width)
    inner = packed[:, 384:768].reshape(8, 4, keep, per, width).transpose(0, 2, 1, 3, 4).reshape(shards, 4 * per, width)
    output = packed[:, 768:864].reshape(shards, per, width)
    return jnp.concatenate([outer, inner, output, jnp.broadcast_to(last[None], (shards, 32, width))], axis=1)


def canonical_heads(packed, shards, parts):
    if shards == 8:
        return packed
    width = packed.shape[2]
    per = 96 * 8 // shards
    made = [packed[:, k * per:(k + 1) * per].reshape(8, 96, width) for k in range(parts)]
    return jnp.concatenate(made + [jnp.zeros((8, 32, width), packed.dtype)], axis=1)


def quarter(pieces):
    part = sum(piece.shape[0] for piece in pieces) // 4

    def taken(k):
        found, at = [], 0
        for piece in pieces:
            low, high = max(k * part - at, 0), min((k + 1) * part - at, piece.shape[0])
            if low < high:
                found.append(piece[low:high])
            at += piece.shape[0]
        return jnp.concatenate(found, axis=0)
    place = lax.axis_index("y") * 2 + lax.axis_index("c")
    return lax.switch(place, [functools.partial(taken, k) for k in range(4)])


def flipped(array, axis, here):
    return jnp.where(here == 0, array, jnp.flip(array, axis))


def body(tokens, lengths, deal_order, w_query, w_key, w_value, w_output, b_query, b_value, b_output,
         ln1_gain, ln1_shift, w_inner, b_inner, w_outer, b_outer, ln2_gain, ln2_shift, cotangent):
    tie = lax.optimization_barrier
    zs = lax.axis_size("z")
    shards = 2 * zs
    scale = 1.0 / (shards * 4)
    seq_count, _, stretch, width = tokens.shape
    per = w_query.shape[0]
    half = zs // 2
    x, y, c = lax.axis_index("x"), lax.axis_index("y"), lax.axis_index("c")

    def deal(ordered):
        return lax.all_to_all(ordered, "z", split_axis=0, concat_axis=0, tiled=True)

    def corner(across, along):
        return [lax.ppermute(across[:half], "y", SWAP), lax.ppermute(along[half:], "x", SWAP)]

    def this_core(own, across, along, corner):
        return jnp.concatenate([own, across, along] + corner, axis=0).reshape(2, 2, zs, stretch, width)

    ordered_a = tokens[:, 0].at[deal_order[0::2]].get(mode="promise_in_bounds")
    first_own = deal(ordered_a)
    _, tokens, w_query, w_key, w_value, b_query, b_value, deal_order = tie(
        (ordered_a, tokens, w_query, w_key, w_value, b_query, b_value, deal_order))
    ordered_b = tokens[:, 0].at[deal_order[1::2]].get(mode="promise_in_bounds")

    def head_columns(matrix):
        heads = matrix.reshape(per, 2, 2, 3, HD)
        mine = lax.dynamic_index_in_dim(heads, y, axis=2, keepdims=False)
        own = lax.dynamic_index_in_dim(mine, 2 * c, axis=2, keepdims=False)
        return [own, mine[:, :, 1]]
    pad = lambda v: jnp.pad(v, (0, width - v.shape[0]))[None]
    columns = jnp.concatenate(
        [col for matrix in (w_query, w_key, w_value) for col in head_columns(matrix)], axis=2).reshape(per, width)
    head_pack = jnp.concatenate([columns, pad(b_query), pad(b_value), jnp.zeros((14, width), bf16)], axis=0)
    (first_own, ordered_b, head_pack, w_outer, w_inner, w_output, b_inner, lengths, w_query, w_key, w_value) = tie(
        (first_own, ordered_b, head_pack, w_outer, w_inner, w_output, b_inner, lengths, w_query, w_key, w_value))
    vectors = (b_output, ln1_gain, ln1_shift, b_outer, ln2_gain, ln2_shift)
    vector_pack = jnp.concatenate([pad(b_inner)] + [pad(v) for v in vectors] + [jnp.zeros((25, width), bf16)], axis=0)
    layer_quarter = quarter(
        [w_outer] + [w_inner[:, n * width:(n + 1) * width] for n in range(4)] + [w_output, vector_pack])
    back_quarter = quarter([w_query, w_key, w_value, jnp.zeros((32, width), bf16)])
    slots = lax.dynamic_slice_in_dim(deal_order, lax.axis_index("z") * 2, 2)
    matches = slots[:, None] == jnp.arange(seq_count, dtype=jnp.int32)[None, :]
    lens = jnp.sum(jnp.where(matches, lengths[None, :], 0), axis=1).astype(jnp.int32)
    last = (lens + 511) // 512 - 1
    counts = 2 * last + 1 + (lens > 512 * last + 2 * stretch).astype(jnp.int32)
    infos = [jnp.stack([lens[n], x, y, c, counts[n]]).astype(jnp.int32) for n in range(2)]
    head_all = lax.all_gather(head_pack, SHARD, axis=0, tiled=False)
    head_weight = canonical_heads(head_all, shards, 1)

    def head_bias(row):
        heads = head_all[:, per + row, :per].reshape(2, 2, 3, HD)
        mine = lax.dynamic_slice(heads, (x, y, 0, 0), (1, 1, 3, HD))[0, 0]
        return [lax.dynamic_index_in_dim(mine, 2 * c, axis=0, keepdims=False), mine[1]]
    bias_row = jnp.concatenate(head_bias(0) + [jnp.zeros((2 * HD,), bf16)] + head_bias(1)).astype(f32)[None]

    across_a, along_a = lax.ppermute(first_own, "x", SWAP), lax.ppermute(first_own, "y", SWAP)
    second_own = deal(ordered_b)
    across_a, along_a, second_own, layer_quarter, back_quarter, *infos = tie(
        (across_a, along_a, second_own, layer_quarter, back_quarter, *infos))
    corner_a = corner(across_a, along_a)
    second_own, *corner_a = tie((second_own, *corner_a))
    near_a = this_core(first_own, across_a, along_a, corner_a)
    far_a = lax.ppermute(near_a, "c", SWAP)
    across_b, along_b = lax.ppermute(second_own, "x", SWAP), lax.ppermute(second_own, "y", SWAP)

    layer_all = lax.all_gather(layer_quarter, ALL, axis=0, tiled=True).reshape(shards, 9 * per + 32, width)
    layer_weights = canonical(layer_all, shards)
    inner_bias = layer_all[:, 9 * per, :4 * per].reshape(1, 4 * width).astype(f32)
    vector_rows = jnp.concatenate(
        [layer_all[:, 9 * per + 1 + n, :per].reshape(1, width) for n in range(6)] + [jnp.zeros((2, width), bf16)],
        axis=0).astype(f32)
    back_all = lax.all_gather(back_quarter, ALL, axis=0, tiled=True).reshape(shards, 3 * per + 32, width)

    def swap(array):
        flat = array.reshape((8,) + array.shape[2:])
        return lax.all_to_all(flat, PAIR, split_axis=0, concat_axis=0, tiled=True)

    def to_tokens(array):
        return swap(array).reshape((4, 2) + array.shape[2:])

    def to_heads(array):
        return swap(array).reshape((2, 4) + array.shape[2:])

    heads_a = project(near_a, far_a, head_weight, bias_row, infos[0])
    heads_a, across_b, along_b = tie((heads_a, across_b, along_b))
    near_b = this_core(second_own, across_b, along_b, corner(across_b, along_b))
    own_first, lse_own_a = attend_forward(False, 0, *heads_a, infos[0], None)
    own_first, near_b = tie((own_first, near_b))
    far_b = lax.ppermute(near_b, "c", SWAP)
    heads_b = project(near_b, far_b, head_weight, bias_row, infos[1])
    own, lse_own_b = attend_forward(False, 1, *heads_b, infos[1], own_first)
    own_t = to_tokens(own)
    own, info_a, info_b = tie((own, *infos))
    sh_first, lse_sh_a = attend_forward(True, 0, *heads_a, info_a, None)
    sh, lse_sh_b = attend_forward(True, 1, *heads_b, info_b, sh_first)
    sh_sent, own_t = tie((sh, own_t))
    sh_t = to_tokens(sh_sent)
    mine_rows = jnp.where(x == 0, jnp.stack([first_own, across_a]), jnp.stack([second_own, across_b]))[None]

    (act, resid, g_own, g_sh, active, d_inner, normed, d_outer, d_branch, vec_sums, bin_sums) = feed_forward(
        mine_rows, own_t, sh_t, cotangent.reshape(-1, width), layer_weights, inner_bias, vector_rows, infos[0])
    g_own_h, g_sh_h = to_heads(g_own), to_heads(g_sh)
    packed = weight_grads(scale, active, d_outer, normed, d_inner, own_t, sh_t, d_branch)
    sums = jnp.concatenate([bin_sums.reshape(4, width), vec_sums, jnp.zeros((20, width), f32)], axis=0) * scale
    ready = from_canonical(packed, sums.astype(bf16), shards)
    ready, back_all, g_own_h = tie((ready, back_all, g_own_h))
    back_weights = canonical_heads(back_all, shards, 3)
    layer_part = lax.psum_scatter(ready.reshape(-1, width), ("z", "x", "c"), scatter_dimension=0, tiled=True)

    qkv_a, qkv_b = heads_a[:3], heads_b[:3]
    first = attend_backward(False, 0, *qkv_a, lse_own_a, own, g_own_h, infos[0], None)
    dqkv_own, = attend_backward(False, 1, *qkv_b, lse_own_b, own, g_own_h, infos[1], first)
    back_own = to_tokens(dqkv_own)
    dqkv_own, info_a, info_b = tie((dqkv_own, *infos))
    first = attend_backward(True, 0, *qkv_a, lse_sh_a, sh, g_sh_h, info_a, None)
    dq_sh, kept, given = attend_backward(True, 1, *qkv_b, lse_sh_b, sh, g_sh_h, info_b, first)
    taken = lax.ppermute(given, "c", SWAP)
    shared_out = jnp.concatenate([(kept.astype(f32) + taken.astype(f32)).astype(bf16), dq_sh], axis=2)
    shared_out, back_own, dqkv_own = tie((shared_out, back_own, dqkv_own))
    back_shared = to_tokens(shared_out.reshape(2, 4, 3, 32, -1))
    d_heads, d_bias = head_grads(scale, (near_a, far_a, near_b, far_b), dqkv_own, dq_sh, kept, given, infos[0])

    head_ready = jnp.concatenate([
        d_heads.reshape(zs, 2, per, 384),
        jnp.broadcast_to(d_bias[:1].astype(bf16)[None, None], (zs, 2, 16, 384))], axis=2)
    head_ready, back_shared = tie((head_ready, back_shared))
    d_rows = token_grad(back_own, back_shared, back_weights, resid)
    if zs == 4:
        group = lax.axis_index("z")
        parts = [lax.dynamic_index_in_dim(head_ready, (group + k) % zs, axis=0, keepdims=False) for k in range(zs)]
        parts = parts[:1] + [
            lax.ppermute(parts[k], "z", [(i, (i + k) % zs) for i in range(zs)]) for k in range(1, zs)]
        head_sum = settle(parts, d_rows)
    else:
        head_sum = lax.psum_scatter(
            head_ready.reshape(-1, 384), "z", scatter_dimension=0, tiled=True).reshape(2, per + 16, 384)
    layer_part, _ = tie((layer_part, d_rows))
    layer_sum = (layer_part.astype(f32) + lax.ppermute(layer_part, "y", SWAP).astype(f32)).astype(bf16)
    returned = lax.all_to_all(
        d_rows.reshape(shards, stretch, width), SHARD, split_axis=0, concat_axis=0, tiled=True)

    def apart(array, bits):
        return lax.ppermute(array, PAIR, [(i, i ^ bits) for i in range(8)]) if bits else array

    halves = [lax.dynamic_index_in_dim(head_sum, x ^ k, axis=0, keepdims=False) for k in range(2)]
    head_eight = jnp.stack([apart(halves[bits >> 2], bits) for bits in range(8)])
    d_wq, d_wk, d_wv, d_bias_rows = head_unpack(head_eight, per, width, infos[0])
    place = lax.axis_index("z") * 2 + x
    own_slice = lambda row, n: lax.dynamic_slice_in_dim(row, place * n, n)
    d_bq, d_bv = own_slice(d_bias_rows[0], per), own_slice(d_bias_rows[1], per)

    layer_grads = flipped(jnp.stack([layer_sum, lax.ppermute(layer_sum, "c", SWAP)]), 0, c)
    layer_grads = layer_grads.reshape(9 * per + 32, width).astype(f32)
    d_wouter = layer_grads[:4 * per]
    d_winner = jnp.concatenate([layer_grads[(4 + n) * per:(5 + n) * per] for n in range(4)], axis=1)
    d_woutput = layer_grads[8 * per:9 * per]
    d_binner = own_slice(layer_grads[9 * per:9 * per + 4].reshape(-1), 4 * per)
    d_bo, d_g1, d_s1, d_bout, d_g2, d_s2 = (own_slice(layer_grads[9 * per + 4 + n], per) for n in range(6))
    small = (d_bq, d_bv, d_binner, d_bo, d_g1, d_s1, d_bout, d_g2, d_s2)
    returned = tie((returned, d_wouter, d_winner, d_woutput, d_wq, d_wk, d_wv) + small)[0]
    steps = jnp.arange(seq_count, dtype=jnp.int32)
    slot_of = jnp.sum(jnp.where(deal_order[:, None] == steps[None, :], steps[:, None], 0), axis=0)
    d_tokens = returned.at[slot_of].get(mode="promise_in_bounds")[:, None]
    return (act.reshape(1, shards, stretch, width), d_tokens, d_wq, d_wk, d_wv, d_woutput, d_bq, d_bv, d_bo,
            d_g1, d_s1, d_winner, d_binner, d_wouter, d_bout, d_g2, d_s2)


def solution(mesh):
    shards, splits = mesh.devices.shape
    fine = Mesh(mesh.devices.reshape(shards // 2, 2, splits // 2, 2), ALL)
    S, Q = SHARD, ("y", "c")
    row, mat = P(S), P(S, None)
    return jax.shard_map(
        body, mesh=fine,
        in_specs=(P(None, S, Q, None), P(), P(), mat, mat, mat, mat, row, row, row, row, row, mat, row, mat, row, row, row,
                  P(S, None, Q, None)),
        out_specs=(P(S, None, Q, None), P(None, S, Q, None), mat, mat, mat, mat, row, row, row, row, row, mat, row, mat,
                   row, row, row),
        check_vma=False)
```

```python
import functools, math
import jax
import jax.numpy as jnp
from jax import lax
from jax.experimental import pallas as pl
from jax.experimental.pallas import tpu as pltpu
from jax.sharding import Mesh, PartitionSpec as P

f32, bf16 = jnp.float32, jnp.bfloat16
LOG2E = 1.4426950408889634
LN2 = 0.6931471805599453
CH = 256
BQ = 2048
RB = 256
FB = 512
PARTS = 2
HD = 64
FAR = -1.0e30

def dg(a, b, ca, cb):
    return lax.dot_general(a, b, (((ca,), (cb,)), ((), ())), preferred_element_type=f32)


def three_parts(row):
    hi = row.astype(bf16).astype(f32)
    rest = row - hi
    mid = rest.astype(bf16).astype(f32)
    return hi, mid, rest - mid


def with_shift(top, shift):
    hi, mid, low = three_parts(shift)
    row = lax.broadcasted_iota(jnp.int32, (HD, top.shape[1]), 0)
    tail = jnp.where(row == 0, -hi, jnp.where(row == 1, -mid, jnp.where(row == 2, -low, jnp.where(row == 3, 1.0, 0.0))))
    return jnp.concatenate([top.astype(f32), tail], axis=0)


def load_rows(rows, ref, spans, x):
    stretch = ref.shape[3]
    for z in range(spans):
        for a in range(2):
            at = (2 * z + a) * stretch
            rows[at:at + stretch] = ref[0, a ^ x, z]


def qkv_kernel(stretch, spans, info, near_ref, far_ref, w_ref, b_ref, q_out, k_out, v_out, size_out, rows):
    away, half = pl.program_id(0), pl.program_id(2)
    owner = ((pl.program_id(1) ^ info[2]) << 1) | (away ^ info[3])

    @pl.when(away == 0)
    def _():
        load_rows(rows, near_ref, spans, info[1])

    @pl.when(away == 1)
    def _():
        load_rows(rows, far_ref, spans, info[1])
    weight = w_ref[...].reshape(rows.shape[1], 384)
    made = dg(rows[...], weight, 1, 0) + b_ref[...]
    count = rows.shape[0]
    q_t = (made[:, :128] * (LOG2E / 8.0)).T
    q_out[0, 0] = q_t[:HD].astype(bf16)
    q_out[1, 0] = q_t[HD:].astype(bf16)
    lane = lax.broadcasted_iota(jnp.int32, (count, 128), 1)
    row = lax.broadcasted_iota(jnp.int32, (count, 128), 0) + half * count
    shift = int(math.log2(stretch))
    position = lax.shift_left(lax.shift_right_logical(row, shift), shift + 2) + owner * stretch + (row & (stretch - 1))
    hidden = jnp.where(position < info[0], 0.0, FAR)
    tail = jnp.where(lane == HD + 3, hidden, jnp.where(lane < HD + 3, 1.0, 0.0))
    keys = made[:, 128:256]
    picks = lax.broadcasted_iota(jnp.int32, (128, 128), 0) // HD == lax.broadcasted_iota(jnp.int32, (128, 128), 1)
    sizes = dg((keys * keys).astype(bf16), jnp.where(picks, 1.0, 0.0).astype(bf16), 1, 0)
    size_out[0, 0] = jnp.max(sizes, axis=0, keepdims=True)
    for head in range(2):
        turned = keys if head == 0 else pltpu.roll(keys, HD, 1)
        full = jnp.where(lane < HD, turned, tail).astype(bf16)
        for j in range(count // 128):
            k_out[head, j, 0] = full[j * 128:(j + 1) * 128]
    v_t = made[:, 256:384].T
    ones = jnp.where(lax.broadcasted_iota(jnp.int32, (HD, count), 0) < 3, 1.0, 0.0)
    for head in range(2):
        full = jnp.concatenate([v_t[head * HD:(head + 1) * HD], ones], axis=0).astype(bf16)
        for j in range(count // 128):
            v_out[head, j, 0] = full[:, j * 128:(j + 1) * 128]


def owner_of(away, across, info):
    return ((across ^ info[2]) << 1) | (away ^ info[3])


def project(near, far, weight, bias, info):
    _, _, zs, stretch, width = near.shape
    local = 2 * zs * stretch
    spans = 1024 // (2 * stretch)
    halves = local // 1024
    spans_of_rows = local // 128
    per = spans_of_rows // halves
    block = (1, 2, spans, stretch, width)
    q, k, v, sizes = pl.pallas_call(
        functools.partial(qkv_kernel, stretch, spans),
        grid_spec=pltpu.PrefetchScalarGridSpec(
            num_scalar_prefetch=1, grid=(2, 2, halves),
            in_specs=[
                pl.BlockSpec(block, lambda a, o, h, n: (jnp.where(a == 0, o, 1), 0, jnp.where(a == 0, h, halves - 1), 0, 0)),
                pl.BlockSpec(block, lambda a, o, h, n: (jnp.where(a == 0, 0, o), 0, jnp.where(a == 0, 0, h), 0, 0)),
                pl.BlockSpec((8, width // 8, 384), lambda a, o, h, n: (0, 0, n[1])),
                pl.BlockSpec((1, 384), lambda a, o, h, n: (0, 0)),
            ],
            out_specs=[
                pl.BlockSpec((2, 1, HD, 1024), lambda a, o, h, n: (0, owner_of(a, o, n), 0, h)),
                pl.BlockSpec((2, per, 1, 128, 128), lambda a, o, h, n: (0, h, o ^ n[2], a ^ n[3], 0)),
                pl.BlockSpec((2, per, 1, 128, 128), lambda a, o, h, n: (0, h, o ^ n[2], 0, a ^ n[3])),
                pl.BlockSpec((1, 1, 1, 128), lambda a, o, h, n: (owner_of(a, o, n), h, 0, 0)),
            ],
            scratch_shapes=[pltpu.VMEM((1024, width), bf16)]),
        out_shape=[
            jax.ShapeDtypeStruct((2, 4, HD, local), bf16),
            jax.ShapeDtypeStruct((2, spans_of_rows, 2, CH, 128), bf16),
            jax.ShapeDtypeStruct((2, spans_of_rows, 2, 128, CH), bf16),
            jax.ShapeDtypeStruct((4, halves, 1, 128), f32),
        ],
        compiler_params=pltpu.CompilerParams(vmem_limit_bytes=60 << 20),
        name="qkv",
        cost_estimate=cost(4 * near.size * 384, near.size * 8),
    )(info, near, far, weight, bias)
    return q, k.reshape(2, -1, CH, 128), v.reshape(2, -1, 128, CH), sizes


def step_on(q, j, count):
    last = j + 1 == count
    return jnp.where(last, q + 1, q), jnp.where(last, 0, j + 1)


def assemble(ref, part, shared, core):
    if not shared:
        return jnp.concatenate([ref[0, 2 * part], ref[0, 2 * part + 1]], axis=1)
    at = pl.multiple_of(core * 512, 512)
    return jnp.concatenate([ref[0, n, :, pl.ds(at, 512)] for n in range(4)], axis=1)


def fwd_kernel(shared, info, q_ref, k_ref, v_ref, size_ref, held_ref, out_ref, lse_ref, acc, probs, qa, shifts):
    count = info[4]
    parts = 1 if shared else 2
    lane = lax.broadcasted_iota(jnp.int32, (1, 128), 1)
    sizes = functools.reduce(jnp.maximum, [size_ref[o, h] for o in range(size_ref.shape[0]) for h in range(size_ref.shape[1])])
    widest = jnp.sqrt(jnp.max(jnp.where(lane == int(shared), sizes, 0.0), axis=1, keepdims=True))

    for part in range(parts):
        q_t = assemble(q_ref, part, shared, info[3])
        wide = q_t.astype(f32)
        shift = jnp.sqrt(jnp.sum(wide * wide, axis=0, keepdims=True)) * widest
        shifts[part] = shift
        qa[part] = with_shift(q_t, shift).astype(bf16)

    def raised(part, j):
        return jnp.exp2(dg(k_ref[0, j], qa[part], 1, 0)).astype(bf16)

    probs[0] = raised(0, 0)

    def body(t, carry, ahead_too=True):
        part, j = carry
        now = t & 1
        part_next, j_next = step_on(part, j, count)
        before = jnp.where(j == 0, 0.0, acc[...])
        acc[...] = before + dg(v_ref[0, j], probs[now], 1, 0)
        if ahead_too:
            probs[1 - now] = raised(part_next, j_next)

        @pl.when(j + 1 == count)
        def _():
            total = acc[HD:HD + 1]
            fine = (jnp.min(total) > 2.0 ** -90) & (jnp.max(total) < 2.0 ** 60)

            @pl.when(jnp.logical_not(fine))
            def _():
                plain = qa[part].astype(f32)
                row = lax.broadcasted_iota(jnp.int32, plain.shape, 0)
                qa[part] = jnp.where((row >= HD) & (row < HD + 3), 0.0, plain).astype(bf16)

                def peak(i, top):
                    return jnp.maximum(top, jnp.max(dg(k_ref[0, i], qa[part], 1, 0), axis=0, keepdims=True))
                shift = lax.fori_loop(0, count, peak, jnp.full((1, BQ), FAR, f32))
                shifts[part] = shift
                qa[part] = with_shift(plain[:HD], shift).astype(bf16)
                acc[...] = jnp.zeros_like(acc)

                def again(i, carry):
                    acc[...] += dg(v_ref[0, i], raised(part, i), 1, 0)
                    return carry
                lax.fori_loop(0, count, again, 0)

            total = acc[HD:HD + 1]
            mixed = (acc[:HD] * (1.0 / total)).astype(bf16)
            lse_ref[part] = shifts[part] + jnp.log2(total)
            if shared:
                for n in range(4):
                    out_ref[0, n] = mixed[:, n * 512:(n + 1) * 512]
            else:
                for n in range(2):
                    out_ref[0, 2 * part + n] = mixed[:, n * 1024:(n + 1) * 1024]
        return part_next, j_next

    turns = parts * count
    body(turns - 1, lax.fori_loop(0, turns - 1, body, (0, 0)), False)


def head_spec(shared, *dims):
    zeros = (0,) * len(dims)
    return pl.BlockSpec((1,) + dims, lambda i, n: (int(shared),) + zeros)


def whole_spec(*dims):
    return pl.BlockSpec(dims, lambda i, n: (0,) * len(dims))


def cost(flops, moved, exps=0):
    return pl.CostEstimate(flops=int(flops), bytes_accessed=int(moved), transcendentals=int(exps))


def attend_forward(shared, seq, q, k, v, sizes, info, held):
    _, owners, _, local = q.shape
    chunks = k.shape[1]
    wide = local // 2 if shared else local
    parts = owners * wide // BQ
    pairs = parts * BQ * chunks * CH * 0.6
    shape = jax.ShapeDtypeStruct((2, owners, HD, wide), bf16)
    first = held is None
    if first:
        kernel = lambda info, q, k, v, size, *rest: fwd_kernel(shared, info, q, k, v, size, None, *rest)
    else:
        kernel = functools.partial(fwd_kernel, shared)
    return pl.pallas_call(
        kernel,
        grid_spec=pltpu.PrefetchScalarGridSpec(
            num_scalar_prefetch=1, grid=(1,),
            in_specs=[
                head_spec(shared, owners, HD, local), head_spec(shared, chunks, CH, 128), head_spec(shared, chunks, 128, CH),
                whole_spec(*sizes.shape),
            ] + ([] if first else [pl.BlockSpec(memory_space=pl.ANY)]),
            out_specs=[pl.BlockSpec((1, owners, HD, wide), lambda i, n: (seq, 0, 0, 0)), whole_spec(parts, 1, BQ)],
            scratch_shapes=[
                pltpu.VMEM((128, BQ), f32), pltpu.VMEM((2, CH, BQ), bf16), pltpu.VMEM((parts, 128, BQ), bf16),
                pltpu.VMEM((parts, 1, BQ), f32),
            ]),
        out_shape=[shape, jax.ShapeDtypeStruct((parts, 1, BQ), f32)],
        input_output_aliases={} if first else {5: 0},
        compiler_params=pltpu.CompilerParams(vmem_limit_bytes=60 << 20),
        cost_estimate=cost(pairs * 1024, chunks * CH * 512, pairs),
        name="attend_forward_shared" if shared else "attend_forward_own",
    )(*((info, q, k, v, sizes) + (() if first else (held,))))


def bwd_kernel(shared, first, info, q_ref, k_ref, v_ref, lse_ref, out_ref, gout_ref, *rest):
    rest = rest if first else rest[3 if shared else 1:]
    if shared:
        dq_ref, kept_ref, given_ref, dk_acc, dv_acc, dq_acc, qa, qat, ga, gat, pb, db = rest
    else:
        dqkv_ref, dk_acc, dv_acc, dq_acc, qa, qat, ga, gat, pb, db = rest
    count = info[4]
    chunks = k_ref.shape[1]
    parts = 1 if shared else 2
    dk_acc[...] = jnp.zeros_like(dk_acc)
    dv_acc[...] = jnp.zeros_like(dv_acc)

    def piece(ref, part):
        return jnp.concatenate([ref[0, n] for n in (range(4) if shared else (2 * part, 2 * part + 1))], axis=1)

    for part in range(parts):
        q_full = with_shift(assemble(q_ref, part, shared, info[3]), lse_ref[part])
        qat[part] = q_full.astype(bf16)
        qa[part] = q_full.T.astype(bf16)
        g_t = piece(gout_ref, part)
        meet = jnp.sum(g_t.astype(f32) * piece(out_ref, part).astype(f32), axis=0, keepdims=True)
        g_full = with_shift(g_t, meet)
        gat[part] = g_full.astype(bf16)
        ga[part] = g_full.T.astype(bf16)

    def ahead(part, j, slot):
        raised = jnp.exp2(dg(qa[part], k_ref[0, j], 1, 1))
        pb[slot] = raised.astype(bf16)
        db[slot] = (raised * dg(ga[part], v_ref[0, j], 1, 0)).astype(bf16)

    ahead(0, 0, 0)

    def body(t, carry, ahead_too=True):
        part, j = carry
        now = t & 1
        part_next, j_next = step_on(part, j, count)
        dv_acc[j] += dg(gat[part], pb[now], 1, 0)[:HD]
        dk_acc[j] += dg(qat[part], db[now], 1, 0)[:HD]
        before = jnp.where(j == 0, 0.0, dq_acc[...])
        dq_acc[...] = before + dg(db[now], k_ref[0, j], 1, 0)
        if ahead_too:
            ahead(part_next, j_next, 1 - now)

        @pl.when(j + 1 == count)
        def _():
            dq_t = (dq_acc[...] * 0.125).T[:HD].astype(bf16)
            if shared:
                for n in range(4):
                    dq_ref[0, n, :, :512] = dq_t[:32, n * 512:(n + 1) * 512]
                    dq_ref[0, n, :, 512:] = dq_t[32:, n * 512:(n + 1) * 512]
            else:
                for n in range(2):
                    dqkv_ref[0, 2 * part + n, 0] = dq_t[:, n * 1024:(n + 1) * 1024]
        return part_next, j_next

    turns = parts * count
    body(turns - 1, lax.fori_loop(0, turns - 1, body, (0, 0)), False)
    for block in range(chunks):
        j, across = block // 2, block % 2
        for owner in (2 * across, 2 * across + 1):
            cols = slice((owner - 2 * across) * 128, (owner - 2 * across + 1) * 128)
            dk_wide, dv_wide = dk_acc[block, :, cols] * LN2, dv_acc[block, :, cols]
            dk, dv = dk_wide.astype(bf16), dv_wide.astype(bf16)
            if shared:
                here = info[3] == 0
                kept_ref[0, owner, :, j * 128:(j + 1) * 128] = jnp.where(here, dk_wide, dv_wide).astype(bf16)
                given_ref[0, owner, :, j * 128:(j + 1) * 128] = jnp.where(here, dv_wide, dk_wide).astype(bf16)
            else:
                dqkv_ref[0, owner, 1, :, j * 128:(j + 1) * 128] = dk
                dqkv_ref[0, owner, 2, :, j * 128:(j + 1) * 128] = dv


def attend_backward(shared, seq, q, k, v, lse, out, g_out, info, held):
    _, owners, _, local = q.shape
    chunks = k.shape[1]
    wide = out.shape[3]
    parts = owners * wide // BQ
    pairs = parts * BQ * chunks * CH * 0.6
    shape = jax.ShapeDtypeStruct
    first = held is None
    if shared:
        out_specs = [pl.BlockSpec((1, owners, rows, local), lambda i, n: (seq, 0, 0, 0)) for rows in (32, HD, HD)]
        out_shape = [shape((2, owners, rows, local), bf16) for rows in (32, HD, HD)]
    else:
        out_specs = [pl.BlockSpec((1, owners, 3, HD, local), lambda i, n: (seq, 0, 0, 0, 0))]
        out_shape = [shape((2, owners, 3, HD, local), bf16)]
    kept = () if first else tuple(held)
    of_seq = pl.BlockSpec((1, owners, HD, wide), lambda i, n: (seq, 0, 0, 0))
    return pl.pallas_call(
        functools.partial(bwd_kernel, shared, first),
        grid_spec=pltpu.PrefetchScalarGridSpec(
            num_scalar_prefetch=1, grid=(1,),
            in_specs=[
                head_spec(shared, owners, HD, local), head_spec(shared, chunks, CH, 128), head_spec(shared, chunks, 128, CH),
                whole_spec(parts, 1, BQ), of_seq, of_seq,
            ] + [pl.BlockSpec(memory_space=pl.ANY)] * len(kept),
            out_specs=out_specs,
            scratch_shapes=[
                pltpu.VMEM((chunks, HD, CH), f32), pltpu.VMEM((chunks, HD, CH), f32), pltpu.VMEM((BQ, 128), f32),
                pltpu.VMEM((parts, BQ, 128), bf16), pltpu.VMEM((parts, 128, BQ), bf16),
                pltpu.VMEM((parts, BQ, 128), bf16), pltpu.VMEM((parts, 128, BQ), bf16),
                pltpu.VMEM((2, BQ, CH), bf16), pltpu.VMEM((2, BQ, CH), bf16),
            ]),
        out_shape=out_shape,
        input_output_aliases={7 + n: n for n in range(len(kept))},
        compiler_params=pltpu.CompilerParams(vmem_limit_bytes=60 << 20),
        cost_estimate=cost(pairs * 100, chunks * CH * 2048),
        name="attend_backward_shared" if shared else "attend_backward_own",
    )(info, q, k, v, lse, out, g_out, *kept)


def gelu_pair(u):
    half = 0.5 * (1.0 + lax.erf(u * 0.7071067811865476))
    return u * half, half + u * (0.3989422804014327 * jnp.exp2(u * u * (-0.5 * LOG2E)))


def norm_stats(v):
    mean = jnp.mean(v, axis=-1, keepdims=True)
    centred = v - mean
    inverse = lax.rsqrt(jnp.mean(centred * centred, axis=-1, keepdims=True) + 1e-12)
    return centred * inverse, inverse


def norm_back(grad, xhat, inverse, gain):
    g = grad * gain
    return (g - jnp.mean(g, axis=-1, keepdims=True) - xhat * jnp.mean(g * xhat, axis=-1, keepdims=True)) * inverse


def weight_part(ref, first, rows):
    part = ref[:, first:first + rows, :]
    return part.reshape(part.shape[0] * rows, part.shape[2])


def ffn_kernel(spans, info, x_ref, own_ref, sh_ref, cot_ref, w_ref, bin_ref, vec_ref,
               act_out, resid_out, gown_out, gsh_out, active_out, dinner_out, normed_out, douter_out, dbranch_out,
               vec_sum, bin_sum, slope, row_block):
    step = pl.program_id(0)
    load_rows(row_block, x_ref, spans, info[1])
    count = row_block.shape[0] // PARTS
    vec = vec_ref[...]
    total = lambda a: jnp.sum(a, axis=0, keepdims=True)
    held = [{"at": slice(n * count, (n + 1) * count)} for n in range(PARTS)]

    def branch(h):
        at = h["at"]
        mixed_t = jnp.concatenate(
            [part for p in range(4) for part in (own_ref[p, 0, :, at], sh_ref[p, 0, :, at], own_ref[p, 1, :, at])], axis=0)
        h["sum1"] = row_block[at].astype(f32) + (dg(mixed_t, weight_part(w_ref, 768, 96), 0, 0) + vec[0:1])

    def first_norm(h):
        h["xhat1"], h["inv1"] = norm_stats(h["sum1"])
        normed = h["xhat1"] * vec[1:2] + vec[2:3]
        normed_out[h["at"]] = normed.astype(bf16)
        h["outer"] = normed + vec[3:4]

    def widen(h):
        at = h["at"]
        for n in range(4):
            cols = slice(n * 768, (n + 1) * 768)
            value, bend = gelu_pair(dg(normed_out[at], weight_part(w_ref, 384 + 96 * n, 96), 1, 0) + bin_ref[:, cols])
            active_out[at, cols] = value.astype(bf16)
            slope[at, cols] = bend.astype(bf16)

    def narrow(h):
        h["outer"] = h["outer"] + dg(active_out[h["at"]], weight_part(w_ref, 0, 384), 1, 0)

    def second_norm(h):
        at = h["at"]
        xhat2, inv2 = norm_stats(h["outer"])
        act_out[at] = (xhat2 * vec[4:5] + vec[5:6]).astype(bf16)
        cot = cot_ref[at].astype(f32)
        d2 = norm_back(cot, xhat2, inv2, vec[4:5])
        d_outer = d2.astype(bf16)
        douter_out[at] = d_outer
        h["d_normed"] = d2
        h["sums"] = [total(d_outer.astype(f32)), total(cot * xhat2), total(cot)]

    def back(h):
        at = h["at"]
        h["inner_sums"] = []
        for n in range(4):
            cols = slice(n * 768, (n + 1) * 768)
            d_active = dg(douter_out[at], weight_part(w_ref.at[2 * n:2 * n + 2], 0, 384), 1, 1)
            d_inner = (d_active * slope[at, cols].astype(f32)).astype(bf16)
            dinner_out[at, cols] = d_inner
            h["inner_sums"].append(total(d_inner.astype(f32)))
            h["d_normed"] = h["d_normed"] + dg(d_inner, weight_part(w_ref, 384 + 96 * n, 96), 1, 1)

    def first_back(h):
        at = h["at"]
        d_normed = h["d_normed"]
        d1 = norm_back(d_normed, h["xhat1"], h["inv1"], vec[1:2])
        resid_out[at] = d1
        d_branch = d1.astype(bf16)
        dbranch_out[at] = d_branch
        h["sums"] = [total(d_branch.astype(f32)), total(d_normed * h["xhat1"]), total(d_normed)] + h["sums"]

    def mix_back(h):
        at = h["at"]
        g_t = dg(weight_part(w_ref, 768, 96), dbranch_out[at], 1, 1).astype(bf16)
        for p in range(4):
            gown_out[p, 0, :, at] = g_t[192 * p:192 * p + 64]
            gsh_out[p, 0, :, at] = g_t[192 * p + 64:192 * p + 128]
            gown_out[p, 1, :, at] = g_t[192 * p + 128:192 * p + 192]

    for products, norm in ((branch, first_norm), (widen, None), (narrow, second_norm), (back, first_back), (mix_back, None)):
        for h in held:
            products(h)
            if norm is not None:
                norm(h)
    sums = jnp.concatenate([
        functools.reduce(jnp.add, [h["sums"][n] for h in held]) for n in range(6)] + [jnp.zeros((2, vec.shape[1]), f32)], axis=0)
    inner_sums = [functools.reduce(jnp.add, [h["inner_sums"][n] for h in held]) for n in range(4)]

    @pl.when(step == 0)
    def _():
        vec_sum[...] = sums
        for n in range(4):
            bin_sum[:, n * 768:(n + 1) * 768] = inner_sums[n]

    @pl.when(step > 0)
    def _():
        vec_sum[...] += sums
        for n in range(4):
            bin_sum[:, n * 768:(n + 1) * 768] += inner_sums[n]


def feed_forward(rows_in, own, sh, cotangent, weights, inner_bias, vectors, info):
    _, _, _, stretch, width = rows_in.shape
    local = cotangent.shape[0]
    spans = FB // (2 * stretch)
    steps = local // FB
    half_steps = steps // 2
    wide = inner_bias.shape[1]
    rows = lambda n: pl.BlockSpec((FB, n), lambda r, a: (r, 0))
    fixed = lambda *dims: pl.BlockSpec(dims, lambda r, a: (0,) * len(dims))
    own_spec = pl.BlockSpec((4, 2, HD, FB), lambda r, a: (0, 0, 0, r))
    sh_spec = pl.BlockSpec((4, 1, HD, FB), lambda r, a: (0, r // half_steps, 0, r % half_steps))
    shape = jax.ShapeDtypeStruct
    return pl.pallas_call(
        functools.partial(ffn_kernel, spans),
        grid_spec=pltpu.PrefetchScalarGridSpec(
            num_scalar_prefetch=1, grid=(steps,),
            in_specs=[
                pl.BlockSpec((1, 2, spans, stretch, width), lambda r, a: (0, 0, r, 0, 0)),
                own_spec, sh_spec, rows(width),
                pl.BlockSpec(weights.shape, lambda r, a: (0, 0, 0), pipeline_mode=pl.Buffered(1)),
                fixed(1, wide), fixed(8, width),
            ],
            out_specs=[
                rows(width), rows(width), own_spec, sh_spec, rows(wide), rows(wide), rows(width), rows(width), rows(width),
                fixed(8, width), fixed(1, wide),
            ],
            scratch_shapes=[pltpu.VMEM((FB, wide), bf16), pltpu.VMEM((FB, width), bf16)]),
        out_shape=[
            shape((local, width), bf16), shape((local, width), f32), shape(own.shape, bf16), shape(sh.shape, bf16),
            shape((local, wide), bf16), shape((local, wide), bf16), shape((local, width), bf16),
            shape((local, width), bf16), shape((local, width), bf16), shape((8, width), f32), shape((1, wide), f32),
        ],
        compiler_params=pltpu.CompilerParams(vmem_limit_bytes=60 << 20),
        name="feed_forward",
        cost_estimate=cost(local * width * (width + 2 * wide) * 4, local * wide * 20),
    )(info, rows_in, own, sh, cotangent, weights, inner_bias, vectors)


def outer_grad_kernel(scale, active_ref, douter_ref, out_ref):
    made = (dg(active_ref[...], douter_ref[...], 0, 0) * scale).astype(bf16)
    out_ref[...] = made.reshape(out_ref.shape)


def inner_grad_kernel(scale, packed_ref, normed_ref, dinner_ref, own_ref, sh_ref, dbranch_ref, out_ref):
    step = pl.program_id(0)

    @pl.when(step < 4)
    def _():
        out_ref[...] = (dg(normed_ref[...], dinner_ref[...], 0, 0) * scale).astype(bf16).reshape(out_ref.shape)

    @pl.when(step == 4)
    def _():
        mixed_t = jnp.concatenate([
            part for p in range(4)
            for part in (own_ref[p, 0], jnp.concatenate([sh_ref[p, 0], sh_ref[p, 1]], axis=1), own_ref[p, 1])], axis=0)
        out_ref[...] = (dg(mixed_t, dbranch_ref[...], 1, 0) * scale).astype(bf16).reshape(out_ref.shape)


def weight_grads(scale, active, d_outer, normed, d_inner, own, sh, d_branch):
    local, wide = active.shape
    width = normed.shape[1]
    packed = pl.pallas_call(
        functools.partial(outer_grad_kernel, scale), grid=(4,),
        in_specs=[pl.BlockSpec((local, width), lambda m: (0, m)), pl.BlockSpec((local, width), lambda m: (0, 0))],
        out_specs=pl.BlockSpec((2, 384, width), lambda m: (m, 0, 0)),
        out_shape=jax.ShapeDtypeStruct((8, 896, width), bf16),
        compiler_params=pltpu.CompilerParams(vmem_limit_bytes=40 << 20), name="outer_grad",
        cost_estimate=cost(2 * local * wide * width, 2 * wide * (local + width)),
    )(active, d_outer)
    fixed = lambda a: pl.BlockSpec(a.shape, lambda n: (0,) * a.ndim)
    return pl.pallas_call(
        functools.partial(inner_grad_kernel, scale), grid=(5,),
        in_specs=[
            pl.BlockSpec(memory_space=pl.ANY), fixed(normed),
            pl.BlockSpec((local, width), lambda n: (0, jnp.minimum(n, 3))), fixed(own), fixed(sh), fixed(d_branch)],
        out_specs=pl.BlockSpec((8, 96, width), lambda n: (0, 4 + n, 0)),
        out_shape=jax.ShapeDtypeStruct((8, 896, width), bf16), input_output_aliases={0: 0},
        compiler_params=pltpu.CompilerParams(vmem_limit_bytes=40 << 20), name="inner_grad",
        cost_estimate=cost(2 * local * (wide + width) * width, 2 * (wide + width) * (local + width)),
    )(packed, normed, d_inner, own, sh, d_branch)


def head_grad_kernel(scale, spans, info, *refs):
    x_refs, (own_ref, dq_ref, kept_ref, given_ref, out_ref, bias_out, acc, bias_acc, rows) = refs[:4], refs[4:]
    seq, away, half = pl.program_id(0), pl.program_id(1), pl.program_id(3)
    last = (seq == 1) & (away == 1) & (pl.program_id(2) == 1) & (half == pl.num_programs(3) - 1)
    for n in range(4):
        @pl.when(seq * 2 + away == n)
        def _(n=n):
            load_rows(rows, x_refs[n], spans, info[1])
    dq_t = jnp.where(half == info[3], jnp.concatenate([dq_ref[0, 0, :, :512], dq_ref[0, 0, :, 512:]], axis=0).astype(f32), 0.0)
    kept, given = kept_ref[0, 0].astype(f32), given_ref[0, 0].astype(f32)
    here = info[3] == 0
    d_t = jnp.concatenate([
        own_ref[0, 0, 0], dq_t.astype(bf16), own_ref[0, 0, 1], jnp.where(here, kept, given).astype(bf16),
        own_ref[0, 0, 2], jnp.where(here, given, kept).astype(bf16)], axis=0)

    @pl.when((seq == 0) & (away == 0) & (pl.program_id(2) == 0) & (half == 0))
    def _():
        acc[...] = jnp.zeros_like(acc)
        bias_acc[...] = jnp.zeros_like(bias_acc)
    acc[...] += dg(d_t, rows[...], 1, 0)
    bias_acc[...] += dg(jnp.ones((8, d_t.shape[1]), bf16), d_t, 1, 1)

    @pl.when(last)
    def _():
        out_ref[...] = (acc[...] * scale).T.astype(bf16)
        bias_out[...] = bias_acc[...] * scale


def head_grads(scale, sources, dqkv_own, dq_sh, kept, given, info):
    _, _, zs, stretch, width = sources[0].shape
    local = 2 * zs * stretch
    spans = 512 // (2 * stretch)
    halves = local // 512

    def source_spec(n):
        def index(s, a, o, h, i):
            now = 2 * s + a
            across = jnp.where(now == n, o, jnp.where(now < n, 0, 1))
            return (across, 0, jnp.where(now == n, h, jnp.where(now < n, 0, halves - 1)), 0, 0)
        return pl.BlockSpec((1, 2, spans, stretch, width), index)
    return pl.pallas_call(
        functools.partial(head_grad_kernel, scale, spans),
        grid_spec=pltpu.PrefetchScalarGridSpec(
            num_scalar_prefetch=1, grid=(2, 2, 2, halves),
            in_specs=[source_spec(n) for n in range(4)] + [
                pl.BlockSpec((1, 1, 3, HD, 512), lambda s, a, o, h, i: (s, owner_of(a, o, i), 0, 0, h)),
                pl.BlockSpec((1, 1, 32, local), lambda s, a, o, h, i: (s, owner_of(a, o, i), 0, 0)),
            ] + [pl.BlockSpec((1, 1, HD, 512), lambda s, a, o, h, i: (s, owner_of(a, o, i), 0, h))] * 2,
            out_specs=[pl.BlockSpec((width, 384), lambda s, a, o, h, i: (0, 0)), pl.BlockSpec((8, 384), lambda s, a, o, h, i: (0, 0))],
            scratch_shapes=[pltpu.VMEM((384, width), f32), pltpu.VMEM((8, 384), f32), pltpu.VMEM((512, width), bf16)]),
        out_shape=[jax.ShapeDtypeStruct((width, 384), bf16), jax.ShapeDtypeStruct((8, 384), f32)],
        compiler_params=pltpu.CompilerParams(vmem_limit_bytes=40 << 20), name="head_grads",
        cost_estimate=cost(8 * local * 768 * width, 8 * local * width * 2),
    )(info, *sources, dqkv_own, dq_sh, kept, given)


def token_grad_kernel(own_ref, low_ref, high_ref, dkv_ref, w_ref, resid_ref, out_ref):
    total = resid_ref[...]
    for kind in range(3):
        made = []
        for p in range(4):
            if kind == 0:
                middle = jnp.concatenate([low_ref[p, 0], high_ref[p, 0]], axis=0)
            else:
                middle = jnp.concatenate([dkv_ref[p, kind - 1, n] for n in range(2)], axis=0)
            made += [own_ref[p, 0, kind], middle, own_ref[p, 1, kind]]
        total = total + dg(jnp.concatenate(made, axis=0), weight_part(w_ref, 96 * kind, 96), 0, 1)
    out_ref[...] = total.astype(bf16)


def token_grad(own, shared, weights, resid):
    local, width = resid.shape
    steps = local // RB
    half_steps = steps // 2
    rows = pl.BlockSpec((RB, width), lambda r: (r, 0))
    return pl.pallas_call(
        token_grad_kernel, grid=(steps,),
        in_specs=[
            pl.BlockSpec((4, 2, 3, HD, RB), lambda r: (0, 0, 0, 0, r)),
            pl.BlockSpec((4, 1, None, 32, RB), lambda r: (0, r // half_steps, 2, 0, r % half_steps)),
            pl.BlockSpec((4, 1, None, 32, RB), lambda r: (0, r // half_steps, 2, 0, half_steps + r % half_steps)),
            pl.BlockSpec((4, 2, 2, 32, RB), lambda r: (0, 0, 0, 0, r)),
            pl.BlockSpec(weights.shape, lambda r: (0, 0, 0)), rows],
        out_specs=rows, out_shape=jax.ShapeDtypeStruct((local, width), bf16),
        compiler_params=pltpu.CompilerParams(vmem_limit_bytes=60 << 20), name="token_grad",
        cost_estimate=cost(local * width * width * 6, local * width * 12),
    )(own, shared, shared, shared, weights, resid)


def head_unpack_kernel(per, info, src_ref, q_out, k_out, v_out, bias_out):
    low = lax.broadcasted_iota(jnp.int32, (src_ref.shape[1], 128), 1) < HD

    def rows_of(p, core, cols):
        at = (((p >> 1) ^ info[1]) << 2) | (((p & 1) ^ info[2]) << 1) | (core ^ info[3])
        return src_ref[at, :, cols].astype(f32)
    for kind, out in enumerate((q_out, k_out, v_out)):
        cols = slice(128 * kind, 128 * kind + 128)
        tiles = []
        for pair in range(2):
            first, second = [], []
            for p in (2 * pair, 2 * pair + 1):
                near, far = rows_of(p, 0, cols), rows_of(p, 1, cols)
                first.append(near + jnp.where(low, 0.0, far))
                second.append(far)
            turned = pltpu.roll(first[1], HD, 1)
            tiles += [first[0], jnp.where(low, second[0], turned), jnp.where(low, turned, pltpu.roll(second[1], HD, 1))]
        made = jnp.concatenate(tiles, axis=1)
        out[...] = made[:per]
        if kind != 1:
            bias_out[kind // 2:kind // 2 + 1] = made[per:per + 1]


def head_unpack(source, per, width, info):
    shape = jax.ShapeDtypeStruct
    full = lambda n: pl.BlockSpec((n, width), lambda i, f: (0, 0))
    return pl.pallas_call(
        functools.partial(head_unpack_kernel, per),
        grid_spec=pltpu.PrefetchScalarGridSpec(
            num_scalar_prefetch=1, grid=(1,),
            in_specs=[pl.BlockSpec(source.shape, lambda i, f: (0, 0, 0))],
            out_specs=[full(per)] * 3 + [full(2)]),
        out_shape=[shape((per, width), f32)] * 3 + [shape((2, width), f32)], name="head_unpack",
    )(info, source)


SWAP = [(0, 1), (1, 0)]
def settle_kernel(*refs):
    refs[-1][...] = sum(ref[...].astype(f32) for ref in refs[:-2]).astype(bf16)


def settle(parts, after):
    whole = pl.BlockSpec(memory_space=pltpu.VMEM)
    return pl.pallas_call(
        settle_kernel, in_specs=[whole] * len(parts) + [pl.BlockSpec(memory_space=pl.ANY)], out_specs=whole,
        out_shape=jax.ShapeDtypeStruct(parts[0].shape, bf16), name="settle",
        cost_estimate=cost(1e9, 1e6),
    )(*parts, after)


PAIR = ("x", "y", "c")
ALL = ("z", "x", "y", "c")
SHARD = ("z", "x")


def canonical(packed, shards):
    if shards == 8:
        return packed
    width = packed.shape[2]
    per, keep = 96 * 8 // shards, shards // 8
    outer = packed[:, :4 * per].reshape(8, 384, width)
    inner = packed[:, 4 * per:8 * per].reshape(8, keep, 4, per, width).transpose(0, 2, 1, 3, 4).reshape(8, 384, width)
    output = packed[:, 8 * per:9 * per].reshape(8, 96, width)
    return jnp.concatenate([outer, inner, output, jnp.zeros((8, 32, width), packed.dtype)], axis=1)


def from_canonical(packed, last, shards):
    width = packed.shape[2]
    if shards == 8:
        return packed.at[:, 864:].set(jnp.broadcast_to(last[None], (8, 32, width)))
    per, keep = 96 * 8 // shards, shards // 8
    outer = packed[:, :384].reshape(shards, 4 * per, width)
    inner = packed[:, 384:768].reshape(8, 4, keep, per, width).transpose(0, 2, 1, 3, 4).reshape(shards, 4 * per, width)
    output = packed[:, 768:864].reshape(shards, per, width)
    return jnp.concatenate([outer, inner, output, jnp.broadcast_to(last[None], (shards, 32, width))], axis=1)


def canonical_heads(packed, shards, parts):
    if shards == 8:
        return packed
    width = packed.shape[2]
    per = 96 * 8 // shards
    made = [packed[:, k * per:(k + 1) * per].reshape(8, 96, width) for k in range(parts)]
    return jnp.concatenate(made + [jnp.zeros((8, 32, width), packed.dtype)], axis=1)


def quarter(pieces):
    part = sum(piece.shape[0] for piece in pieces) // 4

    def taken(k):
        found, at = [], 0
        for piece in pieces:
            low, high = max(k * part - at, 0), min((k + 1) * part - at, piece.shape[0])
            if low < high:
                found.append(piece[low:high])
            at += piece.shape[0]
        return jnp.concatenate(found, axis=0)
    place = lax.axis_index("y") * 2 + lax.axis_index("c")
    return lax.switch(place, [functools.partial(taken, k) for k in range(4)])


def flipped(array, axis, here):
    return jnp.where(here == 0, array, jnp.flip(array, axis))


def body(tokens, lengths, deal_order, w_query, w_key, w_value, w_output, b_query, b_value, b_output,
         ln1_gain, ln1_shift, w_inner, b_inner, w_outer, b_outer, ln2_gain, ln2_shift, cotangent):
    tie = lax.optimization_barrier
    zs = lax.axis_size("z")
    shards = 2 * zs
    scale = 1.0 / (shards * 4)
    seq_count, _, stretch, width = tokens.shape
    per = w_query.shape[0]
    half = zs // 2
    x, y, c = lax.axis_index("x"), lax.axis_index("y"), lax.axis_index("c")

    def deal(ordered):
        return lax.all_to_all(ordered, "z", split_axis=0, concat_axis=0, tiled=True)

    def corner(across, along):
        return [lax.ppermute(across[:half], "y", SWAP), lax.ppermute(along[half:], "x", SWAP)]

    def this_core(own, across, along, corner):
        return jnp.concatenate([own, across, along] + corner, axis=0).reshape(2, 2, zs, stretch, width)

    ordered_a = tokens[:, 0].at[deal_order[0::2]].get(mode="promise_in_bounds")
    first_own = deal(ordered_a)
    _, tokens, w_query, w_key, w_value, b_query, b_value, deal_order = tie(
        (ordered_a, tokens, w_query, w_key, w_value, b_query, b_value, deal_order))
    ordered_b = tokens[:, 0].at[deal_order[1::2]].get(mode="promise_in_bounds")

    def head_columns(matrix):
        heads = matrix.reshape(per, 2, 2, 3, HD)
        mine = lax.dynamic_index_in_dim(heads, y, axis=2, keepdims=False)
        own = lax.dynamic_index_in_dim(mine, 2 * c, axis=2, keepdims=False)
        return [own, mine[:, :, 1]]
    pad = lambda v: jnp.pad(v, (0, width - v.shape[0]))[None]
    columns = jnp.concatenate(
        [col for matrix in (w_query, w_key, w_value) for col in head_columns(matrix)], axis=2).reshape(per, width)
    head_pack = jnp.concatenate([columns, pad(b_query), pad(b_value), jnp.zeros((14, width), bf16)], axis=0)
    (first_own, ordered_b, head_pack, w_outer, w_inner, w_output, b_inner, lengths, w_query, w_key, w_value) = tie(
        (first_own, ordered_b, head_pack, w_outer, w_inner, w_output, b_inner, lengths, w_query, w_key, w_value))
    vectors = (b_output, ln1_gain, ln1_shift, b_outer, ln2_gain, ln2_shift)
    vector_pack = jnp.concatenate([pad(b_inner)] + [pad(v) for v in vectors] + [jnp.zeros((25, width), bf16)], axis=0)
    layer_quarter = quarter(
        [w_outer] + [w_inner[:, n * width:(n + 1) * width] for n in range(4)] + [w_output, vector_pack])
    back_quarter = quarter([w_query, w_key, w_value, jnp.zeros((32, width), bf16)])
    slots = lax.dynamic_slice_in_dim(deal_order, lax.axis_index("z") * 2, 2)
    matches = slots[:, None] == jnp.arange(seq_count, dtype=jnp.int32)[None, :]
    lens = jnp.sum(jnp.where(matches, lengths[None, :], 0), axis=1).astype(jnp.int32)
    last = (lens + 511) // 512 - 1
    counts = 2 * last + 1 + (lens > 512 * last + 2 * stretch).astype(jnp.int32)
    infos = [jnp.stack([lens[n], x, y, c, counts[n]]).astype(jnp.int32) for n in range(2)]
    head_all = lax.all_gather(head_pack, SHARD, axis=0, tiled=False)
    head_weight = canonical_heads(head_all, shards, 1)

    def head_bias(row):
        heads = head_all[:, per + row, :per].reshape(2, 2, 3, HD)
        mine = lax.dynamic_slice(heads, (x, y, 0, 0), (1, 1, 3, HD))[0, 0]
        return [lax.dynamic_index_in_dim(mine, 2 * c, axis=0, keepdims=False), mine[1]]
    bias_row = jnp.concatenate(head_bias(0) + [jnp.zeros((2 * HD,), bf16)] + head_bias(1)).astype(f32)[None]

    across_a, along_a = lax.ppermute(first_own, "x", SWAP), lax.ppermute(first_own, "y", SWAP)
    second_own = deal(ordered_b)
    across_a, along_a, second_own, layer_quarter, back_quarter, *infos = tie(
        (across_a, along_a, second_own, layer_quarter, back_quarter, *infos))
    near_a = this_core(first_own, across_a, along_a, corner(across_a, along_a))
    across_b, along_b = lax.ppermute(second_own, "x", SWAP), lax.ppermute(second_own, "y", SWAP)
    near_a, across_b, along_b = tie((near_a, across_b, along_b))
    far_a = lax.ppermute(near_a, "c", SWAP)
    corner_b = corner(across_b, along_b)

    layer_all = lax.all_gather(layer_quarter, ALL, axis=0, tiled=True).reshape(shards, 9 * per + 32, width)
    layer_weights = canonical(layer_all, shards)
    inner_bias = layer_all[:, 9 * per, :4 * per].reshape(1, 4 * width).astype(f32)
    vector_rows = jnp.concatenate(
        [layer_all[:, 9 * per + 1 + n, :per].reshape(1, width) for n in range(6)] + [jnp.zeros((2, width), bf16)],
        axis=0).astype(f32)
    back_all = lax.all_gather(back_quarter, ALL, axis=0, tiled=True).reshape(shards, 3 * per + 32, width)

    def swap(array):
        flat = array.reshape((8,) + array.shape[2:])
        return lax.all_to_all(flat, PAIR, split_axis=0, concat_axis=0, tiled=True)

    def to_tokens(array):
        return swap(array).reshape((4, 2) + array.shape[2:])

    def to_heads(array):
        return swap(array).reshape((2, 4) + array.shape[2:])

    heads_a = project(near_a, far_a, head_weight, bias_row, infos[0])
    heads_a, *corner_b = tie((heads_a, *corner_b))
    near_b = this_core(second_own, across_b, along_b, corner_b)
    far_b = lax.ppermute(near_b, "c", SWAP)
    own_first, lse_own_a = attend_forward(False, 0, *heads_a, infos[0], None)
    own_first, far_b = tie((own_first, far_b))
    heads_b = project(near_b, far_b, head_weight, bias_row, infos[1])
    own, lse_own_b = attend_forward(False, 1, *heads_b, infos[1], own_first)
    own_t = to_tokens(own)
    own, info_a, info_b = tie((own, *infos))
    sh_first, lse_sh_a = attend_forward(True, 0, *heads_a, info_a, None)
    sh, lse_sh_b = attend_forward(True, 1, *heads_b, info_b, sh_first)
    sh_sent, own_t = tie((sh, own_t))
    sh_t = to_tokens(sh_sent)
    mine_rows = jnp.where(x == 0, jnp.stack([first_own, across_a]), jnp.stack([second_own, across_b]))[None]

    (act, resid, g_own, g_sh, active, d_inner, normed, d_outer, d_branch, vec_sums, bin_sums) = feed_forward(
        mine_rows, own_t, sh_t, cotangent.reshape(-1, width), layer_weights, inner_bias, vector_rows, infos[0])
    g_own_h, g_sh_h = to_heads(g_own), to_heads(g_sh)
    packed = weight_grads(scale, active, d_outer, normed, d_inner, own_t, sh_t, d_branch)
    sums = jnp.concatenate([bin_sums.reshape(4, width), vec_sums, jnp.zeros((20, width), f32)], axis=0) * scale
    ready = from_canonical(packed, sums.astype(bf16), shards)
    ready, back_all, g_own_h = tie((ready, back_all, g_own_h))
    back_weights = canonical_heads(back_all, shards, 3)
    layer_part = lax.psum_scatter(ready.reshape(-1, width), ("z", "x", "c"), scatter_dimension=0, tiled=True)

    qkv_a, qkv_b = heads_a[:3], heads_b[:3]
    first = attend_backward(False, 0, *qkv_a, lse_own_a, own, g_own_h, infos[0], None)
    dqkv_own, = attend_backward(False, 1, *qkv_b, lse_own_b, own, g_own_h, infos[1], first)
    back_own = to_tokens(dqkv_own)
    dqkv_own, info_a, info_b = tie((dqkv_own, *infos))
    first = attend_backward(True, 0, *qkv_a, lse_sh_a, sh, g_sh_h, info_a, None)
    dq_sh, kept, given = attend_backward(True, 1, *qkv_b, lse_sh_b, sh, g_sh_h, info_b, first)
    taken = lax.ppermute(given, "c", SWAP)
    shared_out = jnp.concatenate([(kept.astype(f32) + taken.astype(f32)).astype(bf16), dq_sh], axis=2)
    shared_out, back_own, dqkv_own = tie((shared_out, back_own, dqkv_own))
    back_shared = to_tokens(shared_out.reshape(2, 4, 3, 32, -1))
    d_heads, d_bias = head_grads(scale, (near_a, far_a, near_b, far_b), dqkv_own, dq_sh, kept, given, infos[0])

    head_ready = jnp.concatenate([
        d_heads.reshape(zs, 2, per, 384),
        jnp.broadcast_to(d_bias[:1].astype(bf16)[None, None], (zs, 2, 16, 384))], axis=2)
    head_ready, back_shared = tie((head_ready, back_shared))
    d_rows = token_grad(back_own, back_shared, back_weights, resid)
    if zs == 4:
        group = lax.axis_index("z")
        parts = [lax.dynamic_index_in_dim(head_ready, (group + k) % zs, axis=0, keepdims=False) for k in range(zs)]
        parts = parts[:1] + [
            lax.ppermute(parts[k], "z", [(i, (i + k) % zs) for i in range(zs)]) for k in range(1, zs)]
        head_sum = settle(parts, d_rows)
    else:
        head_sum = lax.psum_scatter(
            head_ready.reshape(-1, 384), "z", scatter_dimension=0, tiled=True).reshape(2, per + 16, 384)
    layer_part, _ = tie((layer_part, d_rows))
    layer_sum = (layer_part.astype(f32) + lax.ppermute(layer_part, "y", SWAP).astype(f32)).astype(bf16)
    returned = lax.all_to_all(
        d_rows.reshape(shards, stretch, width), SHARD, split_axis=0, concat_axis=0, tiled=True)

    def apart(array, bits):
        return lax.ppermute(array, PAIR, [(i, i ^ bits) for i in range(8)]) if bits else array

    halves = [lax.dynamic_index_in_dim(head_sum, x ^ k, axis=0, keepdims=False) for k in range(2)]
    head_eight = jnp.stack([apart(halves[bits >> 2], bits) for bits in range(8)])
    d_wq, d_wk, d_wv, d_bias_rows = head_unpack(head_eight, per, width, infos[0])
    place = lax.axis_index("z") * 2 + x
    own_slice = lambda row, n: lax.dynamic_slice_in_dim(row, place * n, n)
    d_bq, d_bv = own_slice(d_bias_rows[0], per), own_slice(d_bias_rows[1], per)

    layer_grads = flipped(jnp.stack([layer_sum, lax.ppermute(layer_sum, "c", SWAP)]), 0, c)
    layer_grads = layer_grads.reshape(9 * per + 32, width).astype(f32)
    d_wouter = layer_grads[:4 * per]
    d_winner = jnp.concatenate([layer_grads[(4 + n) * per:(5 + n) * per] for n in range(4)], axis=1)
    d_woutput = layer_grads[8 * per:9 * per]
    d_binner = own_slice(layer_grads[9 * per:9 * per + 4].reshape(-1), 4 * per)
    d_bo, d_g1, d_s1, d_bout, d_g2, d_s2 = (own_slice(layer_grads[9 * per + 4 + n], per) for n in range(6))
    small = (d_bq, d_bv, d_binner, d_bo, d_g1, d_s1, d_bout, d_g2, d_s2)
    returned = tie((returned, d_wouter, d_winner, d_woutput, d_wq, d_wk, d_wv) + small)[0]
    steps = jnp.arange(seq_count, dtype=jnp.int32)
    slot_of = jnp.sum(jnp.where(deal_order[:, None] == steps[None, :], steps[:, None], 0), axis=0)
    d_tokens = returned.at[slot_of].get(mode="promise_in_bounds")[:, None]
    return (act.reshape(1, shards, stretch, width), d_tokens, d_wq, d_wk, d_wv, d_woutput, d_bq, d_bv, d_bo,
            d_g1, d_s1, d_winner, d_binner, d_wouter, d_bout, d_g2, d_s2)


def solution(mesh):
    shards, splits = mesh.devices.shape
    fine = Mesh(mesh.devices.reshape(shards // 2, 2, splits // 2, 2), ALL)
    S, Q = SHARD, ("y", "c")
    row, mat = P(S), P(S, None)
    return jax.shard_map(
        body, mesh=fine,
        in_specs=(P(None, S, Q, None), P(), P(), mat, mat, mat, mat, row, row, row, row, row, mat, row, mat, row, row, row,
                  P(S, None, Q, None)),
        out_specs=(P(S, None, Q, None), P(None, S, Q, None), mat, mat, mat, mat, row, row, row, row, row, mat, row, mat,
                   row, row, row),
        check_vma=False)
```

```python
import functools, math
import jax
import jax.numpy as jnp
from jax import lax
from jax.experimental import pallas as pl
from jax.experimental.pallas import tpu as pltpu
from jax.sharding import Mesh, PartitionSpec as P

f32, bf16 = jnp.float32, jnp.bfloat16
LOG2E = 1.4426950408889634
LN2 = 0.6931471805599453
CH = 256
BQ = 2048
RB = 256
FB = 512
PARTS = 2
HD = 64
FAR = -1.0e30

def dg(a, b, ca, cb):
    return lax.dot_general(a, b, (((ca,), (cb,)), ((), ())), preferred_element_type=f32)


def three_parts(row):
    hi = row.astype(bf16).astype(f32)
    rest = row - hi
    mid = rest.astype(bf16).astype(f32)
    return hi, mid, rest - mid


def with_shift(top, shift):
    hi, mid, low = three_parts(shift)
    row = lax.broadcasted_iota(jnp.int32, (HD, top.shape[1]), 0)
    tail = jnp.where(row == 0, -hi, jnp.where(row == 1, -mid, jnp.where(row == 2, -low, jnp.where(row == 3, 1.0, 0.0))))
    return jnp.concatenate([top.astype(f32), tail], axis=0)


def load_rows(rows, ref, spans, x):
    stretch = ref.shape[3]
    for z in range(spans):
        for a in range(2):
            at = (2 * z + a) * stretch
            rows[at:at + stretch] = ref[0, a ^ x, z]


def qkv_kernel(stretch, spans, info, near_ref, far_ref, w_ref, b_ref, q_out, k_out, v_out, size_out, rows):
    away, half = pl.program_id(0), pl.program_id(2)
    owner = ((pl.program_id(1) ^ info[2]) << 1) | (away ^ info[3])

    @pl.when(away == 0)
    def _():
        load_rows(rows, near_ref, spans, info[1])

    @pl.when(away == 1)
    def _():
        load_rows(rows, far_ref, spans, info[1])
    weight = w_ref[...].reshape(rows.shape[1], 384)
    made = dg(rows[...], weight, 1, 0) + b_ref[...]
    count = rows.shape[0]
    q_t = (made[:, :128] * (LOG2E / 8.0)).T
    q_out[0, 0] = q_t[:HD].astype(bf16)
    q_out[1, 0] = q_t[HD:].astype(bf16)
    lane = lax.broadcasted_iota(jnp.int32, (count, 128), 1)
    row = lax.broadcasted_iota(jnp.int32, (count, 128), 0) + half * count
    shift = int(math.log2(stretch))
    position = lax.shift_left(lax.shift_right_logical(row, shift), shift + 2) + owner * stretch + (row & (stretch - 1))
    hidden = jnp.where(position < info[0], 0.0, FAR)
    tail = jnp.where(lane == HD + 3, hidden, jnp.where(lane < HD + 3, 1.0, 0.0))
    keys = made[:, 128:256]
    picks = lax.broadcasted_iota(jnp.int32, (128, 128), 0) // HD == lax.broadcasted_iota(jnp.int32, (128, 128), 1)
    sizes = dg((keys * keys).astype(bf16), jnp.where(picks, 1.0, 0.0).astype(bf16), 1, 0)
    size_out[0, 0] = jnp.max(sizes, axis=0, keepdims=True)
    for head in range(2):
        turned = keys if head == 0 else pltpu.roll(keys, HD, 1)
        full = jnp.where(lane < HD, turned, tail).astype(bf16)
        for j in range(count // 128):
            k_out[head, j, 0] = full[j * 128:(j + 1) * 128]
    v_t = made[:, 256:384].T
    ones = jnp.where(lax.broadcasted_iota(jnp.int32, (HD, count), 0) < 3, 1.0, 0.0)
    for head in range(2):
        full = jnp.concatenate([v_t[head * HD:(head + 1) * HD], ones], axis=0).astype(bf16)
        for j in range(count // 128):
            v_out[head, j, 0] = full[:, j * 128:(j + 1) * 128]


def owner_of(away, across, info):
    return ((across ^ info[2]) << 1) | (away ^ info[3])


def project(near, far, weight, bias, info):
    _, _, zs, stretch, width = near.shape
    local = 2 * zs * stretch
    spans = 1024 // (2 * stretch)
    halves = local // 1024
    spans_of_rows = local // 128
    per = spans_of_rows // halves
    block = (1, 2, spans, stretch, width)
    q, k, v, sizes = pl.pallas_call(
        functools.partial(qkv_kernel, stretch, spans),
        grid_spec=pltpu.PrefetchScalarGridSpec(
            num_scalar_prefetch=1, grid=(2, 2, halves),
            in_specs=[
                pl.BlockSpec(block, lambda a, o, h, n: (jnp.where(a == 0, o, 1), 0, jnp.where(a == 0, h, halves - 1), 0, 0)),
                pl.BlockSpec(block, lambda a, o, h, n: (jnp.where(a == 0, 0, o), 0, jnp.where(a == 0, 0, h), 0, 0)),
                pl.BlockSpec((8, width // 8, 384), lambda a, o, h, n: (0, 0, n[1])),
                pl.BlockSpec((1, 384), lambda a, o, h, n: (0, 0)),
            ],
            out_specs=[
                pl.BlockSpec((2, 1, HD, 1024), lambda a, o, h, n: (0, owner_of(a, o, n), 0, h)),
                pl.BlockSpec((2, per, 1, 128, 128), lambda a, o, h, n: (0, h, o ^ n[2], a ^ n[3], 0)),
                pl.BlockSpec((2, per, 1, 128, 128), lambda a, o, h, n: (0, h, o ^ n[2], 0, a ^ n[3])),
                pl.BlockSpec((1, 1, 1, 128), lambda a, o, h, n: (owner_of(a, o, n), h, 0, 0)),
            ],
            scratch_shapes=[pltpu.VMEM((1024, width), bf16)]),
        out_shape=[
            jax.ShapeDtypeStruct((2, 4, HD, local), bf16),
            jax.ShapeDtypeStruct((2, spans_of_rows, 2, CH, 128), bf16),
            jax.ShapeDtypeStruct((2, spans_of_rows, 2, 128, CH), bf16),
            jax.ShapeDtypeStruct((4, halves, 1, 128), f32),
        ],
        compiler_params=pltpu.CompilerParams(vmem_limit_bytes=60 << 20),
        name="qkv",
        cost_estimate=cost(4 * near.size * 384, near.size * 8),
    )(info, near, far, weight, bias)
    return q, k.reshape(2, -1, CH, 128), v.reshape(2, -1, 128, CH), sizes


def step_on(q, j, count):
    last = j + 1 == count
    return jnp.where(last, q + 1, q), jnp.where(last, 0, j + 1)


def assemble(ref, part, shared, core):
    if not shared:
        return jnp.concatenate([ref[0, 2 * part], ref[0, 2 * part + 1]], axis=1)
    at = pl.multiple_of(core * 512, 512)
    return jnp.concatenate([ref[0, n, :, pl.ds(at, 512)] for n in range(4)], axis=1)


def fwd_kernel(shared, info, q_ref, k_ref, v_ref, size_ref, held_ref, out_ref, lse_ref, acc, probs, qa, shifts):
    count = info[4]
    parts = 1 if shared else 2
    lane = lax.broadcasted_iota(jnp.int32, (1, 128), 1)
    sizes = functools.reduce(jnp.maximum, [size_ref[o, h] for o in range(size_ref.shape[0]) for h in range(size_ref.shape[1])])
    widest = jnp.sqrt(jnp.max(jnp.where(lane == int(shared), sizes, 0.0), axis=1, keepdims=True))

    for part in range(parts):
        q_t = assemble(q_ref, part, shared, info[3])
        wide = q_t.astype(f32)
        shift = jnp.sqrt(jnp.sum(wide * wide, axis=0, keepdims=True)) * widest
        shifts[part] = shift
        qa[part] = with_shift(q_t, shift).astype(bf16)

    def raised(part, j):
        return jnp.exp2(dg(k_ref[0, j], qa[part], 1, 0)).astype(bf16)

    probs[0] = raised(0, 0)

    def body(t, carry, ahead_too=True):
        part, j = carry
        now = t & 1
        part_next, j_next = step_on(part, j, count)
        before = jnp.where(j == 0, 0.0, acc[...])
        acc[...] = before + dg(v_ref[0, j], probs[now], 1, 0)
        if ahead_too:
            probs[1 - now] = raised(part_next, j_next)

        @pl.when(j + 1 == count)
        def _():
            total = acc[HD:HD + 1]
            fine = (jnp.min(total) > 2.0 ** -90) & (jnp.max(total) < 2.0 ** 60)

            @pl.when(jnp.logical_not(fine))
            def _():
                plain = qa[part].astype(f32)
                row = lax.broadcasted_iota(jnp.int32, plain.shape, 0)
                qa[part] = jnp.where((row >= HD) & (row < HD + 3), 0.0, plain).astype(bf16)

                def peak(i, top):
                    return jnp.maximum(top, jnp.max(dg(k_ref[0, i], qa[part], 1, 0), axis=0, keepdims=True))
                shift = lax.fori_loop(0, count, peak, jnp.full((1, BQ), FAR, f32))
                shifts[part] = shift
                qa[part] = with_shift(plain[:HD], shift).astype(bf16)
                acc[...] = jnp.zeros_like(acc)

                def again(i, carry):
                    acc[...] += dg(v_ref[0, i], raised(part, i), 1, 0)
                    return carry
                lax.fori_loop(0, count, again, 0)

            total = acc[HD:HD + 1]
            mixed = (acc[:HD] * (1.0 / total)).astype(bf16)
            lse_ref[part] = shifts[part] + jnp.log2(total)
            if shared:
                for n in range(4):
                    out_ref[0, n] = mixed[:, n * 512:(n + 1) * 512]
            else:
                for n in range(2):
                    out_ref[0, 2 * part + n] = mixed[:, n * 1024:(n + 1) * 1024]
        return part_next, j_next

    turns = parts * count
    body(turns - 1, lax.fori_loop(0, turns - 1, body, (0, 0)), False)


def head_spec(shared, *dims):
    zeros = (0,) * len(dims)
    return pl.BlockSpec((1,) + dims, lambda i, n: (int(shared),) + zeros)


def whole_spec(*dims):
    return pl.BlockSpec(dims, lambda i, n: (0,) * len(dims))


def cost(flops, moved, exps=0):
    return pl.CostEstimate(flops=int(flops), bytes_accessed=int(moved), transcendentals=int(exps))


def attend_forward(shared, seq, q, k, v, sizes, info, held):
    _, owners, _, local = q.shape
    chunks = k.shape[1]
    wide = local // 2 if shared else local
    parts = owners * wide // BQ
    pairs = parts * BQ * chunks * CH * 0.6
    shape = jax.ShapeDtypeStruct((2, owners, HD, wide), bf16)
    first = held is None
    if first:
        kernel = lambda info, q, k, v, size, *rest: fwd_kernel(shared, info, q, k, v, size, None, *rest)
    else:
        kernel = functools.partial(fwd_kernel, shared)
    return pl.pallas_call(
        kernel,
        grid_spec=pltpu.PrefetchScalarGridSpec(
            num_scalar_prefetch=1, grid=(1,),
            in_specs=[
                head_spec(shared, owners, HD, local), head_spec(shared, chunks, CH, 128), head_spec(shared, chunks, 128, CH),
                whole_spec(*sizes.shape),
            ] + ([] if first else [pl.BlockSpec(memory_space=pl.ANY)]),
            out_specs=[pl.BlockSpec((1, owners, HD, wide), lambda i, n: (seq, 0, 0, 0)), whole_spec(parts, 1, BQ)],
            scratch_shapes=[
                pltpu.VMEM((128, BQ), f32), pltpu.VMEM((2, CH, BQ), bf16), pltpu.VMEM((parts, 128, BQ), bf16),
                pltpu.VMEM((parts, 1, BQ), f32),
            ]),
        out_shape=[shape, jax.ShapeDtypeStruct((parts, 1, BQ), f32)],
        input_output_aliases={} if first else {5: 0},
        compiler_params=pltpu.CompilerParams(vmem_limit_bytes=60 << 20),
        cost_estimate=cost(pairs * 1024, chunks * CH * 512, pairs),
        name="attend_forward_shared" if shared else "attend_forward_own",
    )(*((info, q, k, v, sizes) + (() if first else (held,))))


def bwd_kernel(shared, first, info, q_ref, k_ref, v_ref, lse_ref, out_ref, gout_ref, *rest):
    rest = rest if first else rest[3 if shared else 1:]
    if shared:
        dq_ref, kept_ref, given_ref, dk_acc, dv_acc, dq_acc, qa, qat, ga, gat, pb, db = rest
    else:
        dqkv_ref, dk_acc, dv_acc, dq_acc, qa, qat, ga, gat, pb, db = rest
    count = info[4]
    chunks = k_ref.shape[1]
    parts = 1 if shared else 2
    dk_acc[...] = jnp.zeros_like(dk_acc)
    dv_acc[...] = jnp.zeros_like(dv_acc)

    def piece(ref, part):
        return jnp.concatenate([ref[0, n] for n in (range(4) if shared else (2 * part, 2 * part + 1))], axis=1)

    for part in range(parts):
        q_full = with_shift(assemble(q_ref, part, shared, info[3]), lse_ref[part])
        qat[part] = q_full.astype(bf16)
        qa[part] = q_full.T.astype(bf16)
        g_t = piece(gout_ref, part)
        meet = jnp.sum(g_t.astype(f32) * piece(out_ref, part).astype(f32), axis=0, keepdims=True)
        g_full = with_shift(g_t, meet)
        gat[part] = g_full.astype(bf16)
        ga[part] = g_full.T.astype(bf16)

    def ahead(part, j, slot):
        raised = jnp.exp2(dg(qa[part], k_ref[0, j], 1, 1))
        pb[slot] = raised.astype(bf16)
        db[slot] = (raised * dg(ga[part], v_ref[0, j], 1, 0)).astype(bf16)

    ahead(0, 0, 0)

    def body(t, carry, ahead_too=True):
        part, j = carry
        now = t & 1
        part_next, j_next = step_on(part, j, count)
        dv_acc[j] += dg(gat[part], pb[now], 1, 0)[:HD]
        dk_acc[j] += dg(qat[part], db[now], 1, 0)[:HD]
        before = jnp.where(j == 0, 0.0, dq_acc[...])
        dq_acc[...] = before + dg(db[now], k_ref[0, j], 1, 0)
        if ahead_too:
            ahead(part_next, j_next, 1 - now)

        @pl.when(j + 1 == count)
        def _():
            dq_t = (dq_acc[...] * 0.125).T[:HD].astype(bf16)
            if shared:
                for n in range(4):
                    dq_ref[0, n, :, :512] = dq_t[:32, n * 512:(n + 1) * 512]
                    dq_ref[0, n, :, 512:] = dq_t[32:, n * 512:(n + 1) * 512]
            else:
                for n in range(2):
                    dqkv_ref[0, 2 * part + n, 0] = dq_t[:, n * 1024:(n + 1) * 1024]
        return part_next, j_next

    turns = parts * count
    body(turns - 1, lax.fori_loop(0, turns - 1, body, (0, 0)), False)
    for block in range(chunks):
        j, across = block // 2, block % 2
        for owner in (2 * across, 2 * across + 1):
            cols = slice((owner - 2 * across) * 128, (owner - 2 * across + 1) * 128)
            dk_wide, dv_wide = dk_acc[block, :, cols] * LN2, dv_acc[block, :, cols]
            dk, dv = dk_wide.astype(bf16), dv_wide.astype(bf16)
            if shared:
                here = info[3] == 0
                kept_ref[0, owner, :, j * 128:(j + 1) * 128] = jnp.where(here, dk_wide, dv_wide).astype(bf16)
                given_ref[0, owner, :, j * 128:(j + 1) * 128] = jnp.where(here, dv_wide, dk_wide).astype(bf16)
            else:
                dqkv_ref[0, owner, 1, :, j * 128:(j + 1) * 128] = dk
                dqkv_ref[0, owner, 2, :, j * 128:(j + 1) * 128] = dv


def attend_backward(shared, seq, q, k, v, lse, out, g_out, info, held):
    _, owners, _, local = q.shape
    chunks = k.shape[1]
    wide = out.shape[3]
    parts = owners * wide // BQ
    pairs = parts * BQ * chunks * CH * 0.6
    shape = jax.ShapeDtypeStruct
    first = held is None
    if shared:
        out_specs = [pl.BlockSpec((1, owners, rows, local), lambda i, n: (seq, 0, 0, 0)) for rows in (32, HD, HD)]
        out_shape = [shape((2, owners, rows, local), bf16) for rows in (32, HD, HD)]
    else:
        out_specs = [pl.BlockSpec((1, owners, 3, HD, local), lambda i, n: (seq, 0, 0, 0, 0))]
        out_shape = [shape((2, owners, 3, HD, local), bf16)]
    kept = () if first else tuple(held)
    of_seq = pl.BlockSpec((1, owners, HD, wide), lambda i, n: (seq, 0, 0, 0))
    return pl.pallas_call(
        functools.partial(bwd_kernel, shared, first),
        grid_spec=pltpu.PrefetchScalarGridSpec(
            num_scalar_prefetch=1, grid=(1,),
            in_specs=[
                head_spec(shared, owners, HD, local), head_spec(shared, chunks, CH, 128), head_spec(shared, chunks, 128, CH),
                whole_spec(parts, 1, BQ), of_seq, of_seq,
            ] + [pl.BlockSpec(memory_space=pl.ANY)] * len(kept),
            out_specs=out_specs,
            scratch_shapes=[
                pltpu.VMEM((chunks, HD, CH), f32), pltpu.VMEM((chunks, HD, CH), f32), pltpu.VMEM((BQ, 128), f32),
                pltpu.VMEM((parts, BQ, 128), bf16), pltpu.VMEM((parts, 128, BQ), bf16),
                pltpu.VMEM((parts, BQ, 128), bf16), pltpu.VMEM((parts, 128, BQ), bf16),
                pltpu.VMEM((2, BQ, CH), bf16), pltpu.VMEM((2, BQ, CH), bf16),
            ]),
        out_shape=out_shape,
        input_output_aliases={7 + n: n for n in range(len(kept))},
        compiler_params=pltpu.CompilerParams(vmem_limit_bytes=60 << 20),
        cost_estimate=cost(pairs * 100, chunks * CH * 2048),
        name="attend_backward_shared" if shared else "attend_backward_own",
    )(info, q, k, v, lse, out, g_out, *kept)


def gelu_pair(u):
    half = 0.5 * (1.0 + lax.erf(u * 0.7071067811865476))
    return u * half, half + u * (0.3989422804014327 * jnp.exp2(u * u * (-0.5 * LOG2E)))


def norm_stats(v):
    mean = jnp.mean(v, axis=-1, keepdims=True)
    centred = v - mean
    inverse = lax.rsqrt(jnp.mean(centred * centred, axis=-1, keepdims=True) + 1e-12)
    return centred * inverse, inverse


def norm_back(grad, xhat, inverse, gain):
    g = grad * gain
    return (g - jnp.mean(g, axis=-1, keepdims=True) - xhat * jnp.mean(g * xhat, axis=-1, keepdims=True)) * inverse


def weight_part(ref, first, rows):
    part = ref[:, first:first + rows, :]
    return part.reshape(part.shape[0] * rows, part.shape[2])


def ffn_kernel(spans, info, x_ref, own_ref, sh_ref, cot_ref, w_ref, bin_ref, vec_ref,
               act_out, resid_out, gown_out, gsh_out, active_out, dinner_out, normed_out, douter_out, dbranch_out,
               vec_sum, slope, row_block):
    step = pl.program_id(0)
    load_rows(row_block, x_ref, spans, info[1])
    count = row_block.shape[0] // PARTS
    vec = vec_ref[...]
    total = lambda a: jnp.sum(a, axis=0, keepdims=True)
    held = [{"at": slice(n * count, (n + 1) * count)} for n in range(PARTS)]

    def branch(h):
        at = h["at"]
        mixed_t = jnp.concatenate(
            [part for p in range(4) for part in (own_ref[p, 0, :, at], sh_ref[p, 0, :, at], own_ref[p, 1, :, at])], axis=0)
        h["sum1"] = row_block[at].astype(f32) + (dg(mixed_t, weight_part(w_ref, 768, 96), 0, 0) + vec[0:1])

    def first_norm(h):
        h["xhat1"], h["inv1"] = norm_stats(h["sum1"])
        normed = h["xhat1"] * vec[1:2] + vec[2:3]
        normed_out[h["at"]] = normed.astype(bf16)
        h["outer"] = normed + vec[3:4]

    def widen(h):
        at = h["at"]
        for n in range(4):
            cols = slice(n * 768, (n + 1) * 768)
            value, bend = gelu_pair(dg(normed_out[at], weight_part(w_ref, 384 + 96 * n, 96), 1, 0) + bin_ref[:, cols])
            active_out[at, cols] = value.astype(bf16)
            slope[at, cols] = bend.astype(bf16)

    def narrow(h):
        h["outer"] = h["outer"] + dg(active_out[h["at"]], weight_part(w_ref, 0, 384), 1, 0)

    def second_norm(h):
        at = h["at"]
        xhat2, inv2 = norm_stats(h["outer"])
        act_out[at] = (xhat2 * vec[4:5] + vec[5:6]).astype(bf16)
        cot = cot_ref[at].astype(f32)
        d2 = norm_back(cot, xhat2, inv2, vec[4:5])
        d_outer = d2.astype(bf16)
        douter_out[at] = d_outer
        h["d_normed"] = d2
        h["sums"] = [total(d_outer.astype(f32)), total(cot * xhat2), total(cot)]

    def back(h):
        at = h["at"]
        h["inner_sums"] = []
        for n in range(4):
            cols = slice(n * 768, (n + 1) * 768)
            d_active = dg(douter_out[at], weight_part(w_ref.at[2 * n:2 * n + 2], 0, 384), 1, 1)
            d_inner = (d_active * slope[at, cols].astype(f32)).astype(bf16)
            dinner_out[at, cols] = d_inner
            h["inner_sums"].append(total(d_inner.astype(f32)))
            h["d_normed"] = h["d_normed"] + dg(d_inner, weight_part(w_ref, 384 + 96 * n, 96), 1, 1)

    def first_back(h):
        at = h["at"]
        d_normed = h["d_normed"]
        d1 = norm_back(d_normed, h["xhat1"], h["inv1"], vec[1:2])
        resid_out[at] = d1
        d_branch = d1.astype(bf16)
        dbranch_out[at] = d_branch
        h["sums"] = [total(d_branch.astype(f32)), total(d_normed * h["xhat1"]), total(d_normed)] + h["sums"]

    def mix_back(h):
        at = h["at"]
        g_t = dg(weight_part(w_ref, 768, 96), dbranch_out[at], 1, 1).astype(bf16)
        for p in range(4):
            gown_out[p, 0, :, at] = g_t[192 * p:192 * p + 64]
            gsh_out[p, 0, :, at] = g_t[192 * p + 64:192 * p + 128]
            gown_out[p, 1, :, at] = g_t[192 * p + 128:192 * p + 192]

    for products, norm in ((branch, first_norm), (widen, None), (narrow, second_norm), (back, first_back), (mix_back, None)):
        for h in held:
            products(h)
            if norm is not None:
                norm(h)
    added = lambda name, n: functools.reduce(jnp.add, [h[name][n] for h in held])
    sums = jnp.concatenate(
        [added("inner_sums", n) for n in range(4)] + [added("sums", n) for n in range(6)]
        + [jnp.zeros((6, vec.shape[1]), f32)], axis=0)

    @pl.when(step == 0)
    def _():
        vec_sum[...] = sums

    @pl.when(step > 0)
    def _():
        vec_sum[...] += sums


def feed_forward(rows_in, own, sh, cotangent, weights, inner_bias, vectors, info):
    _, _, _, stretch, width = rows_in.shape
    local = cotangent.shape[0]
    spans = FB // (2 * stretch)
    steps = local // FB
    half_steps = steps // 2
    wide = inner_bias.shape[1]
    rows = lambda n: pl.BlockSpec((FB, n), lambda r, a: (r, 0))
    fixed = lambda *dims: pl.BlockSpec(dims, lambda r, a: (0,) * len(dims))
    own_spec = pl.BlockSpec((4, 2, HD, FB), lambda r, a: (0, 0, 0, r))
    sh_spec = pl.BlockSpec((4, 1, HD, FB), lambda r, a: (0, r // half_steps, 0, r % half_steps))
    shape = jax.ShapeDtypeStruct
    return pl.pallas_call(
        functools.partial(ffn_kernel, spans),
        grid_spec=pltpu.PrefetchScalarGridSpec(
            num_scalar_prefetch=1, grid=(steps,),
            in_specs=[
                pl.BlockSpec((1, 2, spans, stretch, width), lambda r, a: (0, 0, r, 0, 0)),
                own_spec, sh_spec, rows(width),
                pl.BlockSpec(weights.shape, lambda r, a: (0, 0, 0), pipeline_mode=pl.Buffered(1)),
                fixed(1, wide), fixed(8, width),
            ],
            out_specs=[
                rows(width), rows(width), own_spec, sh_spec, rows(wide), rows(wide), rows(width), rows(width), rows(width),
                fixed(16, width),
            ],
            scratch_shapes=[pltpu.VMEM((FB, wide), bf16), pltpu.VMEM((FB, width), bf16)]),
        out_shape=[
            shape((local, width), bf16), shape((local, width), f32), shape(own.shape, bf16), shape(sh.shape, bf16),
            shape((local, wide), bf16), shape((local, wide), bf16), shape((local, width), bf16),
            shape((local, width), bf16), shape((local, width), bf16), shape((16, width), f32),
        ],
        compiler_params=pltpu.CompilerParams(vmem_limit_bytes=60 << 20),
        name="feed_forward",
        cost_estimate=cost(local * width * (width + 2 * wide) * 4, local * wide * 20),
    )(info, rows_in, own, sh, cotangent, weights, inner_bias, vectors)


def outer_grad_kernel(scale, active_ref, douter_ref, out_ref):
    made = (dg(active_ref[...], douter_ref[...], 0, 0) * scale).astype(bf16)
    out_ref[...] = made.reshape(out_ref.shape)


def inner_grad_kernel(scale, packed_ref, normed_ref, dinner_ref, own_ref, sh_ref, dbranch_ref, out_ref):
    step = pl.program_id(0)

    @pl.when(step < 4)
    def _():
        out_ref[...] = (dg(normed_ref[...], dinner_ref[...], 0, 0) * scale).astype(bf16).reshape(out_ref.shape)

    @pl.when(step == 4)
    def _():
        mixed_t = jnp.concatenate([
            part for p in range(4)
            for part in (own_ref[p, 0], jnp.concatenate([sh_ref[p, 0], sh_ref[p, 1]], axis=1), own_ref[p, 1])], axis=0)
        out_ref[...] = (dg(mixed_t, dbranch_ref[...], 1, 0) * scale).astype(bf16).reshape(out_ref.shape)


def weight_grads(scale, active, d_outer, normed, d_inner, own, sh, d_branch):
    local, wide = active.shape
    width = normed.shape[1]
    packed = pl.pallas_call(
        functools.partial(outer_grad_kernel, scale), grid=(4,),
        in_specs=[pl.BlockSpec((local, width), lambda m: (0, m)), pl.BlockSpec((local, width), lambda m: (0, 0))],
        out_specs=pl.BlockSpec((2, 384, width), lambda m: (m, 0, 0)),
        out_shape=jax.ShapeDtypeStruct((8, 896, width), bf16),
        compiler_params=pltpu.CompilerParams(vmem_limit_bytes=40 << 20), name="outer_grad",
        cost_estimate=cost(2 * local * wide * width, 2 * wide * (local + width)),
    )(active, d_outer)
    fixed = lambda a: pl.BlockSpec(a.shape, lambda n: (0,) * a.ndim)
    return pl.pallas_call(
        functools.partial(inner_grad_kernel, scale), grid=(5,),
        in_specs=[
            pl.BlockSpec(memory_space=pl.ANY), fixed(normed),
            pl.BlockSpec((local, width), lambda n: (0, jnp.minimum(n, 3))), fixed(own), fixed(sh), fixed(d_branch)],
        out_specs=pl.BlockSpec((8, 96, width), lambda n: (0, 4 + n, 0)),
        out_shape=jax.ShapeDtypeStruct((8, 896, width), bf16), input_output_aliases={0: 0},
        compiler_params=pltpu.CompilerParams(vmem_limit_bytes=40 << 20), name="inner_grad",
        cost_estimate=cost(2 * local * (wide + width) * width, 2 * (wide + width) * (local + width)),
    )(packed, normed, d_inner, own, sh, d_branch)


def head_grad_kernel(scale, spans, info, *refs):
    x_refs, (own_ref, dq_ref, kept_ref, given_ref, out_ref, bias_out, acc, bias_acc, rows) = refs[:4], refs[4:]
    seq, away, half = pl.program_id(0), pl.program_id(1), pl.program_id(3)
    last = (seq == 1) & (away == 1) & (pl.program_id(2) == 1) & (half == pl.num_programs(3) - 1)
    for n in range(4):
        @pl.when(seq * 2 + away == n)
        def _(n=n):
            load_rows(rows, x_refs[n], spans, info[1])
    dq_t = jnp.where(half == info[3], jnp.concatenate([dq_ref[0, 0, :, :512], dq_ref[0, 0, :, 512:]], axis=0).astype(f32), 0.0)
    kept, given = kept_ref[0, 0].astype(f32), given_ref[0, 0].astype(f32)
    here = info[3] == 0
    d_t = jnp.concatenate([
        own_ref[0, 0, 0], dq_t.astype(bf16), own_ref[0, 0, 1], jnp.where(here, kept, given).astype(bf16),
        own_ref[0, 0, 2], jnp.where(here, given, kept).astype(bf16)], axis=0)

    @pl.when((seq == 0) & (away == 0) & (pl.program_id(2) == 0) & (half == 0))
    def _():
        acc[...] = jnp.zeros_like(acc)
        bias_acc[...] = jnp.zeros_like(bias_acc)
    acc[...] += dg(d_t, rows[...], 1, 0)
    bias_acc[...] += dg(jnp.ones((8, d_t.shape[1]), bf16), d_t, 1, 1)

    @pl.when(last)
    def _():
        out_ref[...] = (acc[...] * scale).T.astype(bf16)
        bias_out[...] = bias_acc[...] * scale


def head_grads(scale, sources, dqkv_own, dq_sh, kept, given, info):
    _, _, zs, stretch, width = sources[0].shape
    local = 2 * zs * stretch
    spans = 512 // (2 * stretch)
    halves = local // 512

    def source_spec(n):
        def index(s, a, o, h, i):
            now = 2 * s + a
            across = jnp.where(now == n, o, jnp.where(now < n, 0, 1))
            return (across, 0, jnp.where(now == n, h, jnp.where(now < n, 0, halves - 1)), 0, 0)
        return pl.BlockSpec((1, 2, spans, stretch, width), index)
    return pl.pallas_call(
        functools.partial(head_grad_kernel, scale, spans),
        grid_spec=pltpu.PrefetchScalarGridSpec(
            num_scalar_prefetch=1, grid=(2, 2, 2, halves),
            in_specs=[source_spec(n) for n in range(4)] + [
                pl.BlockSpec((1, 1, 3, HD, 512), lambda s, a, o, h, i: (s, owner_of(a, o, i), 0, 0, h)),
                pl.BlockSpec((1, 1, 32, local), lambda s, a, o, h, i: (s, owner_of(a, o, i), 0, 0)),
            ] + [pl.BlockSpec((1, 1, HD, 512), lambda s, a, o, h, i: (s, owner_of(a, o, i), 0, h))] * 2,
            out_specs=[pl.BlockSpec((width, 384), lambda s, a, o, h, i: (0, 0)), pl.BlockSpec((8, 384), lambda s, a, o, h, i: (0, 0))],
            scratch_shapes=[pltpu.VMEM((384, width), f32), pltpu.VMEM((8, 384), f32), pltpu.VMEM((512, width), bf16)]),
        out_shape=[jax.ShapeDtypeStruct((width, 384), bf16), jax.ShapeDtypeStruct((8, 384), f32)],
        compiler_params=pltpu.CompilerParams(vmem_limit_bytes=40 << 20), name="head_grads",
        cost_estimate=cost(8 * local * 768 * width, 8 * local * width * 2),
    )(info, *sources, dqkv_own, dq_sh, kept, given)


def token_grad_kernel(own_ref, low_ref, high_ref, dkv_ref, w_ref, resid_ref, out_ref):
    total = resid_ref[...]
    for kind in range(3):
        made = []
        for p in range(4):
            if kind == 0:
                middle = jnp.concatenate([low_ref[p, 0], high_ref[p, 0]], axis=0)
            else:
                middle = jnp.concatenate([dkv_ref[p, kind - 1, n] for n in range(2)], axis=0)
            made += [own_ref[p, 0, kind], middle, own_ref[p, 1, kind]]
        total = total + dg(jnp.concatenate(made, axis=0), weight_part(w_ref, 96 * kind, 96), 0, 1)
    out_ref[...] = total.astype(bf16)


def token_grad(own, shared, weights, resid):
    local, width = resid.shape
    steps = local // RB
    half_steps = steps // 2
    rows = pl.BlockSpec((RB, width), lambda r: (r, 0))
    return pl.pallas_call(
        token_grad_kernel, grid=(steps,),
        in_specs=[
            pl.BlockSpec((4, 2, 3, HD, RB), lambda r: (0, 0, 0, 0, r)),
            pl.BlockSpec((4, 1, None, 32, RB), lambda r: (0, r // half_steps, 2, 0, r % half_steps)),
            pl.BlockSpec((4, 1, None, 32, RB), lambda r: (0, r // half_steps, 2, 0, half_steps + r % half_steps)),
            pl.BlockSpec((4, 2, 2, 32, RB), lambda r: (0, 0, 0, 0, r)),
            pl.BlockSpec(weights.shape, lambda r: (0, 0, 0)), rows],
        out_specs=rows, out_shape=jax.ShapeDtypeStruct((local, width), bf16),
        compiler_params=pltpu.CompilerParams(vmem_limit_bytes=60 << 20), name="token_grad",
        cost_estimate=cost(local * width * width * 6, local * width * 12),
    )(own, shared, shared, shared, weights, resid)


def head_unpack_kernel(per, info, src_ref, q_out, k_out, v_out, bias_out):
    low = lax.broadcasted_iota(jnp.int32, (src_ref.shape[1], 128), 1) < HD

    def rows_of(p, core, cols):
        at = (((p >> 1) ^ info[1]) << 2) | (((p & 1) ^ info[2]) << 1) | (core ^ info[3])
        return src_ref[at, :, cols].astype(f32)
    for kind, out in enumerate((q_out, k_out, v_out)):
        cols = slice(128 * kind, 128 * kind + 128)
        tiles = []
        for pair in range(2):
            first, second = [], []
            for p in (2 * pair, 2 * pair + 1):
                near, far = rows_of(p, 0, cols), rows_of(p, 1, cols)
                first.append(near + jnp.where(low, 0.0, far))
                second.append(far)
            turned = pltpu.roll(first[1], HD, 1)
            tiles += [first[0], jnp.where(low, second[0], turned), jnp.where(low, turned, pltpu.roll(second[1], HD, 1))]
        made = jnp.concatenate(tiles, axis=1)
        out[...] = made[:per]
        if kind != 1:
            bias_out[kind // 2:kind // 2 + 1] = made[per:per + 1]


def head_unpack(source, per, width, info):
    shape = jax.ShapeDtypeStruct
    full = lambda n: pl.BlockSpec((n, width), lambda i, f: (0, 0))
    return pl.pallas_call(
        functools.partial(head_unpack_kernel, per),
        grid_spec=pltpu.PrefetchScalarGridSpec(
            num_scalar_prefetch=1, grid=(1,),
            in_specs=[pl.BlockSpec(source.shape, lambda i, f: (0, 0, 0))],
            out_specs=[full(per)] * 3 + [full(2)]),
        out_shape=[shape((per, width), f32)] * 3 + [shape((2, width), f32)], name="head_unpack",
    )(info, source)


SWAP = [(0, 1), (1, 0)]
def settle_kernel(*refs):
    refs[-1][...] = sum(ref[...].astype(f32) for ref in refs[:-2]).astype(bf16)


def settle(parts, after):
    whole = pl.BlockSpec(memory_space=pltpu.VMEM)
    return pl.pallas_call(
        settle_kernel, in_specs=[whole] * len(parts) + [pl.BlockSpec(memory_space=pl.ANY)], out_specs=whole,
        out_shape=jax.ShapeDtypeStruct(parts[0].shape, bf16), name="settle",
        cost_estimate=cost(1e9, 1e6),
    )(*parts, after)


PAIR = ("x", "y", "c")
ALL = ("z", "x", "y", "c")
SHARD = ("z", "x")


def canonical(packed, shards):
    if shards == 8:
        return packed
    width = packed.shape[2]
    per, keep = 96 * 8 // shards, shards // 8
    outer = packed[:, :4 * per].reshape(8, 384, width)
    inner = packed[:, 4 * per:8 * per].reshape(8, keep, 4, per, width).transpose(0, 2, 1, 3, 4).reshape(8, 384, width)
    output = packed[:, 8 * per:9 * per].reshape(8, 96, width)
    return jnp.concatenate([outer, inner, output, jnp.zeros((8, 32, width), packed.dtype)], axis=1)


def from_canonical(packed, last, shards):
    width = packed.shape[2]
    if shards == 8:
        return packed.at[:, 864:].set(jnp.broadcast_to(last[None], (8, 32, width)))
    per, keep = 96 * 8 // shards, shards // 8
    outer = packed[:, :384].reshape(shards, 4 * per, width)
    inner = packed[:, 384:768].reshape(8, 4, keep, per, width).transpose(0, 2, 1, 3, 4).reshape(shards, 4 * per, width)
    output = packed[:, 768:864].reshape(shards, per, width)
    return jnp.concatenate([outer, inner, output, jnp.broadcast_to(last[None], (shards, 32, width))], axis=1)


def canonical_heads(packed, shards, parts):
    if shards == 8:
        return packed
    width = packed.shape[2]
    per = 96 * 8 // shards
    made = [packed[:, k * per:(k + 1) * per].reshape(8, 96, width) for k in range(parts)]
    return jnp.concatenate(made + [jnp.zeros((8, 32, width), packed.dtype)], axis=1)


def quarter(pieces):
    part = sum(piece.shape[0] for piece in pieces) // 4

    def taken(k):
        found, at = [], 0
        for piece in pieces:
            low, high = max(k * part - at, 0), min((k + 1) * part - at, piece.shape[0])
            if low < high:
                found.append(piece[low:high])
            at += piece.shape[0]
        return jnp.concatenate(found, axis=0)
    place = lax.axis_index("y") * 2 + lax.axis_index("c")
    return lax.switch(place, [functools.partial(taken, k) for k in range(4)])


def flipped(array, axis, here):
    return jnp.where(here == 0, array, jnp.flip(array, axis))


def body(tokens, lengths, deal_order, w_query, w_key, w_value, w_output, b_query, b_value, b_output,
         ln1_gain, ln1_shift, w_inner, b_inner, w_outer, b_outer, ln2_gain, ln2_shift, cotangent):
    tie = lax.optimization_barrier
    zs = lax.axis_size("z")
    shards = 2 * zs
    scale = 1.0 / (shards * 4)
    seq_count, _, stretch, width = tokens.shape
    per = w_query.shape[0]
    half = zs // 2
    x, y, c = lax.axis_index("x"), lax.axis_index("y"), lax.axis_index("c")

    def deal(ordered):
        return lax.all_to_all(ordered, "z", split_axis=0, concat_axis=0, tiled=True)

    def corner(across, along):
        return [lax.ppermute(across[:half], "y", SWAP), lax.ppermute(along[half:], "x", SWAP)]

    def this_core(own, across, along, corner):
        return jnp.concatenate([own, across, along] + corner, axis=0).reshape(2, 2, zs, stretch, width)

    ordered_a = tokens[:, 0].at[deal_order[0::2]].get(mode="promise_in_bounds")
    first_own = deal(ordered_a)
    _, tokens, w_query, w_key, w_value, b_query, b_value, deal_order = tie(
        (ordered_a, tokens, w_query, w_key, w_value, b_query, b_value, deal_order))
    ordered_b = tokens[:, 0].at[deal_order[1::2]].get(mode="promise_in_bounds")

    def head_columns(matrix):
        heads = matrix.reshape(per, 2, 2, 3, HD)
        mine = lax.dynamic_index_in_dim(heads, y, axis=2, keepdims=False)
        own = lax.dynamic_index_in_dim(mine, 2 * c, axis=2, keepdims=False)
        return [own, mine[:, :, 1]]
    pad = lambda v: jnp.pad(v, (0, width - v.shape[0]))[None]
    columns = jnp.concatenate(
        [col for matrix in (w_query, w_key, w_value) for col in head_columns(matrix)], axis=2).reshape(per, width)
    head_pack = jnp.concatenate([columns, pad(b_query), pad(b_value), jnp.zeros((14, width), bf16)], axis=0)
    (first_own, ordered_b, head_pack, w_outer, w_inner, w_output, b_inner, lengths, w_query, w_key, w_value) = tie(
        (first_own, ordered_b, head_pack, w_outer, w_inner, w_output, b_inner, lengths, w_query, w_key, w_value))
    vectors = (b_output, ln1_gain, ln1_shift, b_outer, ln2_gain, ln2_shift)
    vector_pack = jnp.concatenate([pad(b_inner)] + [pad(v) for v in vectors] + [jnp.zeros((25, width), bf16)], axis=0)
    layer_quarter = quarter(
        [w_outer] + [w_inner[:, n * width:(n + 1) * width] for n in range(4)] + [w_output, vector_pack])
    back_quarter = quarter([w_query, w_key, w_value, jnp.zeros((32, width), bf16)])
    slots = lax.dynamic_slice_in_dim(deal_order, lax.axis_index("z") * 2, 2)
    matches = slots[:, None] == jnp.arange(seq_count, dtype=jnp.int32)[None, :]
    lens = jnp.sum(jnp.where(matches, lengths[None, :], 0), axis=1).astype(jnp.int32)
    last = (lens + 511) // 512 - 1
    counts = 2 * last + 1 + (lens > 512 * last + 2 * stretch).astype(jnp.int32)
    infos = [jnp.stack([lens[n], x, y, c, counts[n]]).astype(jnp.int32) for n in range(2)]
    head_all = lax.all_gather(head_pack, SHARD, axis=0, tiled=False)
    head_weight = canonical_heads(head_all, shards, 1)

    def head_bias(row):
        heads = head_all[:, per + row, :per].reshape(2, 2, 3, HD)
        mine = lax.dynamic_slice(heads, (x, y, 0, 0), (1, 1, 3, HD))[0, 0]
        return [lax.dynamic_index_in_dim(mine, 2 * c, axis=0, keepdims=False), mine[1]]
    bias_row = jnp.concatenate(head_bias(0) + [jnp.zeros((2 * HD,), bf16)] + head_bias(1)).astype(f32)[None]

    across_a, along_a = lax.ppermute(first_own, "x", SWAP), lax.ppermute(first_own, "y", SWAP)
    second_own = deal(ordered_b)
    across_a, along_a, second_own, layer_quarter, back_quarter, *infos = tie(
        (across_a, along_a, second_own, layer_quarter, back_quarter, *infos))
    near_a = this_core(first_own, across_a, along_a, corner(across_a, along_a))
    across_b, along_b = lax.ppermute(second_own, "x", SWAP), lax.ppermute(second_own, "y", SWAP)
    near_a, across_b, along_b = tie((near_a, across_b, along_b))
    far_a = lax.ppermute(near_a, "c", SWAP)
    corner_b = corner(across_b, along_b)

    layer_all = lax.all_gather(layer_quarter, ALL, axis=0, tiled=True).reshape(shards, 9 * per + 32, width)
    layer_weights = canonical(layer_all, shards)
    inner_bias = layer_all[:, 9 * per, :4 * per].reshape(1, 4 * width).astype(f32)
    vector_rows = jnp.concatenate(
        [layer_all[:, 9 * per + 1 + n, :per].reshape(1, width) for n in range(6)] + [jnp.zeros((2, width), bf16)],
        axis=0).astype(f32)
    back_all = lax.all_gather(back_quarter, ALL, axis=0, tiled=True).reshape(shards, 3 * per + 32, width)

    def swap(array):
        flat = array.reshape((8,) + array.shape[2:])
        return lax.all_to_all(flat, PAIR, split_axis=0, concat_axis=0, tiled=True)

    def to_tokens(array):
        return swap(array).reshape((4, 2) + array.shape[2:])

    def to_heads(array):
        return swap(array).reshape((2, 4) + array.shape[2:])

    heads_a = project(near_a, far_a, head_weight, bias_row, infos[0])
    heads_a, *corner_b = tie((heads_a, *corner_b))
    near_b = this_core(second_own, across_b, along_b, corner_b)
    far_b = lax.ppermute(near_b, "c", SWAP)
    own_first, lse_own_a = attend_forward(False, 0, *heads_a, infos[0], None)
    own_first, far_b = tie((own_first, far_b))
    heads_b = project(near_b, far_b, head_weight, bias_row, infos[1])
    own, lse_own_b = attend_forward(False, 1, *heads_b, infos[1], own_first)
    own_t = to_tokens(own)
    own, info_a, info_b = tie((own, *infos))
    sh_first, lse_sh_a = attend_forward(True, 0, *heads_a, info_a, None)
    sh, lse_sh_b = attend_forward(True, 1, *heads_b, info_b, sh_first)
    sh_sent, own_t = tie((sh, own_t))
    sh_t = to_tokens(sh_sent)
    mine_rows = jnp.where(x == 0, jnp.stack([first_own, across_a]), jnp.stack([second_own, across_b]))[None]

    (act, resid, g_own, g_sh, active, d_inner, normed, d_outer, d_branch, vec_sums) = feed_forward(
        mine_rows, own_t, sh_t, cotangent.reshape(-1, width), layer_weights, inner_bias, vector_rows, infos[0])
    g_own_h, g_sh_h = to_heads(g_own), to_heads(g_sh)
    packed = weight_grads(scale, active, d_outer, normed, d_inner, own_t, sh_t, d_branch)
    sums = jnp.concatenate([vec_sums, jnp.zeros((16, width), f32)], axis=0) * scale
    ready = from_canonical(packed, sums.astype(bf16), shards)
    ready, back_all, g_own_h = tie((ready, back_all, g_own_h))
    back_weights = canonical_heads(back_all, shards, 3)
    layer_part = lax.psum_scatter(ready.reshape(-1, width), ("z", "x", "c"), scatter_dimension=0, tiled=True)

    qkv_a, qkv_b = heads_a[:3], heads_b[:3]
    first = attend_backward(False, 0, *qkv_a, lse_own_a, own, g_own_h, infos[0], None)
    dqkv_own, = attend_backward(False, 1, *qkv_b, lse_own_b, own, g_own_h, infos[1], first)
    back_own = to_tokens(dqkv_own)
    dqkv_own, info_a, info_b = tie((dqkv_own, *infos))
    first = attend_backward(True, 0, *qkv_a, lse_sh_a, sh, g_sh_h, info_a, None)
    dq_sh, kept, given = attend_backward(True, 1, *qkv_b, lse_sh_b, sh, g_sh_h, info_b, first)
    taken = lax.ppermute(given, "c", SWAP)
    shared_out = jnp.concatenate([(kept.astype(f32) + taken.astype(f32)).astype(bf16), dq_sh], axis=2)
    shared_out, back_own, dqkv_own = tie((shared_out, back_own, dqkv_own))
    back_shared = to_tokens(shared_out.reshape(2, 4, 3, 32, -1))
    d_heads, d_bias = head_grads(scale, (near_a, far_a, near_b, far_b), dqkv_own, dq_sh, kept, given, infos[0])

    head_ready = jnp.concatenate([
        d_heads.reshape(zs, 2, per, 384),
        jnp.broadcast_to(d_bias[:1].astype(bf16)[None, None], (zs, 2, 16, 384))], axis=2)
    head_ready, back_shared = tie((head_ready, back_shared))
    d_rows = token_grad(back_own, back_shared, back_weights, resid)
    if zs == 4:
        group = lax.axis_index("z")
        parts = [lax.dynamic_index_in_dim(head_ready, (group + k) % zs, axis=0, keepdims=False) for k in range(zs)]
        parts = parts[:1] + [
            lax.ppermute(parts[k], "z", [(i, (i + k) % zs) for i in range(zs)]) for k in range(1, zs)]
        head_sum = settle(parts, d_rows)
    else:
        head_sum = lax.psum_scatter(
            head_ready.reshape(-1, 384), "z", scatter_dimension=0, tiled=True).reshape(2, per + 16, 384)
    layer_part, _ = tie((layer_part, d_rows))
    layer_sum = (layer_part.astype(f32) + lax.ppermute(layer_part, "y", SWAP).astype(f32)).astype(bf16)
    returned = lax.all_to_all(
        d_rows.reshape(shards, stretch, width), SHARD, split_axis=0, concat_axis=0, tiled=True)

    def apart(array, bits):
        return lax.ppermute(array, PAIR, [(i, i ^ bits) for i in range(8)]) if bits else array

    halves = [lax.dynamic_index_in_dim(head_sum, x ^ k, axis=0, keepdims=False) for k in range(2)]
    head_eight = jnp.stack([apart(halves[bits >> 2], bits) for bits in range(8)])
    d_wq, d_wk, d_wv, d_bias_rows = head_unpack(head_eight, per, width, infos[0])
    place = lax.axis_index("z") * 2 + x
    own_slice = lambda row, n: lax.dynamic_slice_in_dim(row, place * n, n)
    d_bq, d_bv = own_slice(d_bias_rows[0], per), own_slice(d_bias_rows[1], per)

    layer_grads = flipped(jnp.stack([layer_sum, lax.ppermute(layer_sum, "c", SWAP)]), 0, c)
    layer_grads = layer_grads.reshape(9 * per + 32, width).astype(f32)
    d_wouter = layer_grads[:4 * per]
    d_winner = jnp.concatenate([layer_grads[(4 + n) * per:(5 + n) * per] for n in range(4)], axis=1)
    d_woutput = layer_grads[8 * per:9 * per]
    d_binner = own_slice(layer_grads[9 * per:9 * per + 4].reshape(-1), 4 * per)
    d_bo, d_g1, d_s1, d_bout, d_g2, d_s2 = (own_slice(layer_grads[9 * per + 4 + n], per) for n in range(6))
    small = (d_bq, d_bv, d_binner, d_bo, d_g1, d_s1, d_bout, d_g2, d_s2)
    returned = tie((returned, d_wouter, d_winner, d_woutput, d_wq, d_wk, d_wv) + small)[0]
    steps = jnp.arange(seq_count, dtype=jnp.int32)
    slot_of = jnp.sum(jnp.where(deal_order[:, None] == steps[None, :], steps[:, None], 0), axis=0)
    d_tokens = returned.at[slot_of].get(mode="promise_in_bounds")[:, None]
    return (act.reshape(1, shards, stretch, width), d_tokens, d_wq, d_wk, d_wv, d_woutput, d_bq, d_bv, d_bo,
            d_g1, d_s1, d_winner, d_binner, d_wouter, d_bout, d_g2, d_s2)


def solution(mesh):
    shards, splits = mesh.devices.shape
    fine = Mesh(mesh.devices.reshape(shards // 2, 2, splits // 2, 2), ALL)
    S, Q = SHARD, ("y", "c")
    row, mat = P(S), P(S, None)
    return jax.shard_map(
        body, mesh=fine,
        in_specs=(P(None, S, Q, None), P(), P(), mat, mat, mat, mat, row, row, row, row, row, mat, row, mat, row, row, row,
                  P(S, None, Q, None)),
        out_specs=(P(S, None, Q, None), P(None, S, Q, None), mat, mat, mat, mat, row, row, row, row, row, mat, row, mat,
                   row, row, row),
        check_vma=False)
```
